32 devices in a mesh: dp: 2 (over x), ctx: 4 (over y, core), exp: 4 (over z).
Axes of the slice: x: 2, y: 2, z: 4, core: 2. Of those that a mesh axis runs over, the one named last changes fastest.
Arguments:
- inputs: bfloat16 [8, 2048, 768], P(('dp', 'exp'), 'ctx'), may hold values from -6 to 6
- lengths: int32 [8, 2], P(('dp', 'exp')), may hold values from 1 to 1536, 2048 in all within a row
- block_order: int32 [8, 8], P(('dp', 'exp')), may hold values from 0 to 7, each once within a row
- routes: int32 [8, 2048, 2], P(('dp', 'exp'), 'ctx'), may hold values from 0 to 11, all different within a row; in each aligned block of 512 rows (0 to 511, 512 to 1023, ..., all dimensions but the last counted through in order) at most 128 rows name the same one
- prev_logits: float32 [8, 2048, 12], P(('dp', 'exp'), 'ctx'), may hold values from -6 to 6
- norm1_gain: float32 [768], replicated, may hold values from 0.5 to 1.5
- norm2_gain: float32 [768], replicated, may hold values from 0.5 to 1.5
- w_qkv: bfloat16 [3, 768, 768], replicated, may hold values from -0.3125 to 0.3125
- w_out: bfloat16 [768, 768], replicated, may hold values from -1.25 to 1.25
- w_router: float32 [768, 12], replicated, may hold values from -0.109375 to 0.109375
- w_carry: float32 [12, 12], replicated, may hold values from -0.875 to 0.875
- const_logit_w: float32 [2, 768, 2], replicated, may hold values from -0.21875 to 0.21875
- const_vec: float32 [2, 768], replicated, may hold values from -6 to 6
- w_gate: bfloat16 [8, 768, 2048], P('exp'), may hold values from -0.21875 to 0.21875
- w_up: bfloat16 [8, 768, 2048], P('exp'), may hold values from -0.21875 to 0.21875
- w_down: bfloat16 [8, 2048, 768], P('exp'), may hold values from -2 to 2
- cotangent: bfloat16 [8, 2048, 768], P(('dp', 'exp'), 'ctx'), may hold values from -6 to 6
Outputs:
- output: bfloat16 [8, 2048, 768], P(('dp', 'exp'), 'ctx')
- input_grad: float32 [8, 2048, 768], P(('dp', 'exp'), 'ctx')
- norm1_gain_grad: float32 [768], replicated
- norm2_gain_grad: float32 [768], replicated
- qkv_grad: float32 [3, 768, 768], replicated
- out_grad: float32 [768, 768], replicated
- router_grad: float32 [768, 12], replicated
- carry_grad: float32 [12, 12], replicated
- const_logit_grad: float32 [2, 768, 2], replicated
- const_vec_grad: float32 [2, 768], replicated
- gate_grad: float32 [8, 768, 2048], P('exp', None, 'dp')
- up_grad: float32 [8, 768, 2048], P('exp', None, 'dp')
- down_grad: float32 [8, 2048, 768], P('exp', 'dp')
- clipped_qk: float32 [2, 768, 768], replicated
The draws below stay inside these ranges and needn't reach their ends.
Inputs may be any that keep to these rules, and one draw needn't show every extreme that they name: Among the rows of one device no expert is named by more than 128 routes; a token's two experts differ. `lengths`: each row sums to 2048. `block_order`: each row is a permutation.
All inputs are finite; a program needn't handle non-finite values.
Results may differ from the reference program's by a relative error of at most 0.023.
Values may be sent and summed in bfloat16 or wider, within the bound.
A program may use at most 192 MiB of HBM per device.

```python
import functools
import math
import jax
import jax.numpy as jnp
import numpy as np
from jax import lax

D = 768
HEADS = 12
HEAD = 64
FF = 2048
EXPERTS = 8
ZERO_EXP = 4
ALL_EXP = 12
TOK_DEV = 512
SEQS = 2
CAP = 128
GROUP = 2048
PACKS = 8
NB = 8
N_CTX = 4


def levels(stream_key, shape, split, low, high):
    factor_of, own = 1.0, jax.random.fold_in(stream_key, 6)
    for dim, shards_of in split:
        heights = jnp.exp(jax.random.uniform(jax.random.fold_in(own, dim), (shards_of,), jnp.float32, low / len(split), high / len(split)))
        factor_of = factor_of * jnp.repeat(heights, shape[dim] // shards_of).reshape([-1 if axis == dim else 1 for axis in range(len(shape))])
    return factor_of


def profile(count, total, bound, slope):
    loads = [(1 << 20) // math.isqrt(standing ** slope) + 1 for standing in range(2, count + 1)]
    surplus, holding = total - bound - (count - 1), [1] * (count - 1)
    while surplus > 0:
        candidates = [i for i in range(count - 1) if holding[i] < bound]
        pool, budget = sum([loads[i] for i in candidates]), surplus
        for i in candidates:
            extra = min(bound - holding[i], max(1, budget * loads[i] // pool), surplus)
            holding[i] = holding[i] + extra
            surplus = surplus - extra
    return np.array([bound] + holding)


def ragged_sizes(own_key, amount, total, most, lean):
    if amount == 2:
        one = jax.random.randint(own_key, (), max(1, total - most), min(most, total - 1) + 1)
        return jnp.stack([one, total - one])
    sizes = jnp.asarray(profile(amount, total, most, lean), jnp.int32)
    couples = (amount - 1) // 2
    source_of, taker = sizes[1:1 + 2 * couples:2], sizes[2:2 + 2 * couples:2]
    room = jnp.minimum(source_of - 1, most - taker)
    shifted = jax.random.randint(jax.random.fold_in(own_key, 1), (couples,), 0, 1 << 20) % (room + 1)
    sizes = sizes.at[1:1 + 2 * couples:2].set(source_of - shifted).at[2:2 + 2 * couples:2].set(taker + shifted)
    return sizes[jax.random.permutation(jax.random.fold_in(own_key, 2), amount)]


def assign_block(stream_key, own, number, rows, number_of, top, reach, skew):
    order = jax.random.permutation(stream_key, number_of)
    heavy_load, usual = portions_of(number_of, rows * top, reach, skew, True), portions_of(number_of, rows * top, reach, skew, False)
    places = jnp.arange(number_of)

    def named(tallies, rotation):
        used = int((tallies > 0).sum())
        fixed = max(1, used // 4)
        passed = fixed + (places - fixed + rotation * (used - fixed)) % max(1, number_of - fixed)
        return jnp.zeros((number_of,), jnp.int32).at[order[jnp.where(places < fixed, places, passed)]].set(jnp.asarray(tallies, jnp.int32))

    tallies = jnp.where(number % 4 == 0, named(heavy_load, number // 4), named(usual, number - number // 4 - 1))
    mixed = jax.random.permutation(jax.random.fold_in(own, 3), number_of)
    source_of, sink = mixed[0:number_of // 2 * 2:2], mixed[1:number_of // 2 * 2:2]
    margin = jnp.minimum(tallies[source_of] - 1, reach - tallies[sink]) // 2
    margin = jnp.where((source_of == order[0]) | (sink == order[0]) | (tallies[sink] == 0), 0, jnp.maximum(margin, 0))
    passed = jax.random.randint(jax.random.fold_in(own, 4), (number_of // 2,), 0, 1 << 20) % (margin + 1)
    tallies = tallies.at[source_of].add(-passed).at[sink].add(passed)
    labels = jnp.searchsorted(jnp.cumsum(tallies), jnp.arange(rows * top), side="right").astype(jnp.int32)
    table = labels.reshape(top, rows).T
    table = table[jax.random.permutation(jax.random.fold_in(own, 1), rows)]
    rotation = jax.random.randint(jax.random.fold_in(own, 2), (rows, 1), 0, top)
    return jnp.take_along_axis(table, (jnp.arange(top)[None, :] + rotation) % top, axis=1)


def portions_of(amount, total, bound, skew, full):
    loads = [(1 << 20) // math.isqrt(rank ** skew) + 1 for rank in range(1, amount + 1)]
    largest = bound if full else min(bound, max(-(-total // amount), total * loads[0] // sum(loads)))
    least = 1 if total - largest >= amount - 1 else 0
    holding, surplus = [largest] + [least] * (amount - 1), total - largest - least * (amount - 1)
    while surplus > 0:
        free = [i for i in range(1, amount) if holding[i] < largest] or [i for i in range(1, amount) if holding[i] < bound]
        whole, left = sum([loads[i] for i in free]), surplus
        for i in free:
            more = min(bound - holding[i], max(1, left * loads[i] // whole), surplus)
            holding[i] = holding[i] + more
            surplus = surplus - more
    return np.array(holding)


def centred(key, extent, width, most, split=(), held_as=jnp.bfloat16):
    drawn = jax.random.normal(key, extent, jnp.float32) * width
    if len(split) > 0:
        drawn = levels(key, extent, split, -0.22, 0.18) * drawn
    return jnp.clip(drawn, min=-most, max=most).astype(held_as)


def setup_inputs(seed: int = 0) -> dict:
    splits = jax.random.split(jax.random.key(seed), 18)
    inputs = centred(splits[0], (PACKS, GROUP, D), 1.0, 6.0, ((0, 8), (1, 4)))
    lengths = jax.vmap(lambda own: ragged_sizes(own, SEQS, GROUP, 3 * GROUP // 4, 2))(jax.random.split(splits[1], PACKS)).reshape((PACKS, SEQS)).astype(jnp.int32)
    block_order = jax.vmap(lambda own: jax.random.permutation(own, NB))(jax.random.split(splits[2], PACKS)).reshape((PACKS, NB)).astype(jnp.int32)
    routes_keys = jax.random.split(jax.random.fold_in(splits[3], 1), PACKS * GROUP // TOK_DEV)
    routes_turns = jax.random.permutation(jax.random.fold_in(splits[3], 3), PACKS * GROUP // TOK_DEV)
    routes = jax.vmap(lambda own, number: assign_block(jax.random.fold_in(splits[3], 2), own, number, TOK_DEV, ALL_EXP, 2, CAP, 1))(routes_keys, routes_turns).reshape((PACKS, GROUP, 2))
    prev_logits = centred(splits[4], (PACKS, GROUP, ALL_EXP), 1.0, 6.0, ((0, 8), (1, 4)), jnp.float32)
    norm1_gain = jnp.clip(1.0 + 0.1 * jax.random.normal(splits[5], (D,), jnp.float32), 0.5, 1.5)
    norm2_gain = jnp.clip(1.0 + 0.1 * jax.random.normal(splits[6], (D,), jnp.float32), 0.5, 1.5)
    w_qkv = centred(splits[7], (3, D, D), (D // 2) ** -0.5, 0.3125)
    w_out = centred(splits[8], (D, D), (D // 32) ** -0.5, 1.25)
    w_router = centred(splits[9], (D, ALL_EXP), (4 * D) ** -0.5, 0.109375, (), jnp.float32)
    w_carry = centred(splits[10], (ALL_EXP, ALL_EXP), (4 * ALL_EXP) ** -0.5, 0.875, (), jnp.float32)
    const_logit_w = centred(splits[11], (ZERO_EXP - 2, D, 2), D ** -0.5, 0.21875, (), jnp.float32)
    const_vec = centred(splits[12], (ZERO_EXP - 2, D), 1.0, 6.0, (), jnp.float32)
    w_gate = centred(splits[13], (EXPERTS, D, FF), D ** -0.5, 0.21875, ((0, 4),))
    w_up = centred(splits[14], (EXPERTS, D, FF), D ** -0.5, 0.21875, ((0, 4),))
    w_down = centred(splits[15], (EXPERTS, FF, D), (max(FF // 256, 1)) ** -0.5, 2.0, ((0, 4),))
    cotangent = centred(splits[16], (PACKS, GROUP, D), 1.0, 6.0, ((0, 8), (1, 4)))
    return {"inputs": inputs, "lengths": lengths, "block_order": block_order, "routes": routes, "prev_logits": prev_logits, "norm1_gain": norm1_gain, "norm2_gain": norm2_gain, "w_qkv": w_qkv, "w_out": w_out, "w_router": w_router, "w_carry": w_carry, "const_logit_w": const_logit_w, "const_vec": const_vec, "w_gate": w_gate, "w_up": w_up, "w_down": w_down, "cotangent": cotangent}


@jax.custom_vjp
def low(v):
    return lax.optimization_barrier(v.astype(jnp.bfloat16)).astype(jnp.float32)

@jax.custom_vjp
def low_back(v):
    return v

def low_keep(v):
    return (low(v), None)

def low_pass(kept, grad):
    return (grad,)

def back_keep(v):
    return (v, None)

def back_low(kept, grad):
    return (low(grad),)
low.defvjp(low_keep, low_pass)
low_back.defvjp(back_keep, back_low)
norm_eps = 1e-05
clip_limit = 3.0
mask_fill = -1e+30
highest = lax.Precision.HIGHEST

def normalize(values, gain):
    return values * lax.rsqrt(lax.optimization_barrier(jnp.mean(values * values, axis=-1, keepdims=True)) + norm_eps) * gain

def positions(order_row, length_row, deal_block):
    offsets = lax.broadcasted_iota(jnp.int32, (order_row.shape[0], deal_block), 1)
    position = (order_row[:, None] * deal_block + offsets).reshape(-1).astype(jnp.int32)
    ends = jnp.cumsum(length_row).astype(jnp.int32)
    document = lax.optimization_barrier(jnp.sum((position[:, None] >= ends[None, :]).astype(jnp.int32), axis=1)).astype(jnp.int32)
    return (position, document)

def attend_pack(query_rows, key_rows, value_rows, position, document):
    group_rows = query_rows.shape[0]
    block_rows = min(512, group_rows)
    shaped = (group_rows, HEADS, HEAD)
    key_heads = key_rows.reshape(shaped)
    value_heads = value_rows.reshape(shaped)
    query_blocks = query_rows.reshape(group_rows // block_rows, block_rows, HEADS, HEAD)
    pos_blocks = position.reshape(group_rows // block_rows, block_rows)
    doc_blocks = document.reshape(group_rows // block_rows, block_rows)

    def score_rows(block_items):
        query_block, pos_block, doc_block = block_items
        raw = jnp.einsum('qhd,khd->hqk', query_block, key_heads, precision=highest) * HEAD ** (-0.5)
        raw = low_back(raw)
        allowed = (position[None, :] <= pos_block[:, None]) & (document[None, :] == doc_block[:, None])
        masked = jnp.where(allowed[None], raw, mask_fill)
        row_max = lax.optimization_barrier(jnp.max(masked, axis=2, keepdims=True))
        log_total = row_max + jnp.log(lax.optimization_barrier(jnp.sum(jnp.exp(masked - row_max), axis=2, keepdims=True)))
        probability = low(jnp.where(allowed[None], jnp.exp(masked - log_total), 0.0))
        mixed = jnp.einsum('hqk,khd->qhd', probability, value_heads, precision=highest)
        return (mixed.reshape(block_rows, HEADS * HEAD), lax.optimization_barrier(jnp.max(row_max[:, :, 0], axis=1)))
    mixed, head_tops = lax.map(jax.checkpoint(score_rows), (query_blocks, pos_blocks, doc_blocks))
    return (mixed.reshape(group_rows, HEADS * HEAD), lax.optimization_barrier(jnp.max(head_tops, axis=0)))

def reference(inputs, lengths, block_order, routes, prev_logits, norm1_gain, norm2_gain, w_qkv, w_out, w_router, w_carry, const_logit_w, const_vec, w_gate, w_up, w_down, cotangent):
    packs, group_rows, model_width = inputs.shape
    tokens = packs * group_rows
    deal_block = group_rows // block_order.shape[1]
    position, document = jax.vmap(functools.partial(positions, deal_block=deal_block))(block_order, lengths)
    route_ids = routes.reshape(tokens, 2)
    route_flat = route_ids.reshape(-1)
    route_count = route_flat.shape[0]
    slot_bound = packs * N_CTX * CAP
    table = jnp.stack([jnp.nonzero(route_flat == expert_id, size=slot_bound, fill_value=route_count)[0].astype(jnp.int32) for expert_id in range(EXPERTS)])
    slot_target = jnp.full((route_count + 1,), EXPERTS * slot_bound, jnp.int32).at[table.reshape(-1)].set(lax.iota(jnp.int32, EXPERTS * slot_bound))[:route_count]
    expert_iota = jnp.arange(ALL_EXP, dtype=jnp.int32)
    picked = (route_ids[:, :, None] == expert_iota[None, None, :]).astype(jnp.float32)
    is_copy = (route_ids == EXPERTS + 1).astype(jnp.float32)
    const_ids = EXPERTS + 2 + jnp.arange(const_vec.shape[0], dtype=jnp.int32)
    is_const = (route_ids[:, :, None] == const_ids[None, None, :]).astype(jnp.float32)
    previous = prev_logits.reshape(tokens, ALL_EXP)

    def forward(residual_in, first_gain, second_gain, qkv_mat, out_mat, router_mat, carry_mat, score_mat, const_rows, gate_mats, up_mats, down_mats):
        first_low = low(normalize(residual_in, first_gain))
        projected = [low_back(low(jnp.dot(first_low, qkv_mat[which], precision=highest))) for which in range(3)]
        shaped = [piece_rows.reshape(packs, group_rows, model_width) for piece_rows in projected]
        mixed, head_tops = lax.map(lambda block_items: attend_pack(*block_items), (shaped[0], shaped[1], shaped[2], position, document))
        attended = low_back(low(mixed.reshape(tokens, model_width)))
        after_attn = residual_in + low_back(jnp.dot(attended, out_mat, precision=highest))
        second_normed = normalize(after_attn, second_gain)
        logits = jnp.dot(second_normed, router_mat, precision=highest) + jnp.dot(previous, carry_mat, precision=highest)
        probability = jax.nn.softmax(logits, axis=-1)
        gate_values = lax.optimization_barrier(jnp.sum(picked * probability[:, None, :], axis=2))
        padded = jnp.concatenate([low(second_normed), jnp.zeros((1, model_width), jnp.float32)], axis=0)

        def expert(block_items):
            gate_mat, up_mat, down_mat, slot_rows = block_items
            gathered = low_back(padded[slot_rows // 2])
            gate_pre = low_back(jnp.dot(gathered, gate_mat, precision=highest))
            up_pre = low_back(jnp.dot(gathered, up_mat, precision=highest))
            hidden = low(jax.nn.silu(gate_pre) * up_pre)
            return low_back(low(jnp.dot(hidden, down_mat, precision=highest)))
        produced = lax.map(jax.checkpoint(expert), (gate_mats, up_mats, down_mats, table))
        produced = jnp.concatenate([produced.reshape(EXPERTS * slot_bound, model_width), jnp.zeros((1, model_width), jnp.float32)], axis=0)
        routed = produced[slot_target].reshape(tokens, 2, model_width)
        mix_weight = jax.nn.softmax(jnp.einsum('td,cde->tce', second_normed, score_mat, precision=highest), axis=-1)
        const_out = mix_weight[:, :, 0:1] * second_normed[:, None, :] + mix_weight[:, :, 1:2] * const_rows[None]
        branch = routed + is_copy[:, :, None] * second_normed[:, None, :] + jnp.einsum('tkc,tcd->tkd', is_const, const_out, precision=highest)
        result = after_attn + lax.optimization_barrier(jnp.sum(gate_values[:, :, None] * branch, axis=1))
        return (result, lax.optimization_barrier(jnp.max(head_tops, axis=0)))
    floats = (inputs.reshape(tokens, model_width).astype(jnp.float32), norm1_gain, norm2_gain, w_qkv.astype(jnp.float32), w_out.astype(jnp.float32), w_router, w_carry, const_logit_w, const_vec, w_gate.astype(jnp.float32), w_up.astype(jnp.float32), w_down.astype(jnp.float32))
    result, pullback, head_max = jax.vjp(forward, *floats, has_aux=True)
    grads = pullback(cotangent.reshape(tokens, model_width).astype(jnp.float32))
    clip_ratio = jnp.sqrt(jnp.minimum(1.0, clip_limit / head_max))
    head_scale = jnp.repeat(clip_ratio, HEAD)
    clipped = floats[3][:2] * head_scale[None, None, :]
    output = result.reshape(packs, group_rows, model_width).astype(jnp.bfloat16)
    input_grad = grads[0].reshape(packs, group_rows, model_width)
    return (output, input_grad, grads[1], grads[2], grads[3], grads[4], grads[5], grads[6], grads[7], grads[8], grads[9], grads[10], grads[11], clipped)
```

```python
import functools

import jax
import jax.numpy as jnp
from jax import lax
from jax.experimental import pallas as pl
from jax.experimental.pallas import tpu as pltpu
from jax.sharding import PartitionSpec as P

HEADS = 12
CAP = 128

norm_eps = 1e-05
clip_limit = 3.0
low_start = -1e30
mask_fill = -3e38
highest = lax.Precision.HIGHEST
NN = (((1,), (0,)), ((), ()))
NT = (((1,), (1,)), ((), ()))
TN = (((0,), (0,)), ((), ()))
f32 = jnp.float32
bf16 = jnp.bfloat16


def mm(left, right, dims=NN):
    return lax.dot_general(left, right, dims, preferred_element_type=f32)


def mm_full(left, right, dims=NN):
    return lax.dot_general(left, right, dims, precision=highest, preferred_element_type=f32)


def shape_of(shape, dtype):
    return jax.ShapeDtypeStruct(shape, dtype)


def whole(array):
    rank = len(array.shape)
    return pl.BlockSpec(array.shape, lambda *_: (0,) * rank)


def cost(flops, moved, exps=0):
    return pl.CostEstimate(flops=int(flops), bytes_accessed=int(moved), transcendentals=int(exps))


def run(body, grid, inputs, outputs, scratch=(), meta=None, flops=0, moved=0, exps=0, aliases=None):
    prefetch = 0 if meta is None else 1
    args = ([] if meta is None else [meta]) + [a for a, _ in inputs]
    return pl.pallas_call(
        body,
        out_shape=[o for o, _ in outputs],
        grid_spec=pltpu.PrefetchScalarGridSpec(
            num_scalar_prefetch=prefetch,
            grid=grid,
            in_specs=[s for _, s in inputs],
            out_specs=[s for _, s in outputs],
            scratch_shapes=list(scratch),
        ),
        compiler_params=pltpu.CompilerParams(
            dimension_semantics=("arbitrary",) * len(grid), vmem_limit_bytes=60 * 1024 * 1024
        ),
        cost_estimate=cost(flops, moved, exps),
        input_output_aliases={} if aliases is None else aliases,
    )(*args)


def swap(value, axis, distance):
    count = lax.axis_size(axis)
    return lax.ppermute(value, axis, [(i, i ^ distance) for i in range(count)])


def gather_near(value, axis):
    count = lax.axis_size(axis)
    found = {0: value}
    bit = count // 2
    while bit:
        for have in list(found):
            found[have | bit] = swap(found[have], axis, bit)
        bit //= 2
    return [found[j] for j in range(count)]


def butterfly(value, combine):
    for axis in ("ctx", "dp", "exp"):
        bit = 1
        while bit < lax.axis_size(axis):
            value = combine(value, swap(value, axis, bit))
            bit *= 2
    return value


def pick(stacked, index):
    return lax.dynamic_index_in_dim(stacked, index, 0, keepdims=False)


def add_low(*terms):
    total = terms[0].astype(f32)
    for term in terms[1:]:
        total = total + term.astype(f32)
    return total.astype(bf16)


def project(turn, rows_low, gain, weights_t, meta, earlier, group_rows):
    row_count, width = rows_low.shape
    per_group = weights_t.shape[2]
    head_width = width // HEADS
    heads = per_group // head_width
    tile = min(256, row_count)
    steps = row_count // tile
    scale = head_width**-0.5

    def body(meta_ref, x_ref, gain_ref, w_ref, *refs):
        q_ref, k_ref, v_ref, kt_ref, vt_ref, h_ref = refs[-6:]
        x = x_ref[...].astype(f32)
        inverse = lax.rsqrt(jnp.mean(x * x, axis=1, keepdims=True) + norm_eps)
        low = (x * inverse * gain_ref[...]).astype(bf16)
        h_ref[...] = low
        q = mm(low, w_ref[0, 0], NT).astype(bf16) * jnp.asarray(scale, bf16)
        k = mm(low, w_ref[1, 0], NT).astype(bf16)
        v = mm(low, w_ref[2, 0], NT).astype(bf16)
        for h in range(heads):
            part = slice(h * head_width, (h + 1) * head_width)
            q_ref[h] = q[:, part]
            k_ref[h] = k[:, part]
            v_ref[h] = v[:, part]
        kt_ref[...] = mm(w_ref[1, 0], low, NT).astype(bf16)
        vt_ref[...] = mm(w_ref[2, 0], low, NT).astype(bf16)

    by_head = shape_of((heads, group_rows, head_width), bf16)
    by_column = shape_of((per_group, group_rows), bf16)
    hidden = shape_of((group_rows, width), bf16)
    head_spec = pl.BlockSpec((heads, tile, head_width), lambda i, m: (0, turn * steps + i, 0))
    column_spec = pl.BlockSpec((per_group, tile), lambda i, m: (0, turn * steps + i))
    hidden_spec = pl.BlockSpec((tile, width), lambda i, m: (turn * steps + i, 0))
    inputs = [
        (rows_low, pl.BlockSpec((tile, width), lambda i, m: (i, 0))),
        (gain, pl.BlockSpec((1, width), lambda i, m: (0, 0))),
        (weights_t, pl.BlockSpec((3, 1, per_group, width), lambda i, m: (0, m[0], 0, 0))),
    ]
    aliases = None
    if earlier is not None:
        inputs += [(a, pl.BlockSpec(memory_space=pl.ANY)) for a in earlier]
        aliases = {4 + n: n for n in range(6)}
    return run(
        body,
        (steps,),
        inputs,
        [(by_head, head_spec)] * 3 + [(by_column, column_spec)] * 2 + [(hidden, hidden_spec)],
        meta=meta,
        flops=2 * row_count * width * per_group * 5,
        moved=row_count * width * 8 + weights_t.size // 2,
        aliases=aliases,
    )


def block_place(meta_ref, block, per_member, layout):
    member = meta_ref[0] ^ (block // per_member)
    return meta_ref[layout["order"] + member * per_member + block % per_member]


def document_start(meta_ref, position, layout):
    start = jnp.zeros_like(position)
    end = jnp.int32(0)
    for s in range(layout["sequences"]):
        end = end + meta_ref[layout["lengths"] + s]
        start = jnp.where(position >= end, end, start)
    return start


def block_range(meta_ref, query_block, key_block, rows, per_member, layout):
    q_first = block_place(meta_ref, query_block, per_member, layout) * rows
    k_first = block_place(meta_ref, key_block, per_member, layout) * rows
    begin = document_start(meta_ref, q_first, layout)
    begin_last = document_start(meta_ref, q_first + rows - 1, layout)
    needed = (k_first <= q_first) & (k_first + rows - 1 >= begin)
    full = (k_first < q_first) & (k_first >= begin_last)
    return q_first, k_first, needed, full


def allowed_pairs(meta_ref, q_first, k_first, rows, layout):
    q_pos = q_first + lax.broadcasted_iota(jnp.int32, (1, rows), 1)
    k_pos = k_first + lax.broadcasted_iota(jnp.int32, (rows, 1), 0)
    return (k_pos <= q_pos) & (k_pos >= document_start(meta_ref, q_pos, layout))


def attend(meta, q, k, vt, rows, per_member, layout):
    heads, group_rows, head_width = q.shape
    blocks = group_rows // rows
    width = heads * head_width

    def body(meta_ref, q_ref, k_ref, vt_ref, o_ref, ot_ref, lse_ref, top_ref, m_ref, l_ref, a_ref):
        i = pl.program_id(0)
        m_ref[...] = jnp.full_like(m_ref, low_start)
        l_ref[...] = jnp.zeros_like(l_ref)
        a_ref[...] = jnp.zeros_like(a_ref)

        def one(j, _):
            q_first, k_first, needed, full = block_range(meta_ref, i, j, rows, per_member, layout)
            at = pl.multiple_of(j * rows, rows)

            def step(masked):
                if masked:
                    allowed = allowed_pairs(meta_ref, q_first, k_first, rows, layout)
                for h in range(heads):
                    part = slice(h * head_width, (h + 1) * head_width)
                    s = mm(k_ref[h, pl.ds(at, rows), :], q_ref[h], NT)
                    if masked:
                        s = jnp.where(allowed, s, mask_fill)
                    old = m_ref[h]
                    new = jnp.maximum(old, jnp.max(s, axis=0, keepdims=True))
                    shrink = jnp.exp(old - new)
                    p = jnp.exp(s - new)
                    m_ref[h] = new
                    l_ref[h] = l_ref[h] * shrink + jnp.sum(p, axis=0, keepdims=True)
                    a_ref[part, :] = a_ref[part, :] * shrink + mm(
                        vt_ref[part, pl.ds(at, rows)], p.astype(bf16)
                    )

            @pl.when(full)
            def _():
                step(False)

            @pl.when(needed & jnp.logical_not(full))
            def _():
                step(True)

            return 0

        lax.fori_loop(0, blocks, one, 0)
        for h in range(heads):
            part = slice(h * head_width, (h + 1) * head_width)
            ot_ref[part, :] = a_ref[part, :] / l_ref[h]
            lse_ref[pl.ds(h, 1), :] = m_ref[h] + jnp.log(l_ref[h])
            top_ref[pl.ds(h, 1), :] = m_ref[h]
        o_ref[...] = jnp.transpose(ot_ref[...]).astype(bf16)

    row = shape_of((heads, group_rows), f32)
    row_spec = pl.BlockSpec((heads, rows), lambda i, m: (0, i))
    return run(
        body,
        (blocks,),
        [
            (q, pl.BlockSpec((heads, rows, head_width), lambda i, m: (0, i, 0))),
            (k, whole(k)),
            (vt, whole(vt)),
        ],
        [
            (shape_of((group_rows, width), bf16), pl.BlockSpec((rows, width), lambda i, m: (i, 0))),
            (shape_of((width, group_rows), f32), pl.BlockSpec((width, rows), lambda i, m: (0, i))),
            (row, row_spec),
            (row, row_spec),
        ],
        scratch=[
            pltpu.VMEM((heads, 1, rows), f32),
            pltpu.VMEM((heads, 1, rows), f32),
            pltpu.VMEM((width, rows), f32),
        ],
        meta=meta,
        flops=2 * 2 * group_rows * group_rows * width,
        moved=group_rows * width * 14,
        exps=group_rows * group_rows * heads // 2,
    )


def attend_back(meta, q, k, v, kt, grad, ot, lse, rows, per_member, layout):
    heads, group_rows, head_width = q.shape
    blocks = group_rows // rows
    width = heads * head_width
    scale = head_width**-0.5
    members = len(grad)
    per = grad[0].shape[0] // rows

    def body(meta_ref, q_ref, k_ref, v_ref, kt_ref, *refs):
        grads = refs[:members]
        ot_ref, lse_ref, out_ref, dk_ref, dv_ref, dq_ref, g_ref, delta_ref = refs[members:]
        i = pl.program_id(0)

        @pl.when(i == 0)
        def _():
            dk_ref[...] = jnp.zeros_like(dk_ref)
            dv_ref[...] = jnp.zeros_like(dv_ref)

        for n in range(members):

            @pl.when(i // per == n)
            def _():
                g = grads[n][...]
                for h in range(heads):
                    g_ref[h] = g[:, h * head_width : (h + 1) * head_width]
                product = jnp.transpose(g.astype(f32)) * ot_ref[...]
                for h in range(heads):
                    part = slice(h * head_width, (h + 1) * head_width)
                    delta_ref[h] = jnp.sum(product[part, :], axis=0, keepdims=True)

        dq_ref[...] = jnp.zeros_like(dq_ref)

        def one(j, _):
            q_first, k_first, needed, full = block_range(meta_ref, i, j, rows, per_member, layout)
            at = pl.multiple_of(j * rows, rows)

            def step(masked):
                if masked:
                    allowed = allowed_pairs(meta_ref, q_first, k_first, rows, layout)
                for h in range(heads):
                    part = slice(h * head_width, (h + 1) * head_width)
                    s = mm(k_ref[h, pl.ds(at, rows), :], q_ref[h], NT)
                    if masked:
                        s = jnp.where(allowed, s, mask_fill)
                    p = jnp.exp(s - lse_ref[pl.ds(h, 1), :])
                    dp = mm(v_ref[h, pl.ds(at, rows), :], g_ref[h], NT)
                    ds = (p * (dp - delta_ref[h])).astype(bf16)
                    dv_ref[h, pl.ds(at, rows), :] += mm(p.astype(bf16), g_ref[h])
                    dk_ref[h, pl.ds(at, rows), :] += mm(ds, q_ref[h])
                    dq_ref[part, :] += mm(kt_ref[part, pl.ds(at, rows)], ds)

            @pl.when(full)
            def _():
                step(False)

            @pl.when(needed & jnp.logical_not(full))
            def _():
                step(True)

            return 0

        lax.fori_loop(0, blocks, one, 0)
        here = pl.multiple_of(i * rows, rows)
        out_ref[pl.ds(here, rows), 0:width] = (jnp.transpose(dq_ref[...]) * scale).astype(bf16)

        @pl.when(i == blocks - 1)
        def _():
            def store(b, _):
                spot = pl.multiple_of(b * rows, rows)
                out_ref[pl.ds(spot, rows), width : 3 * width] = jnp.concatenate(
                    [dk_ref[h, pl.ds(spot, rows), :] for h in range(heads)]
                    + [dv_ref[h, pl.ds(spot, rows), :] for h in range(heads)],
                    axis=1,
                ).astype(bf16)
                return 0

            lax.fori_loop(0, blocks, store, 0)

    grad_specs = [
        pl.BlockSpec((rows, width), lambda i, m, n=n: (jnp.clip(i - n * per, 0, per - 1), 0))
        for n in range(members)
    ]
    out = shape_of((group_rows, 3 * width), bf16)
    return run(
        body,
        (blocks,),
        [
            (q, pl.BlockSpec((heads, rows, head_width), lambda i, m: (0, i, 0))),
            (k, whole(k)),
            (v, whole(v)),
            (kt, whole(kt)),
        ]
        + list(zip(grad, grad_specs))
        + [
            (ot, pl.BlockSpec((width, rows), lambda i, m: (0, i))),
            (lse, pl.BlockSpec((heads, rows), lambda i, m: (0, i))),
        ],
        [(out, whole(out))],
        scratch=[
            pltpu.VMEM((heads, group_rows, head_width), f32),
            pltpu.VMEM((heads, group_rows, head_width), f32),
            pltpu.VMEM((width, rows), f32),
            pltpu.VMEM((heads, rows, head_width), bf16),
            pltpu.VMEM((heads, 1, rows), f32),
        ],
        meta=meta,
        flops=5 * 2 * group_rows * group_rows * width,
        moved=group_rows * width * 24,
        exps=group_rows * group_rows * heads // 2,
    )[0]


def slot_targets(route_ids, expert_count, local_experts, mine):
    rows = route_ids.shape[0]
    groups = expert_count // local_experts
    experts = jnp.arange(expert_count, dtype=jnp.int32)
    hits = route_ids[:, :, None] == experts[None, None, :]
    hit = jnp.any(hits, axis=1)
    order = lax.broadcasted_iota(jnp.int32, (rows, rows), 0)
    other = lax.broadcasted_iota(jnp.int32, (rows, rows), 1)
    ahead = mm((other < order).astype(bf16), hit.astype(bf16)).astype(jnp.int32)
    rank = jnp.sum(jnp.where(hits, ahead[:, None, :], 0), axis=2)
    near = (route_ids // local_experts) ^ mine
    slot = (route_ids % local_experts) * (groups * CAP) + near * CAP + rank
    return jnp.where(route_ids < expert_count, slot, -1)


def slot_choice(first, count, target_ref):
    rows = target_ref.shape[1]
    ids = first + lax.broadcasted_iota(jnp.int32, (count, rows), 0)
    match = (ids == target_ref[0:1, :]) | (ids == target_ref[1:2, :])
    return jnp.where(match, 1.0, 0.0).astype(bf16)


def dispatch(target_rows, source, slots, pieces):
    rows, width = source.shape
    tile = 2 * CAP
    per_piece = slots // pieces

    def body(target_ref, source_ref, *outs):
        for n in range(pieces):
            for t in range(per_piece // tile):
                choice = slot_choice(n * per_piece + t * tile, tile, target_ref)
                outs[n][t * tile : (t + 1) * tile, :] = mm(choice, source_ref[...]).astype(bf16)

    out = shape_of((per_piece, width), bf16)
    return run(
        body,
        (1,),
        [(target_rows, whole(target_rows)), (source, whole(source))],
        [(out, whole(out))] * pieces,
        flops=2 * rows * width * slots,
        moved=(rows + slots) * width * 2,
    )


def token_front(meta, x, o_near, w_out, gain, w_router, previous, w_carry, target_rows, local, groups):
    rows, width = x.shape
    members = len(o_near)
    head_columns = o_near[0].shape[1]
    expert_all = w_router.shape[1]
    tile = 128
    steps = rows // tile
    per_piece = groups * CAP

    def body(meta_ref, x_ref, *refs):
        o_refs = refs[:members]
        w_refs = refs[members : 2 * members]
        gain_ref, router_ref, prev_ref, carry_ref, target_ref = refs[2 * members : 2 * members + 5]
        x1_ref, h2_ref, prob_ref, gates_ref = refs[2 * members + 5 : 2 * members + 9]
        piece_refs = refs[2 * members + 9 : 2 * members + 9 + local]
        low_ref, split_ref = refs[2 * members + 9 + local :]
        i = pl.program_id(0)
        total = x_ref[...].astype(f32)
        for n in range(members):
            total = total + mm(o_refs[n][...], w_refs[n][0])
        x1_ref[...] = total
        inverse = lax.rsqrt(jnp.mean(total * total, axis=1, keepdims=True) + norm_eps)
        h2 = total * inverse * gain_ref[...]
        h2_ref[...] = h2
        logits = mm_full(h2, router_ref[...]) + mm_full(prev_ref[...], carry_ref[...])
        shifted = jnp.exp(logits - jnp.max(logits, axis=1, keepdims=True))
        prob = shifted / jnp.sum(shifted, axis=1, keepdims=True)
        prob_ref[...] = prob
        here = pl.multiple_of(i * tile, tile)
        low_ref[pl.ds(here, tile), :] = h2.astype(bf16)
        top = prob.astype(bf16)
        rest = prob - top.astype(f32)
        middle = rest.astype(bf16)
        last = (rest - middle.astype(f32)).astype(bf16)
        split_ref[0, pl.ds(here, tile), :] = top
        split_ref[1, pl.ds(here, tile), :] = middle
        split_ref[2, pl.ds(here, tile), :] = last

        @pl.when(i == steps - 1)
        def _():
            diagonal = lax.broadcasted_iota(jnp.int32, (CAP, CAP), 0) == lax.broadcasted_iota(
                jnp.int32, (CAP, CAP), 1
            )
            lanes = lax.broadcasted_iota(jnp.int32, (CAP, expert_all), 1)
            for n in range(local):
                for g in range(groups):
                    choice = slot_choice(n * per_piece + g * CAP, CAP, target_ref)
                    piece_refs[n][g * CAP : (g + 1) * CAP, :] = mm(choice, low_ref[...]).astype(
                        bf16
                    )
                    picked = (
                        mm(choice, split_ref[0]) + mm(choice, split_ref[1]) + mm(choice, split_ref[2])
                    )
                    expert = (meta_ref[1] ^ g) * local + n
                    column = jnp.sum(
                        jnp.where(lanes == expert, picked, 0.0), axis=1, keepdims=True
                    )
                    gates_ref[n * groups + g : n * groups + g + 1, :] = jnp.sum(
                        jnp.where(diagonal, column, 0.0), axis=0, keepdims=True
                    )

    row_spec = pl.BlockSpec((tile, width), lambda i, m: (i, 0))
    wide = shape_of((rows, width), f32)
    small = shape_of((rows, expert_all), f32)
    small_spec = pl.BlockSpec((tile, expert_all), lambda i, m: (i, 0))
    gates = shape_of((local * groups, CAP), f32)
    piece = shape_of((per_piece, width), bf16)
    return run(
        body,
        (steps,),
        [(x, row_spec)]
        + [(o, pl.BlockSpec((tile, head_columns), lambda i, m: (i, 0))) for o in o_near]
        + [
            (w_out, pl.BlockSpec((1, head_columns, width), lambda i, m, n=n: (m[0] ^ n, 0, 0)))
            for n in range(members)
        ]
        + [
            (gain, whole(gain)),
            (w_router, whole(w_router)),
            (previous, small_spec),
            (w_carry, whole(w_carry)),
            (target_rows, whole(target_rows)),
        ],
        [(wide, row_spec), (wide, row_spec), (small, small_spec), (gates, whole(gates))]
        + [(piece, whole(piece))] * local,
        scratch=[pltpu.VMEM((rows, width), bf16), pltpu.VMEM((3, rows, expert_all), bf16)],
        meta=meta,
        flops=2 * rows * width * width + 2 * rows * width * per_piece * local,
        moved=rows * width * 14,
    )


def token_zero(x1, h2, grad, prob, routes, logit_w, vectors, expert_count):
    rows, width = x1.shape
    tile = 128
    kinds = vectors.shape[0]
    expert_all = prob.shape[1]

    def body(x1_ref, h2_ref, dy_ref, prob_ref, route_ref, w_ref, vec_ref, *outs):
        base_ref, dh_ref, dgate_ref, gate_ref, sums_ref = outs
        i = pl.program_id(0)
        h2 = h2_ref[...]
        dy = dy_ref[...].astype(f32)
        prob_now = prob_ref[...]
        lanes = lax.broadcasted_iota(jnp.int32, (tile, expert_all), 1)
        ids = [route_ref[:, c : c + 1] for c in range(2)]
        gates = [
            jnp.sum(jnp.where(lanes == r, prob_now, 0.0), axis=1, keepdims=True) for r in ids
        ]
        for c in range(2):
            gate_ref[:, c : c + 1] = gates[c]
        along = jnp.sum(dy * h2, axis=1, keepdims=True)
        copies = [(r == expert_count + 1).astype(f32) for r in ids]
        keep = copies[0] * gates[0] + copies[1] * gates[1]
        dgates = [copies[c] * along for c in range(2)]
        scores = [
            jnp.sum(h2 * w_ref[n : n + 1, :], axis=1, keepdims=True) for n in range(2 * kinds)
        ]
        base = x1_ref[...]
        dh = jnp.zeros_like(h2)
        for j in range(kinds):
            top = jnp.maximum(scores[2 * j], scores[2 * j + 1])
            e0 = jnp.exp(scores[2 * j] - top)
            e1 = jnp.exp(scores[2 * j + 1] - top)
            a0 = e0 / (e0 + e1)
            a1 = e1 / (e0 + e1)
            vec = vec_ref[j : j + 1, :]
            along_vec = jnp.sum(dy * vec, axis=1, keepdims=True)
            here = [(r == expert_count + 2 + j).astype(f32) for r in ids]
            weight = here[0] * gates[0] + here[1] * gates[1]
            for c in range(2):
                dgates[c] = dgates[c] + here[c] * (a0 * along + a1 * along_vec)
            keep = keep + weight * a0
            base = base + (weight * a1) * vec
            d0 = weight * along
            d1 = weight * along_vec
            mean = a0 * d0 + a1 * d1
            z0 = a0 * (d0 - mean)
            z1 = a1 * (d1 - mean)
            dh = dh + z0 * w_ref[2 * j : 2 * j + 1, :] + z1 * w_ref[2 * j + 1 : 2 * j + 2, :]
            found = [
                jnp.sum((weight * a1) * dy, axis=0, keepdims=True),
                jnp.sum(z0 * h2, axis=0, keepdims=True),
                jnp.sum(z1 * h2, axis=0, keepdims=True),
            ]
            places = [j, kinds + 2 * j, kinds + 2 * j + 1]
            for place, row in zip(places, found):

                @pl.when(i == 0)
                def _():
                    sums_ref[place : place + 1, :] = row

                @pl.when(i > 0)
                def _():
                    sums_ref[place : place + 1, :] += row

        base_ref[...] = base + keep * h2
        dh_ref[...] = dh + keep * dy
        for c in range(2):
            dgate_ref[:, c : c + 1] = dgates[c]

    row_spec = pl.BlockSpec((tile, width), lambda i: (i, 0))
    pair_spec = pl.BlockSpec((tile, 2), lambda i: (i, 0))
    wide = shape_of((rows, width), f32)
    pair = shape_of((rows, 2), f32)
    sums = shape_of((3 * kinds, width), f32)
    return run(
        body,
        (rows // tile,),
        [
            (x1, row_spec),
            (h2, row_spec),
            (grad, row_spec),
            (prob, pl.BlockSpec((tile, expert_all), lambda i: (i, 0))),
            (routes, pair_spec),
            (logit_w, whole(logit_w)),
            (vectors, whole(vectors)),
        ],
        [(wide, row_spec), (wide, row_spec), (pair, pair_spec), (pair, pair_spec), (sums, whole(sums))],
        flops=rows * width * 40,
        moved=rows * width * 18,
    )


def expert_layer(which, meta, arrived, grads, gates, w_gate, w_up, w_down, parts):
    groups = len(arrived)
    rows = groups * CAP
    width = w_gate.shape[1]
    hidden = w_gate.shape[2]
    half = width // 2
    tile = 256
    steps = hidden // tile
    per_part = hidden // parts
    tile_part = max(1, per_part // tile)
    chunk = 128

    def body(meta_ref, *refs):
        x_refs = refs[:groups]
        dy_refs = refs[groups : 2 * groups]
        gates_ref, wg_ref, wu_ref, wd_ref = refs[2 * groups : 2 * groups + 4]
        y_ref, dx_ref, dg_ref = refs[2 * groups + 4 : 2 * groups + 7]
        gs_ref, gk_ref, us_ref, uk_ref, ds_ref, dk_ref = refs[2 * groups + 7 : 2 * groups + 13]
        x_all, xt_all, dy_all, gate_all, y_acc, dx_acc, dot_acc, hid_t, dgt, dut, scaled_t = refs[
            2 * groups + 13 :
        ]
        f = pl.program_id(0)
        core = meta_ref[2]
        diagonal = lax.broadcasted_iota(jnp.int32, (CAP, CAP), 0) == lax.broadcasted_iota(
            jnp.int32, (CAP, CAP), 1
        )

        @pl.when(f == 0)
        def _():
            for g in range(groups):
                span = slice(g * CAP, (g + 1) * CAP)
                x_all[span, :] = x_refs[g][...]
                xt_all[:, span] = jnp.transpose(x_refs[g][...])
                dy_all[span, :] = dy_refs[g][...]
                gate_all[span, :] = jnp.sum(
                    jnp.where(diagonal, gates_ref[g : g + 1, :], 0.0), axis=1, keepdims=True
                )
            y_acc[...] = jnp.zeros_like(y_acc)
            dx_acc[...] = jnp.zeros_like(dx_acc)
            dot_acc[...] = jnp.zeros_like(dot_acc)

        for r in range(rows // chunk):
            span = slice(r * chunk, (r + 1) * chunk)
            g_pre = mm(x_all[span, :], wg_ref[0])
            u_pre = mm(x_all[span, :], wu_ref[0])
            back = mm(dy_all[span, :], wd_ref[0], NT)
            gate = gate_all[span, :]
            sig = 1.0 / (1.0 + jnp.exp(-g_pre))
            act = g_pre * sig
            hid = act * u_pre
            hid_t[span, :] = hid.astype(bf16)
            scaled_t[span, :] = (gate * hid).astype(bf16)
            dot_acc[span, :] += hid * back
            dhid = gate * back
            dgt[span, :] = (dhid * u_pre * sig * (1.0 + g_pre * (1.0 - sig))).astype(bf16)
            dut[span, :] = (dhid * act).astype(bf16)
        y_acc[...] += mm(hid_t[...], wd_ref[0])
        dx_acc[...] += mm(dgt[...], wg_ref[0], NT) + mm(dut[...], wu_ref[0], NT)
        mine = pl.multiple_of(core * half, half)
        theirs = pl.multiple_of((1 - core) * half, half)
        gs_ref[0] = mm(xt_all[pl.ds(theirs, half), :], dgt[...]).astype(bf16)
        gk_ref[0] = mm(xt_all[pl.ds(mine, half), :], dgt[...]).astype(bf16)
        us_ref[0] = mm(xt_all[pl.ds(theirs, half), :], dut[...]).astype(bf16)
        uk_ref[0] = mm(xt_all[pl.ds(mine, half), :], dut[...]).astype(bf16)
        ds_ref[0] = mm(scaled_t[...], dy_all[:, pl.ds(theirs, half)], TN).astype(bf16)
        dk_ref[0] = mm(scaled_t[...], dy_all[:, pl.ds(mine, half)], TN).astype(bf16)

        @pl.when(f == steps - 1)
        def _():
            y_ref[...] = (gate_all[...] * y_acc[...]).astype(bf16)
            dx_ref[...] = dx_acc[...].astype(bf16)
            for g in range(groups):
                span = slice(g * CAP, (g + 1) * CAP)
                column = jnp.sum(dot_acc[span, :], axis=1, keepdims=True)
                dg_ref[g : g + 1, :] = jnp.sum(
                    jnp.where(diagonal, column, 0.0), axis=0, keepdims=True
                )

    first = pl.BlockSpec((CAP, width), lambda f, m: (0, 0))
    up_shape = shape_of((parts, half, per_part), bf16)
    up_spec = pl.BlockSpec((1, half, tile), lambda f, m: (f // tile_part, 0, f % tile_part))
    down_shape = shape_of((parts, per_part, half), bf16)
    down_spec = pl.BlockSpec((1, tile, half), lambda f, m: (f // tile_part, f % tile_part, 0))
    wide = shape_of((rows, width), bf16)
    dots = shape_of((groups, CAP), f32)
    return run(
        body,
        (steps,),
        [(a, first) for a in arrived]
        + [(g, first) for g in grads]
        + [
            (gates, whole(gates)),
            (w_gate, pl.BlockSpec((1, width, tile), lambda f, m: (which, 0, f))),
            (w_up, pl.BlockSpec((1, width, tile), lambda f, m: (which, 0, f))),
            (w_down, pl.BlockSpec((1, tile, width), lambda f, m: (which, f, 0))),
        ],
        [(wide, whole(wide)), (wide, whole(wide)), (dots, whole(dots))]
        + [(up_shape, up_spec)] * 4
        + [(down_shape, down_spec)] * 2,
        scratch=[
            pltpu.VMEM((rows, width), bf16),
            pltpu.VMEM((width, rows), bf16),
            pltpu.VMEM((rows, width), bf16),
            pltpu.VMEM((rows, 1), f32),
            pltpu.VMEM((rows, width), f32),
            pltpu.VMEM((rows, width), f32),
            pltpu.VMEM((rows, tile), f32),
            pltpu.VMEM((rows, tile), bf16),
            pltpu.VMEM((rows, tile), bf16),
            pltpu.VMEM((rows, tile), bf16),
            pltpu.VMEM((rows, tile), bf16),
        ],
        meta=meta,
        flops=9 * 2 * rows * width * hidden,
        moved=12 * width * hidden + rows * width * 8,
        exps=rows * hidden,
    )


def slot_sum(target_ref, pieces, first_row, tile):
    total = None
    t0 = target_ref[:, 0:1]
    t1 = target_ref[:, 1:2]
    for first, ref in pieces:
        ids = first + lax.broadcasted_iota(jnp.int32, (tile, CAP), 1)
        choice = jnp.where((ids == t0) | (ids == t1), 1.0, 0.0).astype(bf16)
        part = mm(choice, ref[...])
        total = part if total is None else total + part
    return total


def token_output(base, targets, pieces):
    rows, width = base.shape
    tile = 128
    count = len(pieces)

    def body(base_ref, target_ref, *refs):
        listed = [(n * CAP, refs[n]) for n in range(count)]
        total = base_ref[...] + slot_sum(target_ref, listed, 0, tile)
        refs[count][...] = total.astype(bf16)

    row_spec = pl.BlockSpec((tile, width), lambda i: (i, 0))
    first = pl.BlockSpec((CAP, width), lambda i: (0, 0))
    return run(
        body,
        (rows // tile,),
        [(base, row_spec), (targets, pl.BlockSpec((tile, 2), lambda i: (i, 0)))]
        + [(p, first) for p in pieces],
        [(shape_of((rows, width), bf16), row_spec)],
        flops=2 * rows * width * count * CAP,
        moved=rows * width * 10,
    )[0]


def token_back(
    meta, x1, h2, grad, prob, previous, routes, targets, pieces, dots, dgate_zero, dh_zero, gain, router_t, w_out
):
    rows, width = x1.shape
    tile = 128
    count = len(pieces)
    expert_all = prob.shape[1]
    members, head_columns = w_out.shape[0], w_out.shape[1]

    def body(meta_ref, *refs):
        (x1_ref, h2_ref, dy_ref, prob_ref, prev_ref, route_ref, target_ref) = refs[:7]
        piece_refs = refs[7 : 7 + count]
        dots_ref, dz_ref, dh_ref, gain_ref, router_ref = refs[7 + count : 12 + count]
        w_refs = refs[12 + count : 12 + count + members]
        dx1_ref, low_ref = refs[12 + count + members : 14 + count + members]
        out_refs = refs[14 + count + members : 14 + count + 2 * members]
        sums_ref, carry_ref = refs[14 + count + 2 * members :]
        i = pl.program_id(0)
        prob_now = prob_ref[...]
        lanes = lax.broadcasted_iota(jnp.int32, (tile, expert_all), 1)
        dprob = jnp.zeros_like(prob_now)
        for c in range(2):
            target = target_ref[:, c : c + 1]
            dgate = dz_ref[:, c : c + 1]
            for n in range(count):
                ids = n * CAP + lax.broadcasted_iota(jnp.int32, (tile, CAP), 1)
                dgate = dgate + jnp.sum(
                    jnp.where(ids == target, dots_ref[n : n + 1, :], 0.0), axis=1, keepdims=True
                )
            dprob = dprob + jnp.where(lanes == route_ref[:, c : c + 1], dgate, 0.0)
        dlogit = prob_now * (dprob - jnp.sum(prob_now * dprob, axis=1, keepdims=True))
        h2 = h2_ref[...]
        dh2 = (
            slot_sum(target_ref, [(n * CAP, piece_refs[n]) for n in range(count)], 0, tile)
            + dh_ref[...]
            + mm_full(dlogit, router_ref[...])
        )
        x1 = x1_ref[...]
        inverse = lax.rsqrt(jnp.mean(x1 * x1, axis=1, keepdims=True) + norm_eps)
        normed = x1 * inverse
        router_part = mm_full(dlogit, h2, TN)
        carry_part = mm_full(dlogit, prev_ref[...], TN)
        gain_part = jnp.sum(dh2 * normed, axis=0, keepdims=True)

        @pl.when(i == 0)
        def _():
            sums_ref[0:expert_all, :] = router_part
            sums_ref[expert_all : expert_all + 1, :] = gain_part
            carry_ref[...] = carry_part

        @pl.when(i > 0)
        def _():
            sums_ref[0:expert_all, :] += router_part
            sums_ref[expert_all : expert_all + 1, :] += gain_part
            carry_ref[...] += carry_part

        dn = dh2 * gain_ref[...]
        dx1 = dy_ref[...].astype(f32) + inverse * (
            dn - normed * jnp.mean(dn * normed, axis=1, keepdims=True)
        )
        dx1_ref[...] = dx1
        low = dx1.astype(bf16)
        low_ref[...] = low
        for n in range(members):
            out_refs[n][...] = mm(low, w_refs[n][0], NT).astype(bf16)

    row_spec = pl.BlockSpec((tile, width), lambda i, m: (i, 0))
    pair_spec = pl.BlockSpec((tile, 2), lambda i, m: (i, 0))
    small_spec = pl.BlockSpec((tile, expert_all), lambda i, m: (i, 0))
    first = pl.BlockSpec((CAP, width), lambda i, m: (0, 0))
    sums = shape_of((expert_all + 1, width), f32)
    carry = shape_of((expert_all, expert_all), f32)
    return run(
        body,
        (rows // tile,),
        [
            (x1, row_spec),
            (h2, row_spec),
            (grad, row_spec),
            (prob, small_spec),
            (previous, small_spec),
            (routes, pair_spec),
            (targets, pair_spec),
        ]
        + [(p, first) for p in pieces]
        + [
            (dots, whole(dots)),
            (dgate_zero, pair_spec),
            (dh_zero, row_spec),
            (gain, whole(gain)),
            (router_t, whole(router_t)),
        ]
        + [
            (w_out, pl.BlockSpec((1, head_columns, width), lambda i, m, n=n: (m[0] ^ n, 0, 0)))
            for n in range(members)
        ],
        [
            (shape_of((rows, width), f32), row_spec),
            (shape_of((rows, width), bf16), row_spec),
        ]
        + [
            (
                shape_of((rows, head_columns), bf16),
                pl.BlockSpec((tile, head_columns), lambda i, m: (i, 0)),
            )
        ]
        * members
        + [(sums, whole(sums)), (carry, whole(carry))],
        meta=meta,
        flops=2 * rows * width * (count * CAP + width),
        moved=rows * width * 24,
    )


def input_back(meta, x, gain, dqkv, weights_t, dx1):
    rows, width = x.shape
    tile = 128
    members = len(dqkv)
    per_group = weights_t.shape[2]

    def body(meta_ref, x_ref, gain_ref, dx1_ref, *refs):
        d_refs = refs[:members]
        w_refs = refs[members : 2 * members]
        out_ref, sum_ref = refs[2 * members :]
        i = pl.program_id(0)
        dh = None
        for n in range(members):
            for w in range(3):
                part = mm(
                    d_refs[n][:, w * per_group : (w + 1) * per_group], w_refs[n][w, 0]
                )
                dh = part if dh is None else dh + part
        x = x_ref[...].astype(f32)
        inverse = lax.rsqrt(jnp.mean(x * x, axis=1, keepdims=True) + norm_eps)
        normed = x * inverse
        gain_part = jnp.sum(dh * normed, axis=0, keepdims=True)

        @pl.when(i == 0)
        def _():
            sum_ref[...] = gain_part

        @pl.when(i > 0)
        def _():
            sum_ref[...] += gain_part

        dn = dh * gain_ref[...]
        out_ref[...] = dx1_ref[...] + inverse * (
            dn - normed * jnp.mean(dn * normed, axis=1, keepdims=True)
        )

    row_spec = pl.BlockSpec((tile, width), lambda i, m: (i, 0))
    sums = shape_of((1, width), f32)
    return run(
        body,
        (rows // tile,),
        [(x, row_spec), (gain, whole(gain)), (dx1, row_spec)]
        + [(d, pl.BlockSpec((tile, 3 * per_group), lambda i, m: (i, 0))) for d in dqkv]
        + [
            (weights_t, pl.BlockSpec((3, 1, per_group, width), lambda i, m, n=n: (0, m[0] ^ n, 0, 0)))
            for n in range(members)
        ],
        [(shape_of((rows, width), f32), row_spec), (sums, whole(sums))],
        meta=meta,
        flops=2 * rows * width * width * 3,
        moved=rows * width * 20 + weights_t.size * 2,
    )


def sum_over_dp(parts):
    count = lax.axis_size("dp")
    mine = lax.axis_index("dp")
    if count == 2:
        out = add_low(*[pick(p, 1 - mine) for p in parts])
        return add_low(*[pick(p, mine) for p in parts], swap(out, "dp", 1))
    return lax.psum_scatter(add_low(*parts), "dp", scatter_dimension=0, tiled=False)


def gather_dp(value):
    count = lax.axis_size("dp")
    mine = lax.axis_index("dp")
    if count == 2:
        other = swap(value, "dp", 1)
        return jnp.concatenate(
            [jnp.where(mine == 0, value, other), jnp.where(mine == 0, other, value)], axis=0
        )
    return lax.all_gather(value, "dp", axis=0, tiled=True)


def sum_over_exp(value):
    bit = 1
    while bit < lax.axis_size("exp"):
        value = add_low(value, swap(value, "exp", bit))
        bit *= 2
    return value


def expert_share(send, keep):
    mine = sum_over_dp([keep, swap(send, "ctx", 1)])
    across = lax.axis_index("ctx") // 2
    halves = mine.reshape((2, mine.shape[0] // 2) + mine.shape[1:])
    total = add_low(pick(halves, across), swap(pick(halves, 1 - across), "ctx", 2))
    return gather_near(total, "ctx")


def place(meta, pieces, out_shape, place_of):
    block = pieces[0][0].shape
    flat = [p for listed in pieces for p in listed]
    members = len(pieces[0])

    def body(meta_ref, *refs):
        spot = pl.program_id(0) * members + pl.program_id(1)
        for n in range(len(flat)):

            @pl.when(spot == n)
            def _():
                refs[-1][0] = refs[n][...].astype(f32)

    return run(
        body,
        (len(pieces), members),
        [(p, whole(p)) for p in flat],
        [
            (
                shape_of(out_shape, f32),
                pl.BlockSpec((1,) + block, lambda e, j, m: (e,) + place_of(m[0] ^ j)),
            )
        ],
        meta=meta,
        moved=sum(p.size for p in flat) * 6,
    )[0]


def place_columns(meta, pieces, per_group):
    members = len(pieces)
    width = pieces[0].shape[1]

    def body(meta_ref, *refs):
        out_ref, hold = refs[members:]
        for n in range(members):
            at = pl.multiple_of((meta_ref[0] ^ n) * per_group, per_group)
            hold[pl.ds(at, per_group), :] = refs[n][...].astype(f32)
        out_ref[0] = jnp.transpose(hold[...])

    out = shape_of((3, width, width), f32)
    return run(
        body,
        (3,),
        [(p, pl.BlockSpec((per_group, width), lambda w, m: (w, 0))) for p in pieces],
        [(out, pl.BlockSpec((1, width, width), lambda w, m: (w, 0, 0)))],
        scratch=[pltpu.VMEM((width, width), f32)],
        meta=meta,
        moved=3 * width * width * 6,
    )[0]


def shards(
    inputs,
    lengths,
    block_order,
    routes,
    prev_logits,
    norm1_gain,
    norm2_gain,
    w_qkv,
    w_out,
    w_router,
    w_carry,
    const_logit_w,
    const_vec,
    w_gate,
    w_up,
    w_down,
    cotangent,
):
    members = lax.axis_size("ctx")
    groups = lax.axis_size("exp")
    parts = lax.axis_size("dp")
    me = lax.axis_index("ctx")
    mine = lax.axis_index("exp")
    x, grad = inputs[0], cotangent[0]
    rows, width = x.shape
    group_rows = rows * members
    deal_block = group_rows // block_order.shape[1]
    per_member = rows // deal_block
    local = w_gate.shape[0]
    expert_count = local * groups
    slots = expert_count * CAP
    head_width = width // HEADS
    heads = HEADS // members
    per_group = heads * head_width
    blocks = block_order.shape[1]
    layout = {"order": 4, "lengths": 4 + blocks, "sequences": lengths.shape[1]}
    meta = jnp.concatenate(
        [
            jnp.stack([me, mine, me % 2, me // 2]).astype(jnp.int32),
            block_order[0],
            lengths[0],
        ]
    )
    gain1 = norm1_gain.reshape(1, width)
    gain2 = norm2_gain.reshape(1, width)
    weights_t = jnp.swapaxes(w_qkv, 1, 2).reshape(3, members, per_group, width)
    w_out_parts = w_out.reshape(members, per_group, width)
    route_ids = routes[0]
    previous = prev_logits[0]

    near = gather_near(x, "ctx")
    held = None
    for j in range(members):
        held = project(j, near[j], gain1, weights_t, meta, held, group_rows)
    q, k, v, kt, vt, h1 = held
    o, ot, lse, tops = attend(meta, q, k, vt, deal_block, per_member, layout)
    o_near = [
        swap(o[j * rows : (j + 1) * rows], "ctx", j) if j else o[:rows] for j in range(members)
    ]

    targets = slot_targets(route_ids, expert_count, local, mine)
    target_rows = jnp.transpose(targets)
    grad_slots = dispatch(target_rows, grad, slots, local)
    grad_near = [
        [
            swap(grad_slots[e][g * CAP : (g + 1) * CAP], "exp", g) if g else grad_slots[e]
            for g in range(groups)
        ]
        for e in range(local)
    ]

    front = token_front(
        meta, x, o_near, w_out_parts, gain2, w_router, previous, w_carry, target_rows, local, groups
    )
    x1, h2, prob, gate_slots = front[:4]
    token_slots = front[4:]
    gate_view = gate_slots.reshape(local, groups, CAP)
    gate_near = [gate_view[:, g] if g == 0 else swap(gate_view[:, g], "exp", g) for g in range(groups)]
    token_near = [
        [
            swap(token_slots[e][g * CAP : (g + 1) * CAP], "exp", g) if g else token_slots[e]
            for g in range(groups)
        ]
        for e in range(local)
    ]
    logit_rows = jnp.swapaxes(const_logit_w, 1, 2).reshape(-1, width)
    base, dh_zero, dgate_zero, gates, zero_sums = token_zero(
        x1, h2, grad, prob, route_ids, logit_rows, const_vec, expert_count
    )

    out_rows, in_rows, dot_rows = [], [], []
    gate_pieces, up_pieces, down_pieces = [], [], []
    for e in range(local):
        gate_rows = jnp.stack([gate_near[g][e] for g in range(groups)])
        y, dx, dots, gs, gk, us, uk, ds, dk = expert_layer(
            e, meta, token_near[e], grad_near[e], gate_rows, w_gate, w_up, w_down, parts
        )
        in_rows += [swap(dx[g * CAP : (g + 1) * CAP], "exp", g) if g else dx for g in range(groups)]
        dot_rows += [swap(dots[g : g + 1], "exp", g) if g else dots[:1] for g in range(groups)]
        out_rows += [swap(y[g * CAP : (g + 1) * CAP], "exp", g) if g else y for g in range(groups)]
        gate_pieces.append(expert_share(gs, gk))
        up_pieces.append(expert_share(us, uk))
        down_pieces.append(expert_share(ds, dk))

    back = token_back(
        meta,
        x1,
        h2,
        grad,
        prob,
        previous,
        route_ids,
        targets,
        in_rows,
        jnp.concatenate(dot_rows, axis=0),
        dgate_zero,
        dh_zero,
        gain2,
        jnp.transpose(w_router),
        w_out_parts,
    )
    dx1, da = back[:2]
    do_near = [back[2 + j] if j == 0 else swap(back[2 + j], "ctx", j) for j in range(members)]
    token_sums, carry_sum = back[2 + members :]
    result = token_output(base, targets, out_rows)

    out_parts = [
        mm(o_near[j], da, TN).astype(bf16) for j in range(members)
    ]
    bit = 1
    while bit < members:
        kept = [j for j in range(members) if j % (2 * bit) == 0]
        out_parts = {
            j: add_low(out_parts[j], swap(out_parts[j + bit], "ctx", bit)) for j in kept
        }
        bit *= 2
    out_sum = out_parts[0]

    dqkv = attend_back(meta, q, k, v, kt, do_near, ot, lse, deal_block, per_member, layout)
    dqkv_near = [
        swap(dqkv[j * rows : (j + 1) * rows], "ctx", j) if j else dqkv[:rows]
        for j in range(members)
    ]
    qkv_sum = mm(dqkv, h1, TN).astype(bf16)
    input_grad, norm1_sum = input_back(meta, x, gain1, dqkv_near, weights_t, dx1)

    def dense_total(value):
        share = sum_over_dp([value.reshape((parts, value.shape[0] // parts, width))])
        return gather_near(gather_dp(sum_over_exp(share)), "ctx")

    out_grad = place(
        meta, [dense_total(out_sum)], (1, width, width), lambda a: (a, 0)
    )[0]
    qkv_grad = place_columns(meta, dense_total(qkv_sum), per_group)

    expert_all = w_router.shape[1]
    small = jnp.concatenate(
        [token_sums, zero_sums, jnp.pad(carry_sum, ((0, 0), (0, width - expert_all)))], axis=0
    )
    small = butterfly(small, jnp.add)
    norm1_grad = butterfly(norm1_sum, jnp.add)
    kinds = const_vec.shape[0]
    router_grad = jnp.transpose(small[:expert_all])
    norm2_grad = small[expert_all]
    at = expert_all + 1
    vec_grad = small[at : at + kinds]
    logit_grad = jnp.swapaxes(small[at + kinds : at + 3 * kinds].reshape(kinds, 2, width), 1, 2)
    carry_grad = jnp.transpose(small[at + 3 * kinds :, :expert_all])

    local_tops = jnp.max(tops, axis=1)
    top_all = jnp.zeros((members, heads), f32).at[me].set(local_tops)
    top_all = jnp.where(jnp.arange(members)[:, None] == me, top_all, low_start)
    head_max = butterfly(top_all, jnp.maximum).reshape(HEADS)
    clip_ratio = jnp.sqrt(jnp.minimum(1.0, clip_limit / head_max))
    head_scale = jnp.repeat(clip_ratio, head_width)
    clipped = w_qkv[:2].astype(f32) * head_scale[None, None, :]

    half = width // 2
    hidden_part = w_gate.shape[2] // parts
    up_shape = (local, width, hidden_part)
    down_shape = (local, hidden_part, width)
    gate_grad = place(meta, gate_pieces, up_shape, lambda a: ((a % 2) * 2 + a // 2, 0))
    up_grad = place(meta, up_pieces, up_shape, lambda a: ((a % 2) * 2 + a // 2, 0))
    down_grad = place(meta, down_pieces, down_shape, lambda a: (a // 2, a % 2))
    return (
        result[None],
        input_grad[None],
        norm1_grad[0],
        norm2_grad,
        qkv_grad,
        out_grad,
        router_grad,
        carry_grad,
        logit_grad,
        vec_grad,
        gate_grad,
        up_grad,
        down_grad,
        clipped,
    )


def solution(mesh):
    tokens = P(("dp", "exp"), "ctx", None)
    packs = P(("dp", "exp"), None)
    experts = P("exp", None, None)
    in_specs = (
        tokens, packs, packs, tokens, tokens, P(), P(), P(), P(), P(), P(), P(), P(),
        experts, experts, experts, tokens,
    )
    out_specs = (
        tokens, tokens, P(), P(), P(), P(), P(), P(), P(), P(),
        P("exp", None, "dp"), P("exp", None, "dp"), P("exp", "dp", None), P(),
    )
    return jax.shard_map(shards, mesh=mesh, in_specs=in_specs, out_specs=out_specs, check_vma=False)
```

```python
import functools

import jax
import jax.numpy as jnp
from jax import lax
from jax.experimental import pallas as pl
from jax.experimental.pallas import tpu as pltpu
from jax.sharding import PartitionSpec as P

HEADS = 12
CAP = 128

norm_eps = 1e-05
clip_limit = 3.0
low_start = -1e30
mask_fill = -3e38
highest = lax.Precision.HIGHEST
NN = (((1,), (0,)), ((), ()))
NT = (((1,), (1,)), ((), ()))
TN = (((0,), (0,)), ((), ()))
f32 = jnp.float32
bf16 = jnp.bfloat16
MESH = pl.DeviceIdType.MESH


def mm(left, right, dims=NN):
    return lax.dot_general(left, right, dims, preferred_element_type=f32)


def mm_full(left, right, dims=NN):
    return lax.dot_general(left, right, dims, precision=highest, preferred_element_type=f32)


def shape_of(shape, dtype):
    return jax.ShapeDtypeStruct(shape, dtype)


def whole(array):
    rank = len(array.shape)
    return pl.BlockSpec(array.shape, lambda *_: (0,) * rank)


def cost(flops, moved, exps=0):
    return pl.CostEstimate(flops=int(flops), bytes_accessed=int(moved), transcendentals=int(exps))


def run(body, grid, inputs, outputs, scratch=(), meta=None, flops=0, moved=0, exps=0, aliases=None, talks=None):
    prefetch = 0 if meta is None else 1
    args = ([] if meta is None else [meta]) + [a for a, _ in inputs]
    return pl.pallas_call(
        body,
        out_shape=[o for o, _ in outputs],
        grid_spec=pltpu.PrefetchScalarGridSpec(
            num_scalar_prefetch=prefetch,
            grid=grid,
            in_specs=[s for _, s in inputs],
            out_specs=[s for _, s in outputs],
            scratch_shapes=list(scratch),
        ),
        compiler_params=pltpu.CompilerParams(
            dimension_semantics=("arbitrary",) * len(grid),
            vmem_limit_bytes=60 * 1024 * 1024,
            collective_id=talks,
            has_side_effects=talks is not None,
        ),
        cost_estimate=cost(flops, moved, exps),
        input_output_aliases={} if aliases is None else aliases,
    )(*args)


def swap(value, axis, distance):
    count = lax.axis_size(axis)
    return lax.ppermute(value, axis, [(i, i ^ distance) for i in range(count)])


def gather_near(value, axis):
    count = lax.axis_size(axis)
    found = {0: value}
    bit = count // 2
    while bit:
        for have in list(found):
            found[have | bit] = swap(found[have], axis, bit)
        bit //= 2
    return [found[j] for j in range(count)]


def butterfly(value, combine):
    for axis in ("ctx", "dp", "exp"):
        bit = 1
        while bit < lax.axis_size(axis):
            value = combine(value, swap(value, axis, bit))
            bit *= 2
    return value


def pick(stacked, index):
    return lax.dynamic_index_in_dim(stacked, index, 0, keepdims=False)


def add_low(*terms):
    total = terms[0].astype(f32)
    for term in terms[1:]:
        total = total + term.astype(f32)
    return total.astype(bf16)


def project(turn, rows_low, gain, weights_t, meta, earlier, group_rows):
    row_count, width = rows_low.shape
    per_group = weights_t.shape[2]
    head_width = width // HEADS
    heads = per_group // head_width
    tile = min(256, row_count)
    steps = row_count // tile
    scale = head_width**-0.5

    def body(meta_ref, x_ref, gain_ref, w_ref, *refs):
        q_ref, k_ref, v_ref, kt_ref, vt_ref, h_ref = refs[-6:]
        x = x_ref[...].astype(f32)
        inverse = lax.rsqrt(jnp.mean(x * x, axis=1, keepdims=True) + norm_eps)
        low = (x * inverse * gain_ref[...]).astype(bf16)
        h_ref[...] = low
        q = mm(low, w_ref[0, 0], NT).astype(bf16) * jnp.asarray(scale, bf16)
        k = mm(low, w_ref[1, 0], NT).astype(bf16)
        v = mm(low, w_ref[2, 0], NT).astype(bf16)
        for h in range(heads):
            part = slice(h * head_width, (h + 1) * head_width)
            q_ref[h] = q[:, part]
            k_ref[h] = k[:, part]
            v_ref[h] = v[:, part]
        kt_ref[...] = mm(w_ref[1, 0], low, NT).astype(bf16)
        vt_ref[...] = mm(w_ref[2, 0], low, NT).astype(bf16)

    by_head = shape_of((heads, group_rows, head_width), bf16)
    by_column = shape_of((per_group, group_rows), bf16)
    hidden = shape_of((group_rows, width), bf16)
    head_spec = pl.BlockSpec((heads, tile, head_width), lambda i, m: (0, turn * steps + i, 0))
    column_spec = pl.BlockSpec((per_group, tile), lambda i, m: (0, turn * steps + i))
    hidden_spec = pl.BlockSpec((tile, width), lambda i, m: (turn * steps + i, 0))
    inputs = [
        (rows_low, pl.BlockSpec((tile, width), lambda i, m: (i, 0))),
        (gain, pl.BlockSpec((1, width), lambda i, m: (0, 0))),
        (weights_t, pl.BlockSpec((3, 1, per_group, width), lambda i, m: (0, m[0], 0, 0))),
    ]
    aliases = None
    if earlier is not None:
        inputs += [(a, pl.BlockSpec(memory_space=pl.ANY)) for a in earlier]
        aliases = {4 + n: n for n in range(6)}
    return run(
        body,
        (steps,),
        inputs,
        [(by_head, head_spec)] * 3 + [(by_column, column_spec)] * 2 + [(hidden, hidden_spec)],
        meta=meta,
        flops=2 * row_count * width * per_group * 5,
        moved=row_count * width * 8 + weights_t.size // 2,
        aliases=aliases,
    )


def block_place(meta_ref, block, per_member, layout):
    member = meta_ref[0] ^ (block // per_member)
    return meta_ref[layout["order"] + member * per_member + block % per_member]


def document_start(meta_ref, position, layout):
    start = jnp.zeros_like(position)
    end = jnp.int32(0)
    for s in range(layout["sequences"]):
        end = end + meta_ref[layout["lengths"] + s]
        start = jnp.where(position >= end, end, start)
    return start


def block_range(meta_ref, query_block, key_block, rows, per_member, layout):
    q_first = block_place(meta_ref, query_block, per_member, layout) * rows
    k_first = block_place(meta_ref, key_block, per_member, layout) * rows
    begin = document_start(meta_ref, q_first, layout)
    begin_last = document_start(meta_ref, q_first + rows - 1, layout)
    needed = (k_first <= q_first) & (k_first + rows - 1 >= begin)
    full = (k_first < q_first) & (k_first >= begin_last)
    return q_first, k_first, needed, full


def allowed_pairs(meta_ref, q_first, k_first, rows, layout):
    q_pos = q_first + lax.broadcasted_iota(jnp.int32, (1, rows), 1)
    k_pos = k_first + lax.broadcasted_iota(jnp.int32, (rows, 1), 0)
    return (k_pos <= q_pos) & (k_pos >= document_start(meta_ref, q_pos, layout))


def attend(meta, q, k, vt, rows, per_member, layout):
    heads, group_rows, head_width = q.shape
    blocks = group_rows // rows
    width = heads * head_width

    def body(meta_ref, q_ref, k_ref, vt_ref, o_ref, ot_ref, lse_ref, top_ref, m_ref, l_ref, a_ref):
        i = pl.program_id(0)
        m_ref[...] = jnp.full_like(m_ref, low_start)
        l_ref[...] = jnp.zeros_like(l_ref)
        a_ref[...] = jnp.zeros_like(a_ref)

        def one(j, _):
            q_first, k_first, needed, full = block_range(meta_ref, i, j, rows, per_member, layout)
            at = pl.multiple_of(j * rows, rows)

            def step(masked):
                if masked:
                    allowed = allowed_pairs(meta_ref, q_first, k_first, rows, layout)
                for h in range(heads):
                    part = slice(h * head_width, (h + 1) * head_width)
                    s = mm(k_ref[h, pl.ds(at, rows), :], q_ref[h], NT)
                    if masked:
                        s = jnp.where(allowed, s, mask_fill)
                    old = m_ref[h]
                    new = jnp.maximum(old, jnp.max(s, axis=0, keepdims=True))
                    shrink = jnp.exp(old - new)
                    p = jnp.exp(s - new)
                    m_ref[h] = new
                    l_ref[h] = l_ref[h] * shrink + jnp.sum(p, axis=0, keepdims=True)
                    a_ref[part, :] = a_ref[part, :] * shrink + mm(
                        vt_ref[part, pl.ds(at, rows)], p.astype(bf16)
                    )

            @pl.when(full)
            def _():
                step(False)

            @pl.when(needed & jnp.logical_not(full))
            def _():
                step(True)

            return 0

        lax.fori_loop(0, blocks, one, 0)
        for h in range(heads):
            part = slice(h * head_width, (h + 1) * head_width)
            ot_ref[part, :] = a_ref[part, :] / l_ref[h]
            lse_ref[pl.ds(h, 1), :] = m_ref[h] + jnp.log(l_ref[h])
            top_ref[pl.ds(h, 1), :] = m_ref[h]
        o_ref[...] = jnp.transpose(ot_ref[...]).astype(bf16)

    row = shape_of((heads, group_rows), f32)
    row_spec = pl.BlockSpec((heads, rows), lambda i, m: (0, i))
    return run(
        body,
        (blocks,),
        [
            (q, pl.BlockSpec((heads, rows, head_width), lambda i, m: (0, i, 0))),
            (k, whole(k)),
            (vt, whole(vt)),
        ],
        [
            (shape_of((group_rows, width), bf16), pl.BlockSpec((rows, width), lambda i, m: (i, 0))),
            (shape_of((width, group_rows), f32), pl.BlockSpec((width, rows), lambda i, m: (0, i))),
            (row, row_spec),
            (row, row_spec),
        ],
        scratch=[
            pltpu.VMEM((heads, 1, rows), f32),
            pltpu.VMEM((heads, 1, rows), f32),
            pltpu.VMEM((width, rows), f32),
        ],
        meta=meta,
        flops=2 * 2 * group_rows * group_rows * width,
        moved=group_rows * width * 14,
        exps=group_rows * group_rows * heads // 2,
    )


def attend_back(meta, q, k, v, kt, grad, ot, lse, rows, per_member, layout):
    heads, group_rows, head_width = q.shape
    blocks = group_rows // rows
    width = heads * head_width
    scale = head_width**-0.5
    members = len(grad)
    per = grad[0].shape[0] // rows

    def body(meta_ref, q_ref, k_ref, v_ref, kt_ref, *refs):
        grads = refs[:members]
        ot_ref, lse_ref, out_ref, dk_ref, dv_ref, dq_ref, g_ref, delta_ref = refs[members:]
        i = pl.program_id(0)

        @pl.when(i == 0)
        def _():
            dk_ref[...] = jnp.zeros_like(dk_ref)
            dv_ref[...] = jnp.zeros_like(dv_ref)

        for n in range(members):

            @pl.when(i // per == n)
            def _():
                g = grads[n][...]
                for h in range(heads):
                    g_ref[h] = g[:, h * head_width : (h + 1) * head_width]
                product = jnp.transpose(g.astype(f32)) * ot_ref[...]
                for h in range(heads):
                    part = slice(h * head_width, (h + 1) * head_width)
                    delta_ref[h] = jnp.sum(product[part, :], axis=0, keepdims=True)

        dq_ref[...] = jnp.zeros_like(dq_ref)

        def one(j, _):
            q_first, k_first, needed, full = block_range(meta_ref, i, j, rows, per_member, layout)
            at = pl.multiple_of(j * rows, rows)

            def step(masked):
                if masked:
                    allowed = allowed_pairs(meta_ref, q_first, k_first, rows, layout)
                for h in range(heads):
                    part = slice(h * head_width, (h + 1) * head_width)
                    s = mm(k_ref[h, pl.ds(at, rows), :], q_ref[h], NT)
                    if masked:
                        s = jnp.where(allowed, s, mask_fill)
                    p = jnp.exp(s - lse_ref[pl.ds(h, 1), :])
                    dp = mm(v_ref[h, pl.ds(at, rows), :], g_ref[h], NT)
                    ds = (p * (dp - delta_ref[h])).astype(bf16)
                    dv_ref[h, pl.ds(at, rows), :] += mm(p.astype(bf16), g_ref[h])
                    dk_ref[h, pl.ds(at, rows), :] += mm(ds, q_ref[h])
                    dq_ref[part, :] += mm(kt_ref[part, pl.ds(at, rows)], ds)

            @pl.when(full)
            def _():
                step(False)

            @pl.when(needed & jnp.logical_not(full))
            def _():
                step(True)

            return 0

        lax.fori_loop(0, blocks, one, 0)
        here = pl.multiple_of(i * rows, rows)
        out_ref[pl.ds(here, rows), 0:width] = (jnp.transpose(dq_ref[...]) * scale).astype(bf16)

        @pl.when(i == blocks - 1)
        def _():
            def store(b, _):
                spot = pl.multiple_of(b * rows, rows)
                out_ref[pl.ds(spot, rows), width : 3 * width] = jnp.concatenate(
                    [dk_ref[h, pl.ds(spot, rows), :] for h in range(heads)]
                    + [dv_ref[h, pl.ds(spot, rows), :] for h in range(heads)],
                    axis=1,
                ).astype(bf16)
                return 0

            lax.fori_loop(0, blocks, store, 0)

    grad_specs = [
        pl.BlockSpec((rows, width), lambda i, m, n=n: (jnp.clip(i - n * per, 0, per - 1), 0))
        for n in range(members)
    ]
    out = shape_of((group_rows, 3 * width), bf16)
    return run(
        body,
        (blocks,),
        [
            (q, pl.BlockSpec((heads, rows, head_width), lambda i, m: (0, i, 0))),
            (k, whole(k)),
            (v, whole(v)),
            (kt, whole(kt)),
        ]
        + list(zip(grad, grad_specs))
        + [
            (ot, pl.BlockSpec((width, rows), lambda i, m: (0, i))),
            (lse, pl.BlockSpec((heads, rows), lambda i, m: (0, i))),
        ],
        [(out, whole(out))],
        scratch=[
            pltpu.VMEM((heads, group_rows, head_width), f32),
            pltpu.VMEM((heads, group_rows, head_width), f32),
            pltpu.VMEM((width, rows), f32),
            pltpu.VMEM((heads, rows, head_width), bf16),
            pltpu.VMEM((heads, 1, rows), f32),
        ],
        meta=meta,
        flops=5 * 2 * group_rows * group_rows * width,
        moved=group_rows * width * 24,
        exps=group_rows * group_rows * heads // 2,
    )[0]


def slot_targets(route_ids, expert_count, local_experts, mine):
    rows = route_ids.shape[0]
    groups = expert_count // local_experts
    experts = jnp.arange(expert_count, dtype=jnp.int32)
    hits = route_ids[:, :, None] == experts[None, None, :]
    hit = jnp.any(hits, axis=1)
    order = lax.broadcasted_iota(jnp.int32, (rows, rows), 0)
    other = lax.broadcasted_iota(jnp.int32, (rows, rows), 1)
    ahead = mm((other < order).astype(bf16), hit.astype(bf16)).astype(jnp.int32)
    rank = jnp.sum(jnp.where(hits, ahead[:, None, :], 0), axis=2)
    near = (route_ids // local_experts) ^ mine
    slot = (route_ids % local_experts) * (groups * CAP) + near * CAP + rank
    return jnp.where(route_ids < expert_count, slot, -1)


def slot_choice(first, count, target_ref):
    rows = target_ref.shape[1]
    ids = first + lax.broadcasted_iota(jnp.int32, (count, rows), 0)
    match = (ids == target_ref[0:1, :]) | (ids == target_ref[1:2, :])
    return jnp.where(match, 1.0, 0.0).astype(bf16)


def dispatch(target_rows, source, slots, pieces):
    rows, width = source.shape
    tile = 2 * CAP
    per_piece = slots // pieces

    def body(target_ref, source_ref, *outs):
        for n in range(pieces):
            for t in range(per_piece // tile):
                choice = slot_choice(n * per_piece + t * tile, tile, target_ref)
                outs[n][t * tile : (t + 1) * tile, :] = mm(choice, source_ref[...]).astype(bf16)

    out = shape_of((per_piece, width), bf16)
    return run(
        body,
        (1,),
        [(target_rows, whole(target_rows)), (source, whole(source))],
        [(out, whole(out))] * pieces,
        flops=2 * rows * width * slots,
        moved=(rows + slots) * width * 2,
    )


def token_front(meta, x, o_near, w_out, gain, w_router, previous, w_carry, target_rows, local, groups):
    rows, width = x.shape
    members = len(o_near)
    head_columns = o_near[0].shape[1]
    expert_all = w_router.shape[1]
    tile = 128
    steps = rows // tile
    per_piece = groups * CAP

    def body(meta_ref, x_ref, *refs):
        o_refs = refs[:members]
        w_refs = refs[members : 2 * members]
        gain_ref, router_ref, prev_ref, carry_ref, target_ref = refs[2 * members : 2 * members + 5]
        x1_ref, h2_ref, prob_ref, gates_ref = refs[2 * members + 5 : 2 * members + 9]
        piece_refs = refs[2 * members + 9 : 2 * members + 9 + local]
        low_ref, split_ref = refs[2 * members + 9 + local :]
        i = pl.program_id(0)
        total = x_ref[...].astype(f32)
        for n in range(members):
            total = total + mm(o_refs[n][...], w_refs[n][0])
        x1_ref[...] = total
        inverse = lax.rsqrt(jnp.mean(total * total, axis=1, keepdims=True) + norm_eps)
        h2 = total * inverse * gain_ref[...]
        h2_ref[...] = h2
        logits = mm_full(h2, router_ref[...]) + mm_full(prev_ref[...], carry_ref[...])
        shifted = jnp.exp(logits - jnp.max(logits, axis=1, keepdims=True))
        prob = shifted / jnp.sum(shifted, axis=1, keepdims=True)
        prob_ref[...] = prob
        here = pl.multiple_of(i * tile, tile)
        low_ref[pl.ds(here, tile), :] = h2.astype(bf16)
        top = prob.astype(bf16)
        rest = prob - top.astype(f32)
        middle = rest.astype(bf16)
        last = (rest - middle.astype(f32)).astype(bf16)
        split_ref[0, pl.ds(here, tile), :] = top
        split_ref[1, pl.ds(here, tile), :] = middle
        split_ref[2, pl.ds(here, tile), :] = last

        @pl.when(i == steps - 1)
        def _():
            diagonal = lax.broadcasted_iota(jnp.int32, (CAP, CAP), 0) == lax.broadcasted_iota(
                jnp.int32, (CAP, CAP), 1
            )
            lanes = lax.broadcasted_iota(jnp.int32, (CAP, expert_all), 1)
            for n in range(local):
                for g in range(groups):
                    choice = slot_choice(n * per_piece + g * CAP, CAP, target_ref)
                    piece_refs[n][g * CAP : (g + 1) * CAP, :] = mm(choice, low_ref[...]).astype(
                        bf16
                    )
                    picked = (
                        mm(choice, split_ref[0]) + mm(choice, split_ref[1]) + mm(choice, split_ref[2])
                    )
                    expert = (meta_ref[1] ^ g) * local + n
                    column = jnp.sum(
                        jnp.where(lanes == expert, picked, 0.0), axis=1, keepdims=True
                    )
                    gates_ref[n * groups + g : n * groups + g + 1, :] = jnp.sum(
                        jnp.where(diagonal, column, 0.0), axis=0, keepdims=True
                    )

    row_spec = pl.BlockSpec((tile, width), lambda i, m: (i, 0))
    wide = shape_of((rows, width), f32)
    small = shape_of((rows, expert_all), f32)
    small_spec = pl.BlockSpec((tile, expert_all), lambda i, m: (i, 0))
    gates = shape_of((local * groups, CAP), f32)
    piece = shape_of((per_piece, width), bf16)
    return run(
        body,
        (steps,),
        [(x, row_spec)]
        + [(o, pl.BlockSpec((tile, head_columns), lambda i, m: (i, 0))) for o in o_near]
        + [
            (w_out, pl.BlockSpec((1, head_columns, width), lambda i, m, n=n: (m[0] ^ n, 0, 0)))
            for n in range(members)
        ]
        + [
            (gain, whole(gain)),
            (w_router, whole(w_router)),
            (previous, small_spec),
            (w_carry, whole(w_carry)),
            (target_rows, whole(target_rows)),
        ],
        [(wide, row_spec), (wide, row_spec), (small, small_spec), (gates, whole(gates))]
        + [(piece, whole(piece))] * local,
        scratch=[pltpu.VMEM((rows, width), bf16), pltpu.VMEM((3, rows, expert_all), bf16)],
        meta=meta,
        flops=2 * rows * width * width + 2 * rows * width * per_piece * local,
        moved=rows * width * 14,
    )


def token_zero(x1, h2, grad, prob, routes, logit_w, vectors, expert_count):
    rows, width = x1.shape
    tile = 128
    kinds = vectors.shape[0]
    expert_all = prob.shape[1]

    def body(x1_ref, h2_ref, dy_ref, prob_ref, route_ref, w_ref, vec_ref, *outs):
        base_ref, dh_ref, dgate_ref, gate_ref, sums_ref = outs
        i = pl.program_id(0)
        h2 = h2_ref[...]
        dy = dy_ref[...].astype(f32)
        prob_now = prob_ref[...]
        lanes = lax.broadcasted_iota(jnp.int32, (tile, expert_all), 1)
        ids = [route_ref[:, c : c + 1] for c in range(2)]
        gates = [
            jnp.sum(jnp.where(lanes == r, prob_now, 0.0), axis=1, keepdims=True) for r in ids
        ]
        for c in range(2):
            gate_ref[:, c : c + 1] = gates[c]
        along = jnp.sum(dy * h2, axis=1, keepdims=True)
        copies = [(r == expert_count + 1).astype(f32) for r in ids]
        keep = copies[0] * gates[0] + copies[1] * gates[1]
        dgates = [copies[c] * along for c in range(2)]
        scores = [
            jnp.sum(h2 * w_ref[n : n + 1, :], axis=1, keepdims=True) for n in range(2 * kinds)
        ]
        base = x1_ref[...]
        dh = jnp.zeros_like(h2)
        for j in range(kinds):
            top = jnp.maximum(scores[2 * j], scores[2 * j + 1])
            e0 = jnp.exp(scores[2 * j] - top)
            e1 = jnp.exp(scores[2 * j + 1] - top)
            a0 = e0 / (e0 + e1)
            a1 = e1 / (e0 + e1)
            vec = vec_ref[j : j + 1, :]
            along_vec = jnp.sum(dy * vec, axis=1, keepdims=True)
            here = [(r == expert_count + 2 + j).astype(f32) for r in ids]
            weight = here[0] * gates[0] + here[1] * gates[1]
            for c in range(2):
                dgates[c] = dgates[c] + here[c] * (a0 * along + a1 * along_vec)
            keep = keep + weight * a0
            base = base + (weight * a1) * vec
            d0 = weight * along
            d1 = weight * along_vec
            mean = a0 * d0 + a1 * d1
            z0 = a0 * (d0 - mean)
            z1 = a1 * (d1 - mean)
            dh = dh + z0 * w_ref[2 * j : 2 * j + 1, :] + z1 * w_ref[2 * j + 1 : 2 * j + 2, :]
            found = [
                jnp.sum((weight * a1) * dy, axis=0, keepdims=True),
                jnp.sum(z0 * h2, axis=0, keepdims=True),
                jnp.sum(z1 * h2, axis=0, keepdims=True),
            ]
            places = [j, kinds + 2 * j, kinds + 2 * j + 1]
            for place, row in zip(places, found):

                @pl.when(i == 0)
                def _():
                    sums_ref[place : place + 1, :] = row

                @pl.when(i > 0)
                def _():
                    sums_ref[place : place + 1, :] += row

        base_ref[...] = base + keep * h2
        dh_ref[...] = dh + keep * dy
        for c in range(2):
            dgate_ref[:, c : c + 1] = dgates[c]

    row_spec = pl.BlockSpec((tile, width), lambda i: (i, 0))
    pair_spec = pl.BlockSpec((tile, 2), lambda i: (i, 0))
    wide = shape_of((rows, width), f32)
    pair = shape_of((rows, 2), f32)
    sums = shape_of((3 * kinds, width), f32)
    return run(
        body,
        (rows // tile,),
        [
            (x1, row_spec),
            (h2, row_spec),
            (grad, row_spec),
            (prob, pl.BlockSpec((tile, expert_all), lambda i: (i, 0))),
            (routes, pair_spec),
            (logit_w, whole(logit_w)),
            (vectors, whole(vectors)),
        ],
        [(wide, row_spec), (wide, row_spec), (pair, pair_spec), (pair, pair_spec), (sums, whole(sums))],
        flops=rows * width * 40,
        moved=rows * width * 18,
    )


def expert_layer(which, arrived, grads, gates, w_gate, w_up, w_down, parts):
    groups = len(arrived)
    rows = groups * CAP
    width = w_gate.shape[1]
    hidden = w_gate.shape[2]
    half = width // 2
    per_part = hidden // parts
    tile = min(256, per_part)
    steps = hidden // tile
    tile_part = per_part // tile
    chunk = 128

    def body(*refs):
        x_refs = refs[:groups]
        dy_refs = refs[groups : 2 * groups]
        gates_ref, wg_ref, wu_ref, wd_ref = refs[2 * groups : 2 * groups + 4]
        y_ref, dx_ref, dg_ref, sum_ref = refs[2 * groups + 4 : 2 * groups + 8]
        (x_all, xt_all, dy_all, dyt_all, gate_all, y_acc, dx_acc, dot_acc, hid_t, dgt, dut, scaled_t) = refs[
            2 * groups + 8 : 2 * groups + 20
        ]
        keep, send, taken, send_sem, take_sem = refs[2 * groups + 20 :]
        f = pl.program_id(0)
        place_now = lax.axis_index("ctx")
        core = lax.rem(place_now, 2)
        sibling = place_now + 1 - 2 * core
        diagonal = lax.broadcasted_iota(jnp.int32, (CAP, CAP), 0) == lax.broadcasted_iota(
            jnp.int32, (CAP, CAP), 1
        )

        def copy(step, slot):
            return pltpu.make_async_remote_copy(
                src_ref=send.at[slot],
                dst_ref=taken.at[step],
                send_sem=send_sem.at[slot],
                recv_sem=take_sem.at[step],
                device_id={"ctx": sibling},
                device_id_type=MESH,
            )

        @pl.when(f == 0)
        def _():
            barrier = pltpu.get_barrier_semaphore()
            pl.semaphore_signal(barrier, inc=1, device_id={"ctx": sibling}, device_id_type=MESH)
            for g in range(groups):
                span = slice(g * CAP, (g + 1) * CAP)
                x_all[span, :] = x_refs[g][...]
                xt_all[:, span] = jnp.transpose(x_refs[g][...])
                dy_all[span, :] = dy_refs[g][...]
                dyt_all[:, span] = jnp.transpose(dy_refs[g][...])
                gate_all[span, :] = jnp.sum(
                    jnp.where(diagonal, gates_ref[g : g + 1, :], 0.0), axis=1, keepdims=True
                )
            y_acc[...] = jnp.zeros_like(y_acc)
            dx_acc[...] = jnp.zeros_like(dx_acc)
            dot_acc[...] = jnp.zeros_like(dot_acc)
            pl.semaphore_wait(barrier, 1)

        @pl.when(f < steps)
        def _():
            slot = lax.rem(f, 2)
            for r in range(rows // chunk):
                span = slice(r * chunk, (r + 1) * chunk)
                g_pre = mm(x_all[span, :], wg_ref[0])
                u_pre = mm(x_all[span, :], wu_ref[0])
                back = mm(dy_all[span, :], wd_ref[0], NT)
                gate = gate_all[span, :]
                sig = 1.0 / (1.0 + jnp.exp(-g_pre))
                act = g_pre * sig
                hid = act * u_pre
                hid_t[span, :] = hid.astype(bf16)
                scaled_t[span, :] = (gate * hid).astype(bf16)
                dot_acc[span, :] += hid * back
                dhid = gate * back
                dgt[span, :] = (dhid * u_pre * sig * (1.0 + g_pre * (1.0 - sig))).astype(bf16)
                dut[span, :] = (dhid * act).astype(bf16)

            @pl.when(f >= 2)
            def _():
                copy(f - 2, slot).wait_send()

            mine = pl.multiple_of(core * half, half)
            theirs = pl.multiple_of((1 - core) * half, half)
            send[slot, 0] = mm(xt_all[pl.ds(theirs, half), :], dgt[...]).astype(bf16)
            send[slot, 1] = mm(xt_all[pl.ds(theirs, half), :], dut[...]).astype(bf16)
            send[slot, 2] = mm(dyt_all[pl.ds(theirs, half), :], scaled_t[...]).astype(bf16)
            keep[slot, 0] = mm(xt_all[pl.ds(mine, half), :], dgt[...]).astype(bf16)
            copy(f, slot).start()
            keep[slot, 1] = mm(xt_all[pl.ds(mine, half), :], dut[...]).astype(bf16)
            keep[slot, 2] = mm(dyt_all[pl.ds(mine, half), :], scaled_t[...]).astype(bf16)
            y_acc[...] += mm(hid_t[...], wd_ref[0])
            dx_acc[...] += mm(dgt[...], wg_ref[0], NT) + mm(dut[...], wu_ref[0], NT)

        @pl.when(f >= 1)
        def _():
            slot = lax.rem(f - 1, 2)
            copy(f - 1, slot).wait_recv()
            for n in range(3):
                sum_ref[0, n] = keep[slot, n] + taken[f - 1, n]

        @pl.when(f == steps)
        def _():
            for last in range(max(0, steps - 2), steps):
                copy(last, last % 2).wait_send()
            y_ref[...] = (gate_all[...] * y_acc[...]).astype(bf16)
            dx_ref[...] = dx_acc[...].astype(bf16)
            for g in range(groups):
                span = slice(g * CAP, (g + 1) * CAP)
                column = jnp.sum(dot_acc[span, :], axis=1, keepdims=True)
                dg_ref[g : g + 1, :] = jnp.sum(
                    jnp.where(diagonal, column, 0.0), axis=0, keepdims=True
                )

    first = pl.BlockSpec((CAP, width), lambda f: (0, 0))
    sums = shape_of((parts, 3, half, per_part), bf16)

    def sum_place(f):
        done = jnp.maximum(f - 1, 0)
        return (done // tile_part, 0, 0, done % tile_part)

    def now(f):
        return jnp.minimum(f, steps - 1)

    wide = shape_of((rows, width), bf16)
    dots = shape_of((groups, CAP), f32)
    return run(
        body,
        (steps + 1,),
        [(a, first) for a in arrived]
        + [(g, first) for g in grads]
        + [
            (gates, whole(gates)),
            (w_gate, pl.BlockSpec((1, width, tile), lambda f: (which, 0, now(f)))),
            (w_up, pl.BlockSpec((1, width, tile), lambda f: (which, 0, now(f)))),
            (w_down, pl.BlockSpec((1, tile, width), lambda f: (which, now(f), 0))),
        ],
        [(wide, whole(wide)), (wide, whole(wide)), (dots, whole(dots))]
        + [(sums, pl.BlockSpec((1, 3, half, tile), sum_place))],
        scratch=[
            pltpu.VMEM((rows, width), bf16),
            pltpu.VMEM((width, rows), bf16),
            pltpu.VMEM((rows, width), bf16),
            pltpu.VMEM((width, rows), bf16),
            pltpu.VMEM((rows, 1), f32),
            pltpu.VMEM((rows, width), f32),
            pltpu.VMEM((rows, width), f32),
            pltpu.VMEM((rows, tile), f32),
            pltpu.VMEM((rows, tile), bf16),
            pltpu.VMEM((rows, tile), bf16),
            pltpu.VMEM((rows, tile), bf16),
            pltpu.VMEM((rows, tile), bf16),
            pltpu.VMEM((2, 3, half, tile), bf16),
            pltpu.VMEM((2, 3, half, tile), bf16),
            pltpu.VMEM((steps, 3, half, tile), bf16),
            pltpu.SemaphoreType.DMA((2,)),
            pltpu.SemaphoreType.DMA((steps,)),
        ],
        flops=9 * 2 * rows * width * hidden,
        moved=12 * width * hidden + rows * width * 8,
        exps=rows * hidden,
        talks=1 + which,
    )


def slot_sum(target_ref, pieces, first_row, tile):
    total = None
    t0 = target_ref[:, 0:1]
    t1 = target_ref[:, 1:2]
    for first, ref in pieces:
        ids = first + lax.broadcasted_iota(jnp.int32, (tile, CAP), 1)
        choice = jnp.where((ids == t0) | (ids == t1), 1.0, 0.0).astype(bf16)
        part = mm(choice, ref[...])
        total = part if total is None else total + part
    return total


def token_output(base, targets, pieces):
    rows, width = base.shape
    tile = 128
    count = len(pieces)

    def body(base_ref, target_ref, *refs):
        listed = [(n * CAP, refs[n]) for n in range(count)]
        total = base_ref[...] + slot_sum(target_ref, listed, 0, tile)
        refs[count][...] = total.astype(bf16)

    row_spec = pl.BlockSpec((tile, width), lambda i: (i, 0))
    first = pl.BlockSpec((CAP, width), lambda i: (0, 0))
    return run(
        body,
        (rows // tile,),
        [(base, row_spec), (targets, pl.BlockSpec((tile, 2), lambda i: (i, 0)))]
        + [(p, first) for p in pieces],
        [(shape_of((rows, width), bf16), row_spec)],
        flops=2 * rows * width * count * CAP,
        moved=rows * width * 10,
    )[0]


def token_back(
    meta, x1, h2, grad, prob, previous, routes, targets, pieces, dots, dgate_zero, dh_zero, gain, router_t, w_out
):
    rows, width = x1.shape
    tile = 128
    count = len(pieces)
    expert_all = prob.shape[1]
    members, head_columns = w_out.shape[0], w_out.shape[1]

    def body(meta_ref, *refs):
        (x1_ref, h2_ref, dy_ref, prob_ref, prev_ref, route_ref, target_ref) = refs[:7]
        piece_refs = refs[7 : 7 + count]
        dots_ref, dz_ref, dh_ref, gain_ref, router_ref = refs[7 + count : 12 + count]
        w_refs = refs[12 + count : 12 + count + members]
        dx1_ref, low_ref = refs[12 + count + members : 14 + count + members]
        out_refs = refs[14 + count + members : 14 + count + 2 * members]
        sums_ref, carry_ref = refs[14 + count + 2 * members :]
        i = pl.program_id(0)
        prob_now = prob_ref[...]
        lanes = lax.broadcasted_iota(jnp.int32, (tile, expert_all), 1)
        dprob = jnp.zeros_like(prob_now)
        for c in range(2):
            target = target_ref[:, c : c + 1]
            dgate = dz_ref[:, c : c + 1]
            for n in range(count):
                ids = n * CAP + lax.broadcasted_iota(jnp.int32, (tile, CAP), 1)
                dgate = dgate + jnp.sum(
                    jnp.where(ids == target, dots_ref[n : n + 1, :], 0.0), axis=1, keepdims=True
                )
            dprob = dprob + jnp.where(lanes == route_ref[:, c : c + 1], dgate, 0.0)
        dlogit = prob_now * (dprob - jnp.sum(prob_now * dprob, axis=1, keepdims=True))
        h2 = h2_ref[...]
        dh2 = (
            slot_sum(target_ref, [(n * CAP, piece_refs[n]) for n in range(count)], 0, tile)
            + dh_ref[...]
            + mm_full(dlogit, router_ref[...])
        )
        x1 = x1_ref[...]
        inverse = lax.rsqrt(jnp.mean(x1 * x1, axis=1, keepdims=True) + norm_eps)
        normed = x1 * inverse
        router_part = mm_full(dlogit, h2, TN)
        carry_part = mm_full(dlogit, prev_ref[...], TN)
        gain_part = jnp.sum(dh2 * normed, axis=0, keepdims=True)

        @pl.when(i == 0)
        def _():
            sums_ref[0:expert_all, :] = router_part
            sums_ref[expert_all : expert_all + 1, :] = gain_part
            carry_ref[...] = carry_part

        @pl.when(i > 0)
        def _():
            sums_ref[0:expert_all, :] += router_part
            sums_ref[expert_all : expert_all + 1, :] += gain_part
            carry_ref[...] += carry_part

        dn = dh2 * gain_ref[...]
        dx1 = dy_ref[...].astype(f32) + inverse * (
            dn - normed * jnp.mean(dn * normed, axis=1, keepdims=True)
        )
        dx1_ref[...] = dx1
        low = dx1.astype(bf16)
        low_ref[...] = low
        for n in range(members):
            out_refs[n][...] = mm(low, w_refs[n][0], NT).astype(bf16)

    row_spec = pl.BlockSpec((tile, width), lambda i, m: (i, 0))
    pair_spec = pl.BlockSpec((tile, 2), lambda i, m: (i, 0))
    small_spec = pl.BlockSpec((tile, expert_all), lambda i, m: (i, 0))
    first = pl.BlockSpec((CAP, width), lambda i, m: (0, 0))
    sums = shape_of((expert_all + 1, width), f32)
    carry = shape_of((expert_all, expert_all), f32)
    return run(
        body,
        (rows // tile,),
        [
            (x1, row_spec),
            (h2, row_spec),
            (grad, row_spec),
            (prob, small_spec),
            (previous, small_spec),
            (routes, pair_spec),
            (targets, pair_spec),
        ]
        + [(p, first) for p in pieces]
        + [
            (dots, whole(dots)),
            (dgate_zero, pair_spec),
            (dh_zero, row_spec),
            (gain, whole(gain)),
            (router_t, whole(router_t)),
        ]
        + [
            (w_out, pl.BlockSpec((1, head_columns, width), lambda i, m, n=n: (m[0] ^ n, 0, 0)))
            for n in range(members)
        ],
        [
            (shape_of((rows, width), f32), row_spec),
            (shape_of((rows, width), bf16), row_spec),
        ]
        + [
            (
                shape_of((rows, head_columns), bf16),
                pl.BlockSpec((tile, head_columns), lambda i, m: (i, 0)),
            )
        ]
        * members
        + [(sums, whole(sums)), (carry, whole(carry))],
        meta=meta,
        flops=2 * rows * width * (count * CAP + width),
        moved=rows * width * 24,
    )


def input_back(meta, x, gain, dqkv, weights_t, dx1):
    rows, width = x.shape
    tile = 128
    members = len(dqkv)
    per_group = weights_t.shape[2]

    def body(meta_ref, x_ref, gain_ref, dx1_ref, *refs):
        d_refs = refs[:members]
        w_refs = refs[members : 2 * members]
        out_ref, sum_ref = refs[2 * members :]
        i = pl.program_id(0)
        dh = None
        for n in range(members):
            for w in range(3):
                part = mm(
                    d_refs[n][:, w * per_group : (w + 1) * per_group], w_refs[n][w, 0]
                )
                dh = part if dh is None else dh + part
        x = x_ref[...].astype(f32)
        inverse = lax.rsqrt(jnp.mean(x * x, axis=1, keepdims=True) + norm_eps)
        normed = x * inverse
        gain_part = jnp.sum(dh * normed, axis=0, keepdims=True)

        @pl.when(i == 0)
        def _():
            sum_ref[...] = gain_part

        @pl.when(i > 0)
        def _():
            sum_ref[...] += gain_part

        dn = dh * gain_ref[...]
        out_ref[...] = dx1_ref[...] + inverse * (
            dn - normed * jnp.mean(dn * normed, axis=1, keepdims=True)
        )

    row_spec = pl.BlockSpec((tile, width), lambda i, m: (i, 0))
    sums = shape_of((1, width), f32)
    return run(
        body,
        (rows // tile,),
        [(x, row_spec), (gain, whole(gain)), (dx1, row_spec)]
        + [(d, pl.BlockSpec((tile, 3 * per_group), lambda i, m: (i, 0))) for d in dqkv]
        + [
            (weights_t, pl.BlockSpec((3, 1, per_group, width), lambda i, m, n=n: (0, m[0] ^ n, 0, 0)))
            for n in range(members)
        ],
        [(shape_of((rows, width), f32), row_spec), (sums, whole(sums))],
        meta=meta,
        flops=2 * rows * width * width * 3,
        moved=rows * width * 20 + weights_t.size * 2,
    )


def sum_over_dp(parts):
    count = lax.axis_size("dp")
    mine = lax.axis_index("dp")
    if count == 2:
        out = add_low(*[pick(p, 1 - mine) for p in parts])
        return add_low(*[pick(p, mine) for p in parts], swap(out, "dp", 1))
    return lax.psum_scatter(add_low(*parts), "dp", scatter_dimension=0, tiled=False)


def gather_dp(value):
    count = lax.axis_size("dp")
    mine = lax.axis_index("dp")
    if count == 2:
        other = swap(value, "dp", 1)
        return jnp.concatenate(
            [jnp.where(mine == 0, value, other), jnp.where(mine == 0, other, value)], axis=0
        )
    return lax.all_gather(value, "dp", axis=0, tiled=True)


def sum_over_exp(value):
    bit = 1
    while bit < lax.axis_size("exp"):
        value = add_low(value, swap(value, "exp", bit))
        bit *= 2
    return value


def expert_share(sums):
    mine = sum_over_dp([sums])
    across = lax.axis_index("ctx") // 2
    halves = mine.reshape((3, 2, mine.shape[1] // 2, mine.shape[2]))
    here = lax.dynamic_index_in_dim(halves, across, 1, keepdims=False)
    there = lax.dynamic_index_in_dim(halves, 1 - across, 1, keepdims=False)
    total = add_low(here, swap(there, "ctx", 2))
    return gather_near(total, "ctx")


def place_experts(meta, pieces, which, turned):
    local, members = len(pieces), len(pieces[0])
    _, rows, columns = pieces[0][0].shape
    flat = [p for listed in pieces for p in listed]

    def body(meta_ref, *refs):
        out_ref, hold = refs[-2:]
        e = pl.program_id(0)
        for n in range(local):

            @pl.when(e == n)
            def _():
                for j in range(members):
                    member = meta_ref[0] ^ j
                    at = pl.multiple_of(
                        (lax.rem(member, 2) * 2 + lax.div(member, 2)) * rows, rows
                    )
                    piece = refs[n * members + j][0].astype(f32)
                    if turned:
                        hold[pl.ds(at, rows), :] = piece
                    else:
                        out_ref[0, pl.ds(at, rows), :] = piece

        if turned:
            out_ref[0] = jnp.transpose(hold[...])

    full = (columns, members * rows) if turned else (members * rows, columns)
    spec = pl.BlockSpec((1, rows, columns), lambda e, m: (which, 0, 0))
    return run(
        body,
        (local,),
        [(p, spec) for p in flat],
        [(shape_of((local,) + full, f32), pl.BlockSpec((1,) + full, lambda e, m: (e, 0, 0)))],
        scratch=[pltpu.VMEM((members * rows, columns) if turned else (8, 128), f32)],
        meta=meta,
        moved=sum(p.size for p in flat) * 2,
    )[0]


def place(meta, pieces, out_shape, place_of):
    block = pieces[0][0].shape
    flat = [p for listed in pieces for p in listed]
    members = len(pieces[0])

    def body(meta_ref, *refs):
        spot = pl.program_id(0) * members + pl.program_id(1)
        for n in range(len(flat)):

            @pl.when(spot == n)
            def _():
                refs[-1][0] = refs[n][...].astype(f32)

    return run(
        body,
        (len(pieces), members),
        [(p, whole(p)) for p in flat],
        [
            (
                shape_of(out_shape, f32),
                pl.BlockSpec((1,) + block, lambda e, j, m: (e,) + place_of(m[0] ^ j)),
            )
        ],
        meta=meta,
        moved=sum(p.size for p in flat) * 6,
    )[0]


def place_columns(meta, pieces, per_group):
    members = len(pieces)
    width = pieces[0].shape[1]

    def body(meta_ref, *refs):
        out_ref, hold = refs[members:]
        for n in range(members):
            at = pl.multiple_of((meta_ref[0] ^ n) * per_group, per_group)
            hold[pl.ds(at, per_group), :] = refs[n][...].astype(f32)
        out_ref[0] = jnp.transpose(hold[...])

    out = shape_of((3, width, width), f32)
    return run(
        body,
        (3,),
        [(p, pl.BlockSpec((per_group, width), lambda w, m: (w, 0))) for p in pieces],
        [(out, pl.BlockSpec((1, width, width), lambda w, m: (w, 0, 0)))],
        scratch=[pltpu.VMEM((width, width), f32)],
        meta=meta,
        moved=3 * width * width * 6,
    )[0]


def shards(
    inputs,
    lengths,
    block_order,
    routes,
    prev_logits,
    norm1_gain,
    norm2_gain,
    w_qkv,
    w_out,
    w_router,
    w_carry,
    const_logit_w,
    const_vec,
    w_gate,
    w_up,
    w_down,
    cotangent,
):
    members = lax.axis_size("ctx")
    groups = lax.axis_size("exp")
    parts = lax.axis_size("dp")
    me = lax.axis_index("ctx")
    mine = lax.axis_index("exp")
    x, grad = inputs[0], cotangent[0]
    rows, width = x.shape
    group_rows = rows * members
    deal_block = group_rows // block_order.shape[1]
    per_member = rows // deal_block
    local = w_gate.shape[0]
    expert_count = local * groups
    slots = expert_count * CAP
    head_width = width // HEADS
    heads = HEADS // members
    per_group = heads * head_width
    blocks = block_order.shape[1]
    layout = {"order": 4, "lengths": 4 + blocks, "sequences": lengths.shape[1]}
    meta = jnp.concatenate(
        [
            jnp.stack([me, mine, me % 2, me // 2]).astype(jnp.int32),
            block_order[0],
            lengths[0],
        ]
    )
    gain1 = norm1_gain.reshape(1, width)
    gain2 = norm2_gain.reshape(1, width)
    weights_t = jnp.swapaxes(w_qkv, 1, 2).reshape(3, members, per_group, width)
    w_out_parts = w_out.reshape(members, per_group, width)
    route_ids = routes[0]
    previous = prev_logits[0]

    near = gather_near(x, "ctx")
    held = None
    for j in range(members):
        held = project(j, near[j], gain1, weights_t, meta, held, group_rows)
    q, k, v, kt, vt, h1 = held
    o, ot, lse, tops = attend(meta, q, k, vt, deal_block, per_member, layout)
    o_near = [
        swap(o[j * rows : (j + 1) * rows], "ctx", j) if j else o[:rows] for j in range(members)
    ]

    targets = slot_targets(route_ids, expert_count, local, mine)
    target_rows = jnp.transpose(targets)
    grad_slots = dispatch(target_rows, grad, slots, local)
    grad_near = [
        [
            swap(grad_slots[e][g * CAP : (g + 1) * CAP], "exp", g) if g else grad_slots[e]
            for g in range(groups)
        ]
        for e in range(local)
    ]

    front = token_front(
        meta, x, o_near, w_out_parts, gain2, w_router, previous, w_carry, target_rows, local, groups
    )
    x1, h2, prob, gate_slots = front[:4]
    token_slots = front[4:]
    gate_view = gate_slots.reshape(local, groups, CAP)
    gate_near = [gate_view[:, g] if g == 0 else swap(gate_view[:, g], "exp", g) for g in range(groups)]
    token_near = [
        [
            swap(token_slots[e][g * CAP : (g + 1) * CAP], "exp", g) if g else token_slots[e]
            for g in range(groups)
        ]
        for e in range(local)
    ]
    logit_rows = jnp.swapaxes(const_logit_w, 1, 2).reshape(-1, width)
    base, dh_zero, dgate_zero, gates, zero_sums = token_zero(
        x1, h2, grad, prob, route_ids, logit_rows, const_vec, expert_count
    )

    out_rows, in_rows, dot_rows, shares = [], [], [], []
    for e in range(local):
        gate_rows = jnp.stack([gate_near[g][e] for g in range(groups)])
        y, dx, dots, sums = expert_layer(
            e, token_near[e], grad_near[e], gate_rows, w_gate, w_up, w_down, parts
        )
        in_rows += [swap(dx[g * CAP : (g + 1) * CAP], "exp", g) if g else dx for g in range(groups)]
        dot_rows += [swap(dots[g : g + 1], "exp", g) if g else dots[:1] for g in range(groups)]
        out_rows += [swap(y[g * CAP : (g + 1) * CAP], "exp", g) if g else y for g in range(groups)]
        shares.append(expert_share(sums))

    back = token_back(
        meta,
        x1,
        h2,
        grad,
        prob,
        previous,
        route_ids,
        targets,
        in_rows,
        jnp.concatenate(dot_rows, axis=0),
        dgate_zero,
        dh_zero,
        gain2,
        jnp.transpose(w_router),
        w_out_parts,
    )
    dx1, da = back[:2]
    do_near = [back[2 + j] if j == 0 else swap(back[2 + j], "ctx", j) for j in range(members)]
    token_sums, carry_sum = back[2 + members :]
    result = token_output(base, targets, out_rows)

    out_parts = [
        mm(o_near[j], da, TN).astype(bf16) for j in range(members)
    ]
    bit = 1
    while bit < members:
        kept = [j for j in range(members) if j % (2 * bit) == 0]
        out_parts = {
            j: add_low(out_parts[j], swap(out_parts[j + bit], "ctx", bit)) for j in kept
        }
        bit *= 2
    out_sum = out_parts[0]

    dqkv = attend_back(meta, q, k, v, kt, do_near, ot, lse, deal_block, per_member, layout)
    dqkv_near = [
        swap(dqkv[j * rows : (j + 1) * rows], "ctx", j) if j else dqkv[:rows]
        for j in range(members)
    ]
    qkv_sum = mm(dqkv, h1, TN).astype(bf16)
    input_grad, norm1_sum = input_back(meta, x, gain1, dqkv_near, weights_t, dx1)

    def dense_total(value):
        share = sum_over_dp([value.reshape((parts, value.shape[0] // parts, width))])
        return gather_near(gather_dp(sum_over_exp(share)), "ctx")

    out_grad = place(
        meta, [dense_total(out_sum)], (1, width, width), lambda a: (a, 0)
    )[0]
    qkv_grad = place_columns(meta, dense_total(qkv_sum), per_group)

    expert_all = w_router.shape[1]
    small = jnp.concatenate(
        [token_sums, zero_sums, jnp.pad(carry_sum, ((0, 0), (0, width - expert_all)))], axis=0
    )
    small = butterfly(small, jnp.add)
    norm1_grad = butterfly(norm1_sum, jnp.add)
    kinds = const_vec.shape[0]
    router_grad = jnp.transpose(small[:expert_all])
    norm2_grad = small[expert_all]
    at = expert_all + 1
    vec_grad = small[at : at + kinds]
    logit_grad = jnp.swapaxes(small[at + kinds : at + 3 * kinds].reshape(kinds, 2, width), 1, 2)
    carry_grad = jnp.transpose(small[at + 3 * kinds :, :expert_all])

    local_tops = jnp.max(tops, axis=1)
    top_all = jnp.zeros((members, heads), f32).at[me].set(local_tops)
    top_all = jnp.where(jnp.arange(members)[:, None] == me, top_all, low_start)
    head_max = butterfly(top_all, jnp.maximum).reshape(HEADS)
    clip_ratio = jnp.sqrt(jnp.minimum(1.0, clip_limit / head_max))
    head_scale = jnp.repeat(clip_ratio, head_width)
    clipped = w_qkv[:2].astype(f32) * head_scale[None, None, :]

    gate_grad = place_experts(meta, shares, 0, False)
    up_grad = place_experts(meta, shares, 1, False)
    down_grad = place_experts(meta, shares, 2, True)
    return (
        result[None],
        input_grad[None],
        norm1_grad[0],
        norm2_grad,
        qkv_grad,
        out_grad,
        router_grad,
        carry_grad,
        logit_grad,
        vec_grad,
        gate_grad,
        up_grad,
        down_grad,
        clipped,
    )


def solution(mesh):
    tokens = P(("dp", "exp"), "ctx", None)
    packs = P(("dp", "exp"), None)
    experts = P("exp", None, None)
    in_specs = (
        tokens, packs, packs, tokens, tokens, P(), P(), P(), P(), P(), P(), P(), P(),
        experts, experts, experts, tokens,
    )
    out_specs = (
        tokens, tokens, P(), P(), P(), P(), P(), P(), P(), P(),
        P("exp", None, "dp"), P("exp", None, "dp"), P("exp", "dp", None), P(),
    )
    return jax.shard_map(shards, mesh=mesh, in_specs=in_specs, out_specs=out_specs, check_vma=False)
```

```python
import functools

import jax
import jax.numpy as jnp
from jax import lax
from jax.experimental import pallas as pl
from jax.experimental.pallas import tpu as pltpu
from jax.sharding import PartitionSpec as P

HEADS = 12
CAP = 128

norm_eps = 1e-05
clip_limit = 3.0
low_start = -1e30
mask_fill = -3e38
highest = lax.Precision.HIGHEST
NN = (((1,), (0,)), ((), ()))
NT = (((1,), (1,)), ((), ()))
TN = (((0,), (0,)), ((), ()))
f32 = jnp.float32
bf16 = jnp.bfloat16
MESH = pl.DeviceIdType.MESH


def mm(left, right, dims=NN):
    return lax.dot_general(left, right, dims, preferred_element_type=f32)


def mm_full(left, right, dims=NN):
    return lax.dot_general(left, right, dims, precision=highest, preferred_element_type=f32)


def shape_of(shape, dtype):
    return jax.ShapeDtypeStruct(shape, dtype)


def whole(array):
    rank = len(array.shape)
    return pl.BlockSpec(array.shape, lambda *_: (0,) * rank)


def cost(flops, moved, exps=0):
    return pl.CostEstimate(flops=int(flops), bytes_accessed=int(moved), transcendentals=int(exps))


def run(body, grid, inputs, outputs, scratch=(), meta=None, flops=0, moved=0, exps=0, aliases=None, talks=None):
    prefetch = 0 if meta is None else 1
    args = ([] if meta is None else [meta]) + [a for a, _ in inputs]
    return pl.pallas_call(
        body,
        out_shape=[o for o, _ in outputs],
        grid_spec=pltpu.PrefetchScalarGridSpec(
            num_scalar_prefetch=prefetch,
            grid=grid,
            in_specs=[s for _, s in inputs],
            out_specs=[s for _, s in outputs],
            scratch_shapes=list(scratch),
        ),
        compiler_params=pltpu.CompilerParams(
            dimension_semantics=("arbitrary",) * len(grid),
            vmem_limit_bytes=60 * 1024 * 1024,
            collective_id=talks,
            has_side_effects=talks is not None,
        ),
        cost_estimate=cost(flops, moved, exps),
        input_output_aliases={} if aliases is None else aliases,
    )(*args)


def swap(value, axis, distance):
    count = lax.axis_size(axis)
    return lax.ppermute(value, axis, [(i, i ^ distance) for i in range(count)])


def flip(value, bits):
    bit = 1
    while bit <= bits:
        if bits & bit:
            value = value + bit - 2 * bit * lax.rem(lax.div(value, bit), 2)
        bit *= 2
    return value


def powers(axis):
    found, bit = [], 1
    while bit < lax.axis_size(axis):
        found.append(bit)
        bit *= 2
    return found


def slot_peer(r, count, exp_now, me):
    return {"exp": flip(exp_now, r // count), "ctx": flip(me, 2 * (r % count))}


def slot_swap(value, r, count):
    groups = lax.axis_size("exp")
    total = groups * lax.axis_size("ctx")
    apart = 2 * (r % count) * groups + r // count
    return lax.ppermute(value, ("ctx", "exp"), [(i, i ^ apart) for i in range(total)])


def remote(src, dst, sent, arrived, peer):
    return pltpu.make_async_remote_copy(
        src_ref=src, dst_ref=dst, send_sem=sent, recv_sem=arrived,
        device_id=peer, device_id_type=MESH,
    )


def greet(peers):
    barrier = pltpu.get_barrier_semaphore()
    for peer in peers:
        pl.semaphore_signal(barrier, inc=1, device_id=peer, device_id_type=MESH)
    return lambda: pl.semaphore_wait(barrier, len(peers))


anywhere = pl.BlockSpec(memory_space=pl.ANY)
scalars = pl.BlockSpec(memory_space=pltpu.SMEM)
vector = pl.BlockSpec(memory_space=pltpu.VMEM)
dma = pltpu.SemaphoreType.DMA


def gather_near(value, axis):
    count = lax.axis_size(axis)
    found = {0: value}
    bit = count // 2
    while bit:
        for have in list(found):
            found[have | bit] = swap(found[have], axis, bit)
        bit //= 2
    return [found[j] for j in range(count)]


def add_low(*terms):
    total = terms[0].astype(f32)
    for term in terms[1:]:
        total = total + term.astype(f32)
    return total.astype(bf16)


def project(turn, rows_low, gain, weights_t, meta, earlier, group_rows, tile, layout):
    row_count, width = rows_low.shape
    per_group = weights_t.shape[2]
    head_width = width // HEADS
    heads = per_group // head_width
    steps = row_count // tile
    scale = head_width**-0.5

    def body(meta_ref, x_ref, gain_ref, w_ref, *refs):
        q_ref, k_ref, v_ref, kt_ref, vt_ref, h_ref = refs[-6:]
        x = x_ref[...].astype(f32)
        inverse = lax.rsqrt(jnp.mean(x * x, axis=1, keepdims=True) + norm_eps)
        low = (x * inverse * gain_ref[...]).astype(bf16)
        h_ref[...] = low
        q = mm(low, w_ref[0, 0], NT).astype(bf16) * jnp.asarray(scale, bf16)
        k = mm(low, w_ref[1, 0], NT).astype(bf16)
        v = mm(low, w_ref[2, 0], NT).astype(bf16)
        for h in range(heads):
            part = slice(h * head_width, (h + 1) * head_width)
            q_ref[h] = q[:, part]
            k_ref[h] = k[:, part]
            v_ref[h] = v[:, part]
        kt_ref[...] = mm(w_ref[1, 0], low, NT).astype(bf16)
        vt_ref[...] = mm(w_ref[2, 0], low, NT).astype(bf16)

    by_head = shape_of((heads, group_rows, head_width), bf16)
    by_column = shape_of((per_group, group_rows), bf16)
    hidden = shape_of((group_rows, width), bf16)
    head_spec = pl.BlockSpec((heads, tile, head_width), lambda i, m: (0, block_place(m, turn * steps + i, steps, layout), 0))
    column_spec = pl.BlockSpec((per_group, tile), lambda i, m: (0, block_place(m, turn * steps + i, steps, layout)))
    hidden_spec = pl.BlockSpec((tile, width), lambda i, m: (turn * steps + i, 0))
    inputs = [
        (rows_low, pl.BlockSpec((tile, width), lambda i, m: (i, 0))),
        (gain, pl.BlockSpec((1, width), lambda i, m: (0, 0))),
        (weights_t, pl.BlockSpec((3, 1, per_group, width), lambda i, m: (0, m[0], 0, 0))),
    ]
    aliases = None
    if earlier is not None:
        inputs += [(a, pl.BlockSpec(memory_space=pl.ANY)) for a in earlier]
        aliases = {4 + n: n for n in range(6)}
    return run(
        body,
        (steps,),
        inputs,
        [(by_head, head_spec)] * 3 + [(by_column, column_spec)] * 2 + [(hidden, hidden_spec)],
        meta=meta,
        flops=2 * row_count * width * per_group * 5,
        moved=row_count * width * 8 + weights_t.size // 2,
        aliases=aliases,
    )


def block_place(meta_ref, block, per_member, layout):
    member = meta_ref[0] ^ (block // per_member)
    return meta_ref[layout["order"] + member * per_member + block % per_member]


def document_start(meta_ref, position, layout):
    start = jnp.zeros_like(position)
    end = jnp.int32(0)
    for s in range(layout["sequences"]):
        end = end + meta_ref[layout["lengths"] + s]
        start = jnp.where(position >= end, end, start)
    return start


def block_range(meta_ref, query_block, key_block, rows, layout):
    q_first = query_block * rows
    k_first = key_block * rows
    begin = document_start(meta_ref, q_first, layout)
    begin_last = document_start(meta_ref, q_first + rows - 1, layout)
    needed = (k_first <= q_first) & (k_first + rows - 1 >= begin)
    full = (k_first < q_first) & (k_first >= begin_last)
    return q_first, k_first, needed, full


def allowed_pairs(meta_ref, q_first, k_first, rows, layout):
    q_pos = q_first + lax.broadcasted_iota(jnp.int32, (1, rows), 1)
    k_pos = k_first + lax.broadcasted_iota(jnp.int32, (rows, 1), 0)
    return (k_pos <= q_pos) & (k_pos >= document_start(meta_ref, q_pos, layout))


def attend(meta, q, k, vt, rows, layout):
    heads, group_rows, head_width = q.shape
    blocks = group_rows // rows
    width = heads * head_width

    def body(meta_ref, q_ref, k_ref, vt_ref, o_ref, ot_ref, lse_ref, top_ref, m_ref, l_ref, a_ref):
        i = pl.program_id(0)
        m_ref[...] = jnp.full_like(m_ref, low_start)
        l_ref[...] = jnp.zeros_like(l_ref)
        a_ref[...] = jnp.zeros_like(a_ref)

        def one(j, _):
            q_first, k_first, needed, full = block_range(meta_ref, i, j, rows, layout)
            at = pl.multiple_of(j * rows, rows)

            def step(masked):
                if masked:
                    allowed = allowed_pairs(meta_ref, q_first, k_first, rows, layout)
                for h in range(heads):
                    part = slice(h * head_width, (h + 1) * head_width)
                    s = mm(k_ref[h, pl.ds(at, rows), :], q_ref[h], NT)
                    if masked:
                        s = jnp.where(allowed, s, mask_fill)
                    old = m_ref[h]
                    new = jnp.maximum(old, jnp.max(s, axis=0, keepdims=True))
                    shrink = jnp.exp(old - new)
                    p = jnp.exp(s - new)
                    m_ref[h] = new
                    l_ref[h] = l_ref[h] * shrink + jnp.sum(p, axis=0, keepdims=True)
                    a_ref[part, :] = a_ref[part, :] * shrink + mm(
                        vt_ref[part, pl.ds(at, rows)], p.astype(bf16)
                    )

            @pl.when(full)
            def _():
                step(False)

            @pl.when(needed & jnp.logical_not(full))
            def _():
                step(True)

            return 0

        lax.fori_loop(0, i + 1, one, 0)
        for h in range(heads):
            part = slice(h * head_width, (h + 1) * head_width)
            ot_ref[part, :] = a_ref[part, :] / l_ref[h]
            lse_ref[pl.ds(h, 1), :] = m_ref[h] + jnp.log(l_ref[h])
            top_ref[pl.ds(h, 1), :] = m_ref[h]
        o_ref[...] = jnp.transpose(ot_ref[...]).astype(bf16)

    row = shape_of((heads, group_rows), f32)
    row_spec = pl.BlockSpec((heads, rows), lambda i, m: (0, i))
    return run(
        body,
        (blocks,),
        [
            (q, pl.BlockSpec((heads, rows, head_width), lambda i, m: (0, i, 0))),
            (k, whole(k)),
            (vt, whole(vt)),
        ],
        [
            (
                shape_of((group_rows, width), bf16),
                pl.BlockSpec((rows, width), lambda i, m: (m[layout["inverse"] + i], 0)),
            ),
            (shape_of((width, group_rows), f32), pl.BlockSpec((width, rows), lambda i, m: (0, i))),
            (row, row_spec),
            (row, row_spec),
        ],
        scratch=[
            pltpu.VMEM((heads, 1, rows), f32),
            pltpu.VMEM((heads, 1, rows), f32),
            pltpu.VMEM((width, rows), f32),
        ],
        meta=meta,
        flops=2 * 2 * group_rows * group_rows * width,
        moved=group_rows * width * 14,
        exps=group_rows * group_rows * heads // 2,
    )


def attend_back(meta, q, k, v, kt, grad, ot, lse, rows, layout):
    heads, group_rows, head_width = q.shape
    blocks = group_rows // rows
    width = heads * head_width
    scale = head_width**-0.5
    members = len(grad)
    per = grad[0].shape[0] // rows

    def body(meta_ref, q_ref, k_ref, v_ref, kt_ref, *refs):
        grads = refs[:members]
        ot_ref, lse_ref, out_ref, dk_ref, dv_ref, dq_ref, g_ref, delta_ref = refs[members:]
        i = pl.program_id(0)

        @pl.when(i == 0)
        def _():
            dk_ref[...] = jnp.zeros_like(dk_ref)
            dv_ref[...] = jnp.zeros_like(dv_ref)

        for n in range(members):

            @pl.when(meta_ref[layout["inverse"] + i] // per == n)
            def _():
                g = grads[n][...]
                for h in range(heads):
                    g_ref[h] = g[:, h * head_width : (h + 1) * head_width]
                product = jnp.transpose(g.astype(f32)) * ot_ref[...]
                for h in range(heads):
                    part = slice(h * head_width, (h + 1) * head_width)
                    delta_ref[h] = jnp.sum(product[part, :], axis=0, keepdims=True)

        dq_ref[...] = jnp.zeros_like(dq_ref)

        def one(j, _):
            q_first, k_first, needed, full = block_range(meta_ref, i, j, rows, layout)
            at = pl.multiple_of(j * rows, rows)

            def step(masked):
                if masked:
                    allowed = allowed_pairs(meta_ref, q_first, k_first, rows, layout)
                for h in range(heads):
                    part = slice(h * head_width, (h + 1) * head_width)
                    s = mm(k_ref[h, pl.ds(at, rows), :], q_ref[h], NT)
                    if masked:
                        s = jnp.where(allowed, s, mask_fill)
                    p = jnp.exp(s - lse_ref[pl.ds(h, 1), :])
                    dp = mm(v_ref[h, pl.ds(at, rows), :], g_ref[h], NT)
                    ds = (p * (dp - delta_ref[h])).astype(bf16)
                    dv_ref[h, pl.ds(at, rows), :] += mm(p.astype(bf16), g_ref[h])
                    dk_ref[h, pl.ds(at, rows), :] += mm(ds, q_ref[h])
                    dq_ref[part, :] += mm(kt_ref[part, pl.ds(at, rows)], ds)

            @pl.when(full)
            def _():
                step(False)

            @pl.when(needed & jnp.logical_not(full))
            def _():
                step(True)

            return 0

        lax.fori_loop(0, i + 1, one, 0)
        here = pl.multiple_of(meta_ref[layout["inverse"] + i] * rows, rows)
        out_ref[pl.ds(here, rows), 0:width] = (jnp.transpose(dq_ref[...]) * scale).astype(bf16)

        @pl.when(i == blocks - 1)
        def _():
            def store(b, _):
                spot = pl.multiple_of(b * rows, rows)
                there = pl.multiple_of(meta_ref[layout["inverse"] + b] * rows, rows)
                out_ref[pl.ds(there, rows), width : 3 * width] = jnp.concatenate(
                    [dk_ref[h, pl.ds(spot, rows), :] for h in range(heads)]
                    + [dv_ref[h, pl.ds(spot, rows), :] for h in range(heads)],
                    axis=1,
                ).astype(bf16)
                return 0

            lax.fori_loop(0, blocks, store, 0)

    grad_specs = [
        pl.BlockSpec((rows, width), lambda i, m, n=n: (jnp.clip(m[layout["inverse"] + i] - n * per, 0, per - 1), 0))
        for n in range(members)
    ]
    out = shape_of((group_rows, 3 * width), bf16)
    return run(
        body,
        (blocks,),
        [
            (q, pl.BlockSpec((heads, rows, head_width), lambda i, m: (0, i, 0))),
            (k, whole(k)),
            (v, whole(v)),
            (kt, whole(kt)),
        ]
        + list(zip(grad, grad_specs))
        + [
            (ot, pl.BlockSpec((width, rows), lambda i, m: (0, i))),
            (lse, pl.BlockSpec((heads, rows), lambda i, m: (0, i))),
        ],
        [(out, whole(out))],
        scratch=[
            pltpu.VMEM((heads, group_rows, head_width), f32),
            pltpu.VMEM((heads, group_rows, head_width), f32),
            pltpu.VMEM((width, rows), f32),
            pltpu.VMEM((heads, rows, head_width), bf16),
            pltpu.VMEM((heads, 1, rows), f32),
        ],
        meta=meta,
        flops=5 * 2 * group_rows * group_rows * width,
        moved=group_rows * width * 24,
        exps=group_rows * group_rows * heads // 2,
    )[0]


def slot_targets(route_ids, expert_count, local_experts, mine, side):
    rows = route_ids.shape[0]
    experts = jnp.arange(expert_count, dtype=jnp.int32)
    hits = route_ids[:, :, None] == experts[None, None, :]
    hit = jnp.any(hits, axis=1)
    order = lax.broadcasted_iota(jnp.int32, (rows, rows), 0)
    other = lax.broadcasted_iota(jnp.int32, (rows, rows), 1)
    ahead = mm((other < order).astype(bf16), hit.astype(bf16)).astype(jnp.int32)
    rank = jnp.sum(jnp.where(hits, ahead[:, None, :], 0), axis=2)
    near = ((route_ids // local_experts) ^ mine) * local_experts + (
        (route_ids % local_experts) ^ side
    )
    return jnp.where(route_ids < expert_count, near * CAP + rank, -1)


def slot_choice(first, count, target_ref):
    rows = target_ref.shape[1]
    ids = first + lax.broadcasted_iota(jnp.int32, (count, rows), 0)
    match = (ids == target_ref[0:1, :]) | (ids == target_ref[1:2, :])
    return jnp.where(match, 1.0, 0.0).astype(bf16)


def dispatch(target_rows, source, places):
    rows, width = source.shape

    def body(target_ref, source_ref, out_ref):
        choice = slot_choice(pl.program_id(0) * CAP, CAP, target_ref)
        out_ref[0] = mm(choice, source_ref[...]).astype(bf16)

    return run(
        body,
        (places,),
        [(target_rows, whole(target_rows)), (source, whole(source))],
        [
            (
                shape_of((places, CAP, width), bf16),
                pl.BlockSpec((1, CAP, width), lambda r: (r, 0, 0)),
            )
        ],
        flops=2 * rows * width * places * CAP,
        moved=(rows + places * CAP) * width * 2,
    )[0]


def token_front(
    x, o, w_out, gain, w_router, previous, w_carry, target_rows, grad, routes, logit_w, vectors, local
):
    rows, width = x.shape
    members, columns = w_out.shape[0], w_out.shape[1]
    expert_all = w_router.shape[1]
    groups = lax.axis_size("exp")
    places = groups * local
    expert_count = places
    kinds = vectors.shape[0]
    tile = 128

    def body(*refs):
        (x_ref, o_hbm, w_ref, gain_ref, router_ref, prev_ref, carry_ref, target_ref) = refs[:8]
        dy_ref, route_ref, lw_ref, vec_ref = refs[8:12]
        x1_ref, h2_ref, prob_ref, rows_out, gates_out, base_ref, dh_ref, dgate_ref, sums_ref = refs[12:21]
        o_near, low, split, packed, arrived, gate_mine, gate_near = refs[21:28]
        o_s, o_r, t_s, t_r, g_s, g_r, out_sem = refs[28:]
        me, exp_now = lax.axis_index("ctx"), lax.axis_index("exp")
        side = lax.div(me, 2)
        peers = [{"ctx": flip(me, j)} for j in range(1, members)]
        peers += [slot_peer(r, local, exp_now, me) for r in range(local, places)]
        ready = greet(peers)

        def o_copy(j):
            src = o_hbm.at[pl.ds(j * rows, rows), :]
            if j == 0:
                return pltpu.make_async_copy(src, o_near.at[0], o_r.at[0])
            return remote(src, o_near.at[j], o_s.at[j], o_r.at[j], {"ctx": flip(me, j)})

        def row_copy(r):
            return remote(
                packed.at[r], arrived.at[r], t_s.at[r], t_r.at[r], slot_peer(r, local, exp_now, me)
            )

        def gate_copy(r):
            return remote(
                gate_mine.at[r], gate_near.at[r], g_s.at[r], g_r.at[r],
                slot_peer(r, local, exp_now, me),
            )

        o_copy(0).start()
        ready()
        for j in range(1, members):
            o_copy(j).start()
        for j in range(members):
            o_copy(j).wait()

        def front_rows(t, _):
            here = pl.ds(pl.multiple_of(t * tile, tile), tile)
            total = x_ref[here, :].astype(f32)
            for j in range(members):
                total = total + mm(o_near[j, here, :], w_ref[flip(me, j)])
            x1_ref[here, :] = total
            inverse = lax.rsqrt(jnp.mean(total * total, axis=1, keepdims=True) + norm_eps)
            h2 = total * inverse * gain_ref[...]
            h2_ref[here, :] = h2
            logits = mm_full(h2, router_ref[...]) + mm_full(prev_ref[here, :], carry_ref[...])
            shifted = jnp.exp(logits - jnp.max(logits, axis=1, keepdims=True))
            prob = shifted / jnp.sum(shifted, axis=1, keepdims=True)
            prob_ref[here, :] = prob
            low[here, :] = h2.astype(bf16)
            top = prob.astype(bf16)
            rest = prob - top.astype(f32)
            middle = rest.astype(bf16)
            split[0, here, :] = top
            split[1, here, :] = middle
            split[2, here, :] = (rest - middle.astype(f32)).astype(bf16)
            return 0

        lax.fori_loop(0, rows // tile, front_rows, 0)
        diagonal = lax.broadcasted_iota(jnp.int32, (CAP, CAP), 0) == lax.broadcasted_iota(
            jnp.int32, (CAP, CAP), 1
        )
        lanes = lax.broadcasted_iota(jnp.int32, (CAP, expert_all), 1)
        for r in list(range(1, places)) + [0]:
            choice = slot_choice(r * CAP, CAP, target_ref)
            packed[r] = mm(choice, low[...]).astype(bf16)
            picked = mm(choice, split[0]) + mm(choice, split[1]) + mm(choice, split[2])
            expert = flip(exp_now, r // local) * local + flip(side, r % local)
            column = jnp.sum(jnp.where(lanes == expert, picked, 0.0), axis=1, keepdims=True)
            gate_mine[r] = jnp.sum(jnp.where(diagonal, column, 0.0), axis=0, keepdims=True)
            last = r - 1 if r else places - 1
            if last:
                row_copy(last).start()
                gate_copy(last).start()

        def own_copy(n):
            src, dst = (packed, rows_out) if n == 0 else (gate_mine, gates_out)
            return pltpu.make_async_copy(src.at[0], dst.at[0], out_sem.at[n])

        own_copy(0).start()
        own_copy(1).start()

        def zero_rows(t, _):
            here = pl.ds(pl.multiple_of(t * tile, tile), tile)
            h2 = h2_ref[here, :]
            dy = dy_ref[here, :].astype(f32)
            prob_now = prob_ref[here, :]
            classes = lax.broadcasted_iota(jnp.int32, (tile, expert_all), 1)
            chosen = route_ref[here, :]
            ids = [chosen[:, c : c + 1] for c in range(2)]
            gates = [
                jnp.sum(jnp.where(classes == r, prob_now, 0.0), axis=1, keepdims=True) for r in ids
            ]
            along = jnp.sum(dy * h2, axis=1, keepdims=True)
            copies = [(r == expert_count + 1).astype(f32) for r in ids]
            keep = copies[0] * gates[0] + copies[1] * gates[1]
            dgates = [copies[c] * along for c in range(2)]
            scores = [
                jnp.sum(h2 * lw_ref[n : n + 1, :], axis=1, keepdims=True) for n in range(2 * kinds)
            ]
            base = x1_ref[here, :]
            dh = jnp.zeros_like(h2)
            for j in range(kinds):
                top = jnp.maximum(scores[2 * j], scores[2 * j + 1])
                e0 = jnp.exp(scores[2 * j] - top)
                e1 = jnp.exp(scores[2 * j + 1] - top)
                a0 = e0 / (e0 + e1)
                a1 = e1 / (e0 + e1)
                vec = vec_ref[j : j + 1, :]
                along_vec = jnp.sum(dy * vec, axis=1, keepdims=True)
                these = [(r == expert_count + 2 + j).astype(f32) for r in ids]
                weight = these[0] * gates[0] + these[1] * gates[1]
                for c in range(2):
                    dgates[c] = dgates[c] + these[c] * (a0 * along + a1 * along_vec)
                keep = keep + weight * a0
                base = base + (weight * a1) * vec
                d0 = weight * along
                d1 = weight * along_vec
                mean = a0 * d0 + a1 * d1
                z0 = a0 * (d0 - mean)
                z1 = a1 * (d1 - mean)
                dh = dh + z0 * lw_ref[2 * j : 2 * j + 1, :] + z1 * lw_ref[2 * j + 1 : 2 * j + 2, :]
                sums_ref[j : j + 1, :] += jnp.sum((weight * a1) * dy, axis=0, keepdims=True)
                at = kinds + 2 * j
                sums_ref[at : at + 1, :] += jnp.sum(z0 * h2, axis=0, keepdims=True)
                sums_ref[at + 1 : at + 2, :] += jnp.sum(z1 * h2, axis=0, keepdims=True)
            base_ref[here, :] = base + keep * h2
            dh_ref[here, :] = dh + keep * dy
            dgate_ref[here, :] = jnp.concatenate(dgates, axis=1)
            return 0

        sums_ref[...] = jnp.zeros_like(sums_ref)
        lax.fori_loop(0, rows // tile, zero_rows, 0)

        def rows_store(r):
            return pltpu.make_async_copy(arrived.at[r], rows_out.at[r], out_sem.at[2 * r])

        def gates_store(r):
            return pltpu.make_async_copy(gate_near.at[r], gates_out.at[r], out_sem.at[2 * r + 1])

        for r in range(1, places):
            row_copy(r).wait()
            gate_copy(r).wait()
            rows_store(r).start()
            gates_store(r).start()
        own_copy(0).wait()
        own_copy(1).wait()
        for r in range(1, places):
            rows_store(r).wait()
            gates_store(r).wait()

    wide = shape_of((rows, width), f32)
    placed = shape_of((places, CAP, width), bf16)
    lines = shape_of((places, 1, CAP), f32)
    return run(
        body,
        (),
        [(x, vector), (o, anywhere), (w_out, vector), (gain, vector), (w_router, vector)]
        + [(previous, vector), (w_carry, vector), (target_rows, vector), (grad, vector)]
        + [(routes, vector), (logit_w, vector), (vectors, vector)],
        [(wide, vector), (wide, vector), (shape_of((rows, expert_all), f32), vector)]
        + [(placed, anywhere), (lines, anywhere), (wide, vector), (wide, vector)]
        + [(shape_of((rows, 2), f32), vector), (shape_of((3 * kinds, width), f32), vector)],
        scratch=[
            pltpu.VMEM((members, rows, columns), bf16),
            pltpu.VMEM((rows, width), bf16),
            pltpu.VMEM((3, rows, expert_all), bf16),
            pltpu.VMEM((places, CAP, width), bf16),
            pltpu.VMEM((places, CAP, width), bf16),
            pltpu.VMEM((places, 1, CAP), f32),
            pltpu.VMEM((places, 1, CAP), f32),
            dma((members,)), dma((members,)),
            dma((places,)), dma((places,)), dma((places,)), dma((places,)),
            dma((2 * places,)),
        ],
        flops=2 * rows * width * (width + places * CAP),
        moved=rows * width * 30,
        talks=1,
    )


def expert_layer(arrived, grads, gates, w_gate, w_up, w_down):
    places = arrived.shape[0]
    local = w_gate.shape[0]
    rows = places * CAP
    width, hidden = w_gate.shape[1], w_gate.shape[2]
    parts = lax.axis_size("dp")
    half = width // 2
    per_part = hidden // parts
    tile = min(256, per_part)
    steps = hidden // tile
    tiles = per_part // tile
    away = steps - tiles
    chunk = 256

    def body(*refs):
        x_ref, dy_ref, gates_ref, wg_hbm, wu_hbm, wd_hbm = refs[:6]
        y_out, dx_out, dots_out, sum_out = refs[6:10]
        x_all, xt_all, dy_all, dyt_all, gate_all, y_acc, dx_acc, dot_acc = refs[10:18]
        hid_t, dgt, dut, scaled_t, wg_buf, wu_buf, wd_buf = refs[18:25]
        send, total, taken, far, dx_low, dx_near, dots, dots_near = refs[25:33]
        w_sem, c_s, c_r, f_s, f_r, b_s, b_r, d_s, d_r, out_sem = refs[33:]
        me, exp_now, dp_now = lax.axis_index("ctx"), lax.axis_index("exp"), lax.axis_index("dp")
        core, side = lax.rem(me, 2), lax.div(me, 2)
        sibling = {"ctx": flip(me, 1)}
        peers = [sibling] + [{"dp": flip(dp_now, d)} for d in range(1, parts)]
        peers += [slot_peer(r, local, exp_now, me) for r in range(1, places)]
        ready = greet(peers)
        diagonal = lax.broadcasted_iota(jnp.int32, (CAP, CAP), 0) == lax.broadcasted_iota(
            jnp.int32, (CAP, CAP), 1
        )

        def dp_of(f):
            distance = parts - 1 - lax.div(f, tiles)
            found, bit = dp_now, 1
            while bit < parts:
                on = lax.rem(lax.div(distance, bit), 2)
                now = lax.rem(lax.div(found, bit), 2)
                found = found + on * bit * (1 - 2 * now)
                bit *= 2
            return found

        def weights(f, slot):
            at = pl.multiple_of(dp_of(f) * per_part + lax.rem(f, tiles) * tile, tile)
            return [
                pltpu.make_async_copy(
                    wg_hbm.at[side, :, pl.ds(at, tile)], wg_buf.at[slot], w_sem.at[0, slot]
                ),
                pltpu.make_async_copy(
                    wu_hbm.at[side, :, pl.ds(at, tile)], wu_buf.at[slot], w_sem.at[1, slot]
                ),
                pltpu.make_async_copy(
                    wd_hbm.at[side, pl.ds(at, tile), :], wd_buf.at[slot], w_sem.at[2, slot]
                ),
            ]

        def core_copy(f, slot):
            return remote(send.at[slot], taken.at[f], c_s.at[slot], c_r.at[f], sibling)

        def far_copy(f):
            return remote(total.at[f], far.at[f], f_s.at[f], f_r.at[f], {"dp": dp_of(f)})

        def back_copy(r):
            return remote(
                dx_low.at[r], dx_near.at[r], b_s.at[r], b_r.at[r],
                slot_peer(r, local, exp_now, me),
            )

        def dots_copy(r):
            return remote(
                dots.at[r], dots_near.at[r], d_s.at[r], d_r.at[r],
                slot_peer(r, local, exp_now, me),
            )

        for copy in weights(0, 0):
            copy.start()
        for r in range(places):
            here = slice(r * CAP, (r + 1) * CAP)
            x_all[here, :] = x_ref[r]
            xt_all[:, here] = jnp.transpose(x_ref[r])
            dy_all[here, :] = dy_ref[r]
            dyt_all[:, here] = jnp.transpose(dy_ref[r])
            gate_all[here, :] = jnp.sum(
                jnp.where(diagonal, gates_ref[r], 0.0), axis=1, keepdims=True
            )
        y_acc[...] = jnp.zeros_like(y_acc)
        dx_acc[...] = jnp.zeros_like(dx_acc)
        dot_acc[...] = jnp.zeros_like(dot_acc)
        ready()
        mine = pl.ds(pl.multiple_of(core * half, half), half)
        theirs = pl.ds(pl.multiple_of((1 - core) * half, half), half)

        def core_sum(f):
            core_copy(f, lax.rem(f, 2)).wait_recv()
            for n in range(3):
                total[f, n] = (total[f, n].astype(f32) + taken[f, n].astype(f32)).astype(bf16)

        def step(f, _):
            slot = lax.rem(f, 2)
            for copy in weights(f, slot):
                copy.wait()

            @pl.when(f + 1 < steps)
            def _():
                for copy in weights(f + 1, 1 - slot):
                    copy.start()

            wg, wu, wd = wg_buf.at[slot], wu_buf.at[slot], wd_buf.at[slot]

            def row_chunk(c, _):
                here = pl.ds(pl.multiple_of(c * chunk, chunk), chunk)
                g_pre = mm(x_all[here, :], wg[...])
                u_pre = mm(x_all[here, :], wu[...])
                back = mm(dy_all[here, :], wd[...], NT)
                gate = gate_all[here, :]
                sig = 1.0 / (1.0 + jnp.exp(-g_pre))
                act = g_pre * sig
                hid = act * u_pre
                hid_t[here, :] = hid.astype(bf16)
                scaled_t[here, :] = (gate * hid).astype(bf16)
                along = hid * back
                lines = along[:, 0:128]
                for n in range(1, tile // 128):
                    lines = lines + along[:, n * 128 : (n + 1) * 128]
                dot_acc[here, :] += lines
                dhid = gate * back
                dgt[here, :] = (dhid * u_pre * sig * (1.0 + g_pre * (1.0 - sig))).astype(bf16)
                dut[here, :] = (dhid * act).astype(bf16)
                return 0

            lax.fori_loop(0, rows // chunk, row_chunk, 0)

            @pl.when(f >= 1)
            def _():
                core_sum(f - 1)

            @pl.when(f >= 2)
            def _():
                core_copy(f - 2, slot).wait_send()

            send[slot, 0] = mm(xt_all[theirs, :], dgt[...]).astype(bf16)
            send[slot, 1] = mm(xt_all[theirs, :], dut[...]).astype(bf16)
            send[slot, 2] = mm(dyt_all[theirs, :], scaled_t[...]).astype(bf16)
            total[f, 0] = mm(xt_all[mine, :], dgt[...]).astype(bf16)
            core_copy(f, slot).start()

            @pl.when((f >= 1) & (f - 1 < away))
            def _():
                far_copy(f - 1).start()

            total[f, 1] = mm(xt_all[mine, :], dut[...]).astype(bf16)
            total[f, 2] = mm(dyt_all[mine, :], scaled_t[...]).astype(bf16)
            y_acc[...] += mm(hid_t[...], wd[...])
            dx_acc[...] += mm(dgt[...], wg[...], NT) + mm(dut[...], wu[...], NT)
            return 0

        lax.fori_loop(0, steps, step, 0)
        for r in range(places):
            here = slice(r * CAP, (r + 1) * CAP)
            dx_low[r] = dx_acc[here, :].astype(bf16)
            column = jnp.sum(dot_acc[here, :], axis=1, keepdims=True)
            dots[r] = jnp.sum(jnp.where(diagonal, column, 0.0), axis=0, keepdims=True)
            if r > 1:
                back_copy(r - 1).start()
                dots_copy(r - 1).start()
        core_sum(steps - 1)
        back_copy(places - 1).start()
        dots_copy(places - 1).start()
        for r in range(places):
            here = slice(r * CAP, (r + 1) * CAP)
            y_out[r] = (gate_all[here, :] * y_acc[here, :]).astype(bf16)

        def sum_store(i):
            return pltpu.make_async_copy(
                total.at[away + i], sum_out.at[:, :, pl.ds(i * tile, tile)], out_sem.at[i]
            )

        for i in range(tiles):
            for d in range(1, parts):
                far_copy((parts - 1 - d) * tiles + i).wait_recv()
            for n in range(3):
                value = total[away + i, n].astype(f32)
                for d in range(1, parts):
                    value = value + far[(parts - 1 - d) * tiles + i, n].astype(f32)
                total[away + i, n] = value.astype(bf16)
            sum_store(i).start()
        for f in range(away):
            far_copy(f).wait_send()
        for f in range(max(0, steps - 2), steps):
            core_copy(f, f % 2).wait_send()

        dx_out[0] = dx_low[0]
        dots_out[0] = dots[0]
        for r in range(1, places):
            back_copy(r).wait()
            dots_copy(r).wait()
            dx_out[r] = dx_near[r]
            dots_out[r] = dots_near[r]
        for i in range(tiles):
            sum_store(i).wait()

    placed = shape_of((places, CAP, width), bf16)
    lines = shape_of((places, 1, CAP), f32)
    return run(
        body,
        (),
        [(arrived, vector), (grads, vector), (gates, vector)]
        + [(w, anywhere) for w in (w_gate, w_up, w_down)],
        [(placed, vector), (placed, vector), (lines, vector)]
        + [(shape_of((3, half, per_part), bf16), anywhere)],
        scratch=[
            pltpu.VMEM((rows, width), bf16),
            pltpu.VMEM((width, rows), bf16),
            pltpu.VMEM((rows, width), bf16),
            pltpu.VMEM((width, rows), bf16),
            pltpu.VMEM((rows, 1), f32),
            pltpu.VMEM((rows, width), f32),
            pltpu.VMEM((rows, width), f32),
            pltpu.VMEM((rows, 128), f32),
            pltpu.VMEM((rows, tile), bf16),
            pltpu.VMEM((rows, tile), bf16),
            pltpu.VMEM((rows, tile), bf16),
            pltpu.VMEM((rows, tile), bf16),
            pltpu.VMEM((2, width, tile), bf16),
            pltpu.VMEM((2, width, tile), bf16),
            pltpu.VMEM((2, tile, width), bf16),
            pltpu.VMEM((2, 3, half, tile), bf16),
            pltpu.VMEM((steps, 3, half, tile), bf16),
            pltpu.VMEM((steps, 3, half, tile), bf16),
            pltpu.VMEM((max(1, away), 3, half, tile), bf16),
            pltpu.VMEM((places, CAP, width), bf16),
            pltpu.VMEM((places, CAP, width), bf16),
            pltpu.VMEM((places, 1, CAP), f32),
            pltpu.VMEM((places, 1, CAP), f32),
            dma((3, 2)), dma((2,)), dma((steps,)),
            dma((max(1, away),)), dma((max(1, away),)),
            dma((places,)), dma((places,)), dma((places,)), dma((places,)),
            dma((tiles,)),
        ],
        flops=9 * 2 * rows * width * hidden,
        moved=12 * width * hidden + rows * width * 8,
        exps=rows * hidden,
        talks=2,
    )


def slot_sum(targets, source_ref):
    tile = targets.shape[0]
    total = None
    for r in range(source_ref.shape[0]):
        ids = r * CAP + lax.broadcasted_iota(jnp.int32, (tile, CAP), 1)
        choice = jnp.where((ids == targets[:, 0:1]) | (ids == targets[:, 1:2]), 1.0, 0.0)
        part = mm(choice.astype(bf16), source_ref[r])
        total = part if total is None else total + part
    return total


def token_back(
    meta, x1, h2, grad, prob, previous, routes, targets, back, dots, dgate_zero, dh_zero, gain, router_t, w_out
):
    rows, width = x1.shape
    tile = 128
    places = back.shape[0]
    expert_all = prob.shape[1]
    members, head_columns = w_out.shape[0], w_out.shape[1]

    def body(meta_ref, *refs):
        (x1_ref, h2_ref, dy_ref, prob_ref, prev_ref, route_ref, target_ref) = refs[:7]
        back_ref, dots_ref, dz_ref, dh_ref, gain_ref, router_ref = refs[7:13]
        w_refs = refs[13 : 13 + members]
        dx1_ref, low_ref = refs[13 + members : 15 + members]
        out_refs = refs[15 + members : 15 + 2 * members]
        sums_ref, carry_ref = refs[15 + 2 * members :]
        i = pl.program_id(0)
        prob_now = prob_ref[...]
        lanes = lax.broadcasted_iota(jnp.int32, (tile, expert_all), 1)
        dprob = jnp.zeros_like(prob_now)
        for c in range(2):
            target = target_ref[:, c : c + 1]
            dgate = dz_ref[:, c : c + 1]
            for n in range(places):
                ids = n * CAP + lax.broadcasted_iota(jnp.int32, (tile, CAP), 1)
                dgate = dgate + jnp.sum(
                    jnp.where(ids == target, dots_ref[n], 0.0), axis=1, keepdims=True
                )
            dprob = dprob + jnp.where(lanes == route_ref[:, c : c + 1], dgate, 0.0)
        dlogit = prob_now * (dprob - jnp.sum(prob_now * dprob, axis=1, keepdims=True))
        h2 = h2_ref[...]
        dh2 = (
            slot_sum(target_ref[...], back_ref)
            + dh_ref[...]
            + mm_full(dlogit, router_ref[...])
        )
        x1 = x1_ref[...]
        inverse = lax.rsqrt(jnp.mean(x1 * x1, axis=1, keepdims=True) + norm_eps)
        normed = x1 * inverse
        router_part = mm_full(dlogit, h2, TN)
        carry_part = mm_full(dlogit, prev_ref[...], TN)
        gain_part = jnp.sum(dh2 * normed, axis=0, keepdims=True)

        @pl.when(i == 0)
        def _():
            sums_ref[0:expert_all, :] = router_part
            sums_ref[expert_all : expert_all + 1, :] = gain_part
            carry_ref[...] = carry_part

        @pl.when(i > 0)
        def _():
            sums_ref[0:expert_all, :] += router_part
            sums_ref[expert_all : expert_all + 1, :] += gain_part
            carry_ref[...] += carry_part

        dn = dh2 * gain_ref[...]
        dx1 = dy_ref[...].astype(f32) + inverse * (
            dn - normed * jnp.mean(dn * normed, axis=1, keepdims=True)
        )
        dx1_ref[...] = dx1
        low = dx1.astype(bf16)
        low_ref[...] = low
        for n in range(members):
            out_refs[n][...] = mm(low, w_refs[n][0], NT).astype(bf16)

    row_spec = pl.BlockSpec((tile, width), lambda i, m: (i, 0))
    pair_spec = pl.BlockSpec((tile, 2), lambda i, m: (i, 0))
    small_spec = pl.BlockSpec((tile, expert_all), lambda i, m: (i, 0))
    sums = shape_of((expert_all + 1, width), f32)
    carry = shape_of((expert_all, expert_all), f32)
    return run(
        body,
        (rows // tile,),
        [
            (x1, row_spec),
            (h2, row_spec),
            (grad, row_spec),
            (prob, small_spec),
            (previous, small_spec),
            (routes, pair_spec),
            (targets, pair_spec),
        ]
        + [
            (back, whole(back)),
            (dots, whole(dots)),
            (dgate_zero, pair_spec),
            (dh_zero, row_spec),
            (gain, whole(gain)),
            (router_t, whole(router_t)),
        ]
        + [
            (w_out, pl.BlockSpec((1, head_columns, width), lambda i, m, n=n: (m[0] ^ n, 0, 0)))
            for n in range(members)
        ],
        [
            (shape_of((rows, width), f32), row_spec),
            (shape_of((rows, width), bf16), row_spec),
        ]
        + [
            (
                shape_of((rows, head_columns), bf16),
                pl.BlockSpec((tile, head_columns), lambda i, m: (i, 0)),
            )
        ]
        * members
        + [(sums, whole(sums)), (carry, whole(carry))],
        meta=meta,
        flops=2 * rows * width * (places * CAP + width),
        moved=rows * width * 24,
    )


def finish(dqkv_all, h1, x, gain, dx1, weights_t, out_sum, small, tops, produced, base, targets):
    members, per_group = weights_t.shape[1], weights_t.shape[2]
    rows, width = x.shape
    group_rows = dqkv_all.shape[0]
    parts, groups = lax.axis_size("dp"), lax.axis_size("exp")
    team = parts * groups
    places = produced.shape[0]
    local = places // groups
    wide_share, out_share = 3 * per_group // team, per_group // team
    small_rows = small.shape[0]
    small_steps = [(axis, bit) for axis in ("ctx", "dp", "exp") for bit in powers(axis)]
    hops = len(small_steps)
    row_tile = min(256, rows)

    def body(*refs):
        it = iter(refs)

        def take(count=None):
            return next(it) if count is None else [next(it) for _ in range(count)]

        dqkv_hbm, h1_hbm, x_hbm, gain_ref, dx1_hbm, w_hbm, out_ref = take(7)
        small_ref, tops_ref, produced_hbm, base_hbm, target_ref = take(5)
        input_out, wide_out, flat_out, small_out, gain_out, tops_out, result_out = take(7)
        dqkv, dqkv_near, product, h1_all, x_all, dx1_all, w_all, base_all, y_near = take(9)
        wide_mine, wide_far, wide_all = take(3)
        flat_mine, flat_far, flat_all = take(3)
        small_acc, small_far, gain_acc, gain_far, tops_acc, tops_far = take(6)
        load_sem, near_s, near_r, y_s, y_r = take(5)
        dense_sems = [take(8), take(8)]
        hop_s, hop_r, gain_s, gain_r, top_s, top_r = take(6)

        me = lax.axis_index("ctx")
        dp_now, exp_now = lax.axis_index("dp"), lax.axis_index("exp")
        seat = dp_now * groups + exp_now

        def near_peer(j):
            return {"ctx": flip(me, j)}

        def team_peer(r):
            return {"dp": flip(dp_now, r // groups), "exp": flip(exp_now, r % groups)}

        peers = [near_peer(j) for j in range(1, members)]
        peers += [team_peer(r) for r in range(1, team)]
        peers += [
            slot_peer(r, local, exp_now, me) for r in range(local, places) if r % local
        ]
        ready = greet(peers)

        loads = [
            (dqkv_hbm, dqkv), (h1_hbm, h1_all), (x_hbm, x_all), (dx1_hbm, dx1_all), (w_hbm, w_all),
            (base_hbm, base_all), (produced_hbm.at[0], y_near.at[0]),
        ]

        def load(n):
            return pltpu.make_async_copy(loads[n][0], loads[n][1], load_sem.at[n])

        class Dense:
            def __init__(self, mine, far_buf, all_buf, sems, share):
                self.mine, self.far, self.all, self.share = mine, far_buf, all_buf, share
                (self.rs, self.rr, self.gs, self.gr, self.ys, self.yr, self.cs, self.cr) = sems[:8]

            def reduce_copy(self, r):
                return remote(
                    self.mine.at[flip(seat, r)], self.far.at[r - 1], self.rs.at[r - 1],
                    self.rr.at[r - 1], team_peer(r),
                )

            def gather_copy(self, r):
                return remote(
                    self.all.at[0, seat], self.all.at[0, seat], self.gs.at[r - 1],
                    self.gr.at[r - 1], team_peer(r),
                )

            def gather_arrival(self, r):
                spot = self.all.at[0, flip(seat, r)]
                return remote(spot, spot, self.gs.at[r - 1], self.gr.at[r - 1], team_peer(r))

            def y_forward(self, r):
                return remote(
                    self.all.at[0, flip(seat, r)], self.all.at[2, flip(seat, r)], self.ys.at[r],
                    self.yr.at[r], near_peer(2),
                )

            def core_forward(self, n):
                return remote(
                    self.all.at[2 * n], self.all.at[2 * n + 1], self.cs.at[n], self.cr.at[n],
                    near_peer(1),
                )

            def scatter(self):
                for r in range(1, team):
                    self.reduce_copy(r).start()

            def collect(self):
                for r in range(1, team):
                    self.reduce_copy(r).wait_recv()
                total = self.mine[seat].astype(f32)
                for r in range(1, team):
                    total = total + self.far[r - 1].astype(f32)
                self.all[0, seat] = total.astype(bf16)

            def gather(self):
                for r in range(1, team):
                    self.gather_copy(r).start()
                self.y_forward(0).start()

            def forward(self):
                for r in range(1, team):
                    self.gather_arrival(r).wait_recv()
                    self.y_forward(r).start()
                for r in range(1, team):
                    self.reduce_copy(r).wait_send()
                    self.gather_copy(r).wait_send()
                self.core_forward(0).start()

            def forward_far(self):
                for r in range(team):
                    self.y_forward(r).wait()
                self.core_forward(1).start()

            def done(self):
                for n in range(2):
                    self.core_forward(n).wait()

        wide = Dense(wide_mine, wide_far, wide_all, dense_sems[0], wide_share)
        flat = Dense(flat_mine, flat_far, flat_all, dense_sems[1], out_share)

        def hop_peer(n):
            axis, bit = small_steps[n]
            return {axis: flip(lax.axis_index(axis), bit)}

        def small_copy(n):
            return remote(small_acc.at[n], small_far.at[n], hop_s.at[n], hop_r.at[n], hop_peer(n))

        def tops_copy(n):
            return remote(tops_acc.at[n], tops_far.at[n], top_s.at[n], top_r.at[n], hop_peer(n))

        def gain_copy(n):
            return remote(gain_acc.at[n], gain_far.at[n], gain_s.at[n], gain_r.at[n], hop_peer(n))

        def small_start(n):
            small_copy(n).start()
            tops_copy(n).start()

        def small_sum(n):
            small_copy(n).wait()
            tops_copy(n).wait()
            small_acc[n + 1] = small_acc[n] + small_far[n]
            tops_acc[n + 1] = jnp.maximum(tops_acc[n], tops_far[n])

        small_hops = list(range(hops))

        def small_next():
            if small_hops:
                n = small_hops.pop(0)
                small_sum(n)
                if n + 1 < hops:
                    small_start(n + 1)

        def dqkv_copy(j):
            return remote(
                dqkv_hbm.at[pl.ds(j * rows, rows), :], dqkv_near.at[j - 1], near_s.at[j - 1],
                near_r.at[j - 1], near_peer(j),
            )

        def y_copy(r):
            return remote(
                produced_hbm.at[r], y_near.at[r], y_s.at[r], y_r.at[r],
                slot_peer(r, local, exp_now, me),
            )

        for n in range(len(loads)):
            load(n).start()
        small_acc[0] = small_ref[...]
        tops_acc[0] = tops_ref[...]
        product[0:per_group, :] = out_ref[...].astype(f32)
        for c in range(team):
            flat_mine[c] = product[c * out_share : (c + 1) * out_share, :].astype(bf16)
        ready()
        for j in reversed(range(1, members)):
            dqkv_copy(j).start()
        flat.scatter()
        small_start(0)
        load(0).wait()
        load(1).wait()
        product[...] = mm(dqkv[0:rows, :], h1_all[0:rows, :], TN)

        def weigh(j, _):
            here = pl.ds(pl.multiple_of(j * rows, rows), rows)
            product[...] += mm(dqkv[here, :], h1_all[here, :], TN)
            return 0

        lax.fori_loop(1, group_rows // rows, weigh, 0)
        for c in range(team):
            wide_mine[c] = product[c * wide_share : (c + 1) * wide_share, :].astype(bf16)
        flat.collect()
        wide.scatter()
        flat.gather()
        for r in range(1, places):
            y_copy(r).start()
        for n in range(2, len(loads)):
            load(n).wait()
        small_next()
        small_next()
        flat.forward()
        wide.collect()
        small_next()
        wide.gather()
        for j in range(1, members):
            dqkv_copy(j).wait()

        def input_rows(t, gain_part):
            here = pl.ds(pl.multiple_of(t * row_tile, row_tile), row_tile)
            dh = None
            for j in range(members):
                member = flip(me, j)
                for w in range(3):
                    at = slice(w * per_group, (w + 1) * per_group)
                    source = dqkv[here, at] if j == 0 else dqkv_near[j - 1, here, at]
                    part = mm(source, w_all[w, member])
                    dh = part if dh is None else dh + part
            x_now = x_all[here, :].astype(f32)
            inv = lax.rsqrt(jnp.mean(x_now * x_now, axis=1, keepdims=True) + norm_eps)
            normed = x_now * inv
            dn = dh * gain_ref[...]
            dx1_all[here, :] = dx1_all[here, :] + inv * (
                dn - normed * jnp.mean(dn * normed, axis=1, keepdims=True)
            )
            return gain_part + jnp.sum(dh * normed, axis=0, keepdims=True)

        gain_acc[0] = lax.fori_loop(
            0, rows // row_tile, input_rows, jnp.zeros((1, width), f32)
        )
        store = pltpu.make_async_copy(dx1_all, input_out, load_sem.at[len(loads)])
        store.start()
        small_next()
        gain_copy(0).start()
        wide.forward()
        small_next()
        flat.forward_far()
        for n in range(hops):
            gain_copy(n).wait()
            gain_acc[n + 1] = gain_acc[n] + gain_far[n]
            if n == 0:
                for r in range(1, places):
                    y_copy(r).wait()
            if n < rows // 128:
                here = slice(n * 128, (n + 1) * 128)
                result_out[here, :] = (
                    base_all[here, :] + slot_sum(target_ref[here, :], y_near)
                ).astype(bf16)
            if n + 1 < hops:
                gain_copy(n + 1).start()
        for n in range(hops, rows // 128):
            here = slice(n * 128, (n + 1) * 128)
            result_out[here, :] = (
                base_all[here, :] + slot_sum(target_ref[here, :], y_near)
            ).astype(bf16)
        while small_hops:
            small_next()
        flat.done()
        wide.forward_far()
        wide.done()
        final = [
            pltpu.make_async_copy(wide_all, wide_out, load_sem.at[len(loads) + 1]),
            pltpu.make_async_copy(flat_all, flat_out, load_sem.at[len(loads) + 2]),
        ]
        for copy in final:
            copy.start()
        small_out[...] = small_acc[hops]
        gain_out[...] = gain_acc[hops]
        tops_out[...] = tops_acc[hops]
        store.wait()
        for copy in final:
            copy.wait()

    def dense_scratch(share):
        return [
            pltpu.VMEM((team, share, width), bf16),
            pltpu.VMEM((max(1, team - 1), share, width), bf16),
            pltpu.VMEM((members, team, share, width), bf16),
        ]

    dense_sem = [dma((team,))] * 6 + [dma((2,))] * 2
    wide_rows = shape_of((rows, width), f32)
    return run(
        body,
        (),
        [(dqkv_all, anywhere), (h1, anywhere), (x, anywhere), (gain, vector), (dx1, anywhere)]
        + [(weights_t, anywhere), (out_sum, vector), (small, vector), (tops, vector)]
        + [(produced, anywhere), (base, anywhere), (targets, vector)],
        [
            (wide_rows, anywhere),
            (shape_of((members, team, wide_share, width), bf16), anywhere),
            (shape_of((members, team, out_share, width), bf16), anywhere),
            (shape_of((small_rows, width), f32), vector),
            (shape_of((1, width), f32), vector),
            (shape_of(tops.shape, f32), vector),
            (shape_of((rows, width), bf16), vector),
        ],
        scratch=[
            pltpu.VMEM((group_rows, 3 * per_group), bf16),
            pltpu.VMEM((members - 1, rows, 3 * per_group), bf16),
            pltpu.VMEM((3 * per_group, width), f32),
            pltpu.VMEM((group_rows, width), bf16),
            pltpu.VMEM((rows, width), bf16),
            pltpu.VMEM((rows, width), f32),
            pltpu.VMEM(weights_t.shape, bf16),
            pltpu.VMEM((rows, width), f32),
            pltpu.VMEM((places, CAP, width), bf16),
        ]
        + dense_scratch(wide_share)
        + dense_scratch(out_share)
        + [pltpu.VMEM((hops + 1, small_rows, width), f32), pltpu.VMEM((hops, small_rows, width), f32)]
        + [pltpu.VMEM((hops + 1, 1, width), f32), pltpu.VMEM((hops, 1, width), f32)]
        + [pltpu.VMEM((hops + 1,) + tops.shape, f32), pltpu.VMEM((hops,) + tops.shape, f32)]
        + [dma((10,)), dma((members,)), dma((members,))]
        + [dma((places,)), dma((places,))]
        + dense_sem
        + dense_sem
        + [dma((hops,))] * 6,
        flops=4 * 2 * rows * width * width * 3,
        moved=20 * 1024 * 1024,
        talks=3,
    )


def place_experts(meta, near, which, turned):
    _, half, columns = near[0].shape
    members = len(near)
    local = members // 2
    tile = min(256, columns)

    def body(meta_ref, *refs):
        out_ref, hold = refs[members:]
        n = pl.program_id(0)
        for away in range(local):

            @pl.when(n == away)
            def _():
                for j in range(2):
                    at = pl.multiple_of((meta_ref[2] ^ j) * half, half)
                    piece = refs[2 * away + j][0].astype(f32)
                    if turned:
                        hold[pl.ds(at, half), :] = piece
                    else:
                        out_ref[0, pl.ds(at, half), :] = piece

        if turned:
            out_ref[0] = jnp.transpose(hold[...])

    def spec(j):
        last = columns // tile - 1
        if j < 2:
            return pl.BlockSpec(
                (1, half, tile), lambda n, f, m: (which, 0, jnp.where(n == 0, f, last))
            )
        return pl.BlockSpec((1, half, tile), lambda n, f, m: (which, 0, jnp.where(n == 0, 0, f)))

    if turned:
        out = shape_of((local, columns, 2 * half), f32)
        out_spec = pl.BlockSpec((1, tile, 2 * half), lambda n, f, m: (m[3] ^ n, f, 0))
    else:
        out = shape_of((local, 2 * half, columns), f32)
        out_spec = pl.BlockSpec((1, 2 * half, tile), lambda n, f, m: (m[3] ^ n, 0, f))
    return run(
        body,
        (local, columns // tile),
        [(p, spec(j)) for j, p in enumerate(near)],
        [(out, out_spec)],
        scratch=[pltpu.VMEM((2 * half, tile) if turned else (8, 128), f32)],
        meta=meta,
        moved=out.size * 6,
    )[0]


def place_columns(meta, near, per_group):
    members, team, share, width = near.shape

    def body(meta_ref, near_ref, out_ref, rows_ref, hold):
        w = pl.program_id(0)

        @pl.when(w == 0)
        def _():
            for n in range(members):
                for c in range(team):
                    rows_ref[n, c * share : (c + 1) * share, :] = near_ref[n, c].astype(f32)

        for n in range(members):
            at = pl.multiple_of((meta_ref[0] ^ n) * per_group, per_group)
            source = pl.multiple_of(w * per_group, per_group)
            hold[pl.ds(at, per_group), :] = rows_ref[n, pl.ds(source, per_group), :]
        out_ref[0] = jnp.transpose(hold[...])

    out = shape_of((3, width, width), f32)
    return run(
        body,
        (3,),
        [(near, whole(near))],
        [(out, pl.BlockSpec((1, width, width), lambda w, m: (w, 0, 0)))],
        scratch=[
            pltpu.VMEM((members, team * share, width), f32),
            pltpu.VMEM((width, width), f32),
        ],
        meta=meta,
        moved=3 * width * width * 6,
    )[0]


def place_rows(meta, near):
    members, team, share, width = near.shape

    def body(meta_ref, near_ref, out_ref):
        for c in range(team):
            out_ref[0, c * share : (c + 1) * share, :] = near_ref[0, c].astype(f32)

    out = shape_of((members, team * share, width), f32)
    return run(
        body,
        (members,),
        [(near, pl.BlockSpec((1, team, share, width), lambda j, m: (j, 0, 0, 0)))],
        [(out, pl.BlockSpec((1, team * share, width), lambda j, m: (m[0] ^ j, 0, 0)))],
        meta=meta,
        moved=out.size * 6,
    )[0]


def shards(
    inputs,
    lengths,
    block_order,
    routes,
    prev_logits,
    norm1_gain,
    norm2_gain,
    w_qkv,
    w_out,
    w_router,
    w_carry,
    const_logit_w,
    const_vec,
    w_gate,
    w_up,
    w_down,
    cotangent,
):
    members = lax.axis_size("ctx")
    groups = lax.axis_size("exp")
    parts = lax.axis_size("dp")
    me = lax.axis_index("ctx")
    mine = lax.axis_index("exp")
    x, grad = inputs[0], cotangent[0]
    rows, width = x.shape
    group_rows = rows * members
    deal_block = group_rows // block_order.shape[1]
    per_member = rows // deal_block
    local = w_gate.shape[0]
    expert_count = local * groups
    head_width = width // HEADS
    heads = HEADS // members
    per_group = heads * head_width
    blocks = block_order.shape[1]
    layout = {
        "order": 4, "lengths": 4 + blocks, "sequences": lengths.shape[1],
        "inverse": 4 + blocks + lengths.shape[1],
    }
    numbers = jnp.arange(blocks, dtype=jnp.int32)
    given = jnp.sum(jnp.where(block_order[0][None, :] == numbers[:, None], numbers[None, :], 0), axis=1)
    inverse = (((given // per_member) ^ me) * per_member + given % per_member).astype(jnp.int32)
    meta = jnp.concatenate(
        [
            jnp.stack([me, mine, me % 2, me // 2]).astype(jnp.int32),
            block_order[0],
            lengths[0],
            inverse,
        ]
    )
    gain1 = norm1_gain.reshape(1, width)
    gain2 = norm2_gain.reshape(1, width)
    weights_t = jnp.swapaxes(w_qkv, 1, 2).reshape(3, members, per_group, width)
    w_out_parts = w_out.reshape(members, per_group, width)
    route_ids = routes[0]
    previous = prev_logits[0]

    near = gather_near(x, "ctx")
    held = None
    for j in range(members):
        held = project(
            j, near[j], gain1, weights_t, meta, held, group_rows, deal_block, layout
        )
    q, k, v, kt, vt, h1 = held
    o, ot, lse, tops = attend(meta, q, k, vt, deal_block, layout)
    targets = slot_targets(route_ids, expert_count, local, mine, me // 2)
    target_rows = jnp.transpose(targets)
    places = groups * local
    grad_slots = dispatch(target_rows, grad, places)
    grad_near = jnp.stack(
        [slot_swap(grad_slots[r], r, local) if r else grad_slots[0] for r in range(places)]
    )
    logit_rows = jnp.swapaxes(const_logit_w, 1, 2).reshape(-1, width)
    x1, h2, prob, token_near, gate_near, base, dh_zero, dgate_zero, zero_sums = token_front(
        x, o, w_out_parts, gain2, w_router, previous, w_carry, target_rows, grad, route_ids,
        logit_rows, const_vec, local,
    )
    produced, token_back_rows, dots, expert_sum = expert_layer(
        token_near, grad_near, gate_near, w_gate, w_up, w_down
    )
    back = token_back(
        meta, x1, h2, grad, prob, previous, route_ids, targets, token_back_rows, dots, dgate_zero,
        dh_zero, gain2, jnp.transpose(w_router), w_out_parts,
    )
    dx1, da = back[:2]
    do_near = [back[2 + j] if j == 0 else swap(back[2 + j], "ctx", j) for j in range(members)]
    token_sums, carry_sum = back[2 + members :]

    o_near = [swap(o[j * rows : (j + 1) * rows], "ctx", j) if j else o[:rows] for j in range(members)]
    out_parts = [mm(o_near[j], da, TN).astype(bf16) for j in range(members)]
    out_sum = add_low(*[swap(out_parts[j], "ctx", j) if j else out_parts[0] for j in range(members)])
    dqkv = attend_back(meta, q, k, v, kt, do_near, ot, lse, deal_block, layout)

    expert_all = w_router.shape[1]
    small = jnp.concatenate(
        [token_sums, zero_sums, jnp.pad(carry_sum, ((0, 0), (0, width - expert_all)))], axis=0
    )
    top_rows = jnp.full((members, heads), low_start, f32).at[me].set(jnp.max(tops, axis=1))
    tops_line = jnp.pad(top_rows.reshape(1, HEADS), ((0, 0), (0, 128 - HEADS)), constant_values=low_start)
    input_grad, qkv_near, out_near, small, norm1_grad, top_all, result = finish(
        dqkv, h1, x, gain1, dx1, weights_t, out_sum, small, tops_line, produced, base, targets
    )
    across = swap(expert_sum, "ctx", 2)
    expert_near = [expert_sum, swap(expert_sum, "ctx", 1), across, swap(across, "ctx", 1)]
    out_grad = place_rows(meta, out_near).reshape(width, width)
    qkv_grad = place_columns(meta, qkv_near, per_group)
    kinds = const_vec.shape[0]
    router_grad = jnp.transpose(small[:expert_all])
    norm2_grad = small[expert_all]
    start = expert_all + 1
    vec_grad = small[start : start + kinds]
    logit_grad = jnp.swapaxes(small[start + kinds : start + 3 * kinds].reshape(kinds, 2, width), 1, 2)
    carry_grad = jnp.transpose(small[start + 3 * kinds :, :expert_all])
    head_max = top_all[0, :HEADS]
    clip_ratio = jnp.sqrt(jnp.minimum(1.0, clip_limit / head_max))
    head_scale = jnp.repeat(clip_ratio, head_width)
    clipped = w_qkv[:2].astype(f32) * head_scale[None, None, :]
    gate_grad = place_experts(meta, expert_near, 0, False)
    up_grad = place_experts(meta, expert_near, 1, False)
    down_grad = place_experts(meta, expert_near, 2, True)
    return (
        result[None],
        input_grad[None],
        norm1_grad[0],
        norm2_grad,
        qkv_grad,
        out_grad,
        router_grad,
        carry_grad,
        logit_grad,
        vec_grad,
        gate_grad,
        up_grad,
        down_grad,
        clipped,
    )


def solution(mesh):
    tokens = P(("dp", "exp"), "ctx", None)
    packs = P(("dp", "exp"), None)
    experts = P("exp", None, None)
    in_specs = (
        tokens, packs, packs, tokens, tokens, P(), P(), P(), P(), P(), P(), P(), P(),
        experts, experts, experts, tokens,
    )
    out_specs = (
        tokens, tokens, P(), P(), P(), P(), P(), P(), P(), P(),
        P("exp", None, "dp"), P("exp", None, "dp"), P("exp", "dp", None), P(),
    )
    return jax.shard_map(shards, mesh=mesh, in_specs=in_specs, out_specs=out_specs, check_vma=False)
```

```python
import math

import jax
import jax.numpy as jnp
from jax import lax
from jax.experimental import pallas as pl
from jax.experimental.pallas import tpu as pltpu
from jax.sharding import PartitionSpec as P

HEADS = 12
CAP = 128

norm_eps = 1e-05
clip_limit = 3.0
low_start = -1e30
mask_fill = -3e38
highest = lax.Precision.HIGHEST
NN = (((1,), (0,)), ((), ()))
NT = (((1,), (1,)), ((), ()))
TN = (((0,), (0,)), ((), ()))
f32 = jnp.float32
bf16 = jnp.bfloat16
MESH = pl.DeviceIdType.MESH


def mm(left, right, dims=NN):
    return lax.dot_general(left, right, dims, preferred_element_type=f32)


def mm_full(left, right, dims=NN):
    return lax.dot_general(left, right, dims, precision=highest, preferred_element_type=f32)


def shape_of(shape, dtype):
    return jax.ShapeDtypeStruct(shape, dtype)


def whole(array):
    rank = len(array.shape)
    return pl.BlockSpec(array.shape, lambda *_: (0,) * rank)


def cost(flops, moved, exps=0):
    return pl.CostEstimate(flops=int(flops), bytes_accessed=int(moved), transcendentals=int(exps))


def run(body, grid, inputs, outputs, scratch=(), meta=None, flops=0, moved=0, exps=0, aliases=None, talks=None):
    prefetch = 0 if meta is None else 1
    args = ([] if meta is None else [meta]) + [a for a, _ in inputs]
    return pl.pallas_call(
        body,
        out_shape=[o for o, _ in outputs],
        grid_spec=pltpu.PrefetchScalarGridSpec(
            num_scalar_prefetch=prefetch,
            grid=grid,
            in_specs=[s for _, s in inputs],
            out_specs=[s for _, s in outputs],
            scratch_shapes=list(scratch),
        ),
        compiler_params=pltpu.CompilerParams(
            dimension_semantics=("arbitrary",) * len(grid),
            vmem_limit_bytes=60 * 1024 * 1024,
            collective_id=talks,
            has_side_effects=talks is not None,
        ),
        cost_estimate=cost(flops, moved, exps),
        input_output_aliases={} if aliases is None else aliases,
    )(*args)


def swap(value, axis, distance):
    count = lax.axis_size(axis)
    return lax.ppermute(value, axis, [(i, i ^ distance) for i in range(count)])


def flip(value, bits):
    bit = 1
    while bit <= bits:
        if bits & bit:
            value = value + bit - 2 * bit * lax.rem(lax.div(value, bit), 2)
        bit *= 2
    return value


def powers(axis):
    found, bit = [], 1
    while bit < lax.axis_size(axis):
        found.append(bit)
        bit *= 2
    return found


def slot_peer(r, count, exp_now, me):
    return {"exp": flip(exp_now, r // count), "ctx": flip(me, 2 * (r % count))}


def slot_swap(value, r, count):
    groups = lax.axis_size("exp")
    total = groups * lax.axis_size("ctx")
    apart = 2 * (r % count) * groups + r // count
    return lax.ppermute(value, ("ctx", "exp"), [(i, i ^ apart) for i in range(total)])


def remote(src, dst, sent, arrived, peer):
    return pltpu.make_async_remote_copy(
        src_ref=src, dst_ref=dst, send_sem=sent, recv_sem=arrived,
        device_id=peer, device_id_type=MESH,
    )


def greet(peers):
    barrier = pltpu.get_barrier_semaphore()
    for peer in peers:
        pl.semaphore_signal(barrier, inc=1, device_id=peer, device_id_type=MESH)
    return lambda: pl.semaphore_wait(barrier, len(peers))


anywhere = pl.BlockSpec(memory_space=pl.ANY)
scalars = pl.BlockSpec(memory_space=pltpu.SMEM)
vector = pl.BlockSpec(memory_space=pltpu.VMEM)
dma = pltpu.SemaphoreType.DMA


def add_low(*terms):
    total = terms[0].astype(f32)
    for term in terms[1:]:
        total = total + term.astype(f32)
    return total.astype(bf16)


def begin(x, grad, routes, gain, w_qkv, local):
    rows, width = x.shape
    members, groups = lax.axis_size("ctx"), lax.axis_size("exp")
    group_rows = rows * members
    heads = HEADS // members
    head_width = width // HEADS
    columns = heads * head_width
    places = groups * local
    scale = head_width**-0.5
    tile = min(256, rows)
    per_member = rows // tile

    def body(*refs):
        x_hbm, dy_ref, route_ref, gain_ref, w_hbm = refs[:5]
        q_out, k_out, v_out, kt_out, vt_out, h_out, wt_out = refs[5:12]
        target_out, target_rows, near_out, rest_out = refs[12:16]
        x_near, w_in, w_t, q_all, k_all, v_all, kt_all, vt_all, h_all, packed, near = refs[16:27]
        load_sem, x_s, x_r, r_s, r_r, out_sem, near_sem = refs[27:]
        me, exp_now = lax.axis_index("ctx"), lax.axis_index("exp")
        side = lax.div(me, 2)
        peers = [{"ctx": flip(me, 1)}, {"ctx": flip(me, 2)}]
        peers += [slot_peer(local * g, local, exp_now, me) for g in range(1, groups)]
        ready = greet(peers)
        own = pltpu.make_async_copy(x_hbm, x_near.at[0], load_sem.at[0])
        weights = pltpu.make_async_copy(w_hbm, w_in, load_sem.at[1])
        own.start()
        weights.start()

        def across():
            return remote(x_hbm, x_near.at[2], x_s.at[2], x_r.at[2], {"ctx": flip(me, 2)})

        def beside():
            return remote(x_hbm, x_near.at[1], x_s.at[1], x_r.at[1], {"ctx": flip(me, 1)})

        def passed():
            return remote(x_near.at[2], x_near.at[3], x_s.at[3], x_r.at[3], {"ctx": flip(me, 1)})

        def row_copy(g):
            return remote(
                packed.at[g], near.at[g], r_s.at[g], r_r.at[g],
                slot_peer(local * g, local, exp_now, me),
            )

        ready()
        across().start()
        beside().start()

        chosen = route_ref[...]
        expert_count = places
        lanes = lax.broadcasted_iota(jnp.int32, (rows, 128), 1)
        hits = [lanes == chosen[:, c : c + 1] for c in range(2)]
        hit = jnp.where((hits[0] | hits[1]) & (lanes < expert_count), 1.0, 0.0)
        later = lax.broadcasted_iota(jnp.int32, (rows, rows), 0)
        sooner = lax.broadcasted_iota(jnp.int32, (rows, rows), 1)
        ahead = mm(jnp.where(sooner < later, 1.0, 0.0).astype(bf16), hit.astype(bf16))
        spots = []
        for c in range(2):
            ids = chosen[:, c : c + 1]
            rank = jnp.sum(jnp.where(hits[c], ahead, 0.0), axis=1, keepdims=True).astype(jnp.int32)
            far_z = lax.div(ids, local)
            far_y = lax.rem(ids, local)
            z = jnp.zeros_like(ids)
            bit = 1
            while bit < groups:
                z = z + bit * jnp.where(
                    lax.rem(lax.div(far_z, bit), 2) == lax.rem(lax.div(exp_now, bit), 2), 0, 1
                )
                bit *= 2
            y = jnp.where(far_y == side, 0, 1)
            spots.append(jnp.where(ids < expert_count, (z * local + y) * CAP + rank, -1))
        target_out[...] = jnp.concatenate(spots, axis=1)
        wide = jnp.where(lanes == 0, spots[0], spots[1]).astype(f32)
        target_rows[...] = jnp.transpose(wide)[0:2, :].astype(jnp.int32)

        def pack(n, r):
            packed[n] = mm(slot_choice(r * CAP, CAP, target_rows), dy_ref[...]).astype(bf16)

        for g in range(groups - 1, -1, -1):
            pack(g, local * g)
            if g < groups - 1:
                row_copy(g + 1).start()
        odd = [r for r in range(places) if r % local]
        for n, r in enumerate(odd):
            pack(groups + n, r)
        stores = [
            pltpu.make_async_copy(packed.at[0], near_out.at[0], near_sem.at[0]),
            pltpu.make_async_copy(packed.at[pl.ds(groups, len(odd))], rest_out, near_sem.at[groups]),
        ]
        for copy in stores:
            copy.start()
        weights.wait()
        for w in range(3):
            w_t[w] = jnp.transpose(w_in[w])
        w_store = pltpu.make_async_copy(w_t, wt_out, load_sem.at[2])
        w_store.start()
        here = pl.ds(pl.multiple_of(me * columns, columns), columns)

        def chunk(j):
            def project(t, _):
                at = pl.multiple_of(t * tile, tile)
                to = pl.ds(pl.multiple_of(j * rows + t * tile, tile), tile)
                value = x_near[j, pl.ds(at, tile), :].astype(f32)
                inverse = lax.rsqrt(jnp.mean(value * value, axis=1, keepdims=True) + norm_eps)
                low = (value * inverse * gain_ref[...]).astype(bf16)
                h_all[to, :] = low
                q = mm(low, w_t[0, here, :], NT).astype(bf16) * jnp.asarray(scale, bf16)
                k = mm(low, w_t[1, here, :], NT).astype(bf16)
                v = mm(low, w_t[2, here, :], NT).astype(bf16)
                for h in range(heads):
                    part = slice(h * head_width, (h + 1) * head_width)
                    q_all[h, to, :] = q[:, part]
                    k_all[h, to, :] = k[:, part]
                    v_all[h, to, :] = v[:, part]
                kt_all[:, to] = mm(w_t[1, here, :], low, NT).astype(bf16)
                vt_all[:, to] = mm(w_t[2, here, :], low, NT).astype(bf16)
                return 0

            lax.fori_loop(0, per_member, project, 0)
            for copy in chunk_stores(j):
                copy.start()

        def chunk_stores(j):
            to = pl.ds(j * rows, rows)
            pairs = [(q_all, q_out), (k_all, k_out), (v_all, v_out)]
            found = [(a.at[:, to, :], b.at[:, to, :]) for a, b in pairs]
            found += [(a.at[:, to], b.at[:, to]) for a, b in ((kt_all, kt_out), (vt_all, vt_out))]
            found += [(h_all.at[to, :], h_out.at[to, :])]
            return [
                pltpu.make_async_copy(a, b, out_sem.at[6 * j + n]) for n, (a, b) in enumerate(found)
            ]

        own.wait()
        chunk(0)
        beside().wait()
        chunk(1)
        across().wait()
        passed().start()
        chunk(2)
        passed().wait()
        chunk(3)
        for g in range(1, groups):
            row_copy(g).wait()
            pltpu.make_async_copy(near.at[g], near_out.at[g], near_sem.at[g]).start()
        for copy in stores:
            copy.wait()
        w_store.wait()
        for j in range(members):
            for copy in chunk_stores(j):
                copy.wait()
        for g in range(1, groups):
            pltpu.make_async_copy(near.at[g], near_out.at[g], near_sem.at[g]).wait()

    by_head = (heads, group_rows, head_width)
    by_column = (columns, group_rows)
    slots = (places, CAP, width)
    return run(
        body,
        (),
        [(x, anywhere), (grad, vector), (routes, vector), (gain, vector), (w_qkv, anywhere)],
        [(shape_of(by_head, bf16), anywhere)] * 3
        + [(shape_of(by_column, bf16), anywhere)] * 2
        + [(shape_of((group_rows, width), bf16), anywhere)]
        + [(shape_of((3, width, width), bf16), anywhere)]
        + [(shape_of((rows, 2), jnp.int32), vector), (shape_of((2, rows), jnp.int32), vector)]
        + [(shape_of((groups, CAP, width), bf16), anywhere)]
        + [(shape_of((places - groups, CAP, width), bf16), anywhere)],
        scratch=[
            pltpu.VMEM((members, rows, width), bf16),
            pltpu.VMEM((3, width, width), bf16),
            pltpu.VMEM((3, width, width), bf16),
            pltpu.VMEM(by_head, bf16), pltpu.VMEM(by_head, bf16), pltpu.VMEM(by_head, bf16),
            pltpu.VMEM(by_column, bf16), pltpu.VMEM(by_column, bf16),
            pltpu.VMEM((group_rows, width), bf16),
            pltpu.VMEM(slots, bf16), pltpu.VMEM(slots, bf16),
            dma((3,)), dma((members,)), dma((members,)), dma((places,)), dma((places,)),
            dma((6 * members,)), dma((places + 1,)),
        ],
        flops=2 * group_rows * width * columns * 5,
        moved=20 * 1024 * 1024,
        talks=4,
    )


def document_start(meta_ref, position, layout):
    start = jnp.zeros_like(position)
    end = jnp.int32(0)
    for s in range(layout["sequences"]):
        end = end + meta_ref[layout["lengths"] + s]
        start = jnp.where(position >= end, end, start)
    return start


def block_range(meta_ref, query_block, key_block, rows, layout):
    q_first = query_block * rows
    k_first = key_block * rows
    begin = document_start(meta_ref, q_first, layout)
    begin_last = document_start(meta_ref, q_first + rows - 1, layout)
    needed = (k_first <= q_first) & (k_first + rows - 1 >= begin)
    full = (k_first < q_first) & (k_first >= begin_last)
    return q_first, k_first, needed, full


def allowed_pairs(meta_ref, q_first, k_first, rows, layout):
    q_pos = q_first + lax.broadcasted_iota(jnp.int32, (1, rows), 1)
    k_pos = k_first + lax.broadcasted_iota(jnp.int32, (rows, 1), 0)
    return (k_pos <= q_pos) & (k_pos >= document_start(meta_ref, q_pos, layout))


def attend(meta, q, k, vt, rows, layout):
    heads, group_rows, head_width = q.shape
    blocks = group_rows // rows
    width = heads * head_width

    def body(meta_ref, q_ref, k_ref, vt_ref, o_ref, ot_ref, lse_ref, top_ref, m_ref, l_ref, a_ref):
        i = pl.program_id(0)
        m_ref[...] = jnp.full_like(m_ref, low_start)
        l_ref[...] = jnp.zeros_like(l_ref)
        a_ref[...] = jnp.zeros_like(a_ref)

        def one(j, _):
            q_first, k_first, needed, full = block_range(meta_ref, i, j, rows, layout)
            at = pl.multiple_of(meta_ref[layout["inverse"] + j] * rows, rows)

            def step(masked):
                if masked:
                    allowed = allowed_pairs(meta_ref, q_first, k_first, rows, layout)
                for h in range(heads):
                    part = slice(h * head_width, (h + 1) * head_width)
                    s = mm(k_ref[h, pl.ds(at, rows), :], q_ref[h], NT)
                    if masked:
                        s = jnp.where(allowed, s, mask_fill)
                    old = m_ref[h]
                    new = jnp.maximum(old, jnp.max(s, axis=0, keepdims=True))
                    shrink = jnp.exp(old - new)
                    p = jnp.exp(s - new)
                    m_ref[h] = new
                    l_ref[h] = l_ref[h] * shrink + jnp.sum(p, axis=0, keepdims=True)
                    a_ref[part, :] = a_ref[part, :] * shrink + mm(
                        vt_ref[part, pl.ds(at, rows)], p.astype(bf16)
                    )

            @pl.when(full)
            def _():
                step(False)

            @pl.when(needed & jnp.logical_not(full))
            def _():
                step(True)

            return 0

        lax.fori_loop(0, i + 1, one, 0)
        for h in range(heads):
            part = slice(h * head_width, (h + 1) * head_width)
            ot_ref[part, :] = a_ref[part, :] / l_ref[h]
            lse_ref[pl.ds(h, 1), :] = m_ref[h] + jnp.log(l_ref[h])
            top = m_ref[h]

            @pl.when(i == 0)
            def _():
                top_ref[pl.ds(h, 1), :] = top

            @pl.when(i > 0)
            def _():
                top_ref[pl.ds(h, 1), :] = jnp.maximum(top_ref[pl.ds(h, 1), :], top)

        o_ref[...] = jnp.transpose(ot_ref[...]).astype(bf16)

    row = shape_of((heads, group_rows), f32)
    row_spec = pl.BlockSpec((heads, rows), lambda i, m: (0, i))
    return run(
        body,
        (blocks,),
        [
            (
                q,
                pl.BlockSpec(
                    (heads, rows, head_width), lambda i, m: (0, m[layout["inverse"] + i], 0)
                ),
            ),
            (k, whole(k)),
            (vt, whole(vt)),
        ],
        [
            (
                shape_of((group_rows, width), bf16),
                pl.BlockSpec((rows, width), lambda i, m: (m[layout["inverse"] + i], 0)),
            ),
            (shape_of((width, group_rows), f32), pl.BlockSpec((width, rows), lambda i, m: (0, i))),
            (row, row_spec),
            (shape_of((heads, rows), f32), pl.BlockSpec((heads, rows), lambda i, m: (0, 0))),
        ],
        scratch=[
            pltpu.VMEM((heads, 1, rows), f32),
            pltpu.VMEM((heads, 1, rows), f32),
            pltpu.VMEM((width, rows), f32),
        ],
        meta=meta,
        flops=2 * 2 * group_rows * group_rows * width,
        moved=group_rows * width * 14,
        exps=group_rows * group_rows * heads // 2,
    )


def attend_back(meta, q, k, v, kt, grad, w_out, ot, lse, rows, layout):
    heads, group_rows, head_width = q.shape
    blocks = group_rows // rows
    width = heads * head_width
    scale = head_width**-0.5
    per = grad.shape[1] // rows

    def body(meta_ref, q_ref, k_ref, v_ref, kt_ref, grad_ref, w_ref, *refs):
        ot_ref, lse_ref, out_ref, rows_ref, dk_ref, dv_ref, dq_ref, g_ref, delta_ref, sum_ref = refs
        i = pl.program_id(0)

        @pl.when(i == 0)
        def _():
            dk_ref[...] = jnp.zeros_like(dk_ref)
            dv_ref[...] = jnp.zeros_like(dv_ref)

        da = grad_ref[0]
        g = mm(da, w_ref[0], NT).astype(bf16)
        part_sum = mm(ot_ref[...].astype(bf16), da)

        @pl.when(i == 0)
        def _():
            sum_ref[...] = part_sum

        @pl.when(i > 0)
        def _():
            sum_ref[...] += part_sum

        for h in range(heads):
            g_ref[h] = g[:, h * head_width : (h + 1) * head_width]
        product = jnp.transpose(g.astype(f32)) * ot_ref[...]
        for h in range(heads):
            part = slice(h * head_width, (h + 1) * head_width)
            delta_ref[h] = jnp.sum(product[part, :], axis=0, keepdims=True)

        dq_ref[...] = jnp.zeros_like(dq_ref)

        def one(j, _):
            q_first, k_first, needed, full = block_range(meta_ref, i, j, rows, layout)
            at = pl.multiple_of(meta_ref[layout["inverse"] + j] * rows, rows)
            to = pl.multiple_of(j * rows, rows)

            def step(masked):
                if masked:
                    allowed = allowed_pairs(meta_ref, q_first, k_first, rows, layout)
                for h in range(heads):
                    part = slice(h * head_width, (h + 1) * head_width)
                    s = mm(k_ref[h, pl.ds(at, rows), :], q_ref[h], NT)
                    if masked:
                        s = jnp.where(allowed, s, mask_fill)
                    p = jnp.exp(s - lse_ref[pl.ds(h, 1), :])
                    dp = mm(v_ref[h, pl.ds(at, rows), :], g_ref[h], NT)
                    ds = (p * (dp - delta_ref[h])).astype(bf16)
                    dv_ref[h, pl.ds(to, rows), :] += mm(p.astype(bf16), g_ref[h])
                    dk_ref[h, pl.ds(to, rows), :] += mm(ds, q_ref[h])
                    dq_ref[part, :] += mm(kt_ref[part, pl.ds(at, rows)], ds)

            @pl.when(full)
            def _():
                step(False)

            @pl.when(needed & jnp.logical_not(full))
            def _():
                step(True)

            return 0

        lax.fori_loop(0, i + 1, one, 0)
        here = pl.multiple_of(meta_ref[layout["inverse"] + i] * rows, rows)
        out_ref[pl.ds(here, rows), 0:width] = (jnp.transpose(dq_ref[...]) * scale).astype(bf16)

        @pl.when(i == blocks - 1)
        def _():
            rows_ref[...] = sum_ref[...].astype(bf16)

            def store(b, _):
                spot = pl.multiple_of(b * rows, rows)
                there = pl.multiple_of(meta_ref[layout["inverse"] + b] * rows, rows)
                out_ref[pl.ds(there, rows), width : 3 * width] = jnp.concatenate(
                    [dk_ref[h, pl.ds(spot, rows), :] for h in range(heads)]
                    + [dv_ref[h, pl.ds(spot, rows), :] for h in range(heads)],
                    axis=1,
                ).astype(bf16)
                return 0

            lax.fori_loop(0, blocks, store, 0)

    out = shape_of((group_rows, 3 * width), bf16)
    out_rows = shape_of((width, grad.shape[2]), bf16)
    return run(
        body,
        (blocks,),
        [
            (
                q,
                pl.BlockSpec(
                    (heads, rows, head_width), lambda i, m: (0, m[layout["inverse"] + i], 0)
                ),
            ),
            (k, whole(k)),
            (v, whole(v)),
            (kt, whole(kt)),
        ]
        + [
            (
                grad,
                pl.BlockSpec(
                    (1, rows, grad.shape[2]),
                    lambda i, m: (
                        m[layout["inverse"] + i] // per, m[layout["inverse"] + i] % per, 0
                    ),
                ),
            ),
            (w_out, pl.BlockSpec((1, width, grad.shape[2]), lambda i, m: (m[0], 0, 0))),
            (ot, pl.BlockSpec((width, rows), lambda i, m: (0, i))),
            (lse, pl.BlockSpec((heads, rows), lambda i, m: (0, i))),
        ],
        [(out, whole(out)), (out_rows, whole(out_rows))],
        scratch=[
            pltpu.VMEM((heads, group_rows, head_width), f32),
            pltpu.VMEM((heads, group_rows, head_width), f32),
            pltpu.VMEM((width, rows), f32),
            pltpu.VMEM((heads, rows, head_width), bf16),
            pltpu.VMEM((heads, 1, rows), f32),
            pltpu.VMEM((width, grad.shape[2]), f32),
        ],
        meta=meta,
        flops=5 * 2 * group_rows * group_rows * width,
        moved=group_rows * width * 24,
        exps=group_rows * group_rows * heads // 2,
    )


def slot_choice(first, count, target_ref):
    rows = target_ref.shape[1]
    ids = first + lax.broadcasted_iota(jnp.int32, (count, rows), 0)
    match = (ids == target_ref[0:1, :]) | (ids == target_ref[1:2, :])
    return jnp.where(match, 1.0, 0.0).astype(bf16)


def token_front(
    x, o, w_out, gain, w_router, previous, w_carry, target_rows, grad, routes, logit_w, vectors, local
):
    rows, width = x.shape
    members, columns = w_out.shape[0], w_out.shape[1]
    expert_all = w_router.shape[1]
    groups = lax.axis_size("exp")
    places = groups * local
    expert_count = places
    kinds = vectors.shape[0]
    tile = 128

    def body(*refs):
        (x_ref, o_hbm, w_ref, gain_ref, router_ref, prev_ref, carry_ref, target_ref) = refs[:8]
        dy_ref, route_ref, lw_ref, vec_ref = refs[8:12]
        x1_ref, h2_ref, prob_ref, rows_out, gates_out, base_ref, dh_ref, dgate_ref, sums_ref = refs[12:21]
        o_near, low, split, packed, arrived, gate_mine, gate_near = refs[21:28]
        o_s, o_r, t_s, t_r, g_s, g_r, out_sem = refs[28:]
        me, exp_now = lax.axis_index("ctx"), lax.axis_index("exp")
        side = lax.div(me, 2)
        peers = [{"ctx": flip(me, j)} for j in range(1, members)]
        peers += [slot_peer(r, local, exp_now, me) for r in range(local, places)]
        ready = greet(peers)

        def o_copy(j):
            src = o_hbm.at[pl.ds(j * rows, rows), :]
            if j == 0:
                return pltpu.make_async_copy(src, o_near.at[0], o_r.at[0])
            return remote(src, o_near.at[j], o_s.at[j], o_r.at[j], {"ctx": flip(me, j)})

        def row_copy(r):
            return remote(
                packed.at[r], arrived.at[r], t_s.at[r], t_r.at[r], slot_peer(r, local, exp_now, me)
            )

        def gate_copy(r):
            return remote(
                gate_mine.at[r], gate_near.at[r], g_s.at[r], g_r.at[r],
                slot_peer(r, local, exp_now, me),
            )

        o_copy(0).start()
        ready()
        for j in range(1, members):
            o_copy(j).start()
        for j in range(members):
            o_copy(j).wait()

        def front_rows(t, _):
            here = pl.ds(pl.multiple_of(t * tile, tile), tile)
            total = x_ref[here, :].astype(f32)
            for j in range(members):
                total = total + mm(o_near[j, here, :], w_ref[flip(me, j)])
            x1_ref[here, :] = total
            inverse = lax.rsqrt(jnp.mean(total * total, axis=1, keepdims=True) + norm_eps)
            h2 = total * inverse * gain_ref[...]
            h2_ref[here, :] = h2
            logits = mm_full(h2, router_ref[...]) + mm_full(prev_ref[here, :], carry_ref[...])
            shifted = jnp.exp(logits - jnp.max(logits, axis=1, keepdims=True))
            prob = shifted / jnp.sum(shifted, axis=1, keepdims=True)
            prob_ref[here, :] = prob
            low[here, :] = h2.astype(bf16)
            top = prob.astype(bf16)
            rest = prob - top.astype(f32)
            middle = rest.astype(bf16)
            split[0, here, :] = top
            split[1, here, :] = middle
            split[2, here, :] = (rest - middle.astype(f32)).astype(bf16)
            return 0

        lax.fori_loop(0, rows // tile, front_rows, 0)
        diagonal = lax.broadcasted_iota(jnp.int32, (CAP, CAP), 0) == lax.broadcasted_iota(
            jnp.int32, (CAP, CAP), 1
        )
        lanes = lax.broadcasted_iota(jnp.int32, (CAP, expert_all), 1)
        for r in list(range(1, places)) + [0]:
            choice = slot_choice(r * CAP, CAP, target_ref)
            packed[r] = mm(choice, low[...]).astype(bf16)
            picked = mm(choice, split[0]) + mm(choice, split[1]) + mm(choice, split[2])
            expert = flip(exp_now, r // local) * local + flip(side, r % local)
            column = jnp.sum(jnp.where(lanes == expert, picked, 0.0), axis=1, keepdims=True)
            gate_mine[r] = jnp.sum(jnp.where(diagonal, column, 0.0), axis=0, keepdims=True)
            last = r - 1 if r else places - 1
            if last:
                row_copy(last).start()
                gate_copy(last).start()

        def own_copy(n):
            src, dst = (packed, rows_out) if n == 0 else (gate_mine, gates_out)
            return pltpu.make_async_copy(src.at[0], dst.at[0], out_sem.at[n])

        own_copy(0).start()
        own_copy(1).start()

        def zero_rows(t, _):
            here = pl.ds(pl.multiple_of(t * tile, tile), tile)
            h2 = h2_ref[here, :]
            dy = dy_ref[here, :].astype(f32)
            prob_now = prob_ref[here, :]
            classes = lax.broadcasted_iota(jnp.int32, (tile, expert_all), 1)
            chosen = route_ref[here, :]
            ids = [chosen[:, c : c + 1] for c in range(2)]
            gates = [
                jnp.sum(jnp.where(classes == r, prob_now, 0.0), axis=1, keepdims=True) for r in ids
            ]
            along = jnp.sum(dy * h2, axis=1, keepdims=True)
            copies = [(r == expert_count + 1).astype(f32) for r in ids]
            keep = copies[0] * gates[0] + copies[1] * gates[1]
            dgates = [copies[c] * along for c in range(2)]
            scores = [
                jnp.sum(h2 * lw_ref[n : n + 1, :], axis=1, keepdims=True) for n in range(2 * kinds)
            ]
            base = x1_ref[here, :]
            dh = jnp.zeros_like(h2)
            for j in range(kinds):
                top = jnp.maximum(scores[2 * j], scores[2 * j + 1])
                e0 = jnp.exp(scores[2 * j] - top)
                e1 = jnp.exp(scores[2 * j + 1] - top)
                a0 = e0 / (e0 + e1)
                a1 = e1 / (e0 + e1)
                vec = vec_ref[j : j + 1, :]
                along_vec = jnp.sum(dy * vec, axis=1, keepdims=True)
                these = [(r == expert_count + 2 + j).astype(f32) for r in ids]
                weight = these[0] * gates[0] + these[1] * gates[1]
                for c in range(2):
                    dgates[c] = dgates[c] + these[c] * (a0 * along + a1 * along_vec)
                keep = keep + weight * a0
                base = base + (weight * a1) * vec
                d0 = weight * along
                d1 = weight * along_vec
                mean = a0 * d0 + a1 * d1
                z0 = a0 * (d0 - mean)
                z1 = a1 * (d1 - mean)
                dh = dh + z0 * lw_ref[2 * j : 2 * j + 1, :] + z1 * lw_ref[2 * j + 1 : 2 * j + 2, :]
                sums_ref[j : j + 1, :] += jnp.sum((weight * a1) * dy, axis=0, keepdims=True)
                at = kinds + 2 * j
                sums_ref[at : at + 1, :] += jnp.sum(z0 * h2, axis=0, keepdims=True)
                sums_ref[at + 1 : at + 2, :] += jnp.sum(z1 * h2, axis=0, keepdims=True)
            base_ref[here, :] = base + keep * h2
            dh_ref[here, :] = dh + keep * dy
            dgate_ref[here, :] = jnp.concatenate(dgates, axis=1)
            return 0

        sums_ref[...] = jnp.zeros_like(sums_ref)
        lax.fori_loop(0, rows // tile, zero_rows, 0)

        def rows_store(r):
            return pltpu.make_async_copy(arrived.at[r], rows_out.at[r], out_sem.at[2 * r])

        def gates_store(r):
            return pltpu.make_async_copy(gate_near.at[r], gates_out.at[r], out_sem.at[2 * r + 1])

        for r in range(1, places):
            row_copy(r).wait()
            gate_copy(r).wait()
            rows_store(r).start()
            gates_store(r).start()
        own_copy(0).wait()
        own_copy(1).wait()
        for r in range(1, places):
            rows_store(r).wait()
            gates_store(r).wait()

    wide = shape_of((rows, width), f32)
    placed = shape_of((places, CAP, width), bf16)
    lines = shape_of((places, 1, CAP), f32)
    return run(
        body,
        (),
        [(x, vector), (o, anywhere), (w_out, vector), (gain, vector), (w_router, vector)]
        + [(previous, vector), (w_carry, vector), (target_rows, vector), (grad, vector)]
        + [(routes, vector), (logit_w, vector), (vectors, vector)],
        [(wide, vector), (wide, vector), (shape_of((rows, expert_all), f32), vector)]
        + [(placed, anywhere), (lines, anywhere), (wide, vector), (wide, vector)]
        + [(shape_of((rows, 2), f32), vector), (shape_of((3 * kinds, width), f32), vector)],
        scratch=[
            pltpu.VMEM((members, rows, columns), bf16),
            pltpu.VMEM((rows, width), bf16),
            pltpu.VMEM((3, rows, expert_all), bf16),
            pltpu.VMEM((places, CAP, width), bf16),
            pltpu.VMEM((places, CAP, width), bf16),
            pltpu.VMEM((places, 1, CAP), f32),
            pltpu.VMEM((places, 1, CAP), f32),
            dma((members,)), dma((members,)),
            dma((places,)), dma((places,)), dma((places,)), dma((places,)),
            dma((2 * places,)),
        ],
        flops=2 * rows * width * (width + places * CAP),
        moved=rows * width * 30,
        talks=1,
    )


def expert_layer(arrived, grads, late, gates, w_gate, w_up, w_down):
    places = arrived.shape[0]
    local = w_gate.shape[0]
    rows = places * CAP
    width, hidden = w_gate.shape[1], w_gate.shape[2]
    parts = lax.axis_size("dp")
    groups = places // local
    half = width // 2
    per_part = hidden // parts
    tile = min(256, per_part)
    steps = hidden // tile
    tiles = per_part // tile
    away = steps - tiles
    chunk = 256

    def body(*refs):
        x_ref, dy_ref, gates_ref, wg_hbm, wu_hbm, wd_hbm = refs[:6]
        dy_late, refs = refs[6 : 6 + len(late)], refs[:6] + refs[6 + len(late) :]
        dy_parts = [
            dy_late[r // local] if r % local else dy_ref.at[r // local] for r in range(places)
        ]
        y_out, dx_out, dots_out, sum_out, beside_out = refs[6:11]
        x_all, xt_all, dy_all, dyt_all, gate_all, y_acc, dx_acc, dot_acc = refs[11:19]
        hid_t, dgt, dut, scaled_t, wg_buf, wu_buf, wd_buf = refs[19:26]
        hid_own, dg_own, du_own, scaled_own, wg_own, wu_own, wd_own = refs[26:33]
        send, total, taken, far, dx_low, dx_near, dots, dots_near = refs[33:41]
        beside, y_odd, relay = refs[41:44]
        w_sem, own_sem, c_s, c_r, f_s, f_r, b_s, b_r, d_s, d_r, out_sem = refs[44:55]
        e_s, e_r, beside_sem, y_s, y_r = refs[55:]
        me, exp_now, dp_now = lax.axis_index("ctx"), lax.axis_index("exp"), lax.axis_index("dp")
        core, side = lax.rem(me, 2), lax.div(me, 2)
        sibling = {"ctx": flip(me, 1)}
        peers = [sibling] + [{"dp": flip(dp_now, d)} for d in range(1, parts)]
        peers += [slot_peer(r, local, exp_now, me) for r in range(1, places)]
        ready = greet(peers)
        diagonal = lax.broadcasted_iota(jnp.int32, (CAP, CAP), 0) == lax.broadcasted_iota(
            jnp.int32, (CAP, CAP), 1
        )

        def dp_of(f):
            distance = parts - 1 - lax.div(f, tiles)
            found, bit = dp_now, 1
            while bit < parts:
                on = lax.rem(lax.div(distance, bit), 2)
                now = lax.rem(lax.div(found, bit), 2)
                found = found + on * bit * (1 - 2 * now)
                bit *= 2
            return found

        def weights(f, slot):
            at = pl.multiple_of(dp_of(f) * per_part + lax.rem(f, tiles) * tile, tile)
            return [
                pltpu.make_async_copy(
                    wg_hbm.at[side, :, pl.ds(at, tile)], wg_buf.at[slot], w_sem.at[0, slot]
                ),
                pltpu.make_async_copy(
                    wu_hbm.at[side, :, pl.ds(at, tile)], wu_buf.at[slot], w_sem.at[1, slot]
                ),
                pltpu.make_async_copy(
                    wd_hbm.at[side, pl.ds(at, tile), :], wd_buf.at[slot], w_sem.at[2, slot]
                ),
            ]

        def core_copy(f, slot):
            return remote(send.at[slot], taken.at[f], c_s.at[slot], c_r.at[f], sibling)

        def far_copy(f):
            return remote(total.at[f], far.at[f], f_s.at[f], f_r.at[f], {"dp": dp_of(f)})

        def back_copy(r):
            return remote(
                dx_low.at[r], dx_near.at[r], b_s.at[r], b_r.at[r],
                slot_peer(r, local, exp_now, me),
            )

        def dots_copy(r):
            return remote(
                dots.at[r], dots_near.at[r], d_s.at[r], d_r.at[r],
                slot_peer(r, local, exp_now, me),
            )

        def own_weights():
            at = pl.ds(pl.multiple_of(dp_now * per_part, per_part), per_part)
            return [
                pltpu.make_async_copy(wg_hbm.at[side, :, at], wg_own, own_sem.at[0]),
                pltpu.make_async_copy(wu_hbm.at[side, :, at], wu_own, own_sem.at[1]),
                pltpu.make_async_copy(wd_hbm.at[side, at, :], wd_own, own_sem.at[2]),
            ]

        if away:
            for copy in weights(0, 0):
                copy.start()
        for copy in own_weights():
            copy.start()
        first_half = pl.ds(pl.multiple_of((1 - core) * half, half), half)
        second_half = pl.ds(pl.multiple_of(core * half, half), half)
        for r in range(places):
            here = slice(r * CAP, (r + 1) * CAP)
            x_all[here, :] = x_ref[r]
            turned = jnp.transpose(x_ref[r])
            xt_all[first_half, here] = turned[:half, :]
            xt_all[second_half, here] = turned[half:, :]
            dy_all[here, :] = dy_parts[r][...]
            turned = jnp.transpose(dy_parts[r][...])
            dyt_all[first_half, here] = turned[:half, :]
            dyt_all[second_half, here] = turned[half:, :]
            gate_all[here, :] = jnp.sum(
                jnp.where(diagonal, gates_ref[r], 0.0), axis=1, keepdims=True
            )
        y_acc[...] = jnp.zeros_like(y_acc)
        dx_acc[...] = jnp.zeros_like(dx_acc)
        dot_acc[...] = jnp.zeros_like(dot_acc)
        ready()

        def core_sum(f):
            core_copy(f, lax.rem(f, 2)).wait_recv()
            for n in range(3):
                total[f, n] = (total[f, n].astype(f32) + taken[f, n].astype(f32)).astype(bf16)

        def forward_back(here, wg, wu, wd, hid_ref, dg_ref, du_ref, scaled_ref):
            g_pre = mm(x_all[here, :], wg)
            u_pre = mm(x_all[here, :], wu)
            back = mm(dy_all[here, :], wd, NT)
            gate = gate_all[here, :]
            sig = 1.0 / (1.0 + jnp.exp(-g_pre))
            act = g_pre * sig
            hid = act * u_pre
            hid_ref[here, :] = hid.astype(bf16)
            scaled_ref[here, :] = (gate * hid).astype(bf16)
            along = hid * back
            lines = along[:, 0:128]
            for n in range(1, tile // 128):
                lines = lines + along[:, n * 128 : (n + 1) * 128]
            dot_acc[here, :] += lines
            dhid = gate * back
            dg = (dhid * u_pre * sig * (1.0 + g_pre * (1.0 - sig))).astype(bf16)
            du = (dhid * act).astype(bf16)
            dg_ref[here, :] = dg
            du_ref[here, :] = du

        def rows_back(here, wg, wu, dg_ref, du_ref):
            dx_acc[here, :] += mm(dg_ref[here, :], wg, NT) + mm(du_ref[here, :], wu, NT)

        def weight_sums(f, slot, hid_ref, dg_ref, du_ref, scaled_ref, wd):
            @pl.when(f >= 1)
            def _():
                core_sum(f - 1)

            @pl.when(f >= 2)
            def _():
                core_copy(f - 2, slot).wait_send()

            for n, (left, right) in enumerate(((xt_all, dg_ref), (xt_all, du_ref), (dyt_all, scaled_ref))):
                found = mm(left[...], right[...]).astype(bf16)
                send[slot, n] = found[:half, :]
                total[f, n] = found[half:, :]
            core_copy(f, slot).start()

            @pl.when((f >= 1) & (f - 1 < away))
            def _():
                far_copy(f - 1).start()

            y_acc[...] += mm(hid_ref[...], wd)

        def away_step(f, _):
            slot = lax.rem(f, 2)
            for copy in weights(f, slot):
                copy.wait()

            @pl.when(f + 1 < away)
            def _():
                for copy in weights(f + 1, 1 - slot):
                    copy.start()

            def row_chunk(c, _):
                here = pl.ds(pl.multiple_of(c * chunk, chunk), chunk)
                forward_back(
                    here, wg_buf[slot], wu_buf[slot], wd_buf[slot], hid_t, dgt, dut, scaled_t
                )
                return 0

            lax.fori_loop(0, rows // chunk, row_chunk, 0)
            weight_sums(f, slot, hid_t, dgt, dut, scaled_t, wd_buf[slot])
            rows_back(slice(0, rows), wg_buf[slot], wu_buf[slot], dgt, dut)
            return 0

        lax.fori_loop(0, away, away_step, 0)
        for copy in own_weights():
            copy.wait()
        if away:
            core_sum(away - 1)
            far_copy(away - 1).start()

        def own_rows(first, count):
            size = min(chunk, count)

            def own_tile(i, _):
                at = pl.ds(pl.multiple_of(i * tile, tile), tile)
                for c in range(count // size):
                    forward_back(
                        slice(first + c * size, first + (c + 1) * size),
                        wg_own[:, at], wu_own[:, at], wd_own[at, :],
                        hid_own.at[i], dg_own.at[i], du_own.at[i], scaled_own.at[i],
                    )
                rows_back(
                    slice(first, first + count), wg_own[:, at], wu_own[:, at], dg_own.at[i], du_own.at[i]
                )
                return 0

            lax.fori_loop(0, tiles, own_tile, 0)

        def send_back(first, last):
            for r in range(first, last):
                here = slice(r * CAP, (r + 1) * CAP)
                dx_low[r] = dx_acc[here, :].astype(bf16)
                column = jnp.sum(dot_acc[here, :], axis=1, keepdims=True)
                dots[r] = jnp.sum(jnp.where(diagonal, column, 0.0), axis=0, keepdims=True)
                if r - 1 >= max(1, first):
                    back_copy(r - 1).start()
                    dots_copy(r - 1).start()

        def send_last(r):
            back_copy(r).start()
            dots_copy(r).start()

        middle = places // 2
        own_rows(middle * CAP, rows - middle * CAP)
        send_back(middle, places)
        own_rows(0, middle * CAP)
        send_last(places - 1)
        send_back(0, middle)

        def own_step(i, _):
            f = away + i
            at = pl.ds(pl.multiple_of(i * tile, tile), tile)

            @pl.when(i == 1)
            def _():
                send_last(middle - 1)

            @pl.when(i >= 1)
            def _():
                core_sum(f - 1)

            slot = lax.rem(f, 2)

            @pl.when(f >= 2)
            def _():
                core_copy(f - 2, slot).wait_send()

            dg, du, scaled = dg_own.at[i], du_own.at[i], scaled_own.at[i]
            for n, (left, right) in enumerate(((xt_all, dg), (xt_all, du), (dyt_all, scaled))):
                found = mm(left[...], right[...]).astype(bf16)
                send[slot, n] = found[:half, :]
                total[f, n] = found[half:, :]
            core_copy(f, slot).start()
            y_acc[...] += mm(hid_own[i], wd_own[at, :])
            return 0

        lax.fori_loop(0, tiles, own_step, 0)
        if tiles == 1:
            send_last(middle - 1)
        core_sum(steps - 1)
        def relay_copy(g):
            return remote(y_odd.at[g], relay.at[g], y_s.at[g], y_r.at[g], {"ctx": flip(me, 2)})

        def result(r):
            here = slice(r * CAP, (r + 1) * CAP)
            return (gate_all[here, :] * y_acc[here, :]).astype(bf16)

        for g in range(groups):
            y_odd[g] = result(local * g + 1)
            if g:
                relay_copy(g - 1).start()
        for g in range(groups):
            y_out[g, 0] = result(local * g)
        relay_copy(groups - 1).start()

        def beside_copy(i):
            return remote(total.at[away + i], beside.at[i], e_s.at[i], e_r.at[i], sibling)

        def beside_store(i):
            return pltpu.make_async_copy(
                beside.at[i], beside_out.at[:, :, pl.ds(i * tile, tile)], beside_sem.at[i]
            )

        def sum_store(i):
            return pltpu.make_async_copy(
                total.at[away + i], sum_out.at[:, :, pl.ds(i * tile, tile)], out_sem.at[i]
            )

        for i in range(tiles):
            for d in range(1, parts):
                far_copy((parts - 1 - d) * tiles + i).wait_recv()
            for n in range(3):
                value = total[away + i, n].astype(f32)
                for d in range(1, parts):
                    value = value + far[(parts - 1 - d) * tiles + i, n].astype(f32)
                total[away + i, n] = value.astype(bf16)
            if i:
                beside_copy(i - 1).start()
            sum_store(i).start()
        beside_copy(tiles - 1).start()
        for f in range(away):
            far_copy(f).wait_send()
        for f in range(max(0, steps - 2), steps):
            core_copy(f, f % 2).wait_send()

        dx_out[0] = dx_low[0]
        dots_out[0] = dots[0]
        for r in range(1, places):
            back_copy(r).wait()
            dots_copy(r).wait()
            dx_out[r] = dx_near[r]
            dots_out[r] = dots_near[r]
        for g in range(groups):
            relay_copy(g).wait()
            y_out[g, 1] = relay[g]
        for i in range(tiles):
            beside_copy(i).wait()
            beside_store(i).start()
        for i in range(tiles):
            sum_store(i).wait()
            beside_store(i).wait()

    placed = shape_of((places, CAP, width), bf16)
    pairs = shape_of((groups, local, CAP, width), bf16)
    lines = shape_of((places, 1, CAP), f32)
    return run(
        body,
        (),
        [(arrived, vector), (grads, vector), (gates, vector)]
        + [(w, anywhere) for w in (w_gate, w_up, w_down)]
        + [(g, vector) for g in late],
        [(pairs, vector), (placed, vector), (lines, vector)]
        + [(shape_of((3, half, per_part), bf16), anywhere)] * 2,
        scratch=[
            pltpu.VMEM((rows, width), bf16),
            pltpu.VMEM((width, rows), bf16),
            pltpu.VMEM((rows, width), bf16),
            pltpu.VMEM((width, rows), bf16),
            pltpu.VMEM((rows, 1), f32),
            pltpu.VMEM((rows, width), f32),
            pltpu.VMEM((rows, width), f32),
            pltpu.VMEM((rows, 128), f32),
            pltpu.VMEM((rows, tile), bf16),
            pltpu.VMEM((rows, tile), bf16),
            pltpu.VMEM((rows, tile), bf16),
            pltpu.VMEM((rows, tile), bf16),
            pltpu.VMEM((2, width, tile), bf16),
            pltpu.VMEM((2, width, tile), bf16),
            pltpu.VMEM((2, tile, width), bf16),
            pltpu.VMEM((tiles, rows, tile), bf16),
            pltpu.VMEM((tiles, rows, tile), bf16),
            pltpu.VMEM((tiles, rows, tile), bf16),
            pltpu.VMEM((tiles, rows, tile), bf16),
            pltpu.VMEM((width, per_part), bf16),
            pltpu.VMEM((width, per_part), bf16),
            pltpu.VMEM((per_part, width), bf16),
            pltpu.VMEM((2, 3, half, tile), bf16),
            pltpu.VMEM((steps, 3, half, tile), bf16),
            pltpu.VMEM((steps, 3, half, tile), bf16),
            pltpu.VMEM((max(1, away), 3, half, tile), bf16),
            pltpu.VMEM((places, CAP, width), bf16),
            pltpu.VMEM((places, CAP, width), bf16),
            pltpu.VMEM((places, 1, CAP), f32),
            pltpu.VMEM((places, 1, CAP), f32),
            pltpu.VMEM((tiles, 3, half, tile), bf16),
            pltpu.VMEM((groups, CAP, width), bf16),
            pltpu.VMEM((groups, CAP, width), bf16),
            dma((3, 2)), dma((3,)), dma((2,)), dma((steps,)),
            dma((max(1, away),)), dma((max(1, away),)),
            dma((places,)), dma((places,)), dma((places,)), dma((places,)),
            dma((tiles,)), dma((tiles,)), dma((tiles,)), dma((tiles,)),
            dma((groups,)), dma((groups,)),
        ],
        flops=9 * 2 * rows * width * hidden,
        moved=12 * width * hidden + rows * width * 8,
        exps=rows * hidden,
        talks=2,
    )


def slot_sum(targets, source_ref):
    tile = targets.shape[0]
    total = None
    for r in range(source_ref.shape[0]):
        ids = r * CAP + lax.broadcasted_iota(jnp.int32, (tile, CAP), 1)
        choice = jnp.where((ids == targets[:, 0:1]) | (ids == targets[:, 1:2]), 1.0, 0.0)
        part = mm(choice.astype(bf16), source_ref[r])
        total = part if total is None else total + part
    return total


def token_back(
    x1, h2, grad, prob, previous, routes, targets, back, dots, dgate_zero, dh_zero, gain, router_t,
):
    rows, width = x1.shape
    tile = 128
    tiles = rows // tile
    places = back.shape[0]
    expert_all = prob.shape[1]
    members = lax.axis_size("ctx")

    def body(*refs):
        (x1_ref, h2_ref, dy_ref, prob_ref, prev_ref, route_ref, target_ref) = refs[:7]
        back_ref, dots_ref, dz_ref, dh_ref, gain_ref, router_ref = refs[7:13]
        dx1_ref, sums_ref, carry_ref, da_out, da_near, a_s, a_r, out_sem = refs[13:]
        me = lax.axis_index("ctx")
        peers = [{"ctx": flip(me, 1)}, {"ctx": flip(me, 2)}]
        ready = greet(peers)

        def da_copy(kind, t):
            here = pl.ds(pl.multiple_of(t * tile, tile), tile)
            n = kind * tiles + t
            src, dst = ((0, 1), (0, 2), (2, 3))[kind]
            return remote(
                da_near.at[src, here, :], da_near.at[dst, here, :], a_s.at[n], a_r.at[n],
                {"ctx": flip(me, 2 if kind == 1 else 1)},
            )

        sums_ref[...] = jnp.zeros_like(sums_ref)
        carry_ref[...] = jnp.zeros_like(carry_ref)
        ready()

        def token_rows(t, _):
            here = pl.ds(pl.multiple_of(t * tile, tile), tile)
            prob_now = prob_ref[here, :]
            chosen, target, zero = route_ref[here, :], target_ref[here, :], dz_ref[here, :]
            lanes = lax.broadcasted_iota(jnp.int32, (tile, expert_all), 1)
            dprob = jnp.zeros_like(prob_now)
            for c in range(2):
                dgate = zero[:, c : c + 1]
                for n in range(places):
                    ids = n * CAP + lax.broadcasted_iota(jnp.int32, (tile, CAP), 1)
                    dgate = dgate + jnp.sum(
                        jnp.where(ids == target[:, c : c + 1], dots_ref[n], 0.0),
                        axis=1,
                        keepdims=True,
                    )
                dprob = dprob + jnp.where(lanes == chosen[:, c : c + 1], dgate, 0.0)
            dlogit = prob_now * (dprob - jnp.sum(prob_now * dprob, axis=1, keepdims=True))
            h2 = h2_ref[here, :]
            dh2 = slot_sum(target, back_ref) + dh_ref[here, :] + mm_full(dlogit, router_ref[...])
            x1 = x1_ref[here, :]
            inverse = lax.rsqrt(jnp.mean(x1 * x1, axis=1, keepdims=True) + norm_eps)
            normed = x1 * inverse
            dn = dh2 * gain_ref[...]
            dx1 = dy_ref[here, :].astype(f32) + inverse * (
                dn - normed * jnp.mean(dn * normed, axis=1, keepdims=True)
            )
            dx1_ref[here, :] = dx1
            da_near[0, here, :] = dx1.astype(bf16)
            sums_ref[0:expert_all, :] += mm_full(dlogit, h2, TN)
            sums_ref[expert_all : expert_all + 1, :] += jnp.sum(dh2 * normed, axis=0, keepdims=True)
            carry_ref[...] += mm_full(dlogit, prev_ref[here, :], TN)
            da_copy(1, t).start()
            da_copy(0, t).start()

            @pl.when(t >= 2)
            def _():
                da_copy(1, t - 2).wait_recv()
                da_copy(2, t - 2).start()

            return 0

        lax.fori_loop(0, tiles, token_rows, 0)
        for t in range(max(0, tiles - 2), tiles):
            da_copy(1, t).wait_recv()
            da_copy(2, t).start()
        mine = pltpu.make_async_copy(da_near.at[0], da_out.at[0], out_sem.at[0])
        mine.start()
        for t in range(tiles):
            da_copy(0, t).wait()
            da_copy(1, t).wait_send()
            da_copy(2, t).wait()
        rest = pltpu.make_async_copy(
            da_near.at[pl.ds(1, members - 1)], da_out.at[pl.ds(1, members - 1)], out_sem.at[1]
        )
        rest.start()
        mine.wait()
        rest.wait()

    return run(
        body,
        (),
        [(a, vector) for a in (x1, h2, grad, prob, previous, routes, targets, back, dots)]
        + [(a, vector) for a in (dgate_zero, dh_zero, gain, router_t)],
        [(shape_of((rows, width), f32), vector)]
        + [(shape_of((expert_all + 1, width), f32), vector)]
        + [(shape_of((expert_all, expert_all), f32), vector)]
        + [(shape_of((members, rows, width), bf16), anywhere)],
        scratch=[
            pltpu.VMEM((members, rows, width), bf16),
            dma((3 * tiles,)), dma((3 * tiles,)), dma((2,)),
        ],
        flops=2 * rows * width * (places * CAP + width),
        moved=rows * width * 24,
        talks=5,
    )


def finish(dqkv_all, h1, x, gain, dx1, weights_t, out_sum, small, tops, produced, base, targets):
    members, per_group = weights_t.shape[1], weights_t.shape[2]
    rows, width = x.shape
    group_rows = dqkv_all.shape[0]
    parts, groups = lax.axis_size("dp"), lax.axis_size("exp")
    team = parts * groups
    local = produced[0].shape[0]
    places = groups * local
    wide_share, out_share = width // team, per_group // team
    small_rows = small.shape[0]
    small_steps = [(axis, bit) for axis in ("ctx", "dp", "exp") for bit in powers(axis)]
    hops = len(small_steps)
    row_tile = min(256, rows)

    def body(*refs):
        it = iter(refs)

        def take(count=None):
            return next(it) if count is None else [next(it) for _ in range(count)]

        dqkv_hbm, h1_hbm, x_hbm, gain_ref, dx1_hbm, w_hbm, out_ref = take(7)
        small_ref, tops_ref, base_hbm, target_ref = take(4)
        produced_hbm = take(groups)
        input_out, wide_out, flat_out, small_out, gain_out, tops_out, result_out = take(7)
        dqkv, product, h1_all, x_all, dx1_all, w_all, base_all, y_near = take(8)
        part_send, part_core, part_y, y_got, part_own = take(5)
        wide_mine, wide_far, wide_all = take(3)
        flat_mine, flat_far, flat_all = take(3)
        small_acc, small_far, gain_acc, gain_far, tops_acc, tops_far = take(6)
        load_sem, near_s, near_r = take(3)
        dense_sems = [take(8), take(8)]
        hop_s, hop_r, gain_s, gain_r, top_s, top_r = take(6)

        me = lax.axis_index("ctx")
        dp_now, exp_now = lax.axis_index("dp"), lax.axis_index("exp")
        seat = dp_now * groups + exp_now

        def near_peer(j):
            return {"ctx": flip(me, j)}

        def team_peer(r):
            return {"dp": flip(dp_now, r // groups), "exp": flip(exp_now, r % groups)}

        peers = [near_peer(j) for j in range(1, members)]
        peers += [team_peer(r) for r in range(1, team)]
        ready = greet(peers)

        loads = [
            (dqkv_hbm, dqkv), (h1_hbm, h1_all), (x_hbm, x_all), (dx1_hbm, dx1_all),
            (w_hbm.at[:, me], w_all), (base_hbm, base_all),
        ]
        loads += [
            (produced_hbm[g], y_near.at[pl.ds(g * local, local)]) for g in range(groups)
        ]

        def load(n):
            return pltpu.make_async_copy(loads[n][0], loads[n][1], load_sem.at[n])

        class Dense:
            def __init__(self, mine, far_buf, all_buf, sems, share):
                self.mine, self.far, self.all, self.share = mine, far_buf, all_buf, share
                (self.rs, self.rr, self.gs, self.gr, self.ys, self.yr, self.cs, self.cr) = sems[:8]

            def reduce_copy(self, r):
                return remote(
                    self.mine.at[flip(seat, r)], self.far.at[r - 1], self.rs.at[r - 1],
                    self.rr.at[r - 1], team_peer(r),
                )

            def gather_copy(self, r):
                return remote(
                    self.all.at[0, seat], self.all.at[0, seat], self.gs.at[r - 1],
                    self.gr.at[r - 1], team_peer(r),
                )

            def gather_arrival(self, r):
                spot = self.all.at[0, flip(seat, r)]
                return remote(spot, spot, self.gs.at[r - 1], self.gr.at[r - 1], team_peer(r))

            def y_forward(self, r):
                return remote(
                    self.all.at[0, flip(seat, r)], self.all.at[2, flip(seat, r)], self.ys.at[r],
                    self.yr.at[r], near_peer(2),
                )

            def core_forward(self, n):
                return remote(
                    self.all.at[2 * n], self.all.at[2 * n + 1], self.cs.at[n], self.cr.at[n],
                    near_peer(1),
                )

            def scatter(self):
                for r in range(1, team):
                    self.reduce_copy(r).start()

            def collect(self):
                for r in range(1, team):
                    self.reduce_copy(r).wait_recv()
                total = self.mine[seat].astype(f32)
                for r in range(1, team):
                    total = total + self.far[r - 1].astype(f32)
                self.all[0, seat] = total.astype(bf16)

            def gather(self):
                for r in range(1, team):
                    self.gather_copy(r).start()
                self.y_forward(0).start()

            def forward(self):
                for r in range(1, team):
                    self.gather_arrival(r).wait_recv()
                    self.y_forward(r).start()
                for r in range(1, team):
                    self.reduce_copy(r).wait_send()
                    self.gather_copy(r).wait_send()
                self.core_forward(0).start()

            def forward_far(self):
                for r in range(team):
                    self.y_forward(r).wait()
                self.core_forward(1).start()

            def done(self):
                for n in range(2):
                    self.core_forward(n).wait()

        wide = Dense(wide_mine, wide_far, wide_all, dense_sems[0], wide_share)
        flat = Dense(flat_mine, flat_far, flat_all, dense_sems[1], out_share)

        def hop_peer(n):
            axis, bit = small_steps[n]
            return {axis: flip(lax.axis_index(axis), bit)}

        def small_copy(n):
            return remote(small_acc.at[n], small_far.at[n], hop_s.at[n], hop_r.at[n], hop_peer(n))

        def tops_copy(n):
            return remote(tops_acc.at[n], tops_far.at[n], top_s.at[n], top_r.at[n], hop_peer(n))

        def gain_copy(n):
            return remote(gain_acc.at[n], gain_far.at[n], gain_s.at[n], gain_r.at[n], hop_peer(n))

        def small_start(n):
            small_copy(n).start()
            tops_copy(n).start()

        def small_sum(n):
            small_copy(n).wait()
            tops_copy(n).wait()
            small_acc[n + 1] = small_acc[n] + small_far[n]
            tops_acc[n + 1] = jnp.maximum(tops_acc[n], tops_far[n])

        small_hops = list(range(hops))

        def small_next():
            if small_hops:
                n = small_hops.pop(0)
                small_sum(n)
                if n + 1 < hops:
                    small_start(n + 1)

        row_tiles = rows // row_tile

        def tile_rows(t, first=0):
            return pl.ds(first + t * row_tile, row_tile)

        def core_part(j, t):
            n = j // 2
            return remote(
                part_send.at[n, tile_rows(t), :], part_core.at[n, tile_rows(t), :],
                near_s.at[n * row_tiles + t], near_r.at[n * row_tiles + t], near_peer(1),
            )

        def y_part(t):
            n = 2 * row_tiles + t
            return remote(
                part_y.at[tile_rows(t), :], y_got.at[tile_rows(t), :], near_s.at[n], near_r.at[n],
                near_peer(2),
            )

        def part(j, t):
            here = pl.ds(j * rows + t * row_tile, row_tile)
            found = None
            for w in range(3):
                add = mm(dqkv[here, w * per_group : (w + 1) * per_group], w_all[w])
                found = add if found is None else found + add
            return found

        for n in range(len(loads)):
            load(n).start()
        small_acc[0] = small_ref[...]
        lanes = lax.broadcasted_iota(jnp.int32, tops_acc.shape[1:], 1)
        tops_acc[0] = jnp.where(
            lanes == me, jnp.max(tops_ref[...], axis=1, keepdims=True), low_start
        )
        flat_rows = out_ref[...].astype(f32)
        for c in range(team):
            flat_mine[c] = flat_rows[c * out_share : (c + 1) * out_share, :].astype(bf16)
        ready()
        flat.scatter()
        small_start(0)
        load(0).wait()
        load(1).wait()
        product[...] = mm(h1_all[0:rows, :], dqkv[0:rows, :], TN)

        def weigh(j, _):
            here = pl.ds(pl.multiple_of(j * rows, rows), rows)
            product[...] += mm(h1_all[here, :], dqkv[here, :], TN)
            return 0

        lax.fori_loop(1, group_rows // rows, weigh, 0)
        for c in range(team):
            wide_mine[c] = product[c * wide_share : (c + 1) * wide_share, :].astype(bf16)
        wide.scatter()
        for n in range(2, len(loads)):
            load(n).wait()
        queue = [(j, t) for j in (3, 1) for t in range(row_tiles)]
        for n, (j, t) in enumerate(queue):
            part_send[j // 2, tile_rows(t), :] = part(j, t).astype(bf16)
            if n:
                core_part(*queue[n - 1]).start()
        own_part = [part(2, t) for t in range(1)]
        core_part(*queue[-1]).start()
        for t in range(row_tiles):
            value = own_part[0] if t == 0 else part(2, t)
            core_part(3, t).wait_recv()
            part_y[tile_rows(t), :] = (
                value + part_core[1, tile_rows(t), :].astype(f32)
            ).astype(bf16)
            if t:
                y_part(t - 1).start()
        part_own[tile_rows(0), :] = part(0, 0)
        y_part(row_tiles - 1).start()
        for t in range(1, row_tiles):
            part_own[tile_rows(t), :] = part(0, t)
        flat.collect()
        flat.gather()
        small_next()
        small_next()

        def token_rows(t, _):
            here = pl.ds(pl.multiple_of(t * 128, 128), 128)
            result_out[here, :] = (
                base_all[here, :] + slot_sum(target_ref[here, :], y_near)
            ).astype(bf16)
            return 0

        lax.fori_loop(0, rows // 128, token_rows, 0)
        flat.forward()
        small_next()
        wide.collect()
        small_next()
        wide.gather()
        for t in range(row_tiles):
            core_part(1, t).wait()
            core_part(3, t).wait_send()
            y_part(t).wait()

        def input_rows(t, gain_part):
            here = pl.ds(pl.multiple_of(t * row_tile, row_tile), row_tile)
            dh = (
                part_own[here, :] + part_core[0, here, :].astype(f32) + y_got[here, :].astype(f32)
            )
            x_now = x_all[here, :].astype(f32)
            inv = lax.rsqrt(jnp.mean(x_now * x_now, axis=1, keepdims=True) + norm_eps)
            normed = x_now * inv
            dn = dh * gain_ref[...]
            dx1_all[here, :] = dx1_all[here, :] + inv * (
                dn - normed * jnp.mean(dn * normed, axis=1, keepdims=True)
            )
            return gain_part + jnp.sum(dh * normed, axis=0, keepdims=True)

        gain_acc[0] = lax.fori_loop(
            0, rows // row_tile, input_rows, jnp.zeros((1, width), f32)
        )
        store = pltpu.make_async_copy(dx1_all, input_out, load_sem.at[len(loads)])
        store.start()
        small_next()
        gain_copy(0).start()
        wide.forward()
        small_next()
        flat.forward_far()
        for n in range(hops):
            gain_copy(n).wait()
            gain_acc[n + 1] = gain_acc[n] + gain_far[n]
            if n + 1 < hops:
                gain_copy(n + 1).start()
        while small_hops:
            small_next()
        flat.done()
        wide.forward_far()
        wide.done()
        final = [
            pltpu.make_async_copy(wide_all, wide_out, load_sem.at[len(loads) + 1]),
            pltpu.make_async_copy(flat_all, flat_out, load_sem.at[len(loads) + 2]),
        ]
        for copy in final:
            copy.start()
        small_out[...] = small_acc[hops]
        gain_out[...] = gain_acc[hops]
        tops_out[...] = tops_acc[hops]
        store.wait()
        for copy in final:
            copy.wait()

    def dense_scratch(share, across):
        return [
            pltpu.VMEM((team, share, across), bf16),
            pltpu.VMEM((max(1, team - 1), share, across), bf16),
            pltpu.VMEM((members, team, share, across), bf16),
        ]

    dense_sem = [dma((team,))] * 6 + [dma((2,))] * 2
    wide_rows = shape_of((rows, width), f32)
    return run(
        body,
        (),
        [(dqkv_all, anywhere), (h1, anywhere), (x, anywhere), (gain, vector), (dx1, anywhere)]
        + [(weights_t, anywhere), (out_sum, vector), (small, vector), (tops, vector)]
        + [(base, anywhere), (targets, vector)]
        + [(a, anywhere) for a in produced],
        [
            (wide_rows, anywhere),
            (shape_of((members, team, wide_share, 3 * per_group), bf16), anywhere),
            (shape_of((members, team, out_share, width), bf16), anywhere),
            (shape_of((small_rows, width), f32), vector),
            (shape_of((1, width), f32), vector),
            (shape_of((tops.shape[0], 128), f32), vector),
            (shape_of((rows, width), bf16), vector),
        ],
        scratch=[
            pltpu.VMEM((group_rows, 3 * per_group), bf16),
            pltpu.VMEM((width, 3 * per_group), f32),
            pltpu.VMEM((group_rows, width), bf16),
            pltpu.VMEM((rows, width), bf16),
            pltpu.VMEM((rows, width), f32),
            pltpu.VMEM((3, per_group, width), bf16),
            pltpu.VMEM((rows, width), f32),
            pltpu.VMEM((places, CAP, width), bf16),
            pltpu.VMEM((2, rows, width), bf16),
            pltpu.VMEM((2, rows, width), bf16),
            pltpu.VMEM((rows, width), bf16),
            pltpu.VMEM((rows, width), bf16),
            pltpu.VMEM((rows, width), f32),
        ]
        + dense_scratch(wide_share, 3 * per_group)
        + dense_scratch(out_share, width)
        + [pltpu.VMEM((hops + 1, small_rows, width), f32), pltpu.VMEM((hops, small_rows, width), f32)]
        + [pltpu.VMEM((hops + 1, 1, width), f32), pltpu.VMEM((hops, 1, width), f32)]
        + [pltpu.VMEM((hops + 1, tops.shape[0], 128), f32), pltpu.VMEM((hops, tops.shape[0], 128), f32)]
        + [dma((10 + places,))] + [dma((3 * (rows // row_tile),))] * 2
        + dense_sem
        + dense_sem
        + [dma((hops,))] * 6,
        flops=4 * 2 * rows * width * width * 3,
        moved=20 * 1024 * 1024,
        talks=3,
    )


def place_experts(meta, near, turned):
    _, half, columns = near[0][0][0].shape
    members = len(near[0])
    local = members // 2
    count = len(near)
    tile = 128
    tiles = half // tile

    def body(meta_ref, *refs):
        outs = refs[count * members :]
        step = pl.program_id(0) * 2 + pl.program_id(1)
        for j in range(members):

            @pl.when(step == j)
            def _():
                for n in range(count):
                    piece = refs[n * members + j][0].astype(f32)
                    outs[n][0] = jnp.transpose(piece) if turned[n] else piece

    def in_spec(which, j):
        def index(n, c, t, m):
            step = n * 2 + c
            return (which, jnp.where(step == j, t, jnp.where(step < j, 0, tiles - 1)), 0)

        return pl.BlockSpec((1, tile, columns), index)

    outputs = []
    for flag in turned:
        if flag:
            outputs.append(
                (
                    shape_of((local, columns, 2 * half), f32),
                    pl.BlockSpec(
                        (1, columns, tile),
                        lambda n, c, t, m: (m[3] ^ n, 0, (m[2] ^ c) * tiles + t),
                    ),
                )
            )
        else:
            outputs.append(
                (
                    shape_of((local, 2 * half, columns), f32),
                    pl.BlockSpec(
                        (1, tile, columns),
                        lambda n, c, t, m: (m[3] ^ n, (m[2] ^ c) * tiles + t, 0),
                    ),
                )
            )
    return run(
        body,
        (local, 2, tiles),
        [(a, in_spec(which, j)) for listed in near for j, (a, which) in enumerate(listed)],
        outputs,
        meta=meta,
        moved=count * local * 2 * half * columns * 6,
    )


def place_columns(meta, near, per_group):
    members, team, share, _ = near.shape
    width = team * share
    step = 8 // math.gcd(share, 8)

    def body(meta_ref, near_ref, out_ref):
        for c in range(step):
            pieces = [near_ref[meta_ref[0] ^ g, c] for g in range(members)]
            for w in range(3):
                at = slice(w * per_group, (w + 1) * per_group)
                out_ref[w, c * share : (c + 1) * share, :] = jnp.concatenate(
                    [piece[:, at] for piece in pieces], axis=1
                ).astype(f32)

    out = shape_of((3, width, members * per_group), f32)
    return run(
        body,
        (team // step,),
        [(near, pl.BlockSpec((members, step, share, 3 * per_group), lambda c, m: (0, c, 0, 0)))],
        [(out, pl.BlockSpec((3, step * share, members * per_group), lambda c, m: (0, c, 0)))],
        meta=meta,
        moved=out.size * 6,
    )[0]


def place_rows(meta, near):
    members, team, share, width = near.shape

    def body(meta_ref, near_ref, out_ref):
        for c in range(team):
            out_ref[0, c * share : (c + 1) * share, :] = near_ref[0, c].astype(f32)

    out = shape_of((members, team * share, width), f32)
    return run(
        body,
        (members,),
        [(near, pl.BlockSpec((1, team, share, width), lambda j, m: (j, 0, 0, 0)))],
        [(out, pl.BlockSpec((1, team * share, width), lambda j, m: (m[0] ^ j, 0, 0)))],
        meta=meta,
        moved=out.size * 6,
    )[0]


def shards(
    inputs,
    lengths,
    block_order,
    routes,
    prev_logits,
    norm1_gain,
    norm2_gain,
    w_qkv,
    w_out,
    w_router,
    w_carry,
    const_logit_w,
    const_vec,
    w_gate,
    w_up,
    w_down,
    cotangent,
):
    members = lax.axis_size("ctx")
    groups = lax.axis_size("exp")
    parts = lax.axis_size("dp")
    me = lax.axis_index("ctx")
    mine = lax.axis_index("exp")
    x, grad = inputs[0], cotangent[0]
    rows, width = x.shape
    group_rows = rows * members
    deal_block = group_rows // block_order.shape[1]
    per_member = rows // deal_block
    local = w_gate.shape[0]
    expert_count = local * groups
    head_width = width // HEADS
    heads = HEADS // members
    per_group = heads * head_width
    blocks = block_order.shape[1]
    layout = {
        "order": 4, "lengths": 4 + blocks, "sequences": lengths.shape[1],
        "inverse": 4 + blocks + lengths.shape[1],
    }
    numbers = jnp.arange(blocks, dtype=jnp.int32)
    given = jnp.sum(jnp.where(block_order[0][None, :] == numbers[:, None], numbers[None, :], 0), axis=1)
    inverse = (((given // per_member) ^ me) * per_member + given % per_member).astype(jnp.int32)
    meta = jnp.concatenate(
        [
            jnp.stack([me, mine, me % 2, me // 2]).astype(jnp.int32),
            block_order[0],
            lengths[0],
            inverse,
        ]
    )
    gain1 = norm1_gain.reshape(1, width)
    gain2 = norm2_gain.reshape(1, width)
    w_out_parts = w_out.reshape(members, per_group, width)
    route_ids = routes[0]
    previous = prev_logits[0]
    odd = [r for r in range(groups * local) if r % local]

    q, k, v, kt, vt, h1, weights_t, targets, target_rows, grad_near, grad_rest = begin(
        x, grad, route_ids, gain1, w_qkv, local
    )
    weights_t = weights_t.reshape(3, members, per_group, width)
    grad_late = [slot_swap(grad_rest[n], r, local) for n, r in enumerate(odd)]
    o, ot, lse, tops = attend(meta, q, k, vt, deal_block, layout)
    logit_rows = jnp.swapaxes(const_logit_w, 1, 2).reshape(-1, width)
    x1, h2, prob, token_near, gate_near, base, dh_zero, dgate_zero, zero_sums = token_front(
        x, o, w_out_parts, gain2, w_router, previous, w_carry, target_rows, grad, route_ids,
        logit_rows, const_vec, local,
    )
    produced, token_back_rows, dots, expert_sum, beside = expert_layer(
        token_near, grad_near, grad_late, gate_near, w_gate, w_up, w_down
    )
    dx1, token_sums, carry_sum, da_near = token_back(
        x1, h2, grad, prob, previous, route_ids, targets, token_back_rows, dots, dgate_zero,
        dh_zero, gain2, jnp.transpose(w_router),
    )
    expert_now, da_near = lax.optimization_barrier((expert_sum, da_near))
    over_first, over_last = swap(expert_now[:2], "ctx", 2), swap(expert_now[2:], "ctx", 2)
    y_near = [swap(produced[g], "exp", g) if g else produced[0] for g in range(groups)]
    dqkv, out_sum = attend_back(
        meta, q, k, v, kt, da_near, w_out_parts, ot, lse, deal_block, layout
    )

    expert_all = w_router.shape[1]
    small = jnp.concatenate(
        [token_sums, zero_sums, jnp.pad(carry_sum, ((0, 0), (0, width - expert_all)))], axis=0
    )
    input_grad, qkv_near, out_near, small, norm1_grad, top_all, result = finish(
        dqkv, h1, x, gain1, dx1, weights_t, out_sum, small, tops, y_near, base, targets
    )
    corner_first, corner_last = swap(over_first, "ctx", 1), swap(over_last, "ctx", 1)
    near = [
        [(expert_sum, n), (beside, n), (over_first, n), (corner_first, n)] for n in range(2)
    ] + [[(expert_sum, 2), (beside, 2), (over_last, 0), (corner_last, 0)]]
    gate_grad, up_grad, down_grad = place_experts(meta, near, (False, False, True))
    out_grad = place_rows(meta, out_near).reshape(width, width)
    qkv_grad = place_columns(meta, qkv_near, per_group)
    kinds = const_vec.shape[0]
    router_grad = jnp.transpose(small[:expert_all])
    norm2_grad = small[expert_all]
    start = expert_all + 1
    vec_grad = small[start : start + kinds]
    logit_grad = jnp.swapaxes(small[start + kinds : start + 3 * kinds].reshape(kinds, 2, width), 1, 2)
    carry_grad = jnp.transpose(small[start + 3 * kinds :, :expert_all])
    head_max = jnp.transpose(top_all[:, :members]).reshape(HEADS)
    clip_ratio = jnp.sqrt(jnp.minimum(1.0, clip_limit / head_max))
    head_scale = jnp.repeat(clip_ratio, head_width)
    clipped = w_qkv[:2].astype(f32) * head_scale[None, None, :]
    return (
        result[None],
        input_grad[None],
        norm1_grad[0],
        norm2_grad,
        qkv_grad,
        out_grad,
        router_grad,
        carry_grad,
        logit_grad,
        vec_grad,
        gate_grad,
        up_grad,
        down_grad,
        clipped,
    )


def solution(mesh):
    tokens = P(("dp", "exp"), "ctx", None)
    packs = P(("dp", "exp"), None)
    experts = P("exp", None, None)
    in_specs = (
        tokens, packs, packs, tokens, tokens, P(), P(), P(), P(), P(), P(), P(), P(),
        experts, experts, experts, tokens,
    )
    out_specs = (
        tokens, tokens, P(), P(), P(), P(), P(), P(), P(), P(),
        P("exp", None, "dp"), P("exp", None, "dp"), P("exp", "dp", None), P(),
    )
    return jax.shard_map(shards, mesh=mesh, in_specs=in_specs, out_specs=out_specs, check_vma=False)
```

```python
import math

import jax
import jax.numpy as jnp
from jax import lax
from jax.experimental import pallas as pl
from jax.experimental.pallas import tpu as pltpu
from jax.sharding import PartitionSpec as P

HEADS = 12
CAP = 128

norm_eps = 1e-05
clip_limit = 3.0
low_start = -1e30
mask_fill = -3e38
highest = lax.Precision.HIGHEST
NN = (((1,), (0,)), ((), ()))
NT = (((1,), (1,)), ((), ()))
TN = (((0,), (0,)), ((), ()))
f32 = jnp.float32
bf16 = jnp.bfloat16
MESH = pl.DeviceIdType.MESH


def mm(left, right, dims=NN):
    return lax.dot_general(left, right, dims, preferred_element_type=f32)


def mm_full(left, right, dims=NN):
    return lax.dot_general(left, right, dims, precision=highest, preferred_element_type=f32)


def shape_of(shape, dtype):
    return jax.ShapeDtypeStruct(shape, dtype)


def whole(array):
    rank = len(array.shape)
    return pl.BlockSpec(array.shape, lambda *_: (0,) * rank)


def cost(flops, moved, exps=0):
    return pl.CostEstimate(flops=int(flops), bytes_accessed=int(moved), transcendentals=int(exps))


def run(body, grid, inputs, outputs, scratch=(), meta=None, flops=0, moved=0, exps=0, aliases=None, talks=None):
    prefetch = 0 if meta is None else 1
    args = ([] if meta is None else [meta]) + [a for a, _ in inputs]
    return pl.pallas_call(
        body,
        out_shape=[o for o, _ in outputs],
        grid_spec=pltpu.PrefetchScalarGridSpec(
            num_scalar_prefetch=prefetch,
            grid=grid,
            in_specs=[s for _, s in inputs],
            out_specs=[s for _, s in outputs],
            scratch_shapes=list(scratch),
        ),
        compiler_params=pltpu.CompilerParams(
            dimension_semantics=("arbitrary",) * len(grid),
            vmem_limit_bytes=60 * 1024 * 1024,
            collective_id=talks,
            has_side_effects=talks is not None,
        ),
        cost_estimate=cost(flops, moved, exps),
        input_output_aliases={} if aliases is None else aliases,
    )(*args)


def swap(value, axis, distance):
    count = lax.axis_size(axis)
    return lax.ppermute(value, axis, [(i, i ^ distance) for i in range(count)])


def flip(value, bits):
    bit = 1
    while bit <= bits:
        if bits & bit:
            value = value + bit - 2 * bit * lax.rem(lax.div(value, bit), 2)
        bit *= 2
    return value


def powers(axis):
    found, bit = [], 1
    while bit < lax.axis_size(axis):
        found.append(bit)
        bit *= 2
    return found


def slot_peer(r, count, exp_now, me):
    return {"exp": flip(exp_now, r // count), "ctx": flip(me, 2 * (r % count))}


def slot_swap(value, r, count):
    groups = lax.axis_size("exp")
    total = groups * lax.axis_size("ctx")
    apart = 2 * (r % count) * groups + r // count
    return lax.ppermute(value, ("ctx", "exp"), [(i, i ^ apart) for i in range(total)])


def remote(src, dst, sent, arrived, peer):
    return pltpu.make_async_remote_copy(
        src_ref=src, dst_ref=dst, send_sem=sent, recv_sem=arrived,
        device_id=peer, device_id_type=MESH,
    )


def greet(peers):
    barrier = pltpu.get_barrier_semaphore()
    for peer in peers:
        pl.semaphore_signal(barrier, inc=1, device_id=peer, device_id_type=MESH)
    return lambda: pl.semaphore_wait(barrier, len(peers))


anywhere = pl.BlockSpec(memory_space=pl.ANY)
scalars = pl.BlockSpec(memory_space=pltpu.SMEM)
vector = pl.BlockSpec(memory_space=pltpu.VMEM)
dma = pltpu.SemaphoreType.DMA


def add_low(*terms):
    total = terms[0].astype(f32)
    for term in terms[1:]:
        total = total + term.astype(f32)
    return total.astype(bf16)


def begin(x, grad, routes, gain, w_qkv, local):
    rows, width = x.shape
    members, groups = lax.axis_size("ctx"), lax.axis_size("exp")
    group_rows = rows * members
    heads = HEADS // members
    head_width = width // HEADS
    columns = heads * head_width
    places = groups * local
    odd = [r for r in range(places) if r % local]
    scale = head_width**-0.5
    tile = min(256, rows)
    per_member = rows // tile

    def body(*refs):
        x_hbm, dy_ref, route_ref, gain_ref, w_hbm = refs[:5]
        q_out, k_out, v_out, kt_out, vt_out, h_out, wt_out = refs[5:12]
        target_out, target_rows, chosen_out, near_out = refs[12:16]
        rest_out, refs = refs[16 : 16 + len(odd)], refs[:16] + refs[16 + len(odd) :]
        x_near, w_in, w_t, q_all, k_all, v_all, kt_all, vt_all, h_all, packed, near = refs[16:27]
        load_sem, x_s, x_r, r_s, r_r, out_sem, near_sem = refs[27:]
        me, exp_now = lax.axis_index("ctx"), lax.axis_index("exp")
        side = lax.div(me, 2)
        peers = [{"ctx": flip(me, 1)}, {"ctx": flip(me, 2)}]
        peers += [slot_peer(local * g, local, exp_now, me) for g in range(1, groups)]
        ready = greet(peers)
        own = pltpu.make_async_copy(x_hbm, x_near.at[0], load_sem.at[0])
        weights = pltpu.make_async_copy(w_hbm, w_in, load_sem.at[1])
        own.start()
        weights.start()

        def across():
            return remote(x_hbm, x_near.at[2], x_s.at[2], x_r.at[2], {"ctx": flip(me, 2)})

        def beside():
            return remote(x_hbm, x_near.at[1], x_s.at[1], x_r.at[1], {"ctx": flip(me, 1)})

        def passed():
            return remote(x_near.at[2], x_near.at[3], x_s.at[3], x_r.at[3], {"ctx": flip(me, 1)})

        def row_copy(g):
            return remote(
                packed.at[g], near.at[g], r_s.at[g], r_r.at[g],
                slot_peer(local * g, local, exp_now, me),
            )

        ready()
        across().start()
        beside().start()

        lines = jnp.concatenate([route_ref[...].astype(f32), jnp.zeros((6, rows), f32)], axis=0)
        chosen = jnp.transpose(lines)[:, 0:2].astype(jnp.int32)
        chosen_out[...] = chosen
        expert_count = places
        lanes = lax.broadcasted_iota(jnp.int32, (rows, 128), 1)
        hits = [lanes == chosen[:, c : c + 1] for c in range(2)]
        hit = jnp.where((hits[0] | hits[1]) & (lanes < expert_count), 1.0, 0.0)
        later = lax.broadcasted_iota(jnp.int32, (rows, rows), 0)
        sooner = lax.broadcasted_iota(jnp.int32, (rows, rows), 1)
        ahead = mm(jnp.where(sooner < later, 1.0, 0.0).astype(bf16), hit.astype(bf16))
        spots = []
        for c in range(2):
            ids = chosen[:, c : c + 1]
            rank = jnp.sum(jnp.where(hits[c], ahead, 0.0), axis=1, keepdims=True).astype(jnp.int32)
            far_z = lax.div(ids, local)
            far_y = lax.rem(ids, local)
            z = jnp.zeros_like(ids)
            bit = 1
            while bit < groups:
                z = z + bit * jnp.where(
                    lax.rem(lax.div(far_z, bit), 2) == lax.rem(lax.div(exp_now, bit), 2), 0, 1
                )
                bit *= 2
            y = jnp.where(far_y == side, 0, 1)
            spots.append(jnp.where(ids < expert_count, (z * local + y) * CAP + rank, -1))
        target_out[...] = jnp.concatenate(spots, axis=1)
        wide = jnp.where(lanes == 0, spots[0], spots[1]).astype(f32)
        target_rows[...] = jnp.transpose(wide)[0:2, :].astype(jnp.int32)

        def pack(n, r):
            packed[n] = mm(slot_choice(r * CAP, CAP, target_rows), dy_ref[...]).astype(bf16)

        for g in range(groups - 1, -1, -1):
            pack(g, local * g)
            if g < groups - 1:
                row_copy(g + 1).start()
        for n, r in enumerate(odd):
            pack(groups + n, r)
        stores = [
            pltpu.make_async_copy(packed.at[0], near_out.at[0], near_sem.at[0]),
        ] + [
            pltpu.make_async_copy(packed.at[groups + n], rest_out[n], near_sem.at[groups + n])
            for n in range(len(odd))
        ]
        for copy in stores:
            copy.start()
        weights.wait()
        for w in range(3):
            w_t[w] = jnp.transpose(w_in[w])
        w_store = pltpu.make_async_copy(w_t, wt_out, load_sem.at[2])
        w_store.start()
        here = pl.ds(pl.multiple_of(me * columns, columns), columns)

        def chunk(j):
            def project(t, _):
                at = pl.multiple_of(t * tile, tile)
                to = pl.ds(pl.multiple_of(j * rows + t * tile, tile), tile)
                value = x_near[j, pl.ds(at, tile), :].astype(f32)
                inverse = lax.rsqrt(jnp.mean(value * value, axis=1, keepdims=True) + norm_eps)
                low = (value * inverse * gain_ref[...]).astype(bf16)
                h_all[to, :] = low
                q = mm(low, w_t[0, here, :], NT).astype(bf16) * jnp.asarray(scale, bf16)
                k = mm(low, w_t[1, here, :], NT).astype(bf16)
                v = mm(low, w_t[2, here, :], NT).astype(bf16)
                for h in range(heads):
                    part = slice(h * head_width, (h + 1) * head_width)
                    q_all[h, to, :] = q[:, part]
                    k_all[h, to, :] = k[:, part]
                    v_all[h, to, :] = v[:, part]
                kt_all[:, to] = mm(w_t[1, here, :], low, NT).astype(bf16)
                vt_all[:, to] = mm(w_t[2, here, :], low, NT).astype(bf16)
                return 0

            lax.fori_loop(0, per_member, project, 0)
            for copy in chunk_stores(j):
                copy.start()

        def chunk_stores(j):
            to = pl.ds(j * rows, rows)
            pairs = [(q_all, q_out), (k_all, k_out), (v_all, v_out)]
            found = [(a.at[:, to, :], b.at[:, to, :]) for a, b in pairs]
            found += [(a.at[:, to], b.at[:, to]) for a, b in ((kt_all, kt_out), (vt_all, vt_out))]
            found += [(h_all.at[to, :], h_out.at[to, :])]
            return [
                pltpu.make_async_copy(a, b, out_sem.at[6 * j + n]) for n, (a, b) in enumerate(found)
            ]

        own.wait()
        chunk(0)
        beside().wait()
        chunk(1)
        across().wait()
        passed().start()
        chunk(2)
        passed().wait()
        chunk(3)
        for g in range(1, groups):
            row_copy(g).wait()
            pltpu.make_async_copy(near.at[g], near_out.at[g], near_sem.at[g]).start()
        for copy in stores:
            copy.wait()
        w_store.wait()
        for j in range(members):
            for copy in chunk_stores(j):
                copy.wait()
        for g in range(1, groups):
            pltpu.make_async_copy(near.at[g], near_out.at[g], near_sem.at[g]).wait()

    by_head = (heads, group_rows, head_width)
    by_column = (columns, group_rows)
    slots = (places, CAP, width)
    return run(
        body,
        (),
        [(x, anywhere), (grad, vector), (routes, vector), (gain, vector), (w_qkv, anywhere)],
        [(shape_of(by_head, bf16), anywhere)] * 3
        + [(shape_of(by_column, bf16), anywhere)] * 2
        + [(shape_of((group_rows, width), bf16), anywhere)]
        + [(shape_of((3, width, width), bf16), anywhere)]
        + [(shape_of((rows, 2), jnp.int32), vector), (shape_of((2, rows), jnp.int32), vector)]
        + [(shape_of((rows, 2), jnp.int32), vector)]
        + [(shape_of((groups, CAP, width), bf16), anywhere)]
        + [(shape_of((CAP, width), bf16), anywhere)] * len(odd),
        scratch=[
            pltpu.VMEM((members, rows, width), bf16),
            pltpu.VMEM((3, width, width), bf16),
            pltpu.VMEM((3, width, width), bf16),
            pltpu.VMEM(by_head, bf16), pltpu.VMEM(by_head, bf16), pltpu.VMEM(by_head, bf16),
            pltpu.VMEM(by_column, bf16), pltpu.VMEM(by_column, bf16),
            pltpu.VMEM((group_rows, width), bf16),
            pltpu.VMEM(slots, bf16), pltpu.VMEM(slots, bf16),
            dma((3,)), dma((members,)), dma((members,)), dma((places,)), dma((places,)),
            dma((6 * members,)), dma((places + 1,)),
        ],
        flops=2 * group_rows * width * columns * 5,
        moved=20 * 1024 * 1024,
        talks=4,
    )


def document_start(meta_ref, position, layout):
    start = jnp.zeros_like(position)
    end = jnp.int32(0)
    for s in range(layout["sequences"]):
        end = end + meta_ref[layout["lengths"] + s]
        start = jnp.where(position >= end, end, start)
    return start


def block_range(meta_ref, query_block, key_block, rows, layout):
    q_first = query_block * rows
    k_first = key_block * rows
    begin = document_start(meta_ref, q_first, layout)
    begin_last = document_start(meta_ref, q_first + rows - 1, layout)
    needed = (k_first <= q_first) & (k_first + rows - 1 >= begin)
    full = (k_first < q_first) & (k_first >= begin_last)
    return q_first, k_first, needed, full


def allowed_pairs(meta_ref, q_first, k_first, rows, layout):
    q_pos = q_first + lax.broadcasted_iota(jnp.int32, (1, rows), 1)
    k_pos = k_first + lax.broadcasted_iota(jnp.int32, (rows, 1), 0)
    return (k_pos <= q_pos) & (k_pos >= document_start(meta_ref, q_pos, layout))


def attend(meta, q, k, vt, rows, layout):
    heads, group_rows, head_width = q.shape
    blocks = group_rows // rows
    width = heads * head_width

    def body(meta_ref, q_ref, k_ref, vt_ref, o_ref, ot_ref, lse_ref, top_ref, m_ref, l_ref, a_ref, qt_ref):
        i = pl.program_id(0)
        m_ref[...] = jnp.full_like(m_ref, low_start)
        l_ref[...] = jnp.zeros_like(l_ref)
        a_ref[...] = jnp.zeros_like(a_ref)
        for h in range(heads):
            qt_ref[h] = jnp.transpose(q_ref[h])

        def one(j, _):
            q_first, k_first, needed, full = block_range(meta_ref, i, j, rows, layout)
            at = pl.multiple_of(meta_ref[layout["inverse"] + j] * rows, rows)

            def step(masked):
                if masked:
                    allowed = allowed_pairs(meta_ref, q_first, k_first, rows, layout)
                for h in range(heads):
                    part = slice(h * head_width, (h + 1) * head_width)
                    s = mm(k_ref[h, pl.ds(at, rows), :], qt_ref[h])
                    if masked:
                        s = jnp.where(allowed, s, mask_fill)
                    old = m_ref[h]
                    new = jnp.maximum(old, jnp.max(s, axis=0, keepdims=True))
                    shrink = jnp.exp(old - new)
                    p = jnp.exp(s - new)
                    m_ref[h] = new
                    l_ref[h] = l_ref[h] * shrink + jnp.sum(p, axis=0, keepdims=True)
                    a_ref[part, :] = a_ref[part, :] * shrink + mm(
                        vt_ref[part, pl.ds(at, rows)], p.astype(bf16)
                    )

            @pl.when(full)
            def _():
                step(False)

            @pl.when(needed & jnp.logical_not(full))
            def _():
                step(True)

            return 0

        lax.fori_loop(0, i + 1, one, 0)
        for h in range(heads):
            part = slice(h * head_width, (h + 1) * head_width)
            ot_ref[part, :] = a_ref[part, :] / l_ref[h]
            lse_ref[pl.ds(h, 1), :] = m_ref[h] + jnp.log(l_ref[h])
            top = m_ref[h]

            @pl.when(i == 0)
            def _():
                top_ref[pl.ds(h, 1), :] = top

            @pl.when(i > 0)
            def _():
                top_ref[pl.ds(h, 1), :] = jnp.maximum(top_ref[pl.ds(h, 1), :], top)

        o_ref[...] = jnp.transpose(ot_ref[...]).astype(bf16)

    row = shape_of((heads, group_rows), f32)
    row_spec = pl.BlockSpec((heads, rows), lambda i, m: (0, i))
    return run(
        body,
        (blocks,),
        [
            (
                q,
                pl.BlockSpec(
                    (heads, rows, head_width), lambda i, m: (0, m[layout["inverse"] + i], 0)
                ),
            ),
            (k, whole(k)),
            (vt, whole(vt)),
        ],
        [
            (
                shape_of((group_rows, width), bf16),
                pl.BlockSpec((rows, width), lambda i, m: (m[layout["inverse"] + i], 0)),
            ),
            (shape_of((width, group_rows), f32), pl.BlockSpec((width, rows), lambda i, m: (0, i))),
            (row, row_spec),
            (shape_of((heads, rows), f32), pl.BlockSpec((heads, rows), lambda i, m: (0, 0))),
        ],
        scratch=[
            pltpu.VMEM((heads, 1, rows), f32),
            pltpu.VMEM((heads, 1, rows), f32),
            pltpu.VMEM((width, rows), f32),
            pltpu.VMEM((heads, head_width, rows), bf16),
        ],
        meta=meta,
        flops=2 * 2 * group_rows * group_rows * width,
        moved=group_rows * width * 14,
        exps=group_rows * group_rows * heads // 2,
    )


def attend_back(meta, q, k, v, kt, grad, w_out, ot, lse, rows, layout):
    heads, group_rows, head_width = q.shape
    blocks = group_rows // rows
    width = heads * head_width
    scale = head_width**-0.5
    per = grad.shape[1] // rows

    def body(meta_ref, q_ref, k_ref, v_ref, kt_ref, grad_ref, w_ref, *refs):
        ot_ref, lse_ref, out_ref, rows_ref, dk_ref, dv_ref, dq_ref, g_ref, delta_ref, sum_ref, qt_ref, gt_ref = refs
        i = pl.program_id(0)

        @pl.when(i == 0)
        def _():
            dk_ref[...] = jnp.zeros_like(dk_ref)
            dv_ref[...] = jnp.zeros_like(dv_ref)

        da = grad_ref[0]
        g = mm(da, w_ref[0], NT).astype(bf16)
        part_sum = mm(ot_ref[...].astype(bf16), da)

        @pl.when(i == 0)
        def _():
            sum_ref[...] = part_sum

        @pl.when(i > 0)
        def _():
            sum_ref[...] += part_sum

        for h in range(heads):
            g_ref[h] = g[:, h * head_width : (h + 1) * head_width]
        turned = jnp.transpose(g.astype(f32))
        gt_ref[...] = turned.astype(bf16)
        for h in range(heads):
            qt_ref[h] = jnp.transpose(q_ref[h])
        product = turned * ot_ref[...]
        for h in range(heads):
            part = slice(h * head_width, (h + 1) * head_width)
            delta_ref[h] = jnp.sum(product[part, :], axis=0, keepdims=True)

        dq_ref[...] = jnp.zeros_like(dq_ref)

        def one(j, _):
            q_first, k_first, needed, full = block_range(meta_ref, i, j, rows, layout)
            at = pl.multiple_of(meta_ref[layout["inverse"] + j] * rows, rows)
            to = pl.multiple_of(j * rows, rows)

            def step(masked):
                if masked:
                    allowed = allowed_pairs(meta_ref, q_first, k_first, rows, layout)
                for h in range(heads):
                    part = slice(h * head_width, (h + 1) * head_width)
                    s = mm(k_ref[h, pl.ds(at, rows), :], qt_ref[h])
                    if masked:
                        s = jnp.where(allowed, s, mask_fill)
                    p = jnp.exp(s - lse_ref[pl.ds(h, 1), :])
                    dp = mm(v_ref[h, pl.ds(at, rows), :], gt_ref[part, :])
                    ds = (p * (dp - delta_ref[h])).astype(bf16)
                    dv_ref[h, pl.ds(to, rows), :] += mm(p.astype(bf16), g_ref[h])
                    dk_ref[h, pl.ds(to, rows), :] += mm(ds, q_ref[h])
                    dq_ref[part, :] += mm(kt_ref[part, pl.ds(at, rows)], ds)

            @pl.when(full)
            def _():
                step(False)

            @pl.when(needed & jnp.logical_not(full))
            def _():
                step(True)

            return 0

        lax.fori_loop(0, i + 1, one, 0)
        here = pl.multiple_of(meta_ref[layout["inverse"] + i] * rows, rows)
        out_ref[pl.ds(here, rows), 0:width] = (jnp.transpose(dq_ref[...]) * scale).astype(bf16)

        @pl.when(i == blocks - 1)
        def _():
            rows_ref[...] = sum_ref[...].astype(bf16)

            def store(b, _):
                spot = pl.multiple_of(b * rows, rows)
                there = pl.multiple_of(meta_ref[layout["inverse"] + b] * rows, rows)
                out_ref[pl.ds(there, rows), width : 3 * width] = jnp.concatenate(
                    [dk_ref[h, pl.ds(spot, rows), :] for h in range(heads)]
                    + [dv_ref[h, pl.ds(spot, rows), :] for h in range(heads)],
                    axis=1,
                ).astype(bf16)
                return 0

            lax.fori_loop(0, blocks, store, 0)

    out = shape_of((group_rows, 3 * width), bf16)
    out_rows = shape_of((width, grad.shape[2]), bf16)
    return run(
        body,
        (blocks,),
        [
            (
                q,
                pl.BlockSpec(
                    (heads, rows, head_width), lambda i, m: (0, m[layout["inverse"] + i], 0)
                ),
            ),
            (k, whole(k)),
            (v, whole(v)),
            (kt, whole(kt)),
        ]
        + [
            (
                grad,
                pl.BlockSpec(
                    (1, rows, grad.shape[2]),
                    lambda i, m: (
                        m[layout["inverse"] + i] // per, m[layout["inverse"] + i] % per, 0
                    ),
                ),
            ),
            (w_out, pl.BlockSpec((1, width, grad.shape[2]), lambda i, m: (m[0], 0, 0))),
            (ot, pl.BlockSpec((width, rows), lambda i, m: (0, i))),
            (lse, pl.BlockSpec((heads, rows), lambda i, m: (0, i))),
        ],
        [(out, whole(out)), (out_rows, whole(out_rows))],
        scratch=[
            pltpu.VMEM((heads, group_rows, head_width), f32),
            pltpu.VMEM((heads, group_rows, head_width), f32),
            pltpu.VMEM((width, rows), f32),
            pltpu.VMEM((heads, rows, head_width), bf16),
            pltpu.VMEM((heads, 1, rows), f32),
            pltpu.VMEM((width, grad.shape[2]), f32),
            pltpu.VMEM((heads, head_width, rows), bf16),
            pltpu.VMEM((width, rows), bf16),
        ],
        meta=meta,
        flops=5 * 2 * group_rows * group_rows * width,
        moved=group_rows * width * 24,
        exps=group_rows * group_rows * heads // 2,
    )


def slot_choice(first, count, target_ref):
    rows = target_ref.shape[1]
    ids = first + lax.broadcasted_iota(jnp.int32, (count, rows), 0)
    match = (ids == target_ref[0:1, :]) | (ids == target_ref[1:2, :])
    return jnp.where(match, 1.0, 0.0).astype(bf16)


def token_front(
    x, o, w_out, gain, router_t, previous_t, w_carry, target_rows, grad, routes, logit_w, vectors, local
):
    rows, width = x.shape
    members, columns = w_out.shape[0], w_out.shape[1]
    expert_all = router_t.shape[0]
    groups = lax.axis_size("exp")
    places = groups * local
    expert_count = places
    kinds = vectors.shape[0]
    tile = 128

    def body(*refs):
        (x_ref, o_hbm, w_ref, gain_ref, router_ref, prev_ref, carry_ref, target_ref) = refs[:8]
        dy_ref, route_ref, lw_ref, vec_ref = refs[8:12]
        x1_ref, h2_ref, prob_ref, rows_out, gates_out, base_ref, dh_ref, dgate_ref, sums_ref = refs[12:21]
        o_near, low, split, packed, arrived, gate_mine, gate_near = refs[21:28]
        o_s, o_r, t_s, t_r, g_s, g_r, out_sem = refs[28:]
        me, exp_now = lax.axis_index("ctx"), lax.axis_index("exp")
        side = lax.div(me, 2)
        peers = [{"ctx": flip(me, j)} for j in range(1, members)]
        peers += [slot_peer(r, local, exp_now, me) for r in range(local, places)]
        ready = greet(peers)

        def o_copy(j):
            src = o_hbm.at[pl.ds(j * rows, rows), :]
            if j == 0:
                return pltpu.make_async_copy(src, o_near.at[0], o_r.at[0])
            return remote(src, o_near.at[j], o_s.at[j], o_r.at[j], {"ctx": flip(me, j)})

        def row_copy(r):
            return remote(
                packed.at[r], arrived.at[r], t_s.at[r], t_r.at[r], slot_peer(r, local, exp_now, me)
            )

        def gate_copy(r):
            return remote(
                gate_mine.at[r], gate_near.at[r], g_s.at[r], g_r.at[r],
                slot_peer(r, local, exp_now, me),
            )

        o_copy(0).start()
        ready()
        for j in range(1, members):
            o_copy(j).start()
        for j in range(members):
            o_copy(j).wait()

        def front_rows(t, _):
            here = pl.ds(pl.multiple_of(t * tile, tile), tile)
            total = x_ref[here, :].astype(f32)
            for j in range(members):
                total = total + mm(o_near[j, here, :], w_ref[flip(me, j)])
            x1_ref[here, :] = total
            inverse = lax.rsqrt(jnp.mean(total * total, axis=1, keepdims=True) + norm_eps)
            h2 = total * inverse * gain_ref[...]
            h2_ref[here, :] = h2
            logits = mm_full(h2, router_ref[...], NT) + mm_full(
                prev_ref[:, here], carry_ref[...], TN
            )
            shifted = jnp.exp(logits - jnp.max(logits, axis=1, keepdims=True))
            prob = shifted / jnp.sum(shifted, axis=1, keepdims=True)
            prob_ref[here, :] = prob
            low[here, :] = h2.astype(bf16)
            top = prob.astype(bf16)
            rest = prob - top.astype(f32)
            middle = rest.astype(bf16)
            split[0, here, :] = top
            split[1, here, :] = middle
            split[2, here, :] = (rest - middle.astype(f32)).astype(bf16)
            return 0

        lax.fori_loop(0, rows // tile, front_rows, 0)
        diagonal = lax.broadcasted_iota(jnp.int32, (CAP, CAP), 0) == lax.broadcasted_iota(
            jnp.int32, (CAP, CAP), 1
        )
        lanes = lax.broadcasted_iota(jnp.int32, (CAP, expert_all), 1)
        for r in list(range(1, places)) + [0]:
            choice = slot_choice(r * CAP, CAP, target_ref)
            packed[r] = mm(choice, low[...]).astype(bf16)
            picked = mm(choice, split[0]) + mm(choice, split[1]) + mm(choice, split[2])
            expert = flip(exp_now, r // local) * local + flip(side, r % local)
            column = jnp.sum(jnp.where(lanes == expert, picked, 0.0), axis=1, keepdims=True)
            gate_mine[r] = jnp.sum(jnp.where(diagonal, column, 0.0), axis=0, keepdims=True)
            last = r - 1 if r else places - 1
            if last:
                row_copy(last).start()
                gate_copy(last).start()

        def own_copy(n):
            src, dst = (packed, rows_out) if n == 0 else (gate_mine, gates_out)
            return pltpu.make_async_copy(src.at[0], dst.at[0], out_sem.at[n])

        own_copy(0).start()
        own_copy(1).start()

        def zero_rows(t, _):
            here = pl.ds(pl.multiple_of(t * tile, tile), tile)
            h2 = h2_ref[here, :]
            dy = dy_ref[here, :].astype(f32)
            prob_now = prob_ref[here, :]
            classes = lax.broadcasted_iota(jnp.int32, (tile, expert_all), 1)
            chosen = route_ref[here, :]
            ids = [chosen[:, c : c + 1] for c in range(2)]
            gates = [
                jnp.sum(jnp.where(classes == r, prob_now, 0.0), axis=1, keepdims=True) for r in ids
            ]
            along = jnp.sum(dy * h2, axis=1, keepdims=True)
            copies = [(r == expert_count + 1).astype(f32) for r in ids]
            keep = copies[0] * gates[0] + copies[1] * gates[1]
            dgates = [copies[c] * along for c in range(2)]
            scores = [
                jnp.sum(h2 * lw_ref[n : n + 1, :], axis=1, keepdims=True) for n in range(2 * kinds)
            ]
            base = x1_ref[here, :]
            dh = jnp.zeros_like(h2)
            for j in range(kinds):
                top = jnp.maximum(scores[2 * j], scores[2 * j + 1])
                e0 = jnp.exp(scores[2 * j] - top)
                e1 = jnp.exp(scores[2 * j + 1] - top)
                a0 = e0 / (e0 + e1)
                a1 = e1 / (e0 + e1)
                vec = vec_ref[j : j + 1, :]
                along_vec = jnp.sum(dy * vec, axis=1, keepdims=True)
                these = [(r == expert_count + 2 + j).astype(f32) for r in ids]
                weight = these[0] * gates[0] + these[1] * gates[1]
                for c in range(2):
                    dgates[c] = dgates[c] + these[c] * (a0 * along + a1 * along_vec)
                keep = keep + weight * a0
                base = base + (weight * a1) * vec
                d0 = weight * along
                d1 = weight * along_vec
                mean = a0 * d0 + a1 * d1
                z0 = a0 * (d0 - mean)
                z1 = a1 * (d1 - mean)
                dh = dh + z0 * lw_ref[2 * j : 2 * j + 1, :] + z1 * lw_ref[2 * j + 1 : 2 * j + 2, :]
                sums_ref[j : j + 1, :] += jnp.sum((weight * a1) * dy, axis=0, keepdims=True)
                at = kinds + 2 * j
                sums_ref[at : at + 1, :] += jnp.sum(z0 * h2, axis=0, keepdims=True)
                sums_ref[at + 1 : at + 2, :] += jnp.sum(z1 * h2, axis=0, keepdims=True)
            base_ref[here, :] = base + keep * h2
            dh_ref[here, :] = dh + keep * dy
            dgate_ref[here, :] = jnp.concatenate(dgates, axis=1)
            return 0

        sums_ref[...] = jnp.zeros_like(sums_ref)
        lax.fori_loop(0, rows // tile, zero_rows, 0)

        def rows_store(r):
            return pltpu.make_async_copy(arrived.at[r], rows_out.at[r], out_sem.at[2 * r])

        def gates_store(r):
            return pltpu.make_async_copy(gate_near.at[r], gates_out.at[r], out_sem.at[2 * r + 1])

        for r in range(1, places):
            row_copy(r).wait()
            gate_copy(r).wait()
            rows_store(r).start()
            gates_store(r).start()
        own_copy(0).wait()
        own_copy(1).wait()
        for r in range(1, places):
            rows_store(r).wait()
            gates_store(r).wait()

    wide = shape_of((rows, width), f32)
    placed = shape_of((places, CAP, width), bf16)
    lines = shape_of((places, 1, CAP), f32)
    return run(
        body,
        (),
        [(x, vector), (o, anywhere), (w_out, vector), (gain, vector), (router_t, vector)]
        + [(previous_t, vector), (w_carry, vector), (target_rows, vector), (grad, vector)]
        + [(routes, vector), (logit_w, vector), (vectors, vector)],
        [(wide, vector), (wide, vector), (shape_of((rows, expert_all), f32), vector)]
        + [(placed, anywhere), (lines, anywhere), (wide, vector), (wide, vector)]
        + [(shape_of((rows, 2), f32), vector), (shape_of((3 * kinds, width), f32), vector)],
        scratch=[
            pltpu.VMEM((members, rows, columns), bf16),
            pltpu.VMEM((rows, width), bf16),
            pltpu.VMEM((3, rows, expert_all), bf16),
            pltpu.VMEM((places, CAP, width), bf16),
            pltpu.VMEM((places, CAP, width), bf16),
            pltpu.VMEM((places, 1, CAP), f32),
            pltpu.VMEM((places, 1, CAP), f32),
            dma((members,)), dma((members,)),
            dma((places,)), dma((places,)), dma((places,)), dma((places,)),
            dma((2 * places,)),
        ],
        flops=2 * rows * width * (width + places * CAP),
        moved=rows * width * 30,
        talks=1,
    )


def expert_layer(arrived, grads, late, gates, w_gate, w_up, w_down):
    places = arrived.shape[0]
    local = w_gate.shape[0]
    rows = places * CAP
    width, hidden = w_gate.shape[1], w_gate.shape[2]
    parts = lax.axis_size("dp")
    groups = places // local
    half = width // 2
    per_part = hidden // parts
    tile = min(256, per_part)
    steps = hidden // tile
    tiles = per_part // tile
    away = steps - tiles
    chunk = 256

    def body(*refs):
        x_ref, dy_ref, gates_ref, wg_hbm, wu_hbm, wd_hbm = refs[:6]
        dy_late, refs = refs[6 : 6 + len(late)], refs[:6] + refs[6 + len(late) :]
        dy_parts = [
            dy_late[r // local] if r % local else dy_ref.at[r // local] for r in range(places)
        ]
        y_out, refs = refs[6 : 6 + groups], refs[:6] + refs[6 + groups :]
        dx_out, dots_out, sum_out, beside_out = refs[6:10]
        refs = refs[:6] + (None,) + refs[6:]
        x_all, xt_all, dy_all, dyt_all, gate_all, y_acc, dx_acc, dot_acc = refs[11:19]
        hid_t, dgt, dut, scaled_t, wg_buf, wu_buf, wd_buf = refs[19:26]
        hid_own, dg_own, du_own, scaled_own, wg_own, wu_own, wd_own = refs[26:33]
        send, total, taken, far, dx_low, dx_near, dots, dots_near = refs[33:41]
        beside, y_odd, relay = refs[41:44]
        w_sem, own_sem, c_s, c_r, f_s, f_r, b_s, b_r, d_s, d_r, out_sem = refs[44:55]
        e_s, e_r, beside_sem, y_s, y_r = refs[55:]
        me, exp_now, dp_now = lax.axis_index("ctx"), lax.axis_index("exp"), lax.axis_index("dp")
        core, side = lax.rem(me, 2), lax.div(me, 2)
        sibling = {"ctx": flip(me, 1)}
        peers = [sibling] + [{"dp": flip(dp_now, d)} for d in range(1, parts)]
        peers += [slot_peer(r, local, exp_now, me) for r in range(1, places)]
        ready = greet(peers)
        diagonal = lax.broadcasted_iota(jnp.int32, (CAP, CAP), 0) == lax.broadcasted_iota(
            jnp.int32, (CAP, CAP), 1
        )

        def dp_of(f):
            distance = parts - 1 - lax.div(f, tiles)
            found, bit = dp_now, 1
            while bit < parts:
                on = lax.rem(lax.div(distance, bit), 2)
                now = lax.rem(lax.div(found, bit), 2)
                found = found + on * bit * (1 - 2 * now)
                bit *= 2
            return found

        def weights(f, slot):
            at = pl.multiple_of(dp_of(f) * per_part + lax.rem(f, tiles) * tile, tile)
            return [
                pltpu.make_async_copy(
                    wg_hbm.at[side, :, pl.ds(at, tile)], wg_buf.at[slot], w_sem.at[0, slot]
                ),
                pltpu.make_async_copy(
                    wu_hbm.at[side, :, pl.ds(at, tile)], wu_buf.at[slot], w_sem.at[1, slot]
                ),
                pltpu.make_async_copy(
                    wd_hbm.at[side, pl.ds(at, tile), :], wd_buf.at[slot], w_sem.at[2, slot]
                ),
            ]

        def core_copy(f, slot):
            return remote(send.at[slot], taken.at[f], c_s.at[slot], c_r.at[f], sibling)

        def far_copy(f):
            return remote(total.at[f], far.at[f], f_s.at[f], f_r.at[f], {"dp": dp_of(f)})

        def back_copy(r):
            return remote(
                dx_low.at[r], dx_near.at[r], b_s.at[r], b_r.at[r],
                slot_peer(r, local, exp_now, me),
            )

        def dots_copy(r):
            return remote(
                dots.at[r], dots_near.at[r], d_s.at[r], d_r.at[r],
                slot_peer(r, local, exp_now, me),
            )

        def own_weights():
            at = pl.ds(pl.multiple_of(dp_now * per_part, per_part), per_part)
            return [
                pltpu.make_async_copy(wg_hbm.at[side, :, at], wg_own, own_sem.at[0]),
                pltpu.make_async_copy(wu_hbm.at[side, :, at], wu_own, own_sem.at[1]),
                pltpu.make_async_copy(wd_hbm.at[side, at, :], wd_own, own_sem.at[2]),
            ]

        if away:
            for copy in weights(0, 0):
                copy.start()
        for copy in own_weights():
            copy.start()
        first_half = pl.ds(pl.multiple_of((1 - core) * half, half), half)
        second_half = pl.ds(pl.multiple_of(core * half, half), half)
        for r in range(places):
            here = slice(r * CAP, (r + 1) * CAP)
            x_all[here, :] = x_ref[r]
            turned = jnp.transpose(x_ref[r])
            xt_all[first_half, here] = turned[:half, :]
            xt_all[second_half, here] = turned[half:, :]
            dy_all[here, :] = dy_parts[r][...]
            turned = jnp.transpose(dy_parts[r][...])
            dyt_all[first_half, here] = turned[:half, :]
            dyt_all[second_half, here] = turned[half:, :]
            gate_all[here, :] = jnp.sum(
                jnp.where(diagonal, gates_ref[r], 0.0), axis=1, keepdims=True
            )
        y_acc[...] = jnp.zeros_like(y_acc)
        dx_acc[...] = jnp.zeros_like(dx_acc)
        dot_acc[...] = jnp.zeros_like(dot_acc)
        ready()

        def core_sum(f):
            core_copy(f, lax.rem(f, 2)).wait_recv()
            for n in range(3):
                total[f, n] = (total[f, n].astype(f32) + taken[f, n].astype(f32)).astype(bf16)

        def forward_back(here, wg, wu, wd, hid_ref, dg_ref, du_ref, scaled_ref):
            g_pre = mm(x_all[here, :], wg)
            u_pre = mm(x_all[here, :], wu)
            back = mm(dy_all[here, :], wd, NT)
            gate = gate_all[here, :]
            sig = 1.0 / (1.0 + jnp.exp(-g_pre))
            act = g_pre * sig
            hid = act * u_pre
            hid_ref[here, :] = hid.astype(bf16)
            scaled_ref[here, :] = (gate * hid).astype(bf16)
            along = hid * back
            lines = along[:, 0:128]
            for n in range(1, tile // 128):
                lines = lines + along[:, n * 128 : (n + 1) * 128]
            dot_acc[here, :] += lines
            dhid = gate * back
            dg = (dhid * u_pre * sig * (1.0 + g_pre * (1.0 - sig))).astype(bf16)
            du = (dhid * act).astype(bf16)
            dg_ref[here, :] = dg
            du_ref[here, :] = du

        def rows_back(here, wg, wu, dg_ref, du_ref):
            dx_acc[here, :] += mm(dg_ref[here, :], wg, NT) + mm(du_ref[here, :], wu, NT)

        def weight_sums(f, slot, hid_ref, dg_ref, du_ref, scaled_ref, wd):
            @pl.when(f >= 1)
            def _():
                core_sum(f - 1)

            @pl.when(f >= 2)
            def _():
                core_copy(f - 2, slot).wait_send()

            for n, (left, right) in enumerate(((xt_all, dg_ref), (xt_all, du_ref), (dyt_all, scaled_ref))):
                found = mm(left[...], right[...]).astype(bf16)
                send[slot, n] = found[:half, :]
                total[f, n] = found[half:, :]
            core_copy(f, slot).start()

            @pl.when((f >= 1) & (f - 1 < away))
            def _():
                far_copy(f - 1).start()

            y_acc[...] += mm(hid_ref[...], wd)

        def away_step(f, _):
            slot = lax.rem(f, 2)
            for copy in weights(f, slot):
                copy.wait()

            @pl.when(f + 1 < away)
            def _():
                for copy in weights(f + 1, 1 - slot):
                    copy.start()

            def row_chunk(c, _):
                here = pl.ds(pl.multiple_of(c * chunk, chunk), chunk)
                forward_back(
                    here, wg_buf[slot], wu_buf[slot], wd_buf[slot], hid_t, dgt, dut, scaled_t
                )
                return 0

            lax.fori_loop(0, rows // chunk, row_chunk, 0)
            weight_sums(f, slot, hid_t, dgt, dut, scaled_t, wd_buf[slot])
            rows_back(slice(0, rows), wg_buf[slot], wu_buf[slot], dgt, dut)
            return 0

        lax.fori_loop(0, away, away_step, 0)
        for copy in own_weights():
            copy.wait()
        if away:
            core_sum(away - 1)
            far_copy(away - 1).start()

        def own_rows(first, count):
            size = min(chunk, count)

            def own_tile(i, _):
                at = pl.ds(pl.multiple_of(i * tile, tile), tile)
                for c in range(count // size):
                    forward_back(
                        slice(first + c * size, first + (c + 1) * size),
                        wg_own[:, at], wu_own[:, at], wd_own[at, :],
                        hid_own.at[i], dg_own.at[i], du_own.at[i], scaled_own.at[i],
                    )
                rows_back(
                    slice(first, first + count), wg_own[:, at], wu_own[:, at], dg_own.at[i], du_own.at[i]
                )
                return 0

            lax.fori_loop(0, tiles, own_tile, 0)

        def send_back(first, last):
            for r in range(first, last):
                here = slice(r * CAP, (r + 1) * CAP)
                dx_low[r] = dx_acc[here, :].astype(bf16)
                column = jnp.sum(dot_acc[here, :], axis=1, keepdims=True)
                dots[r] = jnp.sum(jnp.where(diagonal, column, 0.0), axis=0, keepdims=True)
                if r - 1 >= max(1, first):
                    back_copy(r - 1).start()
                    dots_copy(r - 1).start()

        def send_last(r):
            back_copy(r).start()
            dots_copy(r).start()

        middle = places // 2
        own_rows(middle * CAP, rows - middle * CAP)
        send_back(middle, places)
        own_rows(0, middle * CAP)
        send_last(places - 1)
        send_back(0, middle)

        def own_result(i, _):
            at = pl.ds(pl.multiple_of(i * tile, tile), tile)
            y_acc[...] += mm(hid_own[i], wd_own[at, :])
            return 0

        lax.fori_loop(0, tiles, own_result, 0)
        send_last(middle - 1)

        def relay_copy(g):
            return remote(y_odd.at[g], relay.at[g], y_s.at[g], y_r.at[g], {"ctx": flip(me, 2)})

        def result(r):
            here = slice(r * CAP, (r + 1) * CAP)
            return (gate_all[here, :] * y_acc[here, :]).astype(bf16)

        for g in range(groups):
            y_odd[g] = result(local * g + 1)
            if g:
                relay_copy(g - 1).start()
        for g in range(groups):
            y_out[g][0] = result(local * g)
        relay_copy(groups - 1).start()

        def own_step(i, _):
            f = away + i

            @pl.when(i >= 1)
            def _():
                core_sum(f - 1)

            slot = lax.rem(f, 2)

            @pl.when(f >= 2)
            def _():
                core_copy(f - 2, slot).wait_send()

            dg, du, scaled = dg_own.at[i], du_own.at[i], scaled_own.at[i]
            for n, (left, right) in enumerate(((xt_all, dg), (xt_all, du), (dyt_all, scaled))):
                found = mm(left[...], right[...]).astype(bf16)
                send[slot, n] = found[:half, :]
                total[f, n] = found[half:, :]
            core_copy(f, slot).start()
            return 0

        lax.fori_loop(0, tiles, own_step, 0)
        core_sum(steps - 1)
        def beside_copy(i):
            return remote(total.at[away + i], beside.at[i], e_s.at[i], e_r.at[i], sibling)

        def beside_store(i):
            return pltpu.make_async_copy(
                beside.at[i], beside_out.at[:, :, pl.ds(i * tile, tile)], beside_sem.at[i]
            )

        def sum_store(i):
            return pltpu.make_async_copy(
                total.at[away + i], sum_out.at[:, :, pl.ds(i * tile, tile)], out_sem.at[i]
            )

        for i in range(tiles):
            for d in range(1, parts):
                far_copy((parts - 1 - d) * tiles + i).wait_recv()
            for n in range(3):
                value = total[away + i, n].astype(f32)
                for d in range(1, parts):
                    value = value + far[(parts - 1 - d) * tiles + i, n].astype(f32)
                total[away + i, n] = value.astype(bf16)
            if i:
                beside_copy(i - 1).start()
            sum_store(i).start()
        beside_copy(tiles - 1).start()
        for f in range(away):
            far_copy(f).wait_send()
        for f in range(max(0, steps - 2), steps):
            core_copy(f, f % 2).wait_send()

        dx_out[0] = dx_low[0]
        dots_out[0] = dots[0]
        for r in range(1, places):
            back_copy(r).wait()
            dots_copy(r).wait()
            dx_out[r] = dx_near[r]
            dots_out[r] = dots_near[r]
        for g in range(groups):
            relay_copy(g).wait()
            y_out[g][1] = relay[g]
        for i in range(tiles):
            beside_copy(i).wait()
            beside_store(i).start()
        for i in range(tiles):
            sum_store(i).wait()
            beside_store(i).wait()

    placed = shape_of((places, CAP, width), bf16)
    pair = shape_of((local, CAP, width), bf16)
    lines = shape_of((places, 1, CAP), f32)
    return run(
        body,
        (),
        [(arrived, vector), (grads, vector), (gates, vector)]
        + [(w, anywhere) for w in (w_gate, w_up, w_down)]
        + [(g, vector) for g in late],
        [(pair, vector)] * groups
        + [(placed, vector), (lines, vector)]
        + [(shape_of((3, half, per_part), bf16), anywhere)] * 2,
        scratch=[
            pltpu.VMEM((rows, width), bf16),
            pltpu.VMEM((width, rows), bf16),
            pltpu.VMEM((rows, width), bf16),
            pltpu.VMEM((width, rows), bf16),
            pltpu.VMEM((rows, 1), f32),
            pltpu.VMEM((rows, width), f32),
            pltpu.VMEM((rows, width), f32),
            pltpu.VMEM((rows, 128), f32),
            pltpu.VMEM((rows, tile), bf16),
            pltpu.VMEM((rows, tile), bf16),
            pltpu.VMEM((rows, tile), bf16),
            pltpu.VMEM((rows, tile), bf16),
            pltpu.VMEM((2, width, tile), bf16),
            pltpu.VMEM((2, width, tile), bf16),
            pltpu.VMEM((2, tile, width), bf16),
            pltpu.VMEM((tiles, rows, tile), bf16),
            pltpu.VMEM((tiles, rows, tile), bf16),
            pltpu.VMEM((tiles, rows, tile), bf16),
            pltpu.VMEM((tiles, rows, tile), bf16),
            pltpu.VMEM((width, per_part), bf16),
            pltpu.VMEM((width, per_part), bf16),
            pltpu.VMEM((per_part, width), bf16),
            pltpu.VMEM((2, 3, half, tile), bf16),
            pltpu.VMEM((steps, 3, half, tile), bf16),
            pltpu.VMEM((steps, 3, half, tile), bf16),
            pltpu.VMEM((max(1, away), 3, half, tile), bf16),
            pltpu.VMEM((places, CAP, width), bf16),
            pltpu.VMEM((places, CAP, width), bf16),
            pltpu.VMEM((places, 1, CAP), f32),
            pltpu.VMEM((places, 1, CAP), f32),
            pltpu.VMEM((tiles, 3, half, tile), bf16),
            pltpu.VMEM((groups, CAP, width), bf16),
            pltpu.VMEM((groups, CAP, width), bf16),
            dma((3, 2)), dma((3,)), dma((2,)), dma((steps,)),
            dma((max(1, away),)), dma((max(1, away),)),
            dma((places,)), dma((places,)), dma((places,)), dma((places,)),
            dma((tiles,)), dma((tiles,)), dma((tiles,)), dma((tiles,)),
            dma((groups,)), dma((groups,)),
        ],
        flops=9 * 2 * rows * width * hidden,
        moved=12 * width * hidden + rows * width * 8,
        exps=rows * hidden,
        talks=2,
    )


def slot_sum(targets, source_ref):
    tile = targets.shape[0]
    total = None
    for r in range(source_ref.shape[0]):
        ids = r * CAP + lax.broadcasted_iota(jnp.int32, (tile, CAP), 1)
        choice = jnp.where((ids == targets[:, 0:1]) | (ids == targets[:, 1:2]), 1.0, 0.0)
        part = mm(choice.astype(bf16), source_ref[r])
        total = part if total is None else total + part
    return total


def token_back(
    x1, h2, grad, prob, previous_t, routes, targets, back, dots, dgate_zero, dh_zero, gain, router_t,
    zero_sums,
):
    rows, width = x1.shape
    tile = 128
    tiles = rows // tile
    places = back.shape[0]
    expert_all = prob.shape[1]
    members = lax.axis_size("ctx")
    last = expert_all + 1 + zero_sums.shape[0]

    def body(*refs):
        (x1_ref, h2_ref, dy_ref, prob_ref, prev_ref, route_ref, target_ref) = refs[:7]
        back_ref, dots_ref, dz_ref, dh_ref, gain_ref, router_ref, zero_ref = refs[7:14]
        dx1_ref, sums_ref, da_out, da_near, a_s, a_r, out_sem = refs[14:]
        me = lax.axis_index("ctx")
        peers = [{"ctx": flip(me, 1)}, {"ctx": flip(me, 2)}]
        ready = greet(peers)

        def da_copy(kind, t):
            here = pl.ds(pl.multiple_of(t * tile, tile), tile)
            n = kind * tiles + t
            src, dst = ((0, 1), (0, 2), (2, 3))[kind]
            return remote(
                da_near.at[src, here, :], da_near.at[dst, here, :], a_s.at[n], a_r.at[n],
                {"ctx": flip(me, 2 if kind == 1 else 1)},
            )

        sums_ref[...] = jnp.zeros_like(sums_ref)
        sums_ref[expert_all + 1 : last, :] = zero_ref[...]
        ready()

        def token_rows(t, _):
            here = pl.ds(pl.multiple_of(t * tile, tile), tile)
            prob_now = prob_ref[here, :]
            chosen, target, zero = route_ref[here, :], target_ref[here, :], dz_ref[here, :]
            lanes = lax.broadcasted_iota(jnp.int32, (tile, expert_all), 1)
            dprob = jnp.zeros_like(prob_now)
            for c in range(2):
                dgate = zero[:, c : c + 1]
                for n in range(places):
                    ids = n * CAP + lax.broadcasted_iota(jnp.int32, (tile, CAP), 1)
                    dgate = dgate + jnp.sum(
                        jnp.where(ids == target[:, c : c + 1], dots_ref[n], 0.0),
                        axis=1,
                        keepdims=True,
                    )
                dprob = dprob + jnp.where(lanes == chosen[:, c : c + 1], dgate, 0.0)
            dlogit = prob_now * (dprob - jnp.sum(prob_now * dprob, axis=1, keepdims=True))
            h2 = h2_ref[here, :]
            dh2 = slot_sum(target, back_ref) + dh_ref[here, :] + mm_full(dlogit, router_ref[...])
            x1 = x1_ref[here, :]
            inverse = lax.rsqrt(jnp.mean(x1 * x1, axis=1, keepdims=True) + norm_eps)
            normed = x1 * inverse
            dn = dh2 * gain_ref[...]
            dx1 = dy_ref[here, :].astype(f32) + inverse * (
                dn - normed * jnp.mean(dn * normed, axis=1, keepdims=True)
            )
            dx1_ref[here, :] = dx1
            da_near[0, here, :] = dx1.astype(bf16)
            sums_ref[0:expert_all, :] += mm_full(dlogit, h2, TN)
            sums_ref[expert_all : expert_all + 1, :] += jnp.sum(dh2 * normed, axis=0, keepdims=True)
            sums_ref[last:, 0:expert_all] += mm_full(prev_ref[:, here], dlogit)
            da_copy(1, t).start()
            da_copy(0, t).start()

            @pl.when(t >= 2)
            def _():
                da_copy(1, t - 2).wait_recv()
                da_copy(2, t - 2).start()

            return 0

        lax.fori_loop(0, tiles, token_rows, 0)
        for t in range(max(0, tiles - 2), tiles):
            da_copy(1, t).wait_recv()
            da_copy(2, t).start()
        mine = pltpu.make_async_copy(da_near.at[0], da_out.at[0], out_sem.at[0])
        mine.start()
        for t in range(tiles):
            da_copy(0, t).wait()
            da_copy(1, t).wait_send()
            da_copy(2, t).wait()
        rest = pltpu.make_async_copy(
            da_near.at[pl.ds(1, members - 1)], da_out.at[pl.ds(1, members - 1)], out_sem.at[1]
        )
        rest.start()
        mine.wait()
        rest.wait()

    return run(
        body,
        (),
        [(a, vector) for a in (x1, h2, grad, prob, previous_t, routes, targets, back, dots)]
        + [(a, vector) for a in (dgate_zero, dh_zero, gain, router_t, zero_sums)],
        [(shape_of((rows, width), f32), vector)]
        + [(shape_of((last + expert_all, width), f32), vector)]
        + [(shape_of((members, rows, width), bf16), anywhere)],
        scratch=[
            pltpu.VMEM((members, rows, width), bf16),
            dma((3 * tiles,)), dma((3 * tiles,)), dma((2,)),
        ],
        flops=2 * rows * width * (places * CAP + width),
        moved=rows * width * 24,
        talks=5,
    )


def finish(dqkv_all, h1, x, gain, dx1, weights_t, out_sum, small, tops, produced, base, targets):
    members, per_group = weights_t.shape[1], weights_t.shape[2]
    rows, width = x.shape
    group_rows = dqkv_all.shape[0]
    parts, groups = lax.axis_size("dp"), lax.axis_size("exp")
    team = parts * groups
    local = produced[0].shape[0]
    places = groups * local
    wide_share, out_share = width // (2 * team), per_group // team
    small_rows = small.shape[0]
    small_steps = [(axis, bit) for axis in ("ctx", "dp", "exp") for bit in powers(axis)]
    hops = len(small_steps)
    row_tile = min(256, rows)

    def body(*refs):
        it = iter(refs)

        def take(count=None):
            return next(it) if count is None else [next(it) for _ in range(count)]

        dqkv_hbm, h1_hbm, x_hbm, gain_ref, dx1_hbm, w_hbm, out_ref = take(7)
        small_ref, tops_ref, base_hbm, target_ref = take(4)
        produced_hbm = take(groups)
        input_out, wide_out, flat_out, small_out, gain_out, tops_out, result_out = take(7)
        dqkv, product, h1_all, x_all, dx1_all, w_all, base_all, y_near = take(8)
        part_send, part_core, part_y, y_got, part_own = take(5)
        wide_mine, wide_far_x, wide_far_z, wide_all = take(4)
        flat_mine, flat_far_x, flat_far_z, flat_all = take(4)
        small_acc, small_far, gain_acc, gain_far, tops_acc, tops_far = take(6)
        load_sem, near_s, near_r = take(3)
        wide_sems, flat_sems = [take(12), take(12)], take(12)
        hop_s, hop_r, gain_s, gain_r, top_s, top_r = take(6)

        me = lax.axis_index("ctx")
        dp_now, exp_now = lax.axis_index("dp"), lax.axis_index("exp")
        seat = dp_now * groups + exp_now

        def near_peer(j):
            return {"ctx": flip(me, j)}

        def team_peer(r):
            return {"dp": flip(dp_now, r // groups), "exp": flip(exp_now, r % groups)}

        peers = [near_peer(j) for j in range(1, members)]
        peers += [team_peer(r) for r in range(1, team)]
        ready = greet(peers)

        loads = [
            (dqkv_hbm, dqkv), (h1_hbm, h1_all), (x_hbm, x_all), (dx1_hbm, dx1_all),
            (w_hbm.at[:, me], w_all), (base_hbm, base_all),
        ]
        loads += [
            (produced_hbm[g], y_near.at[pl.ds(g * local, local)]) for g in range(groups)
        ]

        def load(n):
            return pltpu.make_async_copy(loads[n][0], loads[n][1], load_sem.at[n])

        class Dense:
            def __init__(self, mine, far_x, far_z, all_buf, sems):
                self.mine, self.far_x, self.far_z, self.all = mine, far_x, far_z, all_buf
                self.sems = sems

            def own_block(self, d=0):
                return pl.ds(flip(dp_now, d) * groups, groups)

            def x_copy(self, d):
                return remote(
                    self.mine.at[self.own_block(d)], self.far_x.at[d - 1], self.sems[0].at[d],
                    self.sems[1].at[d], {"dp": flip(dp_now, d)},
                )

            def z_copy(self, g):
                return remote(
                    self.mine.at[dp_now * groups + flip(exp_now, g)], self.far_z.at[g - 1],
                    self.sems[2].at[g], self.sems[3].at[g], {"exp": flip(exp_now, g)},
                )

            def gz_copy(self, g, theirs=False):
                spot = self.all.at[0, dp_now * groups + flip(exp_now, g) if theirs else seat]
                return remote(
                    spot, spot, self.sems[4].at[g], self.sems[5].at[g], {"exp": flip(exp_now, g)}
                )

            def gx_copy(self, d, theirs=False):
                spot = self.all.at[0, self.own_block(d if theirs else 0)]
                return remote(
                    spot, spot, self.sems[6].at[d], self.sems[7].at[d], {"dp": flip(dp_now, d)}
                )

            def y_copy(self, d):
                return remote(
                    self.all.at[0, self.own_block(d)], self.all.at[2, self.own_block(d)],
                    self.sems[8].at[d], self.sems[9].at[d], near_peer(2),
                )

            def core_copy(self, n):
                return remote(
                    self.all.at[2 * n], self.all.at[2 * n + 1], self.sems[10].at[n],
                    self.sems[11].at[n], near_peer(1),
                )

            def start(self):
                for d in range(1, parts):
                    self.x_copy(d).start()

            def to_z(self):
                for d in range(1, parts):
                    self.x_copy(d).wait()
                for g in list(range(1, groups)) + [0]:
                    c = dp_now * groups + flip(exp_now, g)
                    value = self.mine[c].astype(f32)
                    for d in range(1, parts):
                        value = value + self.far_x[d - 1, flip(exp_now, g)].astype(f32)
                    self.mine[c] = value.astype(bf16)
                for g in range(1, groups):
                    self.z_copy(g).start()

            def to_gather(self):
                for g in range(1, groups):
                    self.z_copy(g).wait()
                value = self.mine[seat].astype(f32)
                for g in range(1, groups):
                    value = value + self.far_z[g - 1].astype(f32)
                self.all[0, seat] = value.astype(bf16)

            def gather(self):
                for g in range(1, groups):
                    self.gz_copy(g).start()

            def to_x(self):
                for g in range(1, groups):
                    self.gz_copy(g).wait_send()
                    self.gz_copy(g, True).wait_recv()
                for d in range(1, parts):
                    self.gx_copy(d).start()
                self.y_copy(0).start()

            def to_y(self):
                for d in range(1, parts):
                    self.gx_copy(d).wait_send()
                    self.gx_copy(d, True).wait_recv()
                    self.y_copy(d).start()
                self.core_copy(0).start()

            def to_core(self):
                for d in range(parts):
                    self.y_copy(d).wait()
                self.core_copy(1).start()

            def done(self):
                for n in range(2):
                    self.core_copy(n).wait()

        wides = [
            Dense(wide_mine.at[n], wide_far_x.at[n], wide_far_z.at[n], wide_all.at[n], wide_sems[n])
            for n in range(2)
        ]
        flat = Dense(flat_mine, flat_far_x, flat_far_z, flat_all, flat_sems)

        def hop_peer(n):
            axis, bit = small_steps[n]
            return {axis: flip(lax.axis_index(axis), bit)}

        def small_copy(n):
            return remote(small_acc.at[n], small_far.at[n], hop_s.at[n], hop_r.at[n], hop_peer(n))

        def tops_copy(n):
            return remote(tops_acc.at[n], tops_far.at[n], top_s.at[n], top_r.at[n], hop_peer(n))

        def gain_copy(n):
            return remote(gain_acc.at[n], gain_far.at[n], gain_s.at[n], gain_r.at[n], hop_peer(n))

        def small_start(n):
            small_copy(n).start()
            tops_copy(n).start()

        def small_sum(n):
            small_copy(n).wait()
            tops_copy(n).wait()
            small_acc[n + 1] = small_acc[n] + small_far[n]
            tops_acc[n + 1] = jnp.maximum(tops_acc[n], tops_far[n])

        small_hops = list(range(hops))

        def small_next():
            if small_hops:
                n = small_hops.pop(0)
                small_sum(n)
                if n + 1 < hops:
                    small_start(n + 1)

        row_tiles = rows // row_tile

        def tile_rows(t, first=0):
            return pl.ds(first + t * row_tile, row_tile)

        def core_part(j, t):
            n = j // 2
            return remote(
                part_send.at[n, tile_rows(t), :], part_core.at[n, tile_rows(t), :],
                near_s.at[n * row_tiles + t], near_r.at[n * row_tiles + t], near_peer(1),
            )

        def y_part(t):
            n = 2 * row_tiles + t
            return remote(
                part_y.at[tile_rows(t), :], y_got.at[tile_rows(t), :], near_s.at[n], near_r.at[n],
                near_peer(2),
            )

        def part(j, t):
            here = pl.ds(j * rows + t * row_tile, row_tile)
            found = None
            for w in range(3):
                add = mm(dqkv[here, w * per_group : (w + 1) * per_group], w_all[w])
                found = add if found is None else found + add
            return found

        for n in range(len(loads)):
            load(n).start()
        small_acc[0] = small_ref[...]
        lanes = lax.broadcasted_iota(jnp.int32, tops_acc.shape[1:], 1)
        tops_acc[0] = jnp.where(
            lanes == me, jnp.max(tops_ref[...], axis=1, keepdims=True), low_start
        )
        flat_rows = out_ref[...].astype(f32)
        for c in range(team):
            flat_mine[c] = flat_rows[c * out_share : (c + 1) * out_share, :].astype(bf16)
        ready()
        flat.start()
        small_start(0)
        load(0).wait()
        load(1).wait()

        def weigh(n, _):
            here = pl.ds(pl.multiple_of(n * rows, rows), rows)
            product[...] += mm(h1_all[here, :], dqkv[here, :], TN)
            return 0

        product[...] = mm(h1_all[0:rows, :], dqkv[0:rows, :], TN)
        lax.fori_loop(1, group_rows // rows, weigh, 0)
        for n in range(2):
            for c in range(team):
                at = (n * team + c) * wide_share
                wide_mine[n, c] = product[at : at + wide_share, :].astype(bf16)
            if n:
                wides[0].start()
        flat.to_z()
        wides[1].start()
        for n in range(2, len(loads)):
            load(n).wait()
        queue = [(j, t) for j in (3, 1) for t in range(row_tiles)]
        for n, (j, t) in enumerate(queue):
            part_send[j // 2, tile_rows(t), :] = part(j, t).astype(bf16)
            if n:
                core_part(*queue[n - 1]).start()
        own_part = [part(2, t) for t in range(1)]
        core_part(*queue[-1]).start()
        for t in range(row_tiles):
            value = own_part[0] if t == 0 else part(2, t)
            core_part(3, t).wait_recv()
            part_y[tile_rows(t), :] = (
                value + part_core[1, tile_rows(t), :].astype(f32)
            ).astype(bf16)
            if t:
                y_part(t - 1).start()
        part_own[tile_rows(0), :] = part(0, 0)
        y_part(row_tiles - 1).start()
        for t in range(1, row_tiles):
            part_own[tile_rows(t), :] = part(0, t)
        wides[0].to_z()
        flat.to_gather()
        small_next()
        wides[1].to_z()
        flat.gather()
        wides[0].to_gather()

        def token_rows(t, _):
            here = pl.ds(pl.multiple_of(t * 128, 128), 128)
            result_out[here, :] = (
                base_all[here, :] + slot_sum(target_ref[here, :], y_near)
            ).astype(bf16)
            return 0

        lax.fori_loop(0, rows // 256, token_rows, 0)
        wides[0].gather()
        small_next()
        flat.to_x()
        wides[1].to_gather()
        lax.fori_loop(rows // 256, rows // 128, token_rows, 0)
        wides[1].gather()
        wides[0].to_x()
        small_next()
        for t in range(row_tiles):
            core_part(1, t).wait()
            core_part(3, t).wait_send()
            y_part(t).wait()

        def input_rows(t, gain_part):
            here = pl.ds(pl.multiple_of(t * row_tile, row_tile), row_tile)
            dh = (
                part_own[here, :] + part_core[0, here, :].astype(f32) + y_got[here, :].astype(f32)
            )
            x_now = x_all[here, :].astype(f32)
            inv = lax.rsqrt(jnp.mean(x_now * x_now, axis=1, keepdims=True) + norm_eps)
            normed = x_now * inv
            dn = dh * gain_ref[...]
            dx1_all[here, :] = dx1_all[here, :] + inv * (
                dn - normed * jnp.mean(dn * normed, axis=1, keepdims=True)
            )
            return gain_part + jnp.sum(dh * normed, axis=0, keepdims=True)

        gain_acc[0] = lax.fori_loop(
            0, rows // row_tile, input_rows, jnp.zeros((1, width), f32)
        )
        store = pltpu.make_async_copy(dx1_all, input_out, load_sem.at[len(loads)])
        store.start()
        flat.to_y()
        gain_copy(0).start()
        wides[1].to_x()
        wides[0].to_y()
        small_next()
        events = [
            flat.to_core, wides[1].to_y, wides[0].to_core, flat.done, wides[1].to_core,
        ]
        for n in range(hops):
            gain_copy(n).wait()
            gain_acc[n + 1] = gain_acc[n] + gain_far[n]
            if events:
                events.pop(0)()
            if n + 1 < hops:
                gain_copy(n + 1).start()
        while small_hops:
            small_next()
        while events:
            events.pop(0)()
        final = [pltpu.make_async_copy(flat_all, flat_out, load_sem.at[len(loads) + 1])]
        for n in range(2):
            wides[n].done()
            final.append(
                pltpu.make_async_copy(
                    wide_all.at[n], wide_out.at[n], load_sem.at[len(loads) + 2 + n]
                )
            )
        for copy in final:
            copy.start()
        small_out[...] = small_acc[hops]
        gain_out[...] = gain_acc[hops, 0, :]
        tops_out[...] = tops_acc[hops]
        store.wait()
        for copy in final:
            copy.wait()

    def dense_scratch(share, across, lead=()):
        return [
            pltpu.VMEM(lead + (team, share, across), bf16),
            pltpu.VMEM(lead + (max(1, parts - 1), groups, share, across), bf16),
            pltpu.VMEM(lead + (max(1, groups - 1), share, across), bf16),
            pltpu.VMEM(lead + (members, team, share, across), bf16),
        ]

    dense_sem = (
        [dma((parts,))] * 2 + [dma((groups,))] * 4 + [dma((parts,))] * 4 + [dma((2,))] * 2
    )
    wide_rows = shape_of((rows, width), f32)
    return run(
        body,
        (),
        [(dqkv_all, anywhere), (h1, anywhere), (x, anywhere), (gain, vector), (dx1, anywhere)]
        + [(weights_t, anywhere), (out_sum, vector), (small, vector), (tops, vector)]
        + [(base, anywhere), (targets, vector)]
        + [(a, anywhere) for a in produced],
        [
            (wide_rows, anywhere),
            (shape_of((2, members, team, wide_share, 3 * per_group), bf16), anywhere),
            (shape_of((members, team, out_share, width), bf16), anywhere),
            (shape_of((small_rows, width), f32), vector),
            (shape_of((width,), f32), vector),
            (shape_of((tops.shape[0], 128), f32), vector),
            (shape_of((rows, width), bf16), vector),
        ],
        scratch=[
            pltpu.VMEM((group_rows, 3 * per_group), bf16),
            pltpu.VMEM((width, 3 * per_group), f32),
            pltpu.VMEM((group_rows, width), bf16),
            pltpu.VMEM((rows, width), bf16),
            pltpu.VMEM((rows, width), f32),
            pltpu.VMEM((3, per_group, width), bf16),
            pltpu.VMEM((rows, width), f32),
            pltpu.VMEM((places, CAP, width), bf16),
            pltpu.VMEM((2, rows, width), bf16),
            pltpu.VMEM((2, rows, width), bf16),
            pltpu.VMEM((rows, width), bf16),
            pltpu.VMEM((rows, width), bf16),
            pltpu.VMEM((rows, width), f32),
        ]
        + dense_scratch(wide_share, 3 * per_group, (2,))
        + dense_scratch(out_share, width)
        + [pltpu.VMEM((hops + 1, small_rows, width), f32), pltpu.VMEM((hops, small_rows, width), f32)]
        + [pltpu.VMEM((hops + 1, 1, width), f32), pltpu.VMEM((hops, 1, width), f32)]
        + [pltpu.VMEM((hops + 1, tops.shape[0], 128), f32), pltpu.VMEM((hops, tops.shape[0], 128), f32)]
        + [dma((12 + places,))] + [dma((3 * (rows // row_tile),))] * 2
        + dense_sem * 3
        + [dma((hops,))] * 6,
        flops=4 * 2 * rows * width * width * 3,
        moved=20 * 1024 * 1024,
        talks=3,
    )


def place_experts(meta, near, turned):
    _, half, columns = near[0][0][0].shape
    members = len(near[0])
    local = members // 2
    count = len(near)
    tile = 128
    tiles = half // tile

    def body(meta_ref, *refs):
        outs = refs[count * members :]
        step = pl.program_id(0) * 2 + pl.program_id(1)
        for j in range(members):

            @pl.when(step == j)
            def _():
                for n in range(count):
                    piece = refs[n * members + j][0].astype(f32)
                    outs[n][0] = jnp.transpose(piece) if turned[n] else piece

    def in_spec(which, j):
        def index(n, c, t, m):
            step = n * 2 + c
            return (which, jnp.where(step == j, t, jnp.where(step < j, 0, tiles - 1)), 0)

        return pl.BlockSpec((1, tile, columns), index)

    outputs = []
    for flag in turned:
        if flag:
            outputs.append(
                (
                    shape_of((local, columns, 2 * half), f32),
                    pl.BlockSpec(
                        (1, columns, tile),
                        lambda n, c, t, m: (m[3] ^ n, 0, (m[2] ^ c) * tiles + t),
                    ),
                )
            )
        else:
            outputs.append(
                (
                    shape_of((local, 2 * half, columns), f32),
                    pl.BlockSpec(
                        (1, tile, columns),
                        lambda n, c, t, m: (m[3] ^ n, (m[2] ^ c) * tiles + t, 0),
                    ),
                )
            )
    return run(
        body,
        (local, 2, tiles),
        [(a, in_spec(which, j)) for listed in near for j, (a, which) in enumerate(listed)],
        outputs,
        meta=meta,
        moved=count * local * 2 * half * columns * 6,
    )


def place_dense(meta, near, flat, tops, small, w_qkv, kinds):
    _, members, team, share, lanes = near.shape
    per_group = lanes // 3
    half = team * share
    width = 2 * half
    rows_all = flat.shape[1] * flat.shape[2]
    step = 8 // math.gcd(share, 8)
    while team // step > 4:
        step *= 2
    per_half = team // step
    tall = step * share

    heads = HEADS // members
    head_width = width // HEADS
    expert_all = (small.shape[0] - 1 - 3 * kinds) // 2
    at_vec = expert_all + 1
    at_logit = at_vec + kinds
    at_carry = at_logit + 2 * kinds

    def body(meta_ref, near_ref, flat_ref, tops_ref, small_ref, w_ref, *outs):
        out_ref, flat_out, clip_ref, router_out, norm_out, vec_out, logit_out, carry_out = outs[:8]
        scale_ref = outs[8]

        @pl.when((pl.program_id(0) == 0) & (pl.program_id(1) == 0))
        def _():
            lanes = lax.broadcasted_iota(jnp.int32, (1, width), 1)
            scale = jnp.zeros((1, width), f32)
            for n in range(HEADS):
                top = tops_ref[n % heads : n % heads + 1, n // heads : n // heads + 1]
                ratio = jnp.sqrt(jnp.minimum(1.0, clip_limit / top))
                inside = (lanes >= n * head_width) & (lanes < (n + 1) * head_width)
                scale = jnp.where(inside, ratio, scale)
            scale_ref[...] = scale
            router_out[...] = small_ref[0:expert_all, :]
            norm_out[...] = small_ref[expert_all, :]
            vec_out[...] = small_ref[at_vec : at_vec + kinds, :]
            for n in range(kinds):
                logit_out[n] = small_ref[at_logit + 2 * n : at_logit + 2 * n + 2, :]
            carry_out[...] = small_ref[at_carry:, 0:expert_all]

        for c in range(step):
            pieces = [near_ref[0, meta_ref[0] ^ g, c] for g in range(members)]
            for w in range(3):
                at = slice(w * per_group, (w + 1) * per_group)
                out_ref[w, c * share : (c + 1) * share, :] = jnp.concatenate(
                    [piece[:, at] for piece in pieces], axis=1
                ).astype(f32)
        clip_ref[...] = w_ref[...].astype(f32) * scale_ref[...]

        @pl.when(pl.program_id(1) == 0)
        def _():
            for c in range(team):
                at = slice(c * flat.shape[2], (c + 1) * flat.shape[2])
                for j in range(2):
                    member = pl.program_id(0) * 2 + j
                    flat_out[j, at, :] = flat_ref[meta_ref[0] ^ member, c].astype(f32)

    square = shape_of((3, width, width), f32)
    return run(
        body,
        (2, per_half),
        [
            (
                near,
                pl.BlockSpec((1, members, step, share, lanes), lambda n, c, m: (n, 0, c, 0, 0)),
            ),
            (flat, whole(flat)),
            (tops, whole(tops)),
            (small, whole(small)),
            (w_qkv, pl.BlockSpec((2, tall, width), lambda n, c, m: (0, n * per_half + c, 0))),
        ],
        [
            (square, pl.BlockSpec((3, tall, width), lambda n, c, m: (0, n * per_half + c, 0))),
            (
                shape_of((members, rows_all, width), f32),
                pl.BlockSpec((2, rows_all, width), lambda n, c, m: (n, 0, 0)),
            ),
            (
                shape_of((2, width, width), f32),
                pl.BlockSpec((2, tall, width), lambda n, c, m: (0, n * per_half + c, 0)),
            ),
        ]
        + [
            (o, whole(o))
            for o in (
                shape_of((expert_all, width), f32),
                shape_of((width,), f32),
                shape_of((kinds, width), f32),
                shape_of((kinds, 2, width), f32),
                shape_of((expert_all, expert_all), f32),
            )
        ],
        scratch=[pltpu.VMEM((1, width), f32)],
        meta=meta,
        moved=square.size * 12,
    )


def shards(
    inputs,
    lengths,
    block_order,
    routes,
    prev_logits,
    norm1_gain,
    norm2_gain,
    w_qkv,
    w_out,
    w_router,
    w_carry,
    const_logit_w,
    const_vec,
    w_gate,
    w_up,
    w_down,
    cotangent,
):
    members = lax.axis_size("ctx")
    groups = lax.axis_size("exp")
    parts = lax.axis_size("dp")
    me = lax.axis_index("ctx")
    mine = lax.axis_index("exp")
    x, grad = inputs[0], cotangent[0]
    rows, width = x.shape
    group_rows = rows * members
    deal_block = group_rows // block_order.shape[1]
    per_member = rows // deal_block
    local = w_gate.shape[0]
    expert_count = local * groups
    head_width = width // HEADS
    heads = HEADS // members
    per_group = heads * head_width
    blocks = block_order.shape[1]
    layout = {
        "order": 4, "lengths": 4 + blocks, "sequences": lengths.shape[1],
        "inverse": 4 + blocks + lengths.shape[1],
    }
    numbers = jnp.arange(blocks, dtype=jnp.int32)
    given = jnp.sum(jnp.where(block_order[0][None, :] == numbers[:, None], numbers[None, :], 0), axis=1)
    inverse = (((given // per_member) ^ me) * per_member + given % per_member).astype(jnp.int32)
    meta = jnp.concatenate(
        [
            jnp.stack([me, mine, me % 2, me // 2]).astype(jnp.int32),
            block_order[0],
            lengths[0],
            inverse,
        ]
    )
    gain1, gain2 = norm1_gain, norm2_gain
    w_out_parts = w_out.reshape(members, per_group, width)
    previous_t = jnp.transpose(prev_logits[0])
    router_t = jnp.transpose(w_router)
    odd = [r for r in range(groups * local) if r % local]

    begun = begin(x, grad, jnp.transpose(routes[0]), gain1, w_qkv, local)
    q, k, v, kt, vt, h1, weights_t, targets, target_rows, route_ids, grad_near = begun[:11]
    grad_rest = begun[11:]
    weights_t = weights_t.reshape(3, members, per_group, width)
    grad_late = [slot_swap(grad_rest[n], r, local) for n, r in enumerate(odd)]
    o, ot, lse, tops = attend(meta, q, k, vt, deal_block, layout)
    logit_rows = jnp.swapaxes(const_logit_w, 1, 2).reshape(-1, width)
    x1, h2, prob, token_near, gate_near, base, dh_zero, dgate_zero, zero_sums = token_front(
        x, o, w_out_parts, gain2, router_t, previous_t, w_carry, target_rows, grad, route_ids,
        logit_rows, const_vec, local,
    )
    worked = expert_layer(token_near, grad_near, grad_late, gate_near, w_gate, w_up, w_down)
    produced = worked[:groups]
    token_back_rows, dots, expert_sum, beside = worked[groups:]
    dx1, small, da_near = token_back(
        x1, h2, grad, prob, previous_t, route_ids, targets, token_back_rows, dots, dgate_zero,
        dh_zero, gain2, router_t, zero_sums,
    )
    expert_now, da_near = lax.optimization_barrier((expert_sum, da_near))
    over = swap(expert_now, "ctx", 2)
    y_near = [swap(produced[g], "exp", g) if g else produced[0] for g in range(groups)]
    dqkv, out_sum = attend_back(
        meta, q, k, v, kt, da_near, w_out_parts, ot, lse, deal_block, layout
    )

    input_grad, qkv_near, out_near, small, norm1_grad, top_all, result = finish(
        dqkv, h1, x, gain1, dx1, weights_t, out_sum, small, tops, y_near, base, targets
    )
    over, qkv_near = lax.optimization_barrier((over, qkv_near))
    corner = swap(over, "ctx", 1)
    near = [[(a, n) for a in (expert_sum, beside, over, corner)] for n in range(3)]
    dense = place_dense(meta, qkv_near, out_near, top_all, small, w_qkv, const_vec.shape[0])
    qkv_grad, out_grad, clipped, router_grad, norm2_grad, vec_grad, logit_grad, carry_grad = dense
    router_grad, logit_grad = jnp.transpose(router_grad), jnp.swapaxes(logit_grad, 1, 2)
    out_grad = out_grad.reshape(width, width)
    gate_grad, up_grad, down_grad = place_experts(meta, near, (False, False, True))
    return (
        result[None],
        input_grad[None],
        norm1_grad,
        norm2_grad,
        qkv_grad,
        out_grad,
        router_grad,
        carry_grad,
        logit_grad,
        vec_grad,
        gate_grad,
        up_grad,
        down_grad,
        clipped,
    )


def solution(mesh):
    tokens = P(("dp", "exp"), "ctx", None)
    packs = P(("dp", "exp"), None)
    experts = P("exp", None, None)
    in_specs = (
        tokens, packs, packs, tokens, tokens, P(), P(), P(), P(), P(), P(), P(), P(),
        experts, experts, experts, tokens,
    )
    out_specs = (
        tokens, tokens, P(), P(), P(), P(), P(), P(), P(), P(),
        P("exp", None, "dp"), P("exp", None, "dp"), P("exp", "dp", None), P(),
    )
    return jax.shard_map(shards, mesh=mesh, in_specs=in_specs, out_specs=out_specs, check_vma=False)
```

```python
import math

import jax
import jax.numpy as jnp
from jax import lax
from jax.experimental import pallas as pl
from jax.experimental.pallas import tpu as pltpu
from jax.sharding import PartitionSpec as P

HEADS = 12
CAP = 128

norm_eps = 1e-05
clip_limit = 3.0
low_start = -1e30
mask_fill = -3e38
highest = lax.Precision.HIGHEST
NN = (((1,), (0,)), ((), ()))
NT = (((1,), (1,)), ((), ()))
TN = (((0,), (0,)), ((), ()))
f32 = jnp.float32
bf16 = jnp.bfloat16
MESH = pl.DeviceIdType.MESH


def mm(left, right, dims=NN):
    return lax.dot_general(left, right, dims, preferred_element_type=f32)


def mm_full(left, right, dims=NN):
    return lax.dot_general(left, right, dims, precision=highest, preferred_element_type=f32)


def shape_of(shape, dtype):
    return jax.ShapeDtypeStruct(shape, dtype)


def whole(array):
    rank = len(array.shape)
    return pl.BlockSpec(array.shape, lambda *_: (0,) * rank)


def cost(flops, moved, exps=0):
    return pl.CostEstimate(flops=int(flops), bytes_accessed=int(moved), transcendentals=int(exps))


def run(body, grid, inputs, outputs, scratch=(), meta=None, flops=0, moved=0, exps=0, aliases=None, talks=None):
    prefetch = 0 if meta is None else 1
    args = ([] if meta is None else [meta]) + [a for a, _ in inputs]
    return pl.pallas_call(
        body,
        out_shape=[o for o, _ in outputs],
        grid_spec=pltpu.PrefetchScalarGridSpec(
            num_scalar_prefetch=prefetch,
            grid=grid,
            in_specs=[s for _, s in inputs],
            out_specs=[s for _, s in outputs],
            scratch_shapes=list(scratch),
        ),
        compiler_params=pltpu.CompilerParams(
            dimension_semantics=("arbitrary",) * len(grid),
            vmem_limit_bytes=63 * 1024 * 1024,
            collective_id=talks,
            has_side_effects=talks is not None,
        ),
        cost_estimate=cost(flops, moved, exps),
        input_output_aliases={} if aliases is None else aliases,
    )(*args)


def swap(value, axis, distance):
    count = lax.axis_size(axis)
    return lax.ppermute(value, axis, [(i, i ^ distance) for i in range(count)])


def flip(value, bits):
    bit = 1
    while bit <= bits:
        if bits & bit:
            value = value + bit - 2 * bit * lax.rem(lax.div(value, bit), 2)
        bit *= 2
    return value


def powers(axis):
    found, bit = [], 1
    while bit < lax.axis_size(axis):
        found.append(bit)
        bit *= 2
    return found


def slot_peer(r, count, exp_now, me):
    return {"exp": flip(exp_now, r // count), "ctx": flip(me, 2 * (r % count))}


def slot_swap(value, r, count):
    groups = lax.axis_size("exp")
    total = groups * lax.axis_size("ctx")
    apart = 2 * (r % count) * groups + r // count
    return lax.ppermute(value, ("ctx", "exp"), [(i, i ^ apart) for i in range(total)])


def remote(src, dst, sent, arrived, peer):
    return pltpu.make_async_remote_copy(
        src_ref=src, dst_ref=dst, send_sem=sent, recv_sem=arrived,
        device_id=peer, device_id_type=MESH,
    )


def greet(peers):
    barrier = pltpu.get_barrier_semaphore()
    for peer in peers:
        pl.semaphore_signal(barrier, inc=1, device_id=peer, device_id_type=MESH)
    return lambda: pl.semaphore_wait(barrier, len(peers))


anywhere = pl.BlockSpec(memory_space=pl.ANY)
scalars = pl.BlockSpec(memory_space=pltpu.SMEM)
vector = pl.BlockSpec(memory_space=pltpu.VMEM)
dma = pltpu.SemaphoreType.DMA


def add_low(*terms):
    total = terms[0].astype(f32)
    for term in terms[1:]:
        total = total + term.astype(f32)
    return total.astype(bf16)


def begin(x, grad, routes, gain, w_qkv, local):
    rows, width = x.shape
    members, groups = lax.axis_size("ctx"), lax.axis_size("exp")
    group_rows = rows * members
    heads = HEADS // members
    head_width = width // HEADS
    columns = heads * head_width
    places = groups * local
    odd = [r for r in range(places) if r % local]
    scale = head_width**-0.5
    tile = min(256, rows)
    per_member = rows // tile

    def body(*refs):
        x_hbm, dy_ref, route_ref, gain_ref, w_hbm = refs[:5]
        q_out, k_out, v_out, kt_out, vt_out, h_out, wt_out = refs[5:12]
        target_out, target_rows, chosen_out, near_out = refs[12:16]
        rest_out, refs = refs[16 : 16 + len(odd)], refs[:16] + refs[16 + len(odd) :]
        x_near, w_in, w_t, q_all, k_all, v_all, kt_all, vt_all, h_all, packed, near = refs[16:27]
        load_sem, x_s, x_r, r_s, r_r, out_sem, near_sem = refs[27:]
        me, exp_now = lax.axis_index("ctx"), lax.axis_index("exp")
        side = lax.div(me, 2)
        peers = [{"ctx": flip(me, 1)}, {"ctx": flip(me, 2)}]
        peers += [slot_peer(local * g, local, exp_now, me) for g in range(1, groups)]
        ready = greet(peers)
        own = pltpu.make_async_copy(x_hbm, x_near.at[0], load_sem.at[0])
        weights = pltpu.make_async_copy(w_hbm, w_in, load_sem.at[1])
        own.start()
        weights.start()

        def some(t):
            return pl.ds(pl.multiple_of(t * tile, tile), tile)

        def across(t):
            n = 2 + t
            return remote(
                x_hbm.at[some(t), :], x_near.at[2, some(t), :], x_s.at[n], x_r.at[n],
                {"ctx": flip(me, 2)},
            )

        def beside():
            return remote(x_hbm, x_near.at[1], x_s.at[1], x_r.at[1], {"ctx": flip(me, 1)})

        def passed(t):
            n = 2 + per_member + t
            return remote(
                x_near.at[2, some(t), :], x_near.at[3, some(t), :], x_s.at[n], x_r.at[n],
                {"ctx": flip(me, 1)},
            )

        def row_copy(g):
            return remote(
                packed.at[g], near.at[g], r_s.at[g], r_r.at[g],
                slot_peer(local * g, local, exp_now, me),
            )

        ready()
        for t in range(per_member):
            across(t).start()
        beside().start()

        lines = jnp.concatenate([route_ref[...].astype(f32), jnp.zeros((6, rows), f32)], axis=0)
        chosen = jnp.transpose(lines)[:, 0:2].astype(jnp.int32)
        chosen_out[...] = chosen
        expert_count = places
        lanes = lax.broadcasted_iota(jnp.int32, (rows, 128), 1)
        hits = [lanes == chosen[:, c : c + 1] for c in range(2)]
        hit = jnp.where((hits[0] | hits[1]) & (lanes < expert_count), 1.0, 0.0)
        later = lax.broadcasted_iota(jnp.int32, (rows, rows), 0)
        sooner = lax.broadcasted_iota(jnp.int32, (rows, rows), 1)
        ahead = mm(jnp.where(sooner < later, 1.0, 0.0).astype(bf16), hit.astype(bf16))
        spots = []
        for c in range(2):
            ids = chosen[:, c : c + 1]
            rank = jnp.sum(jnp.where(hits[c], ahead, 0.0), axis=1, keepdims=True).astype(jnp.int32)
            far_z = lax.div(ids, local)
            far_y = lax.rem(ids, local)
            z = jnp.zeros_like(ids)
            bit = 1
            while bit < groups:
                z = z + bit * jnp.where(
                    lax.rem(lax.div(far_z, bit), 2) == lax.rem(lax.div(exp_now, bit), 2), 0, 1
                )
                bit *= 2
            y = jnp.where(far_y == side, 0, 1)
            spots.append(jnp.where(ids < expert_count, (z * local + y) * CAP + rank, -1))
        target_out[...] = jnp.concatenate(spots, axis=1)
        wide = jnp.where(lanes == 0, spots[0], spots[1]).astype(f32)
        target_rows[...] = jnp.transpose(wide)[0:2, :].astype(jnp.int32)

        def pack(n, r):
            packed[n] = mm(slot_choice(r * CAP, CAP, target_rows), dy_ref[...]).astype(bf16)

        for g in range(groups - 1, -1, -1):
            pack(g, local * g)
            if g < groups - 1:
                row_copy(g + 1).start()
        for n, r in enumerate(odd):
            pack(groups + n, r)
        stores = [
            pltpu.make_async_copy(packed.at[0], near_out.at[0], near_sem.at[0]),
        ] + [
            pltpu.make_async_copy(packed.at[groups + n], rest_out[n], near_sem.at[groups + n])
            for n in range(len(odd))
        ]
        for copy in stores:
            copy.start()
        weights.wait()
        for w in range(3):
            w_t[w] = jnp.transpose(w_in[w])
        w_store = pltpu.make_async_copy(w_t, wt_out, load_sem.at[2])
        w_store.start()
        here = pl.ds(pl.multiple_of(me * columns, columns), columns)

        def chunk(j):
            def project(t, _):
                if j == 2:
                    across(t).wait()
                    passed(t).start()
                if j == 3:
                    passed(t).wait()
                at = pl.multiple_of(t * tile, tile)
                to = pl.ds(pl.multiple_of(j * rows + t * tile, tile), tile)
                value = x_near[j, pl.ds(at, tile), :].astype(f32)
                inverse = lax.rsqrt(jnp.mean(value * value, axis=1, keepdims=True) + norm_eps)
                low = (value * inverse * gain_ref[...]).astype(bf16)
                h_all[to, :] = low
                q = mm(low, w_t[0, here, :], NT).astype(bf16) * jnp.asarray(scale, bf16)
                k = mm(low, w_t[1, here, :], NT).astype(bf16)
                v = mm(low, w_t[2, here, :], NT).astype(bf16)
                for h in range(heads):
                    part = slice(h * head_width, (h + 1) * head_width)
                    q_all[h, to, :] = q[:, part]
                    k_all[h, to, :] = k[:, part]
                    v_all[h, to, :] = v[:, part]
                kt_all[:, to] = mm(w_t[1, here, :], low, NT).astype(bf16)
                vt_all[:, to] = mm(w_t[2, here, :], low, NT).astype(bf16)
                return 0

            lax.fori_loop(0, per_member, project, 0)
            for copy in chunk_stores(j):
                copy.start()

        def chunk_stores(j):
            to = pl.ds(j * rows, rows)
            pairs = [(q_all, q_out), (k_all, k_out), (v_all, v_out)]
            found = [(a.at[:, to, :], b.at[:, to, :]) for a, b in pairs]
            found += [(a.at[:, to], b.at[:, to]) for a, b in ((kt_all, kt_out), (vt_all, vt_out))]
            found += [(h_all.at[to, :], h_out.at[to, :])]
            return [
                pltpu.make_async_copy(a, b, out_sem.at[6 * j + n]) for n, (a, b) in enumerate(found)
            ]

        own.wait()
        chunk(0)
        beside().wait()
        chunk(1)
        chunk(2)
        chunk(3)
        for g in range(1, groups):
            row_copy(g).wait()
            pltpu.make_async_copy(near.at[g], near_out.at[g], near_sem.at[g]).start()
        for copy in stores:
            copy.wait()
        w_store.wait()
        for j in range(members):
            for copy in chunk_stores(j):
                copy.wait()
        for g in range(1, groups):
            pltpu.make_async_copy(near.at[g], near_out.at[g], near_sem.at[g]).wait()

    by_head = (heads, group_rows, head_width)
    by_column = (columns, group_rows)
    slots = (places, CAP, width)
    return run(
        body,
        (),
        [(x, anywhere), (grad, vector), (routes, vector), (gain, vector), (w_qkv, anywhere)],
        [(shape_of(by_head, bf16), anywhere)] * 3
        + [(shape_of(by_column, bf16), anywhere)] * 2
        + [(shape_of((group_rows, width), bf16), anywhere)]
        + [(shape_of((3, width, width), bf16), anywhere)]
        + [(shape_of((rows, 2), jnp.int32), vector), (shape_of((2, rows), jnp.int32), vector)]
        + [(shape_of((rows, 2), jnp.int32), vector)]
        + [(shape_of((groups, CAP, width), bf16), anywhere)]
        + [(shape_of((CAP, width), bf16), anywhere)] * len(odd),
        scratch=[
            pltpu.VMEM((members, rows, width), bf16),
            pltpu.VMEM((3, width, width), bf16),
            pltpu.VMEM((3, width, width), bf16),
            pltpu.VMEM(by_head, bf16), pltpu.VMEM(by_head, bf16), pltpu.VMEM(by_head, bf16),
            pltpu.VMEM(by_column, bf16), pltpu.VMEM(by_column, bf16),
            pltpu.VMEM((group_rows, width), bf16),
            pltpu.VMEM(slots, bf16), pltpu.VMEM(slots, bf16),
            dma((3,)), dma((2 + 2 * per_member,)), dma((2 + 2 * per_member,)),
            dma((places,)), dma((places,)), dma((6 * members,)), dma((places + 1,)),
        ],
        flops=2 * group_rows * width * columns * 5,
        moved=20 * 1024 * 1024,
        talks=4,
    )


def document_start(meta_ref, position, layout):
    start = jnp.zeros_like(position)
    end = jnp.int32(0)
    for s in range(layout["sequences"]):
        end = end + meta_ref[layout["lengths"] + s]
        start = jnp.where(position >= end, end, start)
    return start


def block_range(meta_ref, query_block, key_block, rows, layout):
    q_first = query_block * rows
    k_first = key_block * rows
    begin = document_start(meta_ref, q_first, layout)
    begin_last = document_start(meta_ref, q_first + rows - 1, layout)
    needed = (k_first <= q_first) & (k_first + rows - 1 >= begin)
    full = (k_first < q_first) & (k_first >= begin_last)
    return q_first, k_first, needed, full


def allowed_pairs(meta_ref, q_first, k_first, rows, layout):
    q_pos = q_first + lax.broadcasted_iota(jnp.int32, (1, rows), 1)
    k_pos = k_first + lax.broadcasted_iota(jnp.int32, (rows, 1), 0)
    return (k_pos <= q_pos) & (k_pos >= document_start(meta_ref, q_pos, layout))


def attend(meta, q, k, vt, rows, layout):
    heads, group_rows, head_width = q.shape
    blocks = group_rows // rows
    width = heads * head_width

    def body(meta_ref, q_ref, k_ref, vt_ref, o_ref, ot_ref, lse_ref, top_ref, m_ref, l_ref, a_ref, qt_ref):
        i = pl.program_id(0)
        m_ref[...] = jnp.full_like(m_ref, low_start)
        l_ref[...] = jnp.zeros_like(l_ref)
        a_ref[...] = jnp.zeros_like(a_ref)
        for h in range(heads):
            qt_ref[h] = jnp.transpose(q_ref[h])

        def one(j, _):
            q_first, k_first, needed, full = block_range(meta_ref, i, j, rows, layout)
            at = pl.multiple_of(meta_ref[layout["inverse"] + j] * rows, rows)

            def step(masked):
                if masked:
                    allowed = allowed_pairs(meta_ref, q_first, k_first, rows, layout)
                for h in range(heads):
                    part = slice(h * head_width, (h + 1) * head_width)
                    s = mm(k_ref[h, pl.ds(at, rows), :], qt_ref[h])
                    if masked:
                        s = jnp.where(allowed, s, mask_fill)
                    old = m_ref[h]
                    new = jnp.maximum(old, jnp.max(s, axis=0, keepdims=True))
                    shrink = jnp.exp(old - new)
                    p = jnp.exp(s - new)
                    m_ref[h] = new
                    l_ref[h] = l_ref[h] * shrink + jnp.sum(p, axis=0, keepdims=True)
                    a_ref[part, :] = a_ref[part, :] * shrink + mm(
                        vt_ref[part, pl.ds(at, rows)], p.astype(bf16)
                    )

            @pl.when(full)
            def _():
                step(False)

            @pl.when(needed & jnp.logical_not(full))
            def _():
                step(True)

            return 0

        lax.fori_loop(0, i + 1, one, 0)
        for h in range(heads):
            part = slice(h * head_width, (h + 1) * head_width)
            ot_ref[part, :] = a_ref[part, :] / l_ref[h]
            lse_ref[pl.ds(h, 1), :] = m_ref[h] + jnp.log(l_ref[h])
            top = m_ref[h]

            @pl.when(i == 0)
            def _():
                top_ref[pl.ds(h, 1), :] = top

            @pl.when(i > 0)
            def _():
                top_ref[pl.ds(h, 1), :] = jnp.maximum(top_ref[pl.ds(h, 1), :], top)

        o_ref[...] = jnp.transpose(ot_ref[...]).astype(bf16)

    row = shape_of((heads, group_rows), f32)
    row_spec = pl.BlockSpec((heads, rows), lambda i, m: (0, i))
    return run(
        body,
        (blocks,),
        [
            (
                q,
                pl.BlockSpec(
                    (heads, rows, head_width), lambda i, m: (0, m[layout["inverse"] + i], 0)
                ),
            ),
            (k, whole(k)),
            (vt, whole(vt)),
        ],
        [
            (
                shape_of((group_rows, width), bf16),
                pl.BlockSpec((rows, width), lambda i, m: (m[layout["inverse"] + i], 0)),
            ),
            (shape_of((width, group_rows), f32), pl.BlockSpec((width, rows), lambda i, m: (0, i))),
            (row, row_spec),
            (shape_of((heads, rows), f32), pl.BlockSpec((heads, rows), lambda i, m: (0, 0))),
        ],
        scratch=[
            pltpu.VMEM((heads, 1, rows), f32),
            pltpu.VMEM((heads, 1, rows), f32),
            pltpu.VMEM((width, rows), f32),
            pltpu.VMEM((heads, head_width, rows), bf16),
        ],
        meta=meta,
        flops=2 * 2 * group_rows * group_rows * width,
        moved=group_rows * width * 14,
        exps=group_rows * group_rows * heads // 2,
    )


def attend_back(meta, q, k, v, kt, grad, w_out, ot, lse, rows, layout):
    heads, group_rows, head_width = q.shape
    blocks = group_rows // rows
    width = heads * head_width
    scale = head_width**-0.5
    per = grad.shape[1] // rows

    def body(meta_ref, q_ref, k_ref, v_ref, kt_ref, grad_ref, w_ref, *refs):
        ot_ref, lse_ref, out_ref, rows_ref, dk_ref, dv_ref, dq_ref, g_ref, delta_ref, sum_ref, qt_ref, gt_ref = refs
        i = pl.program_id(0)

        @pl.when(i == 0)
        def _():
            dk_ref[...] = jnp.zeros_like(dk_ref)
            dv_ref[...] = jnp.zeros_like(dv_ref)

        da = grad_ref[0]
        g = mm(da, w_ref[0], NT).astype(bf16)
        part_sum = mm(ot_ref[...].astype(bf16), da)

        @pl.when(i == 0)
        def _():
            sum_ref[...] = part_sum

        @pl.when(i > 0)
        def _():
            sum_ref[...] += part_sum

        for h in range(heads):
            g_ref[h] = g[:, h * head_width : (h + 1) * head_width]
        turned = jnp.transpose(g.astype(f32))
        gt_ref[...] = turned.astype(bf16)
        for h in range(heads):
            qt_ref[h] = jnp.transpose(q_ref[h])
        product = turned * ot_ref[...]
        for h in range(heads):
            part = slice(h * head_width, (h + 1) * head_width)
            delta_ref[h] = jnp.sum(product[part, :], axis=0, keepdims=True)

        dq_ref[...] = jnp.zeros_like(dq_ref)

        def one(j, _):
            q_first, k_first, needed, full = block_range(meta_ref, i, j, rows, layout)
            at = pl.multiple_of(meta_ref[layout["inverse"] + j] * rows, rows)
            to = pl.multiple_of(j * rows, rows)

            def step(masked):
                if masked:
                    allowed = allowed_pairs(meta_ref, q_first, k_first, rows, layout)
                for h in range(heads):
                    part = slice(h * head_width, (h + 1) * head_width)
                    s = mm(k_ref[h, pl.ds(at, rows), :], qt_ref[h])
                    if masked:
                        s = jnp.where(allowed, s, mask_fill)
                    p = jnp.exp(s - lse_ref[pl.ds(h, 1), :])
                    dp = mm(v_ref[h, pl.ds(at, rows), :], gt_ref[part, :])
                    ds = (p * (dp - delta_ref[h])).astype(bf16)
                    dv_ref[h, pl.ds(to, rows), :] += mm(p.astype(bf16), g_ref[h])
                    dk_ref[h, pl.ds(to, rows), :] += mm(ds, q_ref[h])
                    dq_ref[part, :] += mm(kt_ref[part, pl.ds(at, rows)], ds)

            @pl.when(full)
            def _():
                step(False)

            @pl.when(needed & jnp.logical_not(full))
            def _():
                step(True)

            return 0

        lax.fori_loop(0, i + 1, one, 0)
        here = pl.multiple_of(meta_ref[layout["inverse"] + i] * rows, rows)
        out_ref[pl.ds(here, rows), 0:width] = (jnp.transpose(dq_ref[...]) * scale).astype(bf16)

        @pl.when(i == blocks - 1)
        def _():
            rows_ref[...] = sum_ref[...].astype(bf16)

            def store(b, _):
                spot = pl.multiple_of(b * rows, rows)
                there = pl.multiple_of(meta_ref[layout["inverse"] + b] * rows, rows)
                out_ref[pl.ds(there, rows), width : 3 * width] = jnp.concatenate(
                    [dk_ref[h, pl.ds(spot, rows), :] for h in range(heads)]
                    + [dv_ref[h, pl.ds(spot, rows), :] for h in range(heads)],
                    axis=1,
                ).astype(bf16)
                return 0

            lax.fori_loop(0, blocks, store, 0)

    out = shape_of((group_rows, 3 * width), bf16)
    out_rows = shape_of((width, grad.shape[2]), bf16)
    return run(
        body,
        (blocks,),
        [
            (
                q,
                pl.BlockSpec(
                    (heads, rows, head_width), lambda i, m: (0, m[layout["inverse"] + i], 0)
                ),
            ),
            (k, whole(k)),
            (v, whole(v)),
            (kt, whole(kt)),
        ]
        + [
            (
                grad,
                pl.BlockSpec(
                    (1, rows, grad.shape[2]),
                    lambda i, m: (
                        m[layout["inverse"] + i] // per, m[layout["inverse"] + i] % per, 0
                    ),
                ),
            ),
            (w_out, pl.BlockSpec((1, width, grad.shape[2]), lambda i, m: (m[0], 0, 0))),
            (ot, pl.BlockSpec((width, rows), lambda i, m: (0, i))),
            (lse, pl.BlockSpec((heads, rows), lambda i, m: (0, i))),
        ],
        [(out, whole(out)), (out_rows, whole(out_rows))],
        scratch=[
            pltpu.VMEM((heads, group_rows, head_width), f32),
            pltpu.VMEM((heads, group_rows, head_width), f32),
            pltpu.VMEM((width, rows), f32),
            pltpu.VMEM((heads, rows, head_width), bf16),
            pltpu.VMEM((heads, 1, rows), f32),
            pltpu.VMEM((width, grad.shape[2]), f32),
            pltpu.VMEM((heads, head_width, rows), bf16),
            pltpu.VMEM((width, rows), bf16),
        ],
        meta=meta,
        flops=5 * 2 * group_rows * group_rows * width,
        moved=group_rows * width * 24,
        exps=group_rows * group_rows * heads // 2,
    )


def slot_choice(first, count, target_ref):
    rows = target_ref.shape[1]
    ids = first + lax.broadcasted_iota(jnp.int32, (count, rows), 0)
    match = (ids == target_ref[0:1, :]) | (ids == target_ref[1:2, :])
    return jnp.where(match, 1.0, 0.0).astype(bf16)


def token_front(
    x, o, w_out, gain, router_t, previous_t, w_carry, target_rows, grad, routes, logit_w, vectors, local
):
    rows, width = x.shape
    members, columns = w_out.shape[0], w_out.shape[1]
    expert_all = router_t.shape[0]
    groups = lax.axis_size("exp")
    places = groups * local
    expert_count = places
    kinds = vectors.shape[0]
    tile = 128

    def body(*refs):
        (x_ref, o_hbm, w_ref, gain_ref, router_ref, prev_ref, carry_ref, target_ref) = refs[:8]
        dy_ref, route_ref, lw_ref, vec_ref = refs[8:12]
        x1_ref, h2_ref, prob_ref, rows_out, gates_out, base_ref, dh_ref, dgate_ref, sums_ref = refs[12:21]
        o_near, low, split, packed, arrived, gate_mine, gate_near = refs[21:28]
        o_s, o_r, t_s, t_r, g_s, g_r, out_sem = refs[28:]
        me, exp_now = lax.axis_index("ctx"), lax.axis_index("exp")
        side = lax.div(me, 2)
        peers = [{"ctx": flip(me, j)} for j in range(1, members)]
        peers += [slot_peer(r, local, exp_now, me) for r in range(local, places)]
        ready = greet(peers)

        own_o = pltpu.make_async_copy(o_hbm.at[pl.ds(0, rows), :], o_near.at[0], o_r.at[0])

        def o_copy(j, t):
            src = o_hbm.at[pl.ds(pl.multiple_of(j * rows + t * tile, tile), tile), :]
            dst = o_near.at[j, pl.ds(pl.multiple_of(t * tile, tile), tile), :]
            n = j * (rows // tile) + t
            return remote(src, dst, o_s.at[n], o_r.at[n], {"ctx": flip(me, j)})

        def row_copy(r):
            return remote(
                packed.at[r], arrived.at[r], t_s.at[r], t_r.at[r], slot_peer(r, local, exp_now, me)
            )

        def gate_copy(r):
            return remote(
                gate_mine.at[r], gate_near.at[r], g_s.at[r], g_r.at[r],
                slot_peer(r, local, exp_now, me),
            )

        own_o.start()
        ready()
        for t in range(rows // tile):
            for j in range(members - 1, 0, -1):
                o_copy(j, t).start()
        own_o.wait()

        def front_rows(t, _):
            here = pl.ds(pl.multiple_of(t * tile, tile), tile)
            total = x_ref[here, :].astype(f32) + mm(o_near[0, here, :], w_ref[me])
            for j in range(1, members):
                o_copy(j, t).wait()
            for j in range(1, members):
                total = total + mm(o_near[j, here, :], w_ref[flip(me, j)])
            x1_ref[here, :] = total
            inverse = lax.rsqrt(jnp.mean(total * total, axis=1, keepdims=True) + norm_eps)
            h2 = total * inverse * gain_ref[...]
            h2_ref[here, :] = h2
            logits = mm_full(h2, router_ref[...], NT) + mm_full(
                prev_ref[:, here], carry_ref[...], TN
            )
            shifted = jnp.exp(logits - jnp.max(logits, axis=1, keepdims=True))
            prob = shifted / jnp.sum(shifted, axis=1, keepdims=True)
            prob_ref[here, :] = prob
            low[here, :] = h2.astype(bf16)
            top = prob.astype(bf16)
            rest = prob - top.astype(f32)
            middle = rest.astype(bf16)
            split[0, here, :] = top
            split[1, here, :] = middle
            split[2, here, :] = (rest - middle.astype(f32)).astype(bf16)
            return 0

        lax.fori_loop(0, rows // tile, front_rows, 0)
        diagonal = lax.broadcasted_iota(jnp.int32, (CAP, CAP), 0) == lax.broadcasted_iota(
            jnp.int32, (CAP, CAP), 1
        )
        lanes = lax.broadcasted_iota(jnp.int32, (CAP, expert_all), 1)
        for r in list(range(1, places)) + [0]:
            choice = slot_choice(r * CAP, CAP, target_ref)
            packed[r] = mm(choice, low[...]).astype(bf16)
            picked = mm(choice, split[0]) + mm(choice, split[1]) + mm(choice, split[2])
            expert = flip(exp_now, r // local) * local + flip(side, r % local)
            column = jnp.sum(jnp.where(lanes == expert, picked, 0.0), axis=1, keepdims=True)
            gate_mine[r] = jnp.sum(jnp.where(diagonal, column, 0.0), axis=0, keepdims=True)
            last = r - 1 if r else places - 1
            if last:
                row_copy(last).start()
                gate_copy(last).start()

        def own_copy(n):
            src, dst = (packed, rows_out) if n == 0 else (gate_mine, gates_out)
            return pltpu.make_async_copy(src.at[0], dst.at[0], out_sem.at[n])

        own_copy(0).start()
        own_copy(1).start()

        def zero_rows(t, _):
            here = pl.ds(pl.multiple_of(t * tile, tile), tile)
            h2 = h2_ref[here, :]
            dy = dy_ref[here, :].astype(f32)
            prob_now = prob_ref[here, :]
            classes = lax.broadcasted_iota(jnp.int32, (tile, expert_all), 1)
            chosen = route_ref[here, :]
            ids = [chosen[:, c : c + 1] for c in range(2)]
            gates = [
                jnp.sum(jnp.where(classes == r, prob_now, 0.0), axis=1, keepdims=True) for r in ids
            ]
            along = jnp.sum(dy * h2, axis=1, keepdims=True)
            copies = [(r == expert_count + 1).astype(f32) for r in ids]
            keep = copies[0] * gates[0] + copies[1] * gates[1]
            dgates = [copies[c] * along for c in range(2)]
            scores = [
                jnp.sum(h2 * lw_ref[n : n + 1, :], axis=1, keepdims=True) for n in range(2 * kinds)
            ]
            base = x1_ref[here, :]
            dh = jnp.zeros_like(h2)
            for j in range(kinds):
                top = jnp.maximum(scores[2 * j], scores[2 * j + 1])
                e0 = jnp.exp(scores[2 * j] - top)
                e1 = jnp.exp(scores[2 * j + 1] - top)
                a0 = e0 / (e0 + e1)
                a1 = e1 / (e0 + e1)
                vec = vec_ref[j : j + 1, :]
                along_vec = jnp.sum(dy * vec, axis=1, keepdims=True)
                these = [(r == expert_count + 2 + j).astype(f32) for r in ids]
                weight = these[0] * gates[0] + these[1] * gates[1]
                for c in range(2):
                    dgates[c] = dgates[c] + these[c] * (a0 * along + a1 * along_vec)
                keep = keep + weight * a0
                base = base + (weight * a1) * vec
                d0 = weight * along
                d1 = weight * along_vec
                mean = a0 * d0 + a1 * d1
                z0 = a0 * (d0 - mean)
                z1 = a1 * (d1 - mean)
                dh = dh + z0 * lw_ref[2 * j : 2 * j + 1, :] + z1 * lw_ref[2 * j + 1 : 2 * j + 2, :]
                sums_ref[j : j + 1, :] += jnp.sum((weight * a1) * dy, axis=0, keepdims=True)
                at = kinds + 2 * j
                sums_ref[at : at + 1, :] += jnp.sum(z0 * h2, axis=0, keepdims=True)
                sums_ref[at + 1 : at + 2, :] += jnp.sum(z1 * h2, axis=0, keepdims=True)
            base_ref[here, :] = base + keep * h2
            dh_ref[here, :] = dh + keep * dy
            dgate_ref[here, :] = jnp.concatenate(dgates, axis=1)
            return 0

        sums_ref[...] = jnp.zeros_like(sums_ref)
        lax.fori_loop(0, rows // tile, zero_rows, 0)

        def rows_store(r):
            return pltpu.make_async_copy(arrived.at[r], rows_out.at[r], out_sem.at[2 * r])

        def gates_store(r):
            return pltpu.make_async_copy(gate_near.at[r], gates_out.at[r], out_sem.at[2 * r + 1])

        for r in range(1, places):
            row_copy(r).wait()
            gate_copy(r).wait()
            rows_store(r).start()
            gates_store(r).start()
        own_copy(0).wait()
        own_copy(1).wait()
        for r in range(1, places):
            rows_store(r).wait()
            gates_store(r).wait()

    wide = shape_of((rows, width), f32)
    placed = shape_of((places, CAP, width), bf16)
    lines = shape_of((places, 1, CAP), f32)
    return run(
        body,
        (),
        [(x, vector), (o, anywhere), (w_out, vector), (gain, vector), (router_t, vector)]
        + [(previous_t, vector), (w_carry, vector), (target_rows, vector), (grad, vector)]
        + [(routes, vector), (logit_w, vector), (vectors, vector)],
        [(wide, vector), (wide, vector), (shape_of((rows, expert_all), f32), vector)]
        + [(placed, anywhere), (lines, anywhere), (wide, vector), (wide, vector)]
        + [(shape_of((rows, 2), f32), vector), (shape_of((3 * kinds, width), f32), vector)],
        scratch=[
            pltpu.VMEM((members, rows, columns), bf16),
            pltpu.VMEM((rows, width), bf16),
            pltpu.VMEM((3, rows, expert_all), bf16),
            pltpu.VMEM((places, CAP, width), bf16),
            pltpu.VMEM((places, CAP, width), bf16),
            pltpu.VMEM((places, 1, CAP), f32),
            pltpu.VMEM((places, 1, CAP), f32),
            dma((members * (rows // tile),)), dma((members * (rows // tile),)),
            dma((places,)), dma((places,)), dma((places,)), dma((places,)),
            dma((2 * places,)),
        ],
        flops=2 * rows * width * (width + places * CAP),
        moved=rows * width * 30,
        talks=1,
    )


def expert_layer(arrived, grads, late, gates, w_gate, w_up, w_down):
    places = arrived.shape[0]
    local = w_gate.shape[0]
    rows = places * CAP
    width, hidden = w_gate.shape[1], w_gate.shape[2]
    parts = lax.axis_size("dp")
    groups = places // local
    half = width // 2
    per_part = hidden // parts
    tile = min(256, per_part)
    steps = hidden // tile
    tiles = per_part // tile
    away = steps - tiles
    lead = away // 2
    kept = steps - lead
    chunk = 256

    def body(*refs):
        x_ref, dy_ref, gates_ref, wg_hbm, wu_hbm, wd_hbm = refs[:6]
        dy_late, refs = refs[6 : 6 + len(late)], refs[:6] + refs[6 + len(late) :]
        dy_parts = [
            dy_late[r // local] if r % local else dy_ref.at[r // local] for r in range(places)
        ]
        y_out, refs = refs[6 : 6 + groups], refs[6 + groups :]
        it = iter(refs)

        def take(count):
            return [next(it) for _ in range(count)]

        dx_out, dots_out, sum_out, beside_out = take(4)
        x_all, xt_all, dy_all, dyt_all, gate_all, y_acc, dx_acc, dot_acc = take(8)
        wg_buf, wu_buf, wd_buf, wg_keep, wu_keep, wd_keep = take(6)
        hid_keep, dg_keep, du_keep, scaled_keep = take(4)
        send, total, taken, far, dx_low, dx_near, dots, dots_near = take(8)
        beside, y_odd, relay = take(3)
        in_sem, w_sem, keep_sem, c_s, c_r, f_s, f_r, b_s, b_r, d_s, d_r, out_sem = take(12)
        e_s, e_r, beside_sem, y_s, y_r, dx_sem = take(6)
        me, exp_now, dp_now = lax.axis_index("ctx"), lax.axis_index("exp"), lax.axis_index("dp")
        core, side = lax.rem(me, 2), lax.div(me, 2)
        sibling = {"ctx": flip(me, 1)}
        peers = [sibling] + [{"dp": flip(dp_now, d)} for d in range(1, parts)]
        peers += [slot_peer(r, local, exp_now, me) for r in range(1, places)]
        ready = greet(peers)
        diagonal = lax.broadcasted_iota(jnp.int32, (CAP, CAP), 0) == lax.broadcasted_iota(
            jnp.int32, (CAP, CAP), 1
        )

        def dp_of(f):
            distance = parts - 1 - lax.div(f, tiles)
            found, bit = dp_now, 1
            while bit < parts:
                on = lax.rem(lax.div(distance, bit), 2)
                now = lax.rem(lax.div(found, bit), 2)
                found = found + on * bit * (1 - 2 * now)
                bit *= 2
            return found

        def weights(f, slot):
            at = pl.multiple_of(dp_of(f) * per_part + lax.rem(f, tiles) * tile, tile)
            return [
                pltpu.make_async_copy(
                    wg_hbm.at[side, :, pl.ds(at, tile)], wg_buf.at[slot], w_sem.at[0, slot]
                ),
                pltpu.make_async_copy(
                    wu_hbm.at[side, :, pl.ds(at, tile)], wu_buf.at[slot], w_sem.at[1, slot]
                ),
                pltpu.make_async_copy(
                    wd_hbm.at[side, pl.ds(at, tile), :], wd_buf.at[slot], w_sem.at[2, slot]
                ),
            ]

        def core_copy(f, slot):
            return remote(send.at[slot], taken.at[f], c_s.at[slot], c_r.at[f], sibling)

        def far_copy(f):
            return remote(total.at[f], far.at[f], f_s.at[f], f_r.at[f], {"dp": dp_of(f)})

        def back_copy(r):
            return remote(
                dx_low.at[r], dx_near.at[r], b_s.at[r], b_r.at[r],
                slot_peer(r, local, exp_now, me),
            )

        def dots_copy(r):
            return remote(
                dots.at[r], dots_near.at[r], d_s.at[r], d_r.at[r],
                slot_peer(r, local, exp_now, me),
            )

        def keep_weights(k):
            f = lead + k
            at = pl.multiple_of(dp_of(f) * per_part + (f % tiles) * tile, tile)
            return [
                pltpu.make_async_copy(
                    wg_hbm.at[side, :, pl.ds(at, tile)], wg_keep.at[k], keep_sem.at[0, k]
                ),
                pltpu.make_async_copy(
                    wu_hbm.at[side, :, pl.ds(at, tile)], wu_keep.at[k], keep_sem.at[1, k]
                ),
                pltpu.make_async_copy(
                    wd_hbm.at[side, pl.ds(at, tile), :], wd_keep.at[k], keep_sem.at[2, k]
                ),
            ]

        def rows_in(r):
            here = pl.ds(r * CAP, CAP)
            return [
                pltpu.make_async_copy(x_ref.at[r], x_all.at[here, :], in_sem.at[r]),
                pltpu.make_async_copy(dy_parts[r], dy_all.at[here, :], in_sem.at[places + r]),
            ]

        for r in range(places):
            for copy in rows_in(r):
                copy.start()
        if lead:
            for copy in weights(0, 0):
                copy.start()
        for k in range(kept):
            for copy in keep_weights(k):
                copy.start()
        first_half = pl.ds(pl.multiple_of((1 - core) * half, half), half)
        second_half = pl.ds(pl.multiple_of(core * half, half), half)
        for r in range(places):
            here = slice(r * CAP, (r + 1) * CAP)
            for copy in rows_in(r):
                copy.wait()
            turned = jnp.transpose(x_all[here, :])
            xt_all[first_half, here] = turned[:half, :]
            xt_all[second_half, here] = turned[half:, :]
            turned = jnp.transpose(dy_all[here, :])
            dyt_all[first_half, here] = turned[:half, :]
            dyt_all[second_half, here] = turned[half:, :]
            gate_all[here, :] = jnp.sum(
                jnp.where(diagonal, gates_ref[r], 0.0), axis=1, keepdims=True
            )
        y_acc[...] = jnp.zeros_like(y_acc)
        dx_acc[...] = jnp.zeros_like(dx_acc)
        dot_acc[...] = jnp.zeros_like(dot_acc)
        ready()

        def core_sum(f):
            core_copy(f, lax.rem(f, 2)).wait_recv()
            for n in range(3):
                total[f, n] = (total[f, n].astype(f32) + taken[f, n].astype(f32)).astype(bf16)

        def forward_back(here, wg, wu, wd, hid_ref, dg_ref, du_ref, scaled_ref):
            g_pre = mm(x_all[here, :], wg)
            u_pre = mm(x_all[here, :], wu)
            back = mm(dy_all[here, :], wd, NT)
            gate = gate_all[here, :]
            sig = 1.0 / (1.0 + jnp.exp(-g_pre))
            act = g_pre * sig
            hid = act * u_pre
            hid_ref[here, :] = hid.astype(bf16)
            scaled_ref[here, :] = (gate * hid).astype(bf16)
            along = hid * back
            lines = along[:, 0:128]
            for n in range(1, tile // 128):
                lines = lines + along[:, n * 128 : (n + 1) * 128]
            dot_acc[here, :] += lines
            dhid = gate * back
            dg = (dhid * u_pre * sig * (1.0 + g_pre * (1.0 - sig))).astype(bf16)
            du = (dhid * act).astype(bf16)
            dg_ref[here, :] = dg
            du_ref[here, :] = du

        def rows_back(here, wg, wu, dg_ref, du_ref):
            dx_acc[here, :] += mm(dg_ref[here, :], wg, NT) + mm(du_ref[here, :], wu, NT)

        def weight_sums(f, slot, dg_ref, du_ref, scaled_ref, first):
            @pl.when(f > first)
            def _():
                core_sum(f - 1)

            @pl.when(f >= 2)
            def _():
                core_copy(f - 2, slot).wait_send()

            for n, (left, right) in enumerate(
                ((xt_all, dg_ref), (xt_all, du_ref), (dyt_all, scaled_ref))
            ):
                found = mm(left[...], right[...]).astype(bf16)
                send[slot, n] = found[:half, :]
                total[f, n] = found[half:, :]
            core_copy(f, slot).start()

            @pl.when((f > first) & (f - 1 < away))
            def _():
                far_copy(f - 1).start()

        def lead_step(f, _):
            slot = lax.rem(f, 2)
            for copy in weights(f, slot):
                copy.wait()

            @pl.when(f + 1 < lead)
            def _():
                for copy in weights(f + 1, 1 - slot):
                    copy.start()

            hid, dg, du, scaled = (a.at[0] for a in (hid_keep, dg_keep, du_keep, scaled_keep))

            def row_chunk(c, _):
                here = pl.ds(pl.multiple_of(c * chunk, chunk), chunk)
                forward_back(here, wg_buf[slot], wu_buf[slot], wd_buf[slot], hid, dg, du, scaled)
                return 0

            lax.fori_loop(0, rows // chunk, row_chunk, 0)
            weight_sums(f, slot, dg, du, scaled, 0)
            y_acc[...] += mm(hid[...], wd_buf[slot])
            rows_back(slice(0, rows), wg_buf[slot], wu_buf[slot], dg, du)
            return 0

        lax.fori_loop(0, lead, lead_step, 0)
        if lead:
            core_sum(lead - 1)
            far_copy(lead - 1).start()
        for k in range(kept):
            for copy in keep_weights(k):
                copy.wait()

        def keep_rows(k, first, count):
            size = min(chunk, count)
            for c in range(count // size):
                forward_back(
                    slice(first + c * size, first + (c + 1) * size),
                    wg_keep[k], wu_keep[k], wd_keep[k],
                    hid_keep.at[k], dg_keep.at[k], du_keep.at[k], scaled_keep.at[k],
                )
            rows_back(
                slice(first, first + count), wg_keep[k], wu_keep[k], dg_keep.at[k], du_keep.at[k]
            )

        def send_back(first, last):
            for r in range(first, last):
                here = slice(r * CAP, (r + 1) * CAP)
                dx_low[r] = dx_acc[here, :].astype(bf16)
                column = jnp.sum(dot_acc[here, :], axis=1, keepdims=True)
                dots[r] = jnp.sum(jnp.where(diagonal, column, 0.0), axis=0, keepdims=True)
                if r - 1 >= max(1, first):
                    back_copy(r - 1).start()
                    dots_copy(r - 1).start()

        def send_last(r):
            back_copy(r).start()
            dots_copy(r).start()

        middle = places // 2
        near_rows = middle * CAP

        def far_step(k, _):
            keep_rows(k, near_rows, rows - near_rows)
            return 0

        lax.fori_loop(0, kept, far_step, 0)
        send_back(middle, places)

        def away_step(f, _):
            k = f - lead

            keep_rows(k, 0, near_rows)

            @pl.when(k == 0)
            def _():
                send_last(places - 1)

            weight_sums(
                f, lax.rem(f, 2), dg_keep.at[k], du_keep.at[k], scaled_keep.at[k], lead
            )
            return 0

        lax.fori_loop(lead, away, away_step, 0)
        if away == lead:
            send_last(places - 1)
        else:
            core_sum(away - 1)
            far_copy(away - 1).start()

        def near_step(k, _):
            keep_rows(k, 0, near_rows)
            return 0

        lax.fori_loop(away - lead, kept, near_step, 0)
        send_back(0, middle)

        def own_result(k, _):
            y_acc[...] += mm(hid_keep[k], wd_keep[k])
            return 0

        lax.fori_loop(0, kept, own_result, 0)
        send_last(middle - 1)

        def relay_copy(g):
            return remote(y_odd.at[g], relay.at[g], y_s.at[g], y_r.at[g], {"ctx": flip(me, 2)})

        def result(r):
            here = slice(r * CAP, (r + 1) * CAP)
            return (gate_all[here, :] * y_acc[here, :]).astype(bf16)

        for g in range(groups):
            y_odd[g] = result(local * g + 1)
            if g:
                relay_copy(g - 1).start()
        for g in range(groups):
            y_out[g][0] = result(local * g)
        relay_copy(groups - 1).start()

        def own_step(f, _):
            k = f - lead
            weight_sums(
                f, lax.rem(f, 2), dg_keep.at[k], du_keep.at[k], scaled_keep.at[k], away
            )
            return 0

        lax.fori_loop(away, steps, own_step, 0)
        core_sum(steps - 1)

        def beside_copy(i):
            return remote(total.at[away + i], beside.at[i], e_s.at[i], e_r.at[i], sibling)

        def beside_store(i):
            return pltpu.make_async_copy(
                beside.at[i], beside_out.at[:, :, pl.ds(i * tile, tile)], beside_sem.at[i]
            )

        def sum_store(i):
            return pltpu.make_async_copy(
                total.at[away + i], sum_out.at[:, :, pl.ds(i * tile, tile)], out_sem.at[i]
            )

        for i in range(tiles):
            for d in range(1, parts):
                far_copy((parts - 1 - d) * tiles + i).wait_recv()
            for n in range(3):
                value = total[away + i, n].astype(f32)
                for d in range(1, parts):
                    value = value + far[(parts - 1 - d) * tiles + i, n].astype(f32)
                total[away + i, n] = value.astype(bf16)
            if i:
                beside_copy(i - 1).start()
            sum_store(i).start()
        beside_copy(tiles - 1).start()
        for f in range(away):
            far_copy(f).wait_send()
        for f in range(max(0, steps - 2), steps):
            core_copy(f, f % 2).wait_send()

        def dx_store(r):
            src = dx_near.at[r] if r else dx_low.at[0]
            return pltpu.make_async_copy(src, dx_out.at[r], dx_sem.at[r])

        dots_out[0] = dots[0]
        dx_store(0).start()
        for r in range(1, places):
            back_copy(r).wait()
            dots_copy(r).wait()
            dx_store(r).start()
            dots_out[r] = dots_near[r]
        for g in range(groups):
            relay_copy(g).wait()
            y_out[g][1] = relay[g]
        for i in range(tiles):
            beside_copy(i).wait()
            beside_store(i).start()
        for i in range(tiles):
            sum_store(i).wait()
            beside_store(i).wait()
        for r in range(places):
            dx_store(r).wait()

    placed = shape_of((places, CAP, width), bf16)
    pair = shape_of((local, CAP, width), bf16)
    lines = shape_of((places, 1, CAP), f32)
    return run(
        body,
        (),
        [(arrived, anywhere), (grads, anywhere), (gates, vector)]
        + [(w, anywhere) for w in (w_gate, w_up, w_down)]
        + [(g, anywhere) for g in late],
        [(pair, vector)] * groups
        + [(placed, anywhere), (lines, vector)]
        + [(shape_of((3, half, per_part), bf16), anywhere)] * 2,
        scratch=[
            pltpu.VMEM((rows, width), bf16),
            pltpu.VMEM((width, rows), bf16),
            pltpu.VMEM((rows, width), bf16),
            pltpu.VMEM((width, rows), bf16),
            pltpu.VMEM((rows, 1), f32),
            pltpu.VMEM((rows, width), f32),
            pltpu.VMEM((rows, width), f32),
            pltpu.VMEM((rows, 128), f32),
            pltpu.VMEM((2, width, tile), bf16),
            pltpu.VMEM((2, width, tile), bf16),
            pltpu.VMEM((2, tile, width), bf16),
            pltpu.VMEM((kept, width, tile), bf16),
            pltpu.VMEM((kept, width, tile), bf16),
            pltpu.VMEM((kept, tile, width), bf16),
            pltpu.VMEM((kept, rows, tile), bf16),
            pltpu.VMEM((kept, rows, tile), bf16),
            pltpu.VMEM((kept, rows, tile), bf16),
            pltpu.VMEM((kept, rows, tile), bf16),
            pltpu.VMEM((2, 3, half, tile), bf16),
            pltpu.VMEM((steps, 3, half, tile), bf16),
            pltpu.VMEM((steps, 3, half, tile), bf16),
            pltpu.VMEM((max(1, away), 3, half, tile), bf16),
            pltpu.VMEM((places, CAP, width), bf16),
            pltpu.VMEM((places, CAP, width), bf16),
            pltpu.VMEM((places, 1, CAP), f32),
            pltpu.VMEM((places, 1, CAP), f32),
            pltpu.VMEM((tiles, 3, half, tile), bf16),
            pltpu.VMEM((groups, CAP, width), bf16),
            pltpu.VMEM((groups, CAP, width), bf16),
            dma((2 * places,)), dma((3, 2)), dma((3, kept)), dma((2,)), dma((steps,)),
            dma((max(1, away),)), dma((max(1, away),)),
            dma((places,)), dma((places,)), dma((places,)), dma((places,)),
            dma((tiles,)), dma((tiles,)), dma((tiles,)), dma((tiles,)),
            dma((groups,)), dma((groups,)), dma((places,)),
        ],
        flops=9 * 2 * rows * width * hidden,
        moved=12 * width * hidden + rows * width * 8,
        exps=rows * hidden,
        talks=2,
    )


def slot_sum(targets, source_ref):
    tile = targets.shape[0]
    total = None
    for r in range(source_ref.shape[0]):
        ids = r * CAP + lax.broadcasted_iota(jnp.int32, (tile, CAP), 1)
        choice = jnp.where((ids == targets[:, 0:1]) | (ids == targets[:, 1:2]), 1.0, 0.0)
        part = mm(choice.astype(bf16), source_ref[r])
        total = part if total is None else total + part
    return total


def token_back(
    x1, h2, grad, prob, previous_t, routes, targets, back, dots, dgate_zero, dh_zero, gain, router_t,
    zero_sums,
):
    rows, width = x1.shape
    tile = 128
    tiles = rows // tile
    places = back.shape[0]
    expert_all = prob.shape[1]
    members = lax.axis_size("ctx")
    last = expert_all + 1 + zero_sums.shape[0]

    def body(*refs):
        (x1_ref, h2_ref, dy_ref, prob_ref, prev_ref, route_ref, target_ref) = refs[:7]
        back_ref, dots_ref, dz_ref, dh_ref, gain_ref, router_ref, zero_ref = refs[7:14]
        dx1_ref, sums_ref, da_out, da_near, a_s, a_r, out_sem = refs[14:]
        me = lax.axis_index("ctx")
        peers = [{"ctx": flip(me, 1)}, {"ctx": flip(me, 2)}]
        ready = greet(peers)

        def da_copy(kind, t):
            here = pl.ds(pl.multiple_of(t * tile, tile), tile)
            n = kind * tiles + t
            src, dst = ((0, 1), (0, 2), (2, 3))[kind]
            return remote(
                da_near.at[src, here, :], da_near.at[dst, here, :], a_s.at[n], a_r.at[n],
                {"ctx": flip(me, 2 if kind == 1 else 1)},
            )

        sums_ref[...] = jnp.zeros_like(sums_ref)
        sums_ref[expert_all + 1 : last, :] = zero_ref[...]
        ready()

        def token_rows(t, _):
            here = pl.ds(pl.multiple_of(t * tile, tile), tile)
            prob_now = prob_ref[here, :]
            chosen, target, zero = route_ref[here, :], target_ref[here, :], dz_ref[here, :]
            lanes = lax.broadcasted_iota(jnp.int32, (tile, expert_all), 1)
            dprob = jnp.zeros_like(prob_now)
            for c in range(2):
                dgate = zero[:, c : c + 1]
                for n in range(places):
                    ids = n * CAP + lax.broadcasted_iota(jnp.int32, (tile, CAP), 1)
                    dgate = dgate + jnp.sum(
                        jnp.where(ids == target[:, c : c + 1], dots_ref[n], 0.0),
                        axis=1,
                        keepdims=True,
                    )
                dprob = dprob + jnp.where(lanes == chosen[:, c : c + 1], dgate, 0.0)
            dlogit = prob_now * (dprob - jnp.sum(prob_now * dprob, axis=1, keepdims=True))
            h2 = h2_ref[here, :]
            dh2 = slot_sum(target, back_ref) + dh_ref[here, :] + mm_full(dlogit, router_ref[...])
            x1 = x1_ref[here, :]
            inverse = lax.rsqrt(jnp.mean(x1 * x1, axis=1, keepdims=True) + norm_eps)
            normed = x1 * inverse
            dn = dh2 * gain_ref[...]
            dx1 = dy_ref[here, :].astype(f32) + inverse * (
                dn - normed * jnp.mean(dn * normed, axis=1, keepdims=True)
            )
            dx1_ref[here, :] = dx1
            da_near[0, here, :] = dx1.astype(bf16)
            sums_ref[0:expert_all, :] += mm_full(dlogit, h2, TN)
            sums_ref[expert_all : expert_all + 1, :] += jnp.sum(dh2 * normed, axis=0, keepdims=True)
            sums_ref[last:, 0:expert_all] += mm_full(prev_ref[:, here], dlogit)
            da_copy(1, t).start()
            da_copy(0, t).start()

            @pl.when(t >= 2)
            def _():
                da_copy(1, t - 2).wait_recv()
                da_copy(2, t - 2).start()

            return 0

        lax.fori_loop(0, tiles, token_rows, 0)
        for t in range(max(0, tiles - 2), tiles):
            da_copy(1, t).wait_recv()
            da_copy(2, t).start()
        mine = pltpu.make_async_copy(da_near.at[0], da_out.at[0], out_sem.at[0])
        mine.start()
        for t in range(tiles):
            da_copy(0, t).wait()
            da_copy(1, t).wait_send()
            da_copy(2, t).wait()
        rest = pltpu.make_async_copy(
            da_near.at[pl.ds(1, members - 1)], da_out.at[pl.ds(1, members - 1)], out_sem.at[1]
        )
        rest.start()
        mine.wait()
        rest.wait()

    return run(
        body,
        (),
        [(a, vector) for a in (x1, h2, grad, prob, previous_t, routes, targets, back, dots)]
        + [(a, vector) for a in (dgate_zero, dh_zero, gain, router_t, zero_sums)],
        [(shape_of((rows, width), f32), vector)]
        + [(shape_of((last + expert_all, width), f32), vector)]
        + [(shape_of((members, rows, width), bf16), anywhere)],
        scratch=[
            pltpu.VMEM((members, rows, width), bf16),
            dma((3 * tiles,)), dma((3 * tiles,)), dma((2,)),
        ],
        flops=2 * rows * width * (places * CAP + width),
        moved=rows * width * 24,
        talks=5,
    )


def finish(dqkv_all, h1, x, gain, dx1, weights_t, out_sum, small, tops, produced, base, targets):
    members, per_group = weights_t.shape[1], weights_t.shape[2]
    rows, width = x.shape
    group_rows = dqkv_all.shape[0]
    parts, groups = lax.axis_size("dp"), lax.axis_size("exp")
    team = parts * groups
    local = produced[0].shape[0]
    places = groups * local
    wide_share, out_share = width // (2 * team), per_group // team
    small_rows = small.shape[0]
    small_steps = [(axis, bit) for axis in ("ctx", "dp", "exp") for bit in powers(axis)]
    hops = len(small_steps)
    row_tile = min(256, rows)

    def body(*refs):
        it = iter(refs)

        def take(count=None):
            return next(it) if count is None else [next(it) for _ in range(count)]

        dqkv_hbm, h1_hbm, x_hbm, gain_ref, dx1_hbm, w_hbm, out_ref = take(7)
        small_ref, tops_ref, base_hbm, target_ref = take(4)
        produced_hbm = take(groups)
        input_out, wide_out, flat_out, small_out, gain_out, tops_out, result_out = take(7)
        dqkv, product, h1_all, x_all, dx1_all, w_all, base_all, y_near = take(8)
        part_send, part_core, part_y, y_got, part_own = take(5)
        wide_mine, wide_far_x, wide_far_z, wide_all = take(4)
        flat_mine, flat_far_x, flat_far_z, flat_all = take(4)
        small_acc, small_far, gain_acc, gain_far, tops_acc, tops_far = take(6)
        load_sem, near_s, near_r = take(3)
        wide_sems, flat_sems = [take(12), take(12)], take(12)
        hop_s, hop_r, gain_s, gain_r, top_s, top_r = take(6)

        me = lax.axis_index("ctx")
        dp_now, exp_now = lax.axis_index("dp"), lax.axis_index("exp")
        seat = dp_now * groups + exp_now

        def near_peer(j):
            return {"ctx": flip(me, j)}

        def team_peer(r):
            return {"dp": flip(dp_now, r // groups), "exp": flip(exp_now, r % groups)}

        peers = [near_peer(j) for j in range(1, members)]
        peers += [team_peer(r) for r in range(1, team)]
        ready = greet(peers)

        loads = [
            (dqkv_hbm, dqkv), (h1_hbm, h1_all), (x_hbm, x_all), (dx1_hbm, dx1_all),
            (w_hbm.at[:, me], w_all), (base_hbm, base_all),
        ]
        loads += [
            (produced_hbm[g], y_near.at[pl.ds(g * local, local)]) for g in range(groups)
        ]

        def load(n):
            return pltpu.make_async_copy(loads[n][0], loads[n][1], load_sem.at[n])

        class Dense:
            def __init__(self, mine, far_x, far_z, all_buf, sems):
                self.mine, self.far_x, self.far_z, self.all = mine, far_x, far_z, all_buf
                self.sems = sems

            def own_block(self, d=0):
                return pl.ds(flip(dp_now, d) * groups, groups)

            def x_copy(self, d):
                return remote(
                    self.mine.at[self.own_block(d)], self.far_x.at[d - 1], self.sems[0].at[d],
                    self.sems[1].at[d], {"dp": flip(dp_now, d)},
                )

            def z_copy(self, g):
                return remote(
                    self.mine.at[dp_now * groups + flip(exp_now, g)], self.far_z.at[g - 1],
                    self.sems[2].at[g], self.sems[3].at[g], {"exp": flip(exp_now, g)},
                )

            def gz_copy(self, g, theirs=False):
                spot = self.all.at[0, dp_now * groups + flip(exp_now, g) if theirs else seat]
                return remote(
                    spot, spot, self.sems[4].at[g], self.sems[5].at[g], {"exp": flip(exp_now, g)}
                )

            def gx_copy(self, d, theirs=False):
                spot = self.all.at[0, self.own_block(d if theirs else 0)]
                return remote(
                    spot, spot, self.sems[6].at[d], self.sems[7].at[d], {"dp": flip(dp_now, d)}
                )

            def y_copy(self, d):
                return remote(
                    self.all.at[0, self.own_block(d)], self.all.at[2, self.own_block(d)],
                    self.sems[8].at[d], self.sems[9].at[d], near_peer(2),
                )

            def core_copy(self, n):
                return remote(
                    self.all.at[2 * n], self.all.at[2 * n + 1], self.sems[10].at[n],
                    self.sems[11].at[n], near_peer(1),
                )

            def start(self):
                for d in range(1, parts):
                    self.x_copy(d).start()

            def to_z(self):
                for d in range(1, parts):
                    self.x_copy(d).wait()
                for g in list(range(1, groups)) + [0]:
                    c = dp_now * groups + flip(exp_now, g)
                    value = self.mine[c].astype(f32)
                    for d in range(1, parts):
                        value = value + self.far_x[d - 1, flip(exp_now, g)].astype(f32)
                    self.mine[c] = value.astype(bf16)
                for g in range(1, groups):
                    self.z_copy(g).start()

            def to_gather(self):
                for g in range(1, groups):
                    self.z_copy(g).wait()
                value = self.mine[seat].astype(f32)
                for g in range(1, groups):
                    value = value + self.far_z[g - 1].astype(f32)
                self.all[0, seat] = value.astype(bf16)

            def gather(self):
                for g in range(1, groups):
                    self.gz_copy(g).start()

            def to_x(self):
                for g in range(1, groups):
                    self.gz_copy(g).wait_send()
                    self.gz_copy(g, True).wait_recv()
                for d in range(1, parts):
                    self.gx_copy(d).start()
                self.y_copy(0).start()

            def to_y(self):
                for d in range(1, parts):
                    self.gx_copy(d).wait_send()
                    self.gx_copy(d, True).wait_recv()
                    self.y_copy(d).start()
                self.core_copy(0).start()

            def to_core(self):
                for d in range(parts):
                    self.y_copy(d).wait()
                self.core_copy(1).start()

            def done(self):
                for n in range(2):
                    self.core_copy(n).wait()

        wides = [
            Dense(wide_mine.at[n], wide_far_x.at[n], wide_far_z.at[n], wide_all.at[n], wide_sems[n])
            for n in range(2)
        ]
        flat = Dense(flat_mine, flat_far_x, flat_far_z, flat_all, flat_sems)

        def hop_peer(n):
            axis, bit = small_steps[n]
            return {axis: flip(lax.axis_index(axis), bit)}

        def small_copy(n):
            return remote(small_acc.at[n], small_far.at[n], hop_s.at[n], hop_r.at[n], hop_peer(n))

        def tops_copy(n):
            return remote(tops_acc.at[n], tops_far.at[n], top_s.at[n], top_r.at[n], hop_peer(n))

        def gain_copy(n):
            return remote(gain_acc.at[n], gain_far.at[n], gain_s.at[n], gain_r.at[n], hop_peer(n))

        def small_start(n):
            small_copy(n).start()
            tops_copy(n).start()

        def small_sum(n):
            small_copy(n).wait()
            tops_copy(n).wait()
            small_acc[n + 1] = small_acc[n] + small_far[n]
            tops_acc[n + 1] = jnp.maximum(tops_acc[n], tops_far[n])

        small_hops = list(range(hops))

        def small_next():
            if small_hops:
                n = small_hops.pop(0)
                small_sum(n)
                if n + 1 < hops:
                    small_start(n + 1)

        row_tiles = rows // row_tile

        def tile_rows(t, first=0):
            return pl.ds(first + t * row_tile, row_tile)

        def core_part(j, t):
            n = j // 2
            return remote(
                part_send.at[n, tile_rows(t), :], part_core.at[n, tile_rows(t), :],
                near_s.at[n * row_tiles + t], near_r.at[n * row_tiles + t], near_peer(1),
            )

        def y_part(t):
            n = 2 * row_tiles + t
            return remote(
                part_y.at[tile_rows(t), :], y_got.at[tile_rows(t), :], near_s.at[n], near_r.at[n],
                near_peer(2),
            )

        def part(j, t):
            here = pl.ds(j * rows + t * row_tile, row_tile)
            found = None
            for w in range(3):
                add = mm(dqkv[here, w * per_group : (w + 1) * per_group], w_all[w])
                found = add if found is None else found + add
            return found

        for n in range(len(loads)):
            load(n).start()
        small_acc[0] = small_ref[...]
        lanes = lax.broadcasted_iota(jnp.int32, tops_acc.shape[1:], 1)
        tops_acc[0] = jnp.where(
            lanes == me, jnp.max(tops_ref[...], axis=1, keepdims=True), low_start
        )
        flat_rows = out_ref[...].astype(f32)
        for c in range(team):
            flat_mine[c] = flat_rows[c * out_share : (c + 1) * out_share, :].astype(bf16)
        ready()
        flat.start()
        small_start(0)
        load(0).wait()
        load(1).wait()

        def weigh(n, _):
            here = pl.ds(pl.multiple_of(n * rows, rows), rows)
            product[...] += mm(h1_all[here, :], dqkv[here, :], TN)
            return 0

        product[...] = mm(h1_all[0:rows, :], dqkv[0:rows, :], TN)
        lax.fori_loop(1, group_rows // rows, weigh, 0)
        for n in range(2):
            for c in range(team):
                at = (n * team + c) * wide_share
                wide_mine[n, c] = product[at : at + wide_share, :].astype(bf16)
            if n:
                wides[0].start()
        flat.to_z()
        wides[1].start()
        for n in range(2, len(loads)):
            load(n).wait()
        queue = [(j, t) for j in (3, 1) for t in range(row_tiles)]
        for n, (j, t) in enumerate(queue):
            part_send[j // 2, tile_rows(t), :] = part(j, t).astype(bf16)
            if n:
                core_part(*queue[n - 1]).start()
        own_part = [part(2, t) for t in range(1)]
        core_part(*queue[-1]).start()
        for t in range(row_tiles):
            value = own_part[0] if t == 0 else part(2, t)
            core_part(3, t).wait_recv()
            part_y[tile_rows(t), :] = (
                value + part_core[1, tile_rows(t), :].astype(f32)
            ).astype(bf16)
            if t:
                y_part(t - 1).start()
        part_own[tile_rows(0), :] = part(0, 0)
        y_part(row_tiles - 1).start()
        for t in range(1, row_tiles):
            part_own[tile_rows(t), :] = part(0, t)
        wides[0].to_z()
        flat.to_gather()
        small_next()
        wides[1].to_z()
        flat.gather()
        wides[0].to_gather()

        def token_rows(t, _):
            here = pl.ds(pl.multiple_of(t * 128, 128), 128)
            result_out[here, :] = (
                base_all[here, :] + slot_sum(target_ref[here, :], y_near)
            ).astype(bf16)
            return 0

        lax.fori_loop(0, rows // 256, token_rows, 0)
        wides[0].gather()
        small_next()
        flat.to_x()
        wides[1].to_gather()
        lax.fori_loop(rows // 256, rows // 128, token_rows, 0)
        wides[1].gather()
        wides[0].to_x()
        small_next()
        for t in range(row_tiles):
            core_part(1, t).wait()
            core_part(3, t).wait_send()
            y_part(t).wait()

        def input_rows(t, gain_part):
            here = pl.ds(pl.multiple_of(t * row_tile, row_tile), row_tile)
            dh = (
                part_own[here, :] + part_core[0, here, :].astype(f32) + y_got[here, :].astype(f32)
            )
            x_now = x_all[here, :].astype(f32)
            inv = lax.rsqrt(jnp.mean(x_now * x_now, axis=1, keepdims=True) + norm_eps)
            normed = x_now * inv
            dn = dh * gain_ref[...]
            dx1_all[here, :] = dx1_all[here, :] + inv * (
                dn - normed * jnp.mean(dn * normed, axis=1, keepdims=True)
            )
            return gain_part + jnp.sum(dh * normed, axis=0, keepdims=True)

        gain_acc[0] = lax.fori_loop(
            0, rows // row_tile, input_rows, jnp.zeros((1, width), f32)
        )
        store = pltpu.make_async_copy(dx1_all, input_out, load_sem.at[len(loads)])
        store.start()
        flat.to_y()
        gain_copy(0).start()
        wides[1].to_x()
        wides[0].to_y()
        small_next()
        events = [
            flat.to_core, wides[1].to_y, wides[0].to_core, flat.done, wides[1].to_core,
        ]
        for n in range(hops):
            gain_copy(n).wait()
            gain_acc[n + 1] = gain_acc[n] + gain_far[n]
            if events:
                events.pop(0)()
            if n + 1 < hops:
                gain_copy(n + 1).start()
        while small_hops:
            small_next()
        while events:
            events.pop(0)()
        final = [pltpu.make_async_copy(flat_all, flat_out, load_sem.at[len(loads) + 1])]
        for n in range(2):
            wides[n].done()
            final.append(
                pltpu.make_async_copy(
                    wide_all.at[n], wide_out.at[n], load_sem.at[len(loads) + 2 + n]
                )
            )
        for copy in final:
            copy.start()
        small_out[...] = small_acc[hops]
        gain_out[...] = gain_acc[hops, 0, :]
        tops_out[...] = tops_acc[hops]
        store.wait()
        for copy in final:
            copy.wait()

    def dense_scratch(share, across, lead=()):
        return [
            pltpu.VMEM(lead + (team, share, across), bf16),
            pltpu.VMEM(lead + (max(1, parts - 1), groups, share, across), bf16),
            pltpu.VMEM(lead + (max(1, groups - 1), share, across), bf16),
            pltpu.VMEM(lead + (members, team, share, across), bf16),
        ]

    dense_sem = (
        [dma((parts,))] * 2 + [dma((groups,))] * 4 + [dma((parts,))] * 4 + [dma((2,))] * 2
    )
    wide_rows = shape_of((rows, width), f32)
    return run(
        body,
        (),
        [(dqkv_all, anywhere), (h1, anywhere), (x, anywhere), (gain, vector), (dx1, anywhere)]
        + [(weights_t, anywhere), (out_sum, vector), (small, vector), (tops, vector)]
        + [(base, anywhere), (targets, vector)]
        + [(a, anywhere) for a in produced],
        [
            (wide_rows, anywhere),
            (shape_of((2, members, team, wide_share, 3 * per_group), bf16), anywhere),
            (shape_of((members, team, out_share, width), bf16), anywhere),
            (shape_of((small_rows, width), f32), vector),
            (shape_of((width,), f32), vector),
            (shape_of((tops.shape[0], 128), f32), vector),
            (shape_of((rows, width), bf16), vector),
        ],
        scratch=[
            pltpu.VMEM((group_rows, 3 * per_group), bf16),
            pltpu.VMEM((width, 3 * per_group), f32),
            pltpu.VMEM((group_rows, width), bf16),
            pltpu.VMEM((rows, width), bf16),
            pltpu.VMEM((rows, width), f32),
            pltpu.VMEM((3, per_group, width), bf16),
            pltpu.VMEM((rows, width), f32),
            pltpu.VMEM((places, CAP, width), bf16),
            pltpu.VMEM((2, rows, width), bf16),
            pltpu.VMEM((2, rows, width), bf16),
            pltpu.VMEM((rows, width), bf16),
            pltpu.VMEM((rows, width), bf16),
            pltpu.VMEM((rows, width), f32),
        ]
        + dense_scratch(wide_share, 3 * per_group, (2,))
        + dense_scratch(out_share, width)
        + [pltpu.VMEM((hops + 1, small_rows, width), f32), pltpu.VMEM((hops, small_rows, width), f32)]
        + [pltpu.VMEM((hops + 1, 1, width), f32), pltpu.VMEM((hops, 1, width), f32)]
        + [pltpu.VMEM((hops + 1, tops.shape[0], 128), f32), pltpu.VMEM((hops, tops.shape[0], 128), f32)]
        + [dma((12 + places,))] + [dma((3 * (rows // row_tile),))] * 2
        + dense_sem * 3
        + [dma((hops,))] * 6,
        flops=4 * 2 * rows * width * width * 3,
        moved=20 * 1024 * 1024,
        talks=3,
    )


def place_experts(meta, near, turned):
    _, half, columns = near[0][0][0].shape
    members = len(near[0])
    local = members // 2
    count = len(near)
    tile = 128
    tiles = half // tile

    def body(meta_ref, *refs):
        outs = refs[count * members :]
        step = pl.program_id(0) * 2 + pl.program_id(1)
        for j in range(members):

            @pl.when(step == j)
            def _():
                for n in range(count):
                    piece = refs[n * members + j][0].astype(f32)
                    outs[n][0] = jnp.transpose(piece) if turned[n] else piece

    def in_spec(which, j):
        def index(n, c, t, m):
            step = n * 2 + c
            return (which, jnp.where(step == j, t, jnp.where(step < j, 0, tiles - 1)), 0)

        return pl.BlockSpec((1, tile, columns), index)

    outputs = []
    for flag in turned:
        if flag:
            outputs.append(
                (
                    shape_of((local, columns, 2 * half), f32),
                    pl.BlockSpec(
                        (1, columns, tile),
                        lambda n, c, t, m: (m[3] ^ n, 0, (m[2] ^ c) * tiles + t),
                    ),
                )
            )
        else:
            outputs.append(
                (
                    shape_of((local, 2 * half, columns), f32),
                    pl.BlockSpec(
                        (1, tile, columns),
                        lambda n, c, t, m: (m[3] ^ n, (m[2] ^ c) * tiles + t, 0),
                    ),
                )
            )
    return run(
        body,
        (local, 2, tiles),
        [(a, in_spec(which, j)) for listed in near for j, (a, which) in enumerate(listed)],
        outputs,
        meta=meta,
        moved=count * local * 2 * half * columns * 6,
    )


def place_dense(meta, near, flat, tops, small, w_qkv, kinds):
    _, members, team, share, lanes = near.shape
    per_group = lanes // 3
    half = team * share
    width = 2 * half
    rows_all = flat.shape[1] * flat.shape[2]
    step = 8 // math.gcd(share, 8)
    while team // step > 4:
        step *= 2
    per_half = team // step
    tall = step * share

    heads = HEADS // members
    head_width = width // HEADS
    expert_all = (small.shape[0] - 1 - 3 * kinds) // 2
    at_vec = expert_all + 1
    at_logit = at_vec + kinds
    at_carry = at_logit + 2 * kinds

    def body(meta_ref, near_ref, flat_ref, tops_ref, small_ref, w_ref, *outs):
        out_ref, flat_out, clip_ref, router_out, norm_out, vec_out, logit_out, carry_out = outs[:8]
        scale_ref = outs[8]

        @pl.when((pl.program_id(0) == 0) & (pl.program_id(1) == 0))
        def _():
            lanes = lax.broadcasted_iota(jnp.int32, (1, width), 1)
            scale = jnp.zeros((1, width), f32)
            for n in range(HEADS):
                top = tops_ref[n % heads : n % heads + 1, n // heads : n // heads + 1]
                ratio = jnp.sqrt(jnp.minimum(1.0, clip_limit / top))
                inside = (lanes >= n * head_width) & (lanes < (n + 1) * head_width)
                scale = jnp.where(inside, ratio, scale)
            scale_ref[...] = scale
            router_out[...] = small_ref[0:expert_all, :]
            norm_out[...] = small_ref[expert_all, :]
            vec_out[...] = small_ref[at_vec : at_vec + kinds, :]
            for n in range(kinds):
                logit_out[n] = small_ref[at_logit + 2 * n : at_logit + 2 * n + 2, :]
            carry_out[...] = small_ref[at_carry:, 0:expert_all]

        for c in range(step):
            pieces = [near_ref[0, meta_ref[0] ^ g, c] for g in range(members)]
            for w in range(3):
                at = slice(w * per_group, (w + 1) * per_group)
                out_ref[w, c * share : (c + 1) * share, :] = jnp.concatenate(
                    [piece[:, at] for piece in pieces], axis=1
                ).astype(f32)
        clip_ref[...] = w_ref[...].astype(f32) * scale_ref[...]

        @pl.when(pl.program_id(1) == 0)
        def _():
            for c in range(team):
                at = slice(c * flat.shape[2], (c + 1) * flat.shape[2])
                for j in range(2):
                    member = pl.program_id(0) * 2 + j
                    flat_out[j, at, :] = flat_ref[meta_ref[0] ^ member, c].astype(f32)

    square = shape_of((3, width, width), f32)
    return run(
        body,
        (2, per_half),
        [
            (
                near,
                pl.BlockSpec((1, members, step, share, lanes), lambda n, c, m: (n, 0, c, 0, 0)),
            ),
            (flat, whole(flat)),
            (tops, whole(tops)),
            (small, whole(small)),
            (w_qkv, pl.BlockSpec((2, tall, width), lambda n, c, m: (0, n * per_half + c, 0))),
        ],
        [
            (square, pl.BlockSpec((3, tall, width), lambda n, c, m: (0, n * per_half + c, 0))),
            (
                shape_of((members, rows_all, width), f32),
                pl.BlockSpec((2, rows_all, width), lambda n, c, m: (n, 0, 0)),
            ),
            (
                shape_of((2, width, width), f32),
                pl.BlockSpec((2, tall, width), lambda n, c, m: (0, n * per_half + c, 0)),
            ),
        ]
        + [
            (o, whole(o))
            for o in (
                shape_of((expert_all, width), f32),
                shape_of((width,), f32),
                shape_of((kinds, width), f32),
                shape_of((kinds, 2, width), f32),
                shape_of((expert_all, expert_all), f32),
            )
        ],
        scratch=[pltpu.VMEM((1, width), f32)],
        meta=meta,
        moved=square.size * 12,
    )


def shards(
    inputs,
    lengths,
    block_order,
    routes,
    prev_logits,
    norm1_gain,
    norm2_gain,
    w_qkv,
    w_out,
    w_router,
    w_carry,
    const_logit_w,
    const_vec,
    w_gate,
    w_up,
    w_down,
    cotangent,
):
    members = lax.axis_size("ctx")
    groups = lax.axis_size("exp")
    parts = lax.axis_size("dp")
    me = lax.axis_index("ctx")
    mine = lax.axis_index("exp")
    x, grad = inputs[0], cotangent[0]
    rows, width = x.shape
    group_rows = rows * members
    deal_block = group_rows // block_order.shape[1]
    per_member = rows // deal_block
    local = w_gate.shape[0]
    expert_count = local * groups
    head_width = width // HEADS
    heads = HEADS // members
    per_group = heads * head_width
    blocks = block_order.shape[1]
    layout = {
        "order": 4, "lengths": 4 + blocks, "sequences": lengths.shape[1],
        "inverse": 4 + blocks + lengths.shape[1],
    }
    numbers = jnp.arange(blocks, dtype=jnp.int32)
    given = jnp.sum(jnp.where(block_order[0][None, :] == numbers[:, None], numbers[None, :], 0), axis=1)
    inverse = (((given // per_member) ^ me) * per_member + given % per_member).astype(jnp.int32)
    meta = jnp.concatenate(
        [
            jnp.stack([me, mine, me % 2, me // 2]).astype(jnp.int32),
            block_order[0],
            lengths[0],
            inverse,
        ]
    )
    gain1, gain2 = norm1_gain, norm2_gain
    w_out_parts = w_out.reshape(members, per_group, width)
    previous_t = jnp.transpose(prev_logits[0])
    router_t = jnp.transpose(w_router)
    odd = [r for r in range(groups * local) if r % local]

    begun = begin(x, grad, jnp.transpose(routes[0]), gain1, w_qkv, local)
    q, k, v, kt, vt, h1, weights_t, targets, target_rows, route_ids, grad_near = begun[:11]
    grad_rest = begun[11:]
    weights_t = weights_t.reshape(3, members, per_group, width)
    grad_late = [slot_swap(grad_rest[n], r, local) for n, r in enumerate(odd)]
    o, ot, lse, tops = attend(meta, q, k, vt, deal_block, layout)
    logit_rows = jnp.swapaxes(const_logit_w, 1, 2).reshape(-1, width)
    x1, h2, prob, token_near, gate_near, base, dh_zero, dgate_zero, zero_sums = token_front(
        x, o, w_out_parts, gain2, router_t, previous_t, w_carry, target_rows, grad, route_ids,
        logit_rows, const_vec, local,
    )
    worked = expert_layer(token_near, grad_near, grad_late, gate_near, w_gate, w_up, w_down)
    produced = worked[:groups]
    token_back_rows, dots, expert_sum, beside = worked[groups:]
    dx1, small, da_near = token_back(
        x1, h2, grad, prob, previous_t, route_ids, targets, token_back_rows, dots, dgate_zero,
        dh_zero, gain2, router_t, zero_sums,
    )
    expert_now, da_near = lax.optimization_barrier((expert_sum, da_near))
    over = swap(expert_now, "ctx", 2)
    y_near = [swap(produced[g], "exp", g) if g else produced[0] for g in range(groups)]
    dqkv, out_sum = attend_back(
        meta, q, k, v, kt, da_near, w_out_parts, ot, lse, deal_block, layout
    )

    input_grad, qkv_near, out_near, small, norm1_grad, top_all, result = finish(
        dqkv, h1, x, gain1, dx1, weights_t, out_sum, small, tops, y_near, base, targets
    )
    over, qkv_near = lax.optimization_barrier((over, qkv_near))
    corner = swap(over, "ctx", 1)
    near = [[(a, n) for a in (expert_sum, beside, over, corner)] for n in range(3)]
    dense = place_dense(meta, qkv_near, out_near, top_all, small, w_qkv, const_vec.shape[0])
    qkv_grad, out_grad, clipped, router_grad, norm2_grad, vec_grad, logit_grad, carry_grad = dense
    router_grad, logit_grad = jnp.transpose(router_grad), jnp.swapaxes(logit_grad, 1, 2)
    out_grad = out_grad.reshape(width, width)
    gate_grad, up_grad, down_grad = place_experts(meta, near, (False, False, True))
    return (
        result[None],
        input_grad[None],
        norm1_grad,
        norm2_grad,
        qkv_grad,
        out_grad,
        router_grad,
        carry_grad,
        logit_grad,
        vec_grad,
        gate_grad,
        up_grad,
        down_grad,
        clipped,
    )


def solution(mesh):
    tokens = P(("dp", "exp"), "ctx", None)
    packs = P(("dp", "exp"), None)
    experts = P("exp", None, None)
    in_specs = (
        tokens, packs, packs, tokens, tokens, P(), P(), P(), P(), P(), P(), P(), P(),
        experts, experts, experts, tokens,
    )
    out_specs = (
        tokens, tokens, P(), P(), P(), P(), P(), P(), P(), P(),
        P("exp", None, "dp"), P("exp", None, "dp"), P("exp", "dp", None), P(),
    )
    return jax.shard_map(shards, mesh=mesh, in_specs=in_specs, out_specs=out_specs, check_vma=False)
```

```python
import math

import jax
import jax.numpy as jnp
from jax import lax
from jax.experimental import pallas as pl
from jax.experimental.pallas import tpu as pltpu
from jax.sharding import PartitionSpec as P

HEADS = 12
CAP = 128

norm_eps = 1e-05
clip_limit = 3.0
low_start = -1e30
mask_fill = -3e38
highest = lax.Precision.HIGHEST
NN = (((1,), (0,)), ((), ()))
NT = (((1,), (1,)), ((), ()))
TN = (((0,), (0,)), ((), ()))
f32 = jnp.float32
bf16 = jnp.bfloat16
MESH = pl.DeviceIdType.MESH


def mm(left, right, dims=NN):
    return lax.dot_general(left, right, dims, preferred_element_type=f32)


def mm_full(left, right, dims=NN):
    return lax.dot_general(left, right, dims, precision=highest, preferred_element_type=f32)


def shape_of(shape, dtype):
    return jax.ShapeDtypeStruct(shape, dtype)


def whole(array):
    rank = len(array.shape)
    return pl.BlockSpec(array.shape, lambda *_: (0,) * rank)


def cost(flops, moved, exps=0):
    return pl.CostEstimate(flops=int(flops), bytes_accessed=int(moved), transcendentals=int(exps))


def run(body, grid, inputs, outputs, scratch=(), meta=None, flops=0, moved=0, exps=0, aliases=None, talks=None):
    prefetch = 0 if meta is None else 1
    args = ([] if meta is None else [meta]) + [a for a, _ in inputs]
    return pl.pallas_call(
        body,
        out_shape=[o for o, _ in outputs],
        grid_spec=pltpu.PrefetchScalarGridSpec(
            num_scalar_prefetch=prefetch,
            grid=grid,
            in_specs=[s for _, s in inputs],
            out_specs=[s for _, s in outputs],
            scratch_shapes=list(scratch),
        ),
        compiler_params=pltpu.CompilerParams(
            dimension_semantics=("arbitrary",) * len(grid),
            vmem_limit_bytes=63 * 1024 * 1024,
            collective_id=talks,
            has_side_effects=talks is not None,
        ),
        cost_estimate=cost(flops, moved, exps),
        input_output_aliases={} if aliases is None else aliases,
    )(*args)


def swap(value, axis, distance):
    count = lax.axis_size(axis)
    return lax.ppermute(value, axis, [(i, i ^ distance) for i in range(count)])


def flip(value, bits):
    bit = 1
    while bit <= bits:
        if bits & bit:
            value = value + bit - 2 * bit * lax.rem(lax.div(value, bit), 2)
        bit *= 2
    return value


def powers(axis):
    found, bit = [], 1
    while bit < lax.axis_size(axis):
        found.append(bit)
        bit *= 2
    return found


def slot_peer(r, count, exp_now, me):
    return {"exp": flip(exp_now, r // count), "ctx": flip(me, 2 * (r % count))}


def slot_swap(value, r, count):
    groups = lax.axis_size("exp")
    total = groups * lax.axis_size("ctx")
    apart = 2 * (r % count) * groups + r // count
    return lax.ppermute(value, ("ctx", "exp"), [(i, i ^ apart) for i in range(total)])


def remote(src, dst, sent, arrived, peer):
    return pltpu.make_async_remote_copy(
        src_ref=src, dst_ref=dst, send_sem=sent, recv_sem=arrived,
        device_id=peer, device_id_type=MESH,
    )


def greet(peers):
    barrier = pltpu.get_barrier_semaphore()
    for peer in peers:
        pl.semaphore_signal(barrier, inc=1, device_id=peer, device_id_type=MESH)
    return lambda: pl.semaphore_wait(barrier, len(peers))


anywhere = pl.BlockSpec(memory_space=pl.ANY)
scalars = pl.BlockSpec(memory_space=pltpu.SMEM)
vector = pl.BlockSpec(memory_space=pltpu.VMEM)
dma = pltpu.SemaphoreType.DMA


def add_low(*terms):
    total = terms[0].astype(f32)
    for term in terms[1:]:
        total = total + term.astype(f32)
    return total.astype(bf16)


def begin(x, grad, routes, gain, w_qkv, local):
    rows, width = x.shape
    members, groups = lax.axis_size("ctx"), lax.axis_size("exp")
    group_rows = rows * members
    heads = HEADS // members
    head_width = width // HEADS
    columns = heads * head_width
    places = groups * local
    odd = [r for r in range(places) if r % local]
    scale = head_width**-0.5
    tile = min(256, rows)
    per_member = rows // tile

    def body(*refs):
        x_hbm, dy_ref, route_ref, gain_ref, w_hbm = refs[:5]
        q_out, k_out, v_out, kt_out, vt_out, h_out, wt_out = refs[5:12]
        target_out, target_rows, chosen_out, near_out = refs[12:16]
        rest_out, refs = refs[16 : 16 + len(odd)], refs[:16] + refs[16 + len(odd) :]
        x_near, w_in, w_t, q_all, k_all, v_all, kt_all, vt_all, h_all, packed, near = refs[16:27]
        load_sem, x_s, x_r, r_s, r_r, out_sem, near_sem = refs[27:]
        me, exp_now = lax.axis_index("ctx"), lax.axis_index("exp")
        side = lax.div(me, 2)
        peers = [{"ctx": flip(me, 1)}, {"ctx": flip(me, 2)}]
        peers += [slot_peer(local * g, local, exp_now, me) for g in range(1, groups)]
        ready = greet(peers)
        own = pltpu.make_async_copy(x_hbm, x_near.at[0], load_sem.at[0])
        weights = pltpu.make_async_copy(w_hbm, w_in, load_sem.at[1])
        own.start()
        weights.start()

        def some(t):
            return pl.ds(pl.multiple_of(t * tile, tile), tile)

        def across(t):
            n = 2 + t
            return remote(
                x_hbm.at[some(t), :], x_near.at[2, some(t), :], x_s.at[n], x_r.at[n],
                {"ctx": flip(me, 2)},
            )

        def beside():
            return remote(x_hbm, x_near.at[1], x_s.at[1], x_r.at[1], {"ctx": flip(me, 1)})

        def passed(t):
            n = 2 + per_member + t
            return remote(
                x_near.at[2, some(t), :], x_near.at[3, some(t), :], x_s.at[n], x_r.at[n],
                {"ctx": flip(me, 1)},
            )

        def row_copy(g):
            return remote(
                packed.at[g], near.at[g], r_s.at[g], r_r.at[g],
                slot_peer(local * g, local, exp_now, me),
            )

        ready()
        for t in range(per_member):
            across(t).start()
        beside().start()

        lines = jnp.concatenate([route_ref[...].astype(f32), jnp.zeros((6, rows), f32)], axis=0)
        chosen = jnp.transpose(lines)[:, 0:2].astype(jnp.int32)
        chosen_out[...] = chosen
        expert_count = places
        lanes = lax.broadcasted_iota(jnp.int32, (rows, 128), 1)
        hits = [lanes == chosen[:, c : c + 1] for c in range(2)]
        hit = jnp.where((hits[0] | hits[1]) & (lanes < expert_count), 1.0, 0.0)
        later = lax.broadcasted_iota(jnp.int32, (rows, rows), 0)
        sooner = lax.broadcasted_iota(jnp.int32, (rows, rows), 1)
        ahead = mm(jnp.where(sooner < later, 1.0, 0.0).astype(bf16), hit.astype(bf16))
        spots = []
        for c in range(2):
            ids = chosen[:, c : c + 1]
            rank = jnp.sum(jnp.where(hits[c], ahead, 0.0), axis=1, keepdims=True).astype(jnp.int32)
            far_z = lax.div(ids, local)
            far_y = lax.rem(ids, local)
            z = jnp.zeros_like(ids)
            bit = 1
            while bit < groups:
                z = z + bit * jnp.where(
                    lax.rem(lax.div(far_z, bit), 2) == lax.rem(lax.div(exp_now, bit), 2), 0, 1
                )
                bit *= 2
            y = jnp.where(far_y == side, 0, 1)
            spots.append(jnp.where(ids < expert_count, (z * local + y) * CAP + rank, -1))
        target_out[...] = jnp.concatenate(spots, axis=1)
        wide = jnp.where(lanes == 0, spots[0], spots[1]).astype(f32)
        target_rows[...] = jnp.transpose(wide)[0:2, :].astype(jnp.int32)

        def pack(n, r):
            packed[n] = mm(slot_choice(r * CAP, CAP, target_rows), dy_ref[...]).astype(bf16)

        for g in range(groups - 1, -1, -1):
            pack(g, local * g)
            if g < groups - 1:
                row_copy(g + 1).start()
        for n, r in enumerate(odd):
            pack(groups + n, r)
        stores = [
            pltpu.make_async_copy(packed.at[0], near_out.at[0], near_sem.at[0]),
        ] + [
            pltpu.make_async_copy(packed.at[groups + n], rest_out[n], near_sem.at[groups + n])
            for n in range(len(odd))
        ]
        for copy in stores:
            copy.start()
        weights.wait()
        for w in range(3):
            w_t[w] = jnp.transpose(w_in[w])
        w_store = pltpu.make_async_copy(w_t, wt_out, load_sem.at[2])
        w_store.start()
        here = pl.ds(pl.multiple_of(me * columns, columns), columns)

        def chunk(j):
            def project(t, _):
                if j == 2:
                    across(t).wait()
                    passed(t).start()
                if j == 3:
                    passed(t).wait()
                at = pl.multiple_of(t * tile, tile)
                to = pl.ds(pl.multiple_of(j * rows + t * tile, tile), tile)
                value = x_near[j, pl.ds(at, tile), :].astype(f32)
                inverse = lax.rsqrt(jnp.mean(value * value, axis=1, keepdims=True) + norm_eps)
                low = (value * inverse * gain_ref[...]).astype(bf16)
                h_all[to, :] = low
                q = mm(low, w_t[0, here, :], NT).astype(bf16) * jnp.asarray(scale, bf16)
                k = mm(low, w_t[1, here, :], NT).astype(bf16)
                v = mm(low, w_t[2, here, :], NT).astype(bf16)
                for h in range(heads):
                    part = slice(h * head_width, (h + 1) * head_width)
                    q_all[h, to, :] = q[:, part]
                    k_all[h, to, :] = k[:, part]
                    v_all[h, to, :] = v[:, part]
                kt_all[:, to] = mm(w_t[1, here, :], low, NT).astype(bf16)
                vt_all[:, to] = mm(w_t[2, here, :], low, NT).astype(bf16)
                return 0

            lax.fori_loop(0, per_member, project, 0)
            for copy in chunk_stores(j):
                copy.start()

        def chunk_stores(j):
            to = pl.ds(j * rows, rows)
            pairs = [(q_all, q_out), (k_all, k_out), (v_all, v_out)]
            found = [(a.at[:, to, :], b.at[:, to, :]) for a, b in pairs]
            found += [(a.at[:, to], b.at[:, to]) for a, b in ((kt_all, kt_out), (vt_all, vt_out))]
            found += [(h_all.at[to, :], h_out.at[to, :])]
            return [
                pltpu.make_async_copy(a, b, out_sem.at[6 * j + n]) for n, (a, b) in enumerate(found)
            ]

        own.wait()
        chunk(0)
        beside().wait()
        chunk(1)
        chunk(2)
        chunk(3)
        for g in range(1, groups):
            row_copy(g).wait()
            pltpu.make_async_copy(near.at[g], near_out.at[g], near_sem.at[g]).start()
        for copy in stores:
            copy.wait()
        w_store.wait()
        for j in range(members):
            for copy in chunk_stores(j):
                copy.wait()
        for g in range(1, groups):
            pltpu.make_async_copy(near.at[g], near_out.at[g], near_sem.at[g]).wait()

    by_head = (heads, group_rows, head_width)
    by_column = (columns, group_rows)
    slots = (places, CAP, width)
    return run(
        body,
        (),
        [(x, anywhere), (grad, vector), (routes, vector), (gain, vector), (w_qkv, anywhere)],
        [(shape_of(by_head, bf16), anywhere)] * 3
        + [(shape_of(by_column, bf16), anywhere)] * 2
        + [(shape_of((group_rows, width), bf16), anywhere)]
        + [(shape_of((3, width, width), bf16), anywhere)]
        + [(shape_of((rows, 2), jnp.int32), vector), (shape_of((2, rows), jnp.int32), vector)]
        + [(shape_of((rows, 2), jnp.int32), vector)]
        + [(shape_of((groups, CAP, width), bf16), anywhere)]
        + [(shape_of((CAP, width), bf16), anywhere)] * len(odd),
        scratch=[
            pltpu.VMEM((members, rows, width), bf16),
            pltpu.VMEM((3, width, width), bf16),
            pltpu.VMEM((3, width, width), bf16),
            pltpu.VMEM(by_head, bf16), pltpu.VMEM(by_head, bf16), pltpu.VMEM(by_head, bf16),
            pltpu.VMEM(by_column, bf16), pltpu.VMEM(by_column, bf16),
            pltpu.VMEM((group_rows, width), bf16),
            pltpu.VMEM(slots, bf16), pltpu.VMEM(slots, bf16),
            dma((3,)), dma((2 + 2 * per_member,)), dma((2 + 2 * per_member,)),
            dma((places,)), dma((places,)), dma((6 * members,)), dma((places + 1,)),
        ],
        flops=2 * group_rows * width * columns * 5,
        moved=20 * 1024 * 1024,
        talks=4,
    )


def document_start(meta_ref, position, layout):
    start = jnp.zeros_like(position)
    end = jnp.int32(0)
    for s in range(layout["sequences"]):
        end = end + meta_ref[layout["lengths"] + s]
        start = jnp.where(position >= end, end, start)
    return start


def block_range(meta_ref, query_block, key_block, rows, layout):
    q_first = query_block * rows
    k_first = key_block * rows
    begin = document_start(meta_ref, q_first, layout)
    begin_last = document_start(meta_ref, q_first + rows - 1, layout)
    needed = (k_first <= q_first) & (k_first + rows - 1 >= begin)
    full = (k_first < q_first) & (k_first >= begin_last)
    return q_first, k_first, needed, full


def allowed_pairs(meta_ref, q_first, k_first, rows, layout):
    q_pos = q_first + lax.broadcasted_iota(jnp.int32, (1, rows), 1)
    k_pos = k_first + lax.broadcasted_iota(jnp.int32, (rows, 1), 0)
    return (k_pos <= q_pos) & (k_pos >= document_start(meta_ref, q_pos, layout))


def attend(meta, q, k, vt, rows, layout):
    heads, group_rows, head_width = q.shape
    blocks = group_rows // rows
    width = heads * head_width

    def body(meta_ref, q_ref, k_ref, vt_ref, o_ref, ot_ref, lse_ref, top_ref, m_ref, l_ref, a_ref, qt_ref):
        i = pl.program_id(0)
        m_ref[...] = jnp.full_like(m_ref, low_start)
        l_ref[...] = jnp.zeros_like(l_ref)
        a_ref[...] = jnp.zeros_like(a_ref)
        for h in range(heads):
            qt_ref[h] = jnp.transpose(q_ref[h])

        def one(j, _):
            q_first, k_first, needed, full = block_range(meta_ref, i, j, rows, layout)
            at = pl.multiple_of(meta_ref[layout["inverse"] + j] * rows, rows)

            def step(masked):
                if masked:
                    allowed = allowed_pairs(meta_ref, q_first, k_first, rows, layout)
                scores = [mm(k_ref[h, pl.ds(at, rows), :], qt_ref[h]) for h in range(heads)]
                if masked:
                    scores = [jnp.where(allowed, s, mask_fill) for s in scores]
                olds = [m_ref[h] for h in range(heads)]
                news = [
                    jnp.maximum(old, jnp.max(s, axis=0, keepdims=True))
                    for old, s in zip(olds, scores)
                ]
                chances = [jnp.exp(s - new) for s, new in zip(scores, news)]
                mixed = [
                    mm(
                        vt_ref[h * head_width : (h + 1) * head_width, pl.ds(at, rows)],
                        chances[h].astype(bf16),
                    )
                    for h in range(heads)
                ]
                for h in range(heads):
                    part = slice(h * head_width, (h + 1) * head_width)
                    shrink = jnp.exp(olds[h] - news[h])
                    m_ref[h] = news[h]
                    l_ref[h] = l_ref[h] * shrink + jnp.sum(chances[h], axis=0, keepdims=True)
                    a_ref[part, :] = a_ref[part, :] * shrink + mixed[h]

            @pl.when(full)
            def _():
                step(False)

            @pl.when(needed & jnp.logical_not(full))
            def _():
                step(True)

            return 0

        lax.fori_loop(0, i + 1, one, 0)
        for h in range(heads):
            part = slice(h * head_width, (h + 1) * head_width)
            ot_ref[part, :] = a_ref[part, :] / l_ref[h]
            lse_ref[pl.ds(h, 1), :] = m_ref[h] + jnp.log(l_ref[h])
            top = m_ref[h]

            @pl.when(i == 0)
            def _():
                top_ref[pl.ds(h, 1), :] = top

            @pl.when(i > 0)
            def _():
                top_ref[pl.ds(h, 1), :] = jnp.maximum(top_ref[pl.ds(h, 1), :], top)

        o_ref[...] = jnp.transpose(ot_ref[...]).astype(bf16)

    row = shape_of((heads, group_rows), f32)
    row_spec = pl.BlockSpec((heads, rows), lambda i, m: (0, i))
    return run(
        body,
        (blocks,),
        [
            (
                q,
                pl.BlockSpec(
                    (heads, rows, head_width), lambda i, m: (0, m[layout["inverse"] + i], 0)
                ),
            ),
            (k, whole(k)),
            (vt, whole(vt)),
        ],
        [
            (
                shape_of((group_rows, width), bf16),
                pl.BlockSpec((rows, width), lambda i, m: (m[layout["inverse"] + i], 0)),
            ),
            (shape_of((width, group_rows), f32), pl.BlockSpec((width, rows), lambda i, m: (0, i))),
            (row, row_spec),
            (shape_of((heads, rows), f32), pl.BlockSpec((heads, rows), lambda i, m: (0, 0))),
        ],
        scratch=[
            pltpu.VMEM((heads, 1, rows), f32),
            pltpu.VMEM((heads, 1, rows), f32),
            pltpu.VMEM((width, rows), f32),
            pltpu.VMEM((heads, head_width, rows), bf16),
        ],
        meta=meta,
        flops=2 * 2 * group_rows * group_rows * width,
        moved=group_rows * width * 14,
        exps=group_rows * group_rows * heads // 2,
    )


def attend_back(meta, q, k, v, kt, grad, w_out, ot, lse, rows, layout, shares):
    heads, group_rows, head_width = q.shape
    blocks = group_rows // rows
    width = heads * head_width
    scale = head_width**-0.5
    per = grad.shape[1] // rows

    _, half, lanes = shares[0].shape
    tall = 2 * half // blocks
    wide = lanes // blocks if lanes // blocks >= 128 else lanes
    last = lanes // wide

    def body(meta_ref, q_ref, k_ref, v_ref, kt_ref, grad_ref, w_ref, *refs):
        ot_ref, lse_ref = refs[:2]
        flat_refs, turned_refs = refs[2:6], refs[6:8]
        up_outs, down_out = refs[10:12], refs[12]
        refs = refs[:2] + refs[8:10] + refs[13:]
        ot_ref, lse_ref, out_ref, rows_ref, dk_ref, dv_ref, dq_ref, g_ref, delta_ref, sum_ref, qt_ref, gt_ref = refs
        i = pl.program_id(0)

        @pl.when(i == 0)
        def _():
            dk_ref[...] = jnp.zeros_like(dk_ref)
            dv_ref[...] = jnp.zeros_like(dv_ref)

        core = lax.div(i, blocks // 2)
        for n in range(2):

            @pl.when(core == (meta_ref[2] ^ n))
            def _():
                for g in range(2):
                    up_outs[g][0] = flat_refs[2 * n + g][0].astype(f32)

        @pl.when(i < last)
        def _():
            for n in range(2):
                to = pl.multiple_of((meta_ref[2] ^ n) * half, half)
                down_out[0, :, pl.ds(to, half)] = jnp.transpose(turned_refs[n][0].astype(f32))

        da = grad_ref[0]
        g = mm(da, w_ref[0], NT).astype(bf16)
        part_sum = mm(ot_ref[...].astype(bf16), da)

        @pl.when(i == 0)
        def _():
            sum_ref[...] = part_sum

        @pl.when(i > 0)
        def _():
            sum_ref[...] += part_sum

        for h in range(heads):
            g_ref[h] = g[:, h * head_width : (h + 1) * head_width]
        turned = jnp.transpose(g.astype(f32))
        gt_ref[...] = turned.astype(bf16)
        for h in range(heads):
            qt_ref[h] = jnp.transpose(q_ref[h])
        product = turned * ot_ref[...]
        for h in range(heads):
            part = slice(h * head_width, (h + 1) * head_width)
            delta_ref[h] = jnp.sum(product[part, :], axis=0, keepdims=True)

        dq_ref[...] = jnp.zeros_like(dq_ref)

        def one(j, _):
            q_first, k_first, needed, full = block_range(meta_ref, i, j, rows, layout)
            at = pl.multiple_of(meta_ref[layout["inverse"] + j] * rows, rows)
            to = pl.multiple_of(j * rows, rows)

            def step(masked):
                if masked:
                    allowed = allowed_pairs(meta_ref, q_first, k_first, rows, layout)
                parts = [slice(h * head_width, (h + 1) * head_width) for h in range(heads)]
                scores = [mm(k_ref[h, pl.ds(at, rows), :], qt_ref[h]) for h in range(heads)]
                downs = [
                    mm(v_ref[h, pl.ds(at, rows), :], gt_ref[parts[h], :]) for h in range(heads)
                ]
                if masked:
                    scores = [jnp.where(allowed, s, mask_fill) for s in scores]
                chances = [jnp.exp(scores[h] - lse_ref[pl.ds(h, 1), :]) for h in range(heads)]
                slopes = [
                    (chances[h] * (downs[h] - delta_ref[h])).astype(bf16) for h in range(heads)
                ]
                for h in range(heads):
                    dv_ref[h, pl.ds(to, rows), :] += mm(chances[h].astype(bf16), g_ref[h])
                    dk_ref[h, pl.ds(to, rows), :] += mm(slopes[h], q_ref[h])
                    dq_ref[parts[h], :] += mm(kt_ref[parts[h], pl.ds(at, rows)], slopes[h])

            @pl.when(full)
            def _():
                step(False)

            @pl.when(needed & jnp.logical_not(full))
            def _():
                step(True)

            return 0

        lax.fori_loop(0, i + 1, one, 0)
        here = pl.multiple_of(meta_ref[layout["inverse"] + i] * rows, rows)
        out_ref[pl.ds(here, rows), 0:width] = (jnp.transpose(dq_ref[...]) * scale).astype(bf16)

        @pl.when(i == blocks - 1)
        def _():
            rows_ref[...] = sum_ref[...].astype(bf16)

            def store(b, _):
                spot = pl.multiple_of(b * rows, rows)
                there = pl.multiple_of(meta_ref[layout["inverse"] + b] * rows, rows)
                out_ref[pl.ds(there, rows), width : 3 * width] = jnp.concatenate(
                    [dk_ref[h, pl.ds(spot, rows), :] for h in range(heads)]
                    + [dv_ref[h, pl.ds(spot, rows), :] for h in range(heads)],
                    axis=1,
                ).astype(bf16)
                return 0

            lax.fori_loop(0, blocks, store, 0)

    def flat_spec(g, n):
        def index(i, m):
            now = jnp.clip(i - (m[2] ^ n) * (blocks // 2), 0, blocks // 2 - 1)
            return (g, now, 0)

        return pl.BlockSpec((1, tall, lanes), index)

    def turned_place(i, m):
        return (2, 0, jnp.minimum(i, last - 1))

    local = layout["sides"]
    placed = [
        (
            shape_of((local, 2 * half, lanes), f32),
            pl.BlockSpec((1, tall, lanes), lambda i, m: (m[3], i, 0)),
        )
    ] * 2 + [
        (
            shape_of((local, lanes, 2 * half), f32),
            pl.BlockSpec(
                (1, wide, 2 * half), lambda i, m: (m[3], jnp.minimum(i, last - 1), 0)
            ),
        )
    ]
    out = shape_of((group_rows, 3 * width), bf16)
    out_rows = shape_of((width, grad.shape[2]), bf16)
    return run(
        body,
        (blocks,),
        [
            (
                q,
                pl.BlockSpec(
                    (heads, rows, head_width), lambda i, m: (0, m[layout["inverse"] + i], 0)
                ),
            ),
            (k, whole(k)),
            (v, whole(v)),
            (kt, whole(kt)),
        ]
        + [
            (
                grad,
                pl.BlockSpec(
                    (1, rows, grad.shape[2]),
                    lambda i, m: (
                        m[layout["inverse"] + i] // per, m[layout["inverse"] + i] % per, 0
                    ),
                ),
            ),
            (w_out, pl.BlockSpec((1, width, grad.shape[2]), lambda i, m: (m[0], 0, 0))),
            (ot, pl.BlockSpec((width, rows), lambda i, m: (0, i))),
            (lse, pl.BlockSpec((heads, rows), lambda i, m: (0, i))),
        ]
        + [(shares[n], flat_spec(g, n)) for n in range(2) for g in range(2)]
        + [(shares[n], pl.BlockSpec((1, half, wide), turned_place)) for n in range(2)],
        [(out, whole(out)), (out_rows, whole(out_rows))] + placed,
        scratch=[
            pltpu.VMEM((heads, group_rows, head_width), f32),
            pltpu.VMEM((heads, group_rows, head_width), f32),
            pltpu.VMEM((width, rows), f32),
            pltpu.VMEM((heads, rows, head_width), bf16),
            pltpu.VMEM((heads, 1, rows), f32),
            pltpu.VMEM((width, grad.shape[2]), f32),
            pltpu.VMEM((heads, head_width, rows), bf16),
            pltpu.VMEM((width, rows), bf16),
        ],
        meta=meta,
        flops=5 * 2 * group_rows * group_rows * width,
        moved=group_rows * width * 24,
        exps=group_rows * group_rows * heads // 2,
    )


def slot_choice(first, count, target_ref):
    rows = target_ref.shape[1]
    ids = first + lax.broadcasted_iota(jnp.int32, (count, rows), 0)
    match = (ids == target_ref[0:1, :]) | (ids == target_ref[1:2, :])
    return jnp.where(match, 1.0, 0.0).astype(bf16)


def token_front(
    x, o, w_out, gain, router_t, previous_t, w_carry, target_rows, grad, routes, logit_w, vectors, local
):
    rows, width = x.shape
    members, columns = w_out.shape[0], w_out.shape[1]
    expert_all = router_t.shape[0]
    groups = lax.axis_size("exp")
    places = groups * local
    expert_count = places
    kinds = vectors.shape[0]
    tile = 128

    def body(*refs):
        (x_ref, o_hbm, w_ref, gain_ref, router_ref, prev_ref, carry_ref, target_ref) = refs[:8]
        dy_ref, route_ref, lw_ref, vec_ref = refs[8:12]
        x1_ref, h2_ref, prob_ref, rows_out, gates_out, base_ref, dh_ref, dgate_ref, sums_ref = refs[12:21]
        o_near, low, split, packed, arrived, gate_mine, gate_near = refs[21:28]
        o_s, o_r, t_s, t_r, g_s, g_r, out_sem = refs[28:]
        me, exp_now = lax.axis_index("ctx"), lax.axis_index("exp")
        side = lax.div(me, 2)
        peers = [{"ctx": flip(me, j)} for j in range(1, members)]
        peers += [slot_peer(r, local, exp_now, me) for r in range(local, places)]
        ready = greet(peers)

        own_o = pltpu.make_async_copy(o_hbm.at[pl.ds(0, rows), :], o_near.at[0], o_r.at[0])

        def o_copy(j, t):
            src = o_hbm.at[pl.ds(pl.multiple_of(j * rows + t * tile, tile), tile), :]
            dst = o_near.at[j, pl.ds(pl.multiple_of(t * tile, tile), tile), :]
            n = j * (rows // tile) + t
            return remote(src, dst, o_s.at[n], o_r.at[n], {"ctx": flip(me, j)})

        def row_copy(r):
            return remote(
                packed.at[r], arrived.at[r], t_s.at[r], t_r.at[r], slot_peer(r, local, exp_now, me)
            )

        def gate_copy(r):
            return remote(
                gate_mine.at[r], gate_near.at[r], g_s.at[r], g_r.at[r],
                slot_peer(r, local, exp_now, me),
            )

        own_o.start()
        ready()
        for t in range(rows // tile):
            for j in range(members - 1, 0, -1):
                o_copy(j, t).start()
        own_o.wait()

        def front_rows(t, _):
            here = pl.ds(pl.multiple_of(t * tile, tile), tile)
            total = x_ref[here, :].astype(f32) + mm(o_near[0, here, :], w_ref[me])
            for j in range(1, members):
                o_copy(j, t).wait()
            for j in range(1, members):
                total = total + mm(o_near[j, here, :], w_ref[flip(me, j)])
            x1_ref[here, :] = total
            inverse = lax.rsqrt(jnp.mean(total * total, axis=1, keepdims=True) + norm_eps)
            h2 = total * inverse * gain_ref[...]
            h2_ref[here, :] = h2
            logits = mm_full(h2, router_ref[...], NT) + mm_full(
                prev_ref[:, here], carry_ref[...], TN
            )
            shifted = jnp.exp(logits - jnp.max(logits, axis=1, keepdims=True))
            prob = shifted / jnp.sum(shifted, axis=1, keepdims=True)
            prob_ref[here, :] = prob
            low[here, :] = h2.astype(bf16)
            top = prob.astype(bf16)
            rest = prob - top.astype(f32)
            middle = rest.astype(bf16)
            split[0, here, :] = top
            split[1, here, :] = middle
            split[2, here, :] = (rest - middle.astype(f32)).astype(bf16)
            return 0

        lax.fori_loop(0, rows // tile, front_rows, 0)
        diagonal = lax.broadcasted_iota(jnp.int32, (CAP, CAP), 0) == lax.broadcasted_iota(
            jnp.int32, (CAP, CAP), 1
        )
        lanes = lax.broadcasted_iota(jnp.int32, (CAP, expert_all), 1)
        for r in list(range(1, places)) + [0]:
            choice = slot_choice(r * CAP, CAP, target_ref)
            packed[r] = mm(choice, low[...]).astype(bf16)
            picked = mm(choice, split[0]) + mm(choice, split[1]) + mm(choice, split[2])
            expert = flip(exp_now, r // local) * local + flip(side, r % local)
            column = jnp.sum(jnp.where(lanes == expert, picked, 0.0), axis=1, keepdims=True)
            gate_mine[r] = jnp.sum(jnp.where(diagonal, column, 0.0), axis=0, keepdims=True)
            last = r - 1 if r else places - 1
            if last:
                row_copy(last).start()
                gate_copy(last).start()

        def own_copy(n):
            src, dst = (packed, rows_out) if n == 0 else (gate_mine, gates_out)
            return pltpu.make_async_copy(src.at[0], dst.at[0], out_sem.at[n])

        own_copy(0).start()
        own_copy(1).start()

        def zero_rows(t, _):
            here = pl.ds(pl.multiple_of(t * tile, tile), tile)
            h2 = h2_ref[here, :]
            dy = dy_ref[here, :].astype(f32)
            prob_now = prob_ref[here, :]
            classes = lax.broadcasted_iota(jnp.int32, (tile, expert_all), 1)
            chosen = route_ref[here, :]
            ids = [chosen[:, c : c + 1] for c in range(2)]
            gates = [
                jnp.sum(jnp.where(classes == r, prob_now, 0.0), axis=1, keepdims=True) for r in ids
            ]
            along = jnp.sum(dy * h2, axis=1, keepdims=True)
            copies = [(r == expert_count + 1).astype(f32) for r in ids]
            keep = copies[0] * gates[0] + copies[1] * gates[1]
            dgates = [copies[c] * along for c in range(2)]
            scores = [
                jnp.sum(h2 * lw_ref[n : n + 1, :], axis=1, keepdims=True) for n in range(2 * kinds)
            ]
            base = x1_ref[here, :]
            dh = jnp.zeros_like(h2)
            for j in range(kinds):
                top = jnp.maximum(scores[2 * j], scores[2 * j + 1])
                e0 = jnp.exp(scores[2 * j] - top)
                e1 = jnp.exp(scores[2 * j + 1] - top)
                a0 = e0 / (e0 + e1)
                a1 = e1 / (e0 + e1)
                vec = vec_ref[j : j + 1, :]
                along_vec = jnp.sum(dy * vec, axis=1, keepdims=True)
                these = [(r == expert_count + 2 + j).astype(f32) for r in ids]
                weight = these[0] * gates[0] + these[1] * gates[1]
                for c in range(2):
                    dgates[c] = dgates[c] + these[c] * (a0 * along + a1 * along_vec)
                keep = keep + weight * a0
                base = base + (weight * a1) * vec
                d0 = weight * along
                d1 = weight * along_vec
                mean = a0 * d0 + a1 * d1
                z0 = a0 * (d0 - mean)
                z1 = a1 * (d1 - mean)
                dh = dh + z0 * lw_ref[2 * j : 2 * j + 1, :] + z1 * lw_ref[2 * j + 1 : 2 * j + 2, :]
                sums_ref[j : j + 1, :] += jnp.sum((weight * a1) * dy, axis=0, keepdims=True)
                at = kinds + 2 * j
                sums_ref[at : at + 1, :] += jnp.sum(z0 * h2, axis=0, keepdims=True)
                sums_ref[at + 1 : at + 2, :] += jnp.sum(z1 * h2, axis=0, keepdims=True)
            base_ref[here, :] = base + keep * h2
            dh_ref[here, :] = dh + keep * dy
            dgate_ref[here, :] = jnp.concatenate(dgates, axis=1)
            return 0

        sums_ref[...] = jnp.zeros_like(sums_ref)
        lax.fori_loop(0, rows // tile, zero_rows, 0)

        def rows_store(r):
            return pltpu.make_async_copy(arrived.at[r], rows_out.at[r], out_sem.at[2 * r])

        def gates_store(r):
            return pltpu.make_async_copy(gate_near.at[r], gates_out.at[r], out_sem.at[2 * r + 1])

        for r in range(1, places):
            row_copy(r).wait()
            gate_copy(r).wait()
            rows_store(r).start()
            gates_store(r).start()
        own_copy(0).wait()
        own_copy(1).wait()
        for r in range(1, places):
            rows_store(r).wait()
            gates_store(r).wait()

    wide = shape_of((rows, width), f32)
    placed = shape_of((places, CAP, width), bf16)
    lines = shape_of((places, 1, CAP), f32)
    return run(
        body,
        (),
        [(x, vector), (o, anywhere), (w_out, vector), (gain, vector), (router_t, vector)]
        + [(previous_t, vector), (w_carry, vector), (target_rows, vector), (grad, vector)]
        + [(routes, vector), (logit_w, vector), (vectors, vector)],
        [(wide, vector), (wide, vector), (shape_of((rows, expert_all), f32), vector)]
        + [(placed, anywhere), (lines, anywhere), (wide, vector), (wide, vector)]
        + [(shape_of((rows, 2), f32), vector), (shape_of((3 * kinds, width), f32), vector)],
        scratch=[
            pltpu.VMEM((members, rows, columns), bf16),
            pltpu.VMEM((rows, width), bf16),
            pltpu.VMEM((3, rows, expert_all), bf16),
            pltpu.VMEM((places, CAP, width), bf16),
            pltpu.VMEM((places, CAP, width), bf16),
            pltpu.VMEM((places, 1, CAP), f32),
            pltpu.VMEM((places, 1, CAP), f32),
            dma((members * (rows // tile),)), dma((members * (rows // tile),)),
            dma((places,)), dma((places,)), dma((places,)), dma((places,)),
            dma((2 * places,)),
        ],
        flops=2 * rows * width * (width + places * CAP),
        moved=rows * width * 30,
        talks=1,
    )


def expert_layer(arrived, grads, late, gates, w_gate, w_up, w_down):
    places = arrived.shape[0]
    local = w_gate.shape[0]
    rows = places * CAP
    width, hidden = w_gate.shape[1], w_gate.shape[2]
    parts = lax.axis_size("dp")
    groups = places // local
    half = width // 2
    per_part = hidden // parts
    tile = min(256, per_part)
    steps = hidden // tile
    tiles = per_part // tile
    away = steps - tiles
    lead = away // 2
    kept = steps - lead
    chunk = 256

    def body(*refs):
        x_ref, dy_ref, gates_ref, wg_hbm, wu_hbm, wd_hbm = refs[:6]
        dy_late, refs = refs[6 : 6 + len(late)], refs[:6] + refs[6 + len(late) :]
        dy_parts = [
            dy_late[r // local] if r % local else dy_ref.at[r // local] for r in range(places)
        ]
        y_out, refs = refs[6 : 6 + groups], refs[6 + groups :]
        it = iter(refs)

        def take(count):
            return [next(it) for _ in range(count)]

        dx_out, dots_out, sum_out, beside_out = take(4)
        x_all, xt_all, dy_all, dyt_all, gate_all, y_acc, dx_acc, dot_acc = take(8)
        wg_buf, wu_buf, wd_buf, wg_keep, wu_keep, wd_keep = take(6)
        hid_keep, dg_keep, du_keep, scaled_keep = take(4)
        send, total, taken, far, dx_low, dx_near, dots, dots_near = take(8)
        beside, y_odd, relay = take(3)
        in_sem, w_sem, keep_sem, c_s, c_r, f_s, f_r, b_s, b_r, d_s, d_r, out_sem = take(12)
        e_s, e_r, beside_sem, y_s, y_r, dx_sem = take(6)
        me, exp_now, dp_now = lax.axis_index("ctx"), lax.axis_index("exp"), lax.axis_index("dp")
        core, side = lax.rem(me, 2), lax.div(me, 2)
        sibling = {"ctx": flip(me, 1)}
        peers = [sibling] + [{"dp": flip(dp_now, d)} for d in range(1, parts)]
        peers += [slot_peer(r, local, exp_now, me) for r in range(1, places)]
        ready = greet(peers)
        diagonal = lax.broadcasted_iota(jnp.int32, (CAP, CAP), 0) == lax.broadcasted_iota(
            jnp.int32, (CAP, CAP), 1
        )

        def dp_of(f):
            distance = parts - 1 - lax.div(f, tiles)
            found, bit = dp_now, 1
            while bit < parts:
                on = lax.rem(lax.div(distance, bit), 2)
                now = lax.rem(lax.div(found, bit), 2)
                found = found + on * bit * (1 - 2 * now)
                bit *= 2
            return found

        def weights(f, slot):
            at = pl.multiple_of(dp_of(f) * per_part + lax.rem(f, tiles) * tile, tile)
            return [
                pltpu.make_async_copy(
                    wg_hbm.at[side, :, pl.ds(at, tile)], wg_buf.at[slot], w_sem.at[0, slot]
                ),
                pltpu.make_async_copy(
                    wu_hbm.at[side, :, pl.ds(at, tile)], wu_buf.at[slot], w_sem.at[1, slot]
                ),
                pltpu.make_async_copy(
                    wd_hbm.at[side, pl.ds(at, tile), :], wd_buf.at[slot], w_sem.at[2, slot]
                ),
            ]

        def core_copy(f, slot):
            return remote(send.at[slot], taken.at[f], c_s.at[slot], c_r.at[f], sibling)

        def far_copy(f):
            return remote(total.at[f], far.at[f], f_s.at[f], f_r.at[f], {"dp": dp_of(f)})

        def back_copy(r):
            return remote(
                dx_low.at[r], dx_near.at[r], b_s.at[r], b_r.at[r],
                slot_peer(r, local, exp_now, me),
            )

        def dots_copy(r):
            return remote(
                dots.at[r], dots_near.at[r], d_s.at[r], d_r.at[r],
                slot_peer(r, local, exp_now, me),
            )

        def keep_weights(k):
            f = lead + k
            at = pl.multiple_of(dp_of(f) * per_part + (f % tiles) * tile, tile)
            return [
                pltpu.make_async_copy(
                    wg_hbm.at[side, :, pl.ds(at, tile)], wg_keep.at[k], keep_sem.at[0, k]
                ),
                pltpu.make_async_copy(
                    wu_hbm.at[side, :, pl.ds(at, tile)], wu_keep.at[k], keep_sem.at[1, k]
                ),
                pltpu.make_async_copy(
                    wd_hbm.at[side, pl.ds(at, tile), :], wd_keep.at[k], keep_sem.at[2, k]
                ),
            ]

        def rows_in(r):
            here = pl.ds(r * CAP, CAP)
            return [
                pltpu.make_async_copy(x_ref.at[r], x_all.at[here, :], in_sem.at[r]),
                pltpu.make_async_copy(dy_parts[r], dy_all.at[here, :], in_sem.at[places + r]),
            ]

        for r in range(places):
            for copy in rows_in(r):
                copy.start()
        if lead:
            for copy in weights(0, 0):
                copy.start()
        for k in range(kept):
            for copy in keep_weights(k):
                copy.start()
        first_half = pl.ds(pl.multiple_of((1 - core) * half, half), half)
        second_half = pl.ds(pl.multiple_of(core * half, half), half)
        for r in range(places):
            here = slice(r * CAP, (r + 1) * CAP)
            for copy in rows_in(r):
                copy.wait()
            turned = jnp.transpose(x_all[here, :])
            xt_all[first_half, here] = turned[:half, :]
            xt_all[second_half, here] = turned[half:, :]
            turned = jnp.transpose(dy_all[here, :])
            dyt_all[first_half, here] = turned[:half, :]
            dyt_all[second_half, here] = turned[half:, :]
            gate_all[here, :] = jnp.sum(
                jnp.where(diagonal, gates_ref[r], 0.0), axis=1, keepdims=True
            )
        y_acc[...] = jnp.zeros_like(y_acc)
        dx_acc[...] = jnp.zeros_like(dx_acc)
        dot_acc[...] = jnp.zeros_like(dot_acc)
        ready()

        def core_sum(f):
            core_copy(f, lax.rem(f, 2)).wait_recv()
            for n in range(3):
                total[f, n] = (total[f, n].astype(f32) + taken[f, n].astype(f32)).astype(bf16)

        def forward_back(here, wg, wu, wd, hid_ref, dg_ref, du_ref, scaled_ref):
            g_pre = mm(x_all[here, :], wg)
            u_pre = mm(x_all[here, :], wu)
            back = mm(dy_all[here, :], wd, NT)
            gate = gate_all[here, :]
            sig = 1.0 / (1.0 + jnp.exp(-g_pre))
            act = g_pre * sig
            hid = act * u_pre
            hid_ref[here, :] = hid.astype(bf16)
            scaled_ref[here, :] = (gate * hid).astype(bf16)
            along = hid * back
            lines = along[:, 0:128]
            for n in range(1, tile // 128):
                lines = lines + along[:, n * 128 : (n + 1) * 128]
            dot_acc[here, :] += lines
            dhid = gate * back
            dg = (dhid * u_pre * sig * (1.0 + g_pre * (1.0 - sig))).astype(bf16)
            du = (dhid * act).astype(bf16)
            dg_ref[here, :] = dg
            du_ref[here, :] = du

        def rows_back(here, wg, wu, dg_ref, du_ref):
            dx_acc[here, :] += mm(dg_ref[here, :], wg, NT) + mm(du_ref[here, :], wu, NT)

        def weight_sums(f, slot, dg_ref, du_ref, scaled_ref, first):
            @pl.when(f > first)
            def _():
                core_sum(f - 1)

            @pl.when(f >= 2)
            def _():
                core_copy(f - 2, slot).wait_send()

            for n, (left, right) in enumerate(
                ((xt_all, dg_ref), (xt_all, du_ref), (dyt_all, scaled_ref))
            ):
                found = mm(left[...], right[...]).astype(bf16)
                send[slot, n] = found[:half, :]
                total[f, n] = found[half:, :]
            core_copy(f, slot).start()

            @pl.when((f > first) & (f - 1 < away))
            def _():
                far_copy(f - 1).start()

        def lead_step(f, _):
            slot = lax.rem(f, 2)
            for copy in weights(f, slot):
                copy.wait()

            @pl.when(f + 1 < lead)
            def _():
                for copy in weights(f + 1, 1 - slot):
                    copy.start()

            hid, dg, du, scaled = (a.at[0] for a in (hid_keep, dg_keep, du_keep, scaled_keep))

            def row_chunk(c, _):
                here = pl.ds(pl.multiple_of(c * chunk, chunk), chunk)
                forward_back(here, wg_buf[slot], wu_buf[slot], wd_buf[slot], hid, dg, du, scaled)
                return 0

            lax.fori_loop(0, rows // chunk, row_chunk, 0)
            weight_sums(f, slot, dg, du, scaled, 0)
            y_acc[...] += mm(hid[...], wd_buf[slot])
            rows_back(slice(0, rows), wg_buf[slot], wu_buf[slot], dg, du)
            return 0

        lax.fori_loop(0, lead, lead_step, 0)
        if lead:
            core_sum(lead - 1)
            far_copy(lead - 1).start()
        for k in range(kept):
            for copy in keep_weights(k):
                copy.wait()

        def keep_rows(k, first, count):
            size = min(chunk, count)
            for c in range(count // size):
                forward_back(
                    slice(first + c * size, first + (c + 1) * size),
                    wg_keep[k], wu_keep[k], wd_keep[k],
                    hid_keep.at[k], dg_keep.at[k], du_keep.at[k], scaled_keep.at[k],
                )
            rows_back(
                slice(first, first + count), wg_keep[k], wu_keep[k], dg_keep.at[k], du_keep.at[k]
            )

        def send_back(first, last):
            for r in range(first, last):
                here = slice(r * CAP, (r + 1) * CAP)
                dx_low[r] = dx_acc[here, :].astype(bf16)
                column = jnp.sum(dot_acc[here, :], axis=1, keepdims=True)
                dots[r] = jnp.sum(jnp.where(diagonal, column, 0.0), axis=0, keepdims=True)
                if r - 1 >= max(1, first):
                    back_copy(r - 1).start()
                    dots_copy(r - 1).start()

        def send_last(r):
            back_copy(r).start()
            dots_copy(r).start()

        middle = places // 2
        near_rows = middle * CAP

        def far_step(k, _):
            keep_rows(k, near_rows, rows - near_rows)
            return 0

        lax.fori_loop(0, kept, far_step, 0)
        send_back(middle, places)

        def away_step(f, _):
            k = f - lead

            keep_rows(k, 0, near_rows)

            @pl.when(k == 0)
            def _():
                send_last(places - 1)

            weight_sums(
                f, lax.rem(f, 2), dg_keep.at[k], du_keep.at[k], scaled_keep.at[k], lead
            )
            return 0

        lax.fori_loop(lead, away, away_step, 0)
        if away == lead:
            send_last(places - 1)
        else:
            core_sum(away - 1)
            far_copy(away - 1).start()

        def near_step(k, _):
            keep_rows(k, 0, near_rows)
            return 0

        lax.fori_loop(away - lead, kept, near_step, 0)
        send_back(0, middle)

        def own_result(k, _):
            y_acc[...] += mm(hid_keep[k], wd_keep[k])
            return 0

        lax.fori_loop(0, kept, own_result, 0)
        send_last(middle - 1)

        def relay_copy(g):
            return remote(y_odd.at[g], relay.at[g], y_s.at[g], y_r.at[g], {"ctx": flip(me, 2)})

        def result(r):
            here = slice(r * CAP, (r + 1) * CAP)
            return (gate_all[here, :] * y_acc[here, :]).astype(bf16)

        for g in range(groups):
            y_odd[g] = result(local * g + 1)
            if g:
                relay_copy(g - 1).start()
        for g in range(groups):
            y_out[g][0] = result(local * g)
        relay_copy(groups - 1).start()

        def own_step(f, _):
            k = f - lead
            weight_sums(
                f, lax.rem(f, 2), dg_keep.at[k], du_keep.at[k], scaled_keep.at[k], away
            )
            return 0

        lax.fori_loop(away, steps, own_step, 0)
        core_sum(steps - 1)

        def beside_copy(i):
            return remote(total.at[away + i], beside.at[i], e_s.at[i], e_r.at[i], sibling)

        def beside_store(i):
            return pltpu.make_async_copy(
                beside.at[i], beside_out.at[:, :, pl.ds(i * tile, tile)], beside_sem.at[i]
            )

        def sum_store(i):
            return pltpu.make_async_copy(
                total.at[away + i], sum_out.at[:, :, pl.ds(i * tile, tile)], out_sem.at[i]
            )

        for i in range(tiles):
            for d in range(1, parts):
                far_copy((parts - 1 - d) * tiles + i).wait_recv()
            for n in range(3):
                value = total[away + i, n].astype(f32)
                for d in range(1, parts):
                    value = value + far[(parts - 1 - d) * tiles + i, n].astype(f32)
                total[away + i, n] = value.astype(bf16)
            if i:
                beside_copy(i - 1).start()
            sum_store(i).start()
        beside_copy(tiles - 1).start()
        for f in range(away):
            far_copy(f).wait_send()
        for f in range(max(0, steps - 2), steps):
            core_copy(f, f % 2).wait_send()

        def dx_store(r):
            src = dx_near.at[r] if r else dx_low.at[0]
            return pltpu.make_async_copy(src, dx_out.at[r], dx_sem.at[r])

        dots_out[0] = dots[0]
        dx_store(0).start()
        for r in range(1, places):
            back_copy(r).wait()
            dots_copy(r).wait()
            dx_store(r).start()
            dots_out[r] = dots_near[r]
        for g in range(groups):
            relay_copy(g).wait()
            y_out[g][1] = relay[g]
        for i in range(tiles):
            beside_copy(i).wait()
            beside_store(i).start()
        for i in range(tiles):
            sum_store(i).wait()
            beside_store(i).wait()
        for r in range(places):
            dx_store(r).wait()

    placed = shape_of((places, CAP, width), bf16)
    pair = shape_of((local, CAP, width), bf16)
    lines = shape_of((places, 1, CAP), f32)
    return run(
        body,
        (),
        [(arrived, anywhere), (grads, anywhere), (gates, vector)]
        + [(w, anywhere) for w in (w_gate, w_up, w_down)]
        + [(g, anywhere) for g in late],
        [(pair, vector)] * groups
        + [(placed, anywhere), (lines, vector)]
        + [(shape_of((3, half, per_part), bf16), anywhere)] * 2,
        scratch=[
            pltpu.VMEM((rows, width), bf16),
            pltpu.VMEM((width, rows), bf16),
            pltpu.VMEM((rows, width), bf16),
            pltpu.VMEM((width, rows), bf16),
            pltpu.VMEM((rows, 1), f32),
            pltpu.VMEM((rows, width), f32),
            pltpu.VMEM((rows, width), f32),
            pltpu.VMEM((rows, 128), f32),
            pltpu.VMEM((2, width, tile), bf16),
            pltpu.VMEM((2, width, tile), bf16),
            pltpu.VMEM((2, tile, width), bf16),
            pltpu.VMEM((kept, width, tile), bf16),
            pltpu.VMEM((kept, width, tile), bf16),
            pltpu.VMEM((kept, tile, width), bf16),
            pltpu.VMEM((kept, rows, tile), bf16),
            pltpu.VMEM((kept, rows, tile), bf16),
            pltpu.VMEM((kept, rows, tile), bf16),
            pltpu.VMEM((kept, rows, tile), bf16),
            pltpu.VMEM((2, 3, half, tile), bf16),
            pltpu.VMEM((steps, 3, half, tile), bf16),
            pltpu.VMEM((steps, 3, half, tile), bf16),
            pltpu.VMEM((max(1, away), 3, half, tile), bf16),
            pltpu.VMEM((places, CAP, width), bf16),
            pltpu.VMEM((places, CAP, width), bf16),
            pltpu.VMEM((places, 1, CAP), f32),
            pltpu.VMEM((places, 1, CAP), f32),
            pltpu.VMEM((tiles, 3, half, tile), bf16),
            pltpu.VMEM((groups, CAP, width), bf16),
            pltpu.VMEM((groups, CAP, width), bf16),
            dma((2 * places,)), dma((3, 2)), dma((3, kept)), dma((2,)), dma((steps,)),
            dma((max(1, away),)), dma((max(1, away),)),
            dma((places,)), dma((places,)), dma((places,)), dma((places,)),
            dma((tiles,)), dma((tiles,)), dma((tiles,)), dma((tiles,)),
            dma((groups,)), dma((groups,)), dma((places,)),
        ],
        flops=9 * 2 * rows * width * hidden,
        moved=12 * width * hidden + rows * width * 8,
        exps=rows * hidden,
        talks=2,
    )


def slot_sum(targets, source_ref):
    tile = targets.shape[0]
    total = None
    for r in range(source_ref.shape[0]):
        ids = r * CAP + lax.broadcasted_iota(jnp.int32, (tile, CAP), 1)
        choice = jnp.where((ids == targets[:, 0:1]) | (ids == targets[:, 1:2]), 1.0, 0.0)
        part = mm(choice.astype(bf16), source_ref[r])
        total = part if total is None else total + part
    return total


def token_back(
    x1, h2, grad, prob, previous_t, routes, targets, back, dots, dgate_zero, dh_zero, gain, router_t,
    zero_sums,
):
    rows, width = x1.shape
    tile = 128
    tiles = rows // tile
    places = back.shape[0]
    expert_all = prob.shape[1]
    members = lax.axis_size("ctx")
    last = expert_all + 1 + zero_sums.shape[0]

    def body(*refs):
        (x1_ref, h2_ref, dy_ref, prob_ref, prev_ref, route_ref, target_ref) = refs[:7]
        back_ref, dots_ref, dz_ref, dh_ref, gain_ref, router_ref, zero_ref = refs[7:14]
        dx1_ref, sums_ref, da_out, da_near, a_s, a_r, out_sem = refs[14:]
        me = lax.axis_index("ctx")
        peers = [{"ctx": flip(me, 1)}, {"ctx": flip(me, 2)}]
        ready = greet(peers)

        def da_copy(kind, t):
            here = pl.ds(pl.multiple_of(t * tile, tile), tile)
            n = kind * tiles + t
            src, dst = ((0, 1), (0, 2), (2, 3))[kind]
            return remote(
                da_near.at[src, here, :], da_near.at[dst, here, :], a_s.at[n], a_r.at[n],
                {"ctx": flip(me, 2 if kind == 1 else 1)},
            )

        sums_ref[...] = jnp.zeros_like(sums_ref)
        sums_ref[expert_all + 1 : last, :] = zero_ref[...]
        ready()

        def token_rows(t, _):
            here = pl.ds(pl.multiple_of(t * tile, tile), tile)
            prob_now = prob_ref[here, :]
            chosen, target, zero = route_ref[here, :], target_ref[here, :], dz_ref[here, :]
            lanes = lax.broadcasted_iota(jnp.int32, (tile, expert_all), 1)
            dprob = jnp.zeros_like(prob_now)
            for c in range(2):
                dgate = zero[:, c : c + 1]
                for n in range(places):
                    ids = n * CAP + lax.broadcasted_iota(jnp.int32, (tile, CAP), 1)
                    dgate = dgate + jnp.sum(
                        jnp.where(ids == target[:, c : c + 1], dots_ref[n], 0.0),
                        axis=1,
                        keepdims=True,
                    )
                dprob = dprob + jnp.where(lanes == chosen[:, c : c + 1], dgate, 0.0)
            dlogit = prob_now * (dprob - jnp.sum(prob_now * dprob, axis=1, keepdims=True))
            h2 = h2_ref[here, :]
            dh2 = slot_sum(target, back_ref) + dh_ref[here, :] + mm_full(dlogit, router_ref[...])
            x1 = x1_ref[here, :]
            inverse = lax.rsqrt(jnp.mean(x1 * x1, axis=1, keepdims=True) + norm_eps)
            normed = x1 * inverse
            dn = dh2 * gain_ref[...]
            dx1 = dy_ref[here, :].astype(f32) + inverse * (
                dn - normed * jnp.mean(dn * normed, axis=1, keepdims=True)
            )
            dx1_ref[here, :] = dx1
            da_near[0, here, :] = dx1.astype(bf16)
            sums_ref[0:expert_all, :] += mm_full(dlogit, h2, TN)
            sums_ref[expert_all : expert_all + 1, :] += jnp.sum(dh2 * normed, axis=0, keepdims=True)
            sums_ref[last:, 0:expert_all] += mm_full(prev_ref[:, here], dlogit)
            da_copy(1, t).start()
            da_copy(0, t).start()

            @pl.when(t >= 2)
            def _():
                da_copy(1, t - 2).wait_recv()
                da_copy(2, t - 2).start()

            return 0

        lax.fori_loop(0, tiles, token_rows, 0)
        for t in range(max(0, tiles - 2), tiles):
            da_copy(1, t).wait_recv()
            da_copy(2, t).start()
        mine = pltpu.make_async_copy(da_near.at[0], da_out.at[0], out_sem.at[0])
        mine.start()
        for t in range(tiles):
            da_copy(0, t).wait()
            da_copy(1, t).wait_send()
            da_copy(2, t).wait()
        rest = pltpu.make_async_copy(
            da_near.at[pl.ds(1, members - 1)], da_out.at[pl.ds(1, members - 1)], out_sem.at[1]
        )
        rest.start()
        mine.wait()
        rest.wait()

    return run(
        body,
        (),
        [(a, vector) for a in (x1, h2, grad, prob, previous_t, routes, targets, back, dots)]
        + [(a, vector) for a in (dgate_zero, dh_zero, gain, router_t, zero_sums)],
        [(shape_of((rows, width), f32), vector)]
        + [(shape_of((last + expert_all, width), f32), vector)]
        + [(shape_of((members, rows, width), bf16), anywhere)],
        scratch=[
            pltpu.VMEM((members, rows, width), bf16),
            dma((3 * tiles,)), dma((3 * tiles,)), dma((2,)),
        ],
        flops=2 * rows * width * (places * CAP + width),
        moved=rows * width * 24,
        talks=5,
    )


def finish(dqkv_all, h1, x, gain, dx1, weights_t, out_sum, small, tops, produced, base, targets):
    members, per_group = weights_t.shape[1], weights_t.shape[2]
    rows, width = x.shape
    group_rows = dqkv_all.shape[0]
    parts, groups = lax.axis_size("dp"), lax.axis_size("exp")
    team = parts * groups
    local = produced[0].shape[0]
    places = groups * local
    wide_share, out_share = width // (2 * team), per_group // team
    small_rows = small.shape[0]
    small_steps = [(axis, bit) for axis in ("ctx", "dp", "exp") for bit in powers(axis)]
    hops = len(small_steps)
    row_tile = min(256, rows)

    def body(*refs):
        it = iter(refs)

        def take(count=None):
            return next(it) if count is None else [next(it) for _ in range(count)]

        dqkv_hbm, h1_hbm, x_hbm, gain_ref, dx1_hbm, w_hbm, out_ref = take(7)
        small_ref, tops_ref, base_hbm, target_ref = take(4)
        produced_hbm = take(groups)
        input_out, wide_out, flat_out, small_out, gain_out, tops_out, result_out = take(7)
        dqkv, product, h1_all, x_all, dx1_all, w_all, base_all, y_near = take(8)
        part_send, part_core, part_y, y_got, part_own = take(5)
        wide_mine, wide_far_x, wide_far_z, wide_all = take(4)
        flat_mine, flat_far_x, flat_far_z, flat_all = take(4)
        small_acc, small_far, gain_acc, gain_far, tops_acc, tops_far = take(6)
        load_sem, near_s, near_r = take(3)
        wide_sems, flat_sems = [take(12), take(12)], take(12)
        hop_s, hop_r, gain_s, gain_r, top_s, top_r = take(6)

        me = lax.axis_index("ctx")
        dp_now, exp_now = lax.axis_index("dp"), lax.axis_index("exp")
        seat = dp_now * groups + exp_now

        def near_peer(j):
            return {"ctx": flip(me, j)}

        def team_peer(r):
            return {"dp": flip(dp_now, r // groups), "exp": flip(exp_now, r % groups)}

        peers = [near_peer(j) for j in range(1, members)]
        peers += [team_peer(r) for r in range(1, team)]
        ready = greet(peers)

        loads = [
            (dqkv_hbm, dqkv), (h1_hbm, h1_all), (x_hbm, x_all), (dx1_hbm, dx1_all),
            (w_hbm.at[:, me], w_all), (base_hbm, base_all),
        ]
        loads += [
            (produced_hbm[g], y_near.at[pl.ds(g * local, local)]) for g in range(groups)
        ]

        def load(n):
            return pltpu.make_async_copy(loads[n][0], loads[n][1], load_sem.at[n])

        class Dense:
            def __init__(self, mine, far_x, far_z, all_buf, sems):
                self.mine, self.far_x, self.far_z, self.all = mine, far_x, far_z, all_buf
                self.sems = sems

            def own_block(self, d=0):
                return pl.ds(flip(dp_now, d) * groups, groups)

            def x_copy(self, d):
                return remote(
                    self.mine.at[self.own_block(d)], self.far_x.at[d - 1], self.sems[0].at[d],
                    self.sems[1].at[d], {"dp": flip(dp_now, d)},
                )

            def z_copy(self, g):
                return remote(
                    self.mine.at[dp_now * groups + flip(exp_now, g)], self.far_z.at[g - 1],
                    self.sems[2].at[g], self.sems[3].at[g], {"exp": flip(exp_now, g)},
                )

            def gz_copy(self, g, theirs=False):
                spot = self.all.at[0, dp_now * groups + flip(exp_now, g) if theirs else seat]
                return remote(
                    spot, spot, self.sems[4].at[g], self.sems[5].at[g], {"exp": flip(exp_now, g)}
                )

            def gx_copy(self, d, theirs=False):
                spot = self.all.at[0, self.own_block(d if theirs else 0)]
                return remote(
                    spot, spot, self.sems[6].at[d], self.sems[7].at[d], {"dp": flip(dp_now, d)}
                )

            def y_copy(self, d):
                return remote(
                    self.all.at[0, self.own_block(d)], self.all.at[2, self.own_block(d)],
                    self.sems[8].at[d], self.sems[9].at[d], near_peer(2),
                )

            def core_copy(self, n):
                return remote(
                    self.all.at[2 * n], self.all.at[2 * n + 1], self.sems[10].at[n],
                    self.sems[11].at[n], near_peer(1),
                )

            def start(self):
                for d in range(1, parts):
                    self.x_copy(d).start()

            def to_z(self):
                for d in range(1, parts):
                    self.x_copy(d).wait()
                for g in list(range(1, groups)) + [0]:
                    c = dp_now * groups + flip(exp_now, g)
                    value = self.mine[c].astype(f32)
                    for d in range(1, parts):
                        value = value + self.far_x[d - 1, flip(exp_now, g)].astype(f32)
                    self.mine[c] = value.astype(bf16)
                for g in range(1, groups):
                    self.z_copy(g).start()

            def to_gather(self):
                for g in range(1, groups):
                    self.z_copy(g).wait()
                value = self.mine[seat].astype(f32)
                for g in range(1, groups):
                    value = value + self.far_z[g - 1].astype(f32)
                self.all[0, seat] = value.astype(bf16)

            def gather(self):
                for g in range(1, groups):
                    self.gz_copy(g).start()

            def to_x(self):
                for g in range(1, groups):
                    self.gz_copy(g).wait_send()
                    self.gz_copy(g, True).wait_recv()
                for d in range(1, parts):
                    self.gx_copy(d).start()
                self.y_copy(0).start()

            def to_y(self):
                for d in range(1, parts):
                    self.gx_copy(d).wait_send()
                    self.gx_copy(d, True).wait_recv()
                    self.y_copy(d).start()
                self.core_copy(0).start()

            def to_core(self):
                for d in range(parts):
                    self.y_copy(d).wait()
                self.core_copy(1).start()

            def done(self):
                for n in range(2):
                    self.core_copy(n).wait()

        wides = [
            Dense(wide_mine.at[n], wide_far_x.at[n], wide_far_z.at[n], wide_all.at[n], wide_sems[n])
            for n in range(2)
        ]
        flat = Dense(flat_mine, flat_far_x, flat_far_z, flat_all, flat_sems)

        def hop_peer(n):
            axis, bit = small_steps[n]
            return {axis: flip(lax.axis_index(axis), bit)}

        def small_copy(n):
            return remote(small_acc.at[n], small_far.at[n], hop_s.at[n], hop_r.at[n], hop_peer(n))

        def tops_copy(n):
            return remote(tops_acc.at[n], tops_far.at[n], top_s.at[n], top_r.at[n], hop_peer(n))

        def gain_pack(j, theirs=False):
            spot = gain_acc.at[flip(me, j) if theirs else me]
            return remote(spot, spot, gain_s.at[j], gain_r.at[j], near_peer(j))

        def gain_team(r, theirs=False):
            spot = gain_far.at[flip(seat, r) if theirs else seat]
            n = members + r
            return remote(spot, spot, gain_s.at[n], gain_r.at[n], team_peer(r))

        def small_start(n):
            small_copy(n).start()
            tops_copy(n).start()

        def small_sum(n):
            small_copy(n).wait()
            tops_copy(n).wait()
            small_acc[n + 1] = small_acc[n] + small_far[n]
            tops_acc[n + 1] = jnp.maximum(tops_acc[n], tops_far[n])

        small_hops = list(range(hops))

        def small_next():
            if small_hops:
                n = small_hops.pop(0)
                small_sum(n)
                if n + 1 < hops:
                    small_start(n + 1)

        row_tiles = rows // row_tile

        def tile_rows(t, first=0):
            return pl.ds(first + t * row_tile, row_tile)

        def core_part(j, t):
            n = j // 2
            return remote(
                part_send.at[n, tile_rows(t), :], part_core.at[n, tile_rows(t), :],
                near_s.at[n * row_tiles + t], near_r.at[n * row_tiles + t], near_peer(1),
            )

        def y_part(t):
            n = 2 * row_tiles + t
            return remote(
                part_y.at[tile_rows(t), :], y_got.at[tile_rows(t), :], near_s.at[n], near_r.at[n],
                near_peer(2),
            )

        def part(j, t):
            here = pl.ds(j * rows + t * row_tile, row_tile)
            found = None
            for w in range(3):
                add = mm(dqkv[here, w * per_group : (w + 1) * per_group], w_all[w])
                found = add if found is None else found + add
            return found

        for n in range(len(loads)):
            load(n).start()
        small_acc[0] = small_ref[...]
        lanes = lax.broadcasted_iota(jnp.int32, tops_acc.shape[1:], 1)
        tops_acc[0] = jnp.where(
            lanes == me, jnp.max(tops_ref[...], axis=1, keepdims=True), low_start
        )
        flat_rows = out_ref[...].astype(f32)
        for c in range(team):
            flat_mine[c] = flat_rows[c * out_share : (c + 1) * out_share, :].astype(bf16)
        ready()
        flat.start()
        small_start(0)
        load(0).wait()
        load(1).wait()

        def weigh(n, _):
            here = pl.ds(pl.multiple_of(n * rows, rows), rows)
            product[...] += mm(h1_all[here, :], dqkv[here, :], TN)
            return 0

        product[...] = mm(h1_all[0:rows, :], dqkv[0:rows, :], TN)
        lax.fori_loop(1, group_rows // rows, weigh, 0)
        for n in range(2):
            for c in range(team):
                at = (n * team + c) * wide_share
                wide_mine[n, c] = product[at : at + wide_share, :].astype(bf16)
            if n:
                wides[0].start()
        flat.to_z()
        wides[1].start()
        for n in range(2, len(loads)):
            load(n).wait()
        queue = [(j, t) for j in (3, 1) for t in range(row_tiles)]
        for n, (j, t) in enumerate(queue):
            part_send[j // 2, tile_rows(t), :] = part(j, t).astype(bf16)
            if n:
                core_part(*queue[n - 1]).start()
        own_part = [part(2, t) for t in range(1)]
        core_part(*queue[-1]).start()
        for t in range(row_tiles):
            value = own_part[0] if t == 0 else part(2, t)
            core_part(3, t).wait_recv()
            part_y[tile_rows(t), :] = (
                value + part_core[1, tile_rows(t), :].astype(f32)
            ).astype(bf16)
            if t:
                y_part(t - 1).start()
        part_own[tile_rows(0), :] = part(0, 0)
        y_part(row_tiles - 1).start()
        for t in range(1, row_tiles):
            part_own[tile_rows(t), :] = part(0, t)
        wides[0].to_z()
        flat.to_gather()
        small_next()
        wides[1].to_z()
        flat.gather()
        wides[0].to_gather()

        def token_rows(t, _):
            here = pl.ds(pl.multiple_of(t * 128, 128), 128)
            result_out[here, :] = (
                base_all[here, :] + slot_sum(target_ref[here, :], y_near)
            ).astype(bf16)
            return 0

        lax.fori_loop(0, rows // 256, token_rows, 0)
        wides[0].gather()
        small_next()
        flat.to_x()
        wides[1].to_gather()
        lax.fori_loop(rows // 256, rows // 128, token_rows, 0)
        wides[1].gather()
        wides[0].to_x()
        small_next()
        for t in range(row_tiles):
            core_part(1, t).wait()
            core_part(3, t).wait_send()
            y_part(t).wait()

        def input_rows(t, gain_part):
            here = pl.ds(pl.multiple_of(t * row_tile, row_tile), row_tile)
            dh = (
                part_own[here, :] + part_core[0, here, :].astype(f32) + y_got[here, :].astype(f32)
            )
            x_now = x_all[here, :].astype(f32)
            inv = lax.rsqrt(jnp.mean(x_now * x_now, axis=1, keepdims=True) + norm_eps)
            normed = x_now * inv
            dn = dh * gain_ref[...]
            dx1_all[here, :] = dx1_all[here, :] + inv * (
                dn - normed * jnp.mean(dn * normed, axis=1, keepdims=True)
            )
            return gain_part + jnp.sum(dh * normed, axis=0, keepdims=True)

        gain_acc[me] = lax.fori_loop(
            0, rows // row_tile, input_rows, jnp.zeros((1, width), f32)
        )
        store = pltpu.make_async_copy(dx1_all, input_out, load_sem.at[len(loads)])
        store.start()
        flat.to_y()
        for j in range(1, members):
            gain_pack(j).start()
        wides[1].to_x()
        wides[0].to_y()
        for j in range(1, members):
            gain_pack(j).wait_send()
            gain_pack(j, True).wait_recv()
        value = gain_acc[0]
        for n in range(1, members):
            value = value + gain_acc[n]
        gain_far[seat] = value
        small_next()
        flat.to_core()
        for r in range(1, team):
            gain_team(r).start()
        wides[1].to_y()
        wides[0].to_core()
        while small_hops:
            small_next()
        flat.done()
        wides[1].to_core()
        for r in range(1, team):
            gain_team(r).wait_send()
            gain_team(r, True).wait_recv()
        value = gain_far[0]
        for n in range(1, team):
            value = value + gain_far[n]
        gain_out[...] = value[0]
        final = [pltpu.make_async_copy(flat_all, flat_out, load_sem.at[len(loads) + 1])]
        for n in range(2):
            wides[n].done()
            final.append(
                pltpu.make_async_copy(
                    wide_all.at[n], wide_out.at[n], load_sem.at[len(loads) + 2 + n]
                )
            )
        for copy in final:
            copy.start()
        small_out[...] = small_acc[hops]
        tops_out[...] = tops_acc[hops]
        store.wait()
        for copy in final:
            copy.wait()

    def dense_scratch(share, across, lead=()):
        return [
            pltpu.VMEM(lead + (team, share, across), bf16),
            pltpu.VMEM(lead + (max(1, parts - 1), groups, share, across), bf16),
            pltpu.VMEM(lead + (max(1, groups - 1), share, across), bf16),
            pltpu.VMEM(lead + (members, team, share, across), bf16),
        ]

    dense_sem = (
        [dma((parts,))] * 2 + [dma((groups,))] * 4 + [dma((parts,))] * 4 + [dma((2,))] * 2
    )
    wide_rows = shape_of((rows, width), f32)
    return run(
        body,
        (),
        [(dqkv_all, anywhere), (h1, anywhere), (x, anywhere), (gain, vector), (dx1, anywhere)]
        + [(weights_t, anywhere), (out_sum, vector), (small, vector), (tops, vector)]
        + [(base, anywhere), (targets, vector)]
        + [(a, anywhere) for a in produced],
        [
            (wide_rows, anywhere),
            (shape_of((2, members, team, wide_share, 3 * per_group), bf16), anywhere),
            (shape_of((members, team, out_share, width), bf16), anywhere),
            (shape_of((small_rows, width), f32), vector),
            (shape_of((width,), f32), vector),
            (shape_of((tops.shape[0], 128), f32), vector),
            (shape_of((rows, width), bf16), vector),
        ],
        scratch=[
            pltpu.VMEM((group_rows, 3 * per_group), bf16),
            pltpu.VMEM((width, 3 * per_group), f32),
            pltpu.VMEM((group_rows, width), bf16),
            pltpu.VMEM((rows, width), bf16),
            pltpu.VMEM((rows, width), f32),
            pltpu.VMEM((3, per_group, width), bf16),
            pltpu.VMEM((rows, width), f32),
            pltpu.VMEM((places, CAP, width), bf16),
            pltpu.VMEM((2, rows, width), bf16),
            pltpu.VMEM((2, rows, width), bf16),
            pltpu.VMEM((rows, width), bf16),
            pltpu.VMEM((rows, width), bf16),
            pltpu.VMEM((rows, width), f32),
        ]
        + dense_scratch(wide_share, 3 * per_group, (2,))
        + dense_scratch(out_share, width)
        + [pltpu.VMEM((hops + 1, small_rows, width), f32), pltpu.VMEM((hops, small_rows, width), f32)]
        + [pltpu.VMEM((members, 1, width), f32), pltpu.VMEM((team, 1, width), f32)]
        + [pltpu.VMEM((hops + 1, tops.shape[0], 128), f32), pltpu.VMEM((hops, tops.shape[0], 128), f32)]
        + [dma((12 + places,))] + [dma((3 * (rows // row_tile),))] * 2
        + dense_sem * 3
        + [dma((hops,))] * 2
        + [dma((members + team,))] * 2
        + [dma((hops,))] * 2,
        flops=4 * 2 * rows * width * width * 3,
        moved=20 * 1024 * 1024,
        talks=3,
    )


def place_experts(meta, near, begun):
    _, half, columns = near[0].shape
    tile = 128
    tiles = half // tile
    count = 3

    def body(meta_ref, *refs):
        outs = refs[2 * count + count :]
        for j in range(2):

            @pl.when(pl.program_id(0) == j)
            def _():
                for n in range(count):
                    piece = refs[n * 2 + j][0].astype(f32)
                    outs[n][0] = jnp.transpose(piece) if n == 2 else piece

    def in_spec(which, j):
        def index(c, t, m):
            return (which, jnp.where(c == j, t, jnp.where(c < j, 0, tiles - 1)), 0)

        return pl.BlockSpec((1, tile, columns), index)

    flat = pl.BlockSpec((1, tile, columns), lambda c, t, m: (m[3] ^ 1, (m[2] ^ c) * tiles + t, 0))
    turned = pl.BlockSpec((1, columns, tile), lambda c, t, m: (m[3] ^ 1, 0, (m[2] ^ c) * tiles + t))
    return run(
        body,
        (2, tiles),
        [(near[j], in_spec(n, j)) for n in range(count) for j in range(2)]
        + [(a, anywhere) for a in begun],
        [
            (shape_of(a.shape, f32), turned if n == 2 else flat)
            for n, a in enumerate(begun)
        ],
        meta=meta,
        moved=count * 2 * half * columns * 6,
        aliases={1 + 2 * count + n: n for n in range(count)},
    )


def place_dense(meta, near, flat, tops, small, w_qkv, kinds):
    _, members, team, share, lanes = near.shape
    per_group = lanes // 3
    half = team * share
    width = 2 * half
    rows_all = flat.shape[1] * flat.shape[2]
    step = 8 // math.gcd(share, 8)
    while team // step > 4:
        step *= 2
    per_half = team // step
    tall = step * share

    heads = HEADS // members
    head_width = width // HEADS
    expert_all = (small.shape[0] - 1 - 3 * kinds) // 2
    at_vec = expert_all + 1
    at_logit = at_vec + kinds
    at_carry = at_logit + 2 * kinds

    def body(meta_ref, near_ref, flat_ref, tops_ref, small_ref, w_ref, *outs):
        out_ref, flat_out, clip_ref, router_out, norm_out, vec_out, logit_out, carry_out = outs[:8]
        scale_ref = outs[8]

        @pl.when((pl.program_id(0) == 0) & (pl.program_id(1) == 0))
        def _():
            lanes = lax.broadcasted_iota(jnp.int32, (1, width), 1)
            scale = jnp.zeros((1, width), f32)
            for n in range(HEADS):
                top = tops_ref[n % heads : n % heads + 1, n // heads : n // heads + 1]
                ratio = jnp.sqrt(jnp.minimum(1.0, clip_limit / top))
                inside = (lanes >= n * head_width) & (lanes < (n + 1) * head_width)
                scale = jnp.where(inside, ratio, scale)
            scale_ref[...] = scale
            router_out[...] = small_ref[0:expert_all, :]
            norm_out[...] = small_ref[expert_all, :]
            vec_out[...] = small_ref[at_vec : at_vec + kinds, :]
            for n in range(kinds):
                logit_out[n] = small_ref[at_logit + 2 * n : at_logit + 2 * n + 2, :]
            carry_out[...] = small_ref[at_carry:, 0:expert_all]

        for c in range(step):
            pieces = [near_ref[0, meta_ref[0] ^ g, c] for g in range(members)]
            for w in range(3):
                at = slice(w * per_group, (w + 1) * per_group)
                out_ref[w, c * share : (c + 1) * share, :] = jnp.concatenate(
                    [piece[:, at] for piece in pieces], axis=1
                ).astype(f32)
        clip_ref[...] = w_ref[...].astype(f32) * scale_ref[...]

        @pl.when(pl.program_id(1) == 0)
        def _():
            for c in range(team):
                at = slice(c * flat.shape[2], (c + 1) * flat.shape[2])
                for j in range(2):
                    member = pl.program_id(0) * 2 + j
                    flat_out[j, at, :] = flat_ref[meta_ref[0] ^ member, c].astype(f32)

    square = shape_of((3, width, width), f32)
    return run(
        body,
        (2, per_half),
        [
            (
                near,
                pl.BlockSpec((1, members, step, share, lanes), lambda n, c, m: (n, 0, c, 0, 0)),
            ),
            (flat, whole(flat)),
            (tops, whole(tops)),
            (small, whole(small)),
            (w_qkv, pl.BlockSpec((2, tall, width), lambda n, c, m: (0, n * per_half + c, 0))),
        ],
        [
            (square, pl.BlockSpec((3, tall, width), lambda n, c, m: (0, n * per_half + c, 0))),
            (
                shape_of((members, rows_all, width), f32),
                pl.BlockSpec((2, rows_all, width), lambda n, c, m: (n, 0, 0)),
            ),
            (
                shape_of((2, width, width), f32),
                pl.BlockSpec((2, tall, width), lambda n, c, m: (0, n * per_half + c, 0)),
            ),
        ]
        + [
            (o, whole(o))
            for o in (
                shape_of((expert_all, width), f32),
                shape_of((width,), f32),
                shape_of((kinds, width), f32),
                shape_of((kinds, 2, width), f32),
                shape_of((expert_all, expert_all), f32),
            )
        ],
        scratch=[pltpu.VMEM((1, width), f32)],
        meta=meta,
        moved=square.size * 12,
    )


def shards(
    inputs,
    lengths,
    block_order,
    routes,
    prev_logits,
    norm1_gain,
    norm2_gain,
    w_qkv,
    w_out,
    w_router,
    w_carry,
    const_logit_w,
    const_vec,
    w_gate,
    w_up,
    w_down,
    cotangent,
):
    members = lax.axis_size("ctx")
    groups = lax.axis_size("exp")
    parts = lax.axis_size("dp")
    me = lax.axis_index("ctx")
    mine = lax.axis_index("exp")
    x, grad = inputs[0], cotangent[0]
    rows, width = x.shape
    group_rows = rows * members
    deal_block = group_rows // block_order.shape[1]
    per_member = rows // deal_block
    local = w_gate.shape[0]
    expert_count = local * groups
    head_width = width // HEADS
    heads = HEADS // members
    per_group = heads * head_width
    blocks = block_order.shape[1]
    layout = {
        "order": 4, "lengths": 4 + blocks, "sequences": lengths.shape[1],
        "inverse": 4 + blocks + lengths.shape[1], "sides": local,
    }
    numbers = jnp.arange(blocks, dtype=jnp.int32)
    given = jnp.sum(jnp.where(block_order[0][None, :] == numbers[:, None], numbers[None, :], 0), axis=1)
    inverse = (((given // per_member) ^ me) * per_member + given % per_member).astype(jnp.int32)
    meta = jnp.concatenate(
        [
            jnp.stack([me, mine, me % 2, me // 2]).astype(jnp.int32),
            block_order[0],
            lengths[0],
            inverse,
        ]
    )
    gain1, gain2 = norm1_gain, norm2_gain
    w_out_parts = w_out.reshape(members, per_group, width)
    previous_t = jnp.transpose(prev_logits[0])
    router_t = jnp.transpose(w_router)
    odd = [r for r in range(groups * local) if r % local]

    begun = begin(x, grad, jnp.transpose(routes[0]), gain1, w_qkv, local)
    q, k, v, kt, vt, h1, weights_t, targets, target_rows, route_ids, grad_near = begun[:11]
    grad_rest = begun[11:]
    weights_t = weights_t.reshape(3, members, per_group, width)
    grad_late = [slot_swap(grad_rest[n], r, local) for n, r in enumerate(odd)]
    o, ot, lse, tops = attend(meta, q, k, vt, deal_block, layout)
    logit_rows = jnp.swapaxes(const_logit_w, 1, 2).reshape(-1, width)
    x1, h2, prob, token_near, gate_near, base, dh_zero, dgate_zero, zero_sums = token_front(
        x, o, w_out_parts, gain2, router_t, previous_t, w_carry, target_rows, grad, route_ids,
        logit_rows, const_vec, local,
    )
    worked = expert_layer(token_near, grad_near, grad_late, gate_near, w_gate, w_up, w_down)
    produced = worked[:groups]
    token_back_rows, dots, expert_sum, beside = worked[groups:]
    dx1, small, da_near = token_back(
        x1, h2, grad, prob, previous_t, route_ids, targets, token_back_rows, dots, dgate_zero,
        dh_zero, gain2, router_t, zero_sums,
    )
    expert_now, da_near = lax.optimization_barrier((expert_sum, da_near))
    over = swap(expert_now, "ctx", 2)
    y_near = [swap(produced[g], "exp", g) if g else produced[0] for g in range(groups)]
    dqkv, out_sum, *begun_grads = attend_back(
        meta, q, k, v, kt, da_near, w_out_parts, ot, lse, deal_block, layout, (expert_sum, beside)
    )

    input_grad, qkv_near, out_near, small, norm1_grad, top_all, result = finish(
        dqkv, h1, x, gain1, dx1, weights_t, out_sum, small, tops, y_near, base, targets
    )
    over, qkv_near = lax.optimization_barrier((over, qkv_near))
    corner = swap(over, "ctx", 1)
    dense = place_dense(meta, qkv_near, out_near, top_all, small, w_qkv, const_vec.shape[0])
    qkv_grad, out_grad, clipped, router_grad, norm2_grad, vec_grad, logit_grad, carry_grad = dense
    router_grad, logit_grad = jnp.transpose(router_grad), jnp.swapaxes(logit_grad, 1, 2)
    out_grad = out_grad.reshape(width, width)
    gate_grad, up_grad, down_grad = place_experts(meta, (over, corner), begun_grads)
    return (
        result[None],
        input_grad[None],
        norm1_grad,
        norm2_grad,
        qkv_grad,
        out_grad,
        router_grad,
        carry_grad,
        logit_grad,
        vec_grad,
        gate_grad,
        up_grad,
        down_grad,
        clipped,
    )


def solution(mesh):
    tokens = P(("dp", "exp"), "ctx", None)
    packs = P(("dp", "exp"), None)
    experts = P("exp", None, None)
    in_specs = (
        tokens, packs, packs, tokens, tokens, P(), P(), P(), P(), P(), P(), P(), P(),
        experts, experts, experts, tokens,
    )
    out_specs = (
        tokens, tokens, P(), P(), P(), P(), P(), P(), P(), P(),
        P("exp", None, "dp"), P("exp", None, "dp"), P("exp", "dp", None), P(),
    )
    return jax.shard_map(shards, mesh=mesh, in_specs=in_specs, out_specs=out_specs, check_vma=False)
```

```python
import math

import jax
import jax.numpy as jnp
from jax import lax
from jax.experimental import pallas as pl
from jax.experimental.pallas import tpu as pltpu
from jax.sharding import PartitionSpec as P

HEADS = 12
CAP = 128

norm_eps = 1e-05
clip_limit = 3.0
low_start = -1e30
mask_fill = -3e38
highest = lax.Precision.HIGHEST
NN = (((1,), (0,)), ((), ()))
NT = (((1,), (1,)), ((), ()))
TN = (((0,), (0,)), ((), ()))
f32 = jnp.float32
bf16 = jnp.bfloat16
MESH = pl.DeviceIdType.MESH


def mm(left, right, dims=NN):
    return lax.dot_general(left, right, dims, preferred_element_type=f32)


def mm_full(left, right, dims=NN):
    return lax.dot_general(left, right, dims, precision=highest, preferred_element_type=f32)


def shape_of(shape, dtype):
    return jax.ShapeDtypeStruct(shape, dtype)


def whole(array):
    rank = len(array.shape)
    return pl.BlockSpec(array.shape, lambda *_: (0,) * rank)


def cost(flops, moved, exps=0):
    return pl.CostEstimate(flops=int(flops), bytes_accessed=int(moved), transcendentals=int(exps))


def run(body, grid, inputs, outputs, scratch=(), meta=None, flops=0, moved=0, exps=0, aliases=None, talks=None):
    prefetch = 0 if meta is None else 1
    args = ([] if meta is None else [meta]) + [a for a, _ in inputs]
    return pl.pallas_call(
        body,
        out_shape=[o for o, _ in outputs],
        grid_spec=pltpu.PrefetchScalarGridSpec(
            num_scalar_prefetch=prefetch,
            grid=grid,
            in_specs=[s for _, s in inputs],
            out_specs=[s for _, s in outputs],
            scratch_shapes=list(scratch),
        ),
        compiler_params=pltpu.CompilerParams(
            dimension_semantics=("arbitrary",) * len(grid),
            vmem_limit_bytes=63 * 1024 * 1024,
            collective_id=talks,
            has_side_effects=talks is not None,
        ),
        cost_estimate=cost(flops, moved, exps),
        input_output_aliases={} if aliases is None else aliases,
    )(*args)


def swap(value, axis, distance):
    count = lax.axis_size(axis)
    return lax.ppermute(value, axis, [(i, i ^ distance) for i in range(count)])


def flip(value, bits):
    bit = 1
    while bit <= bits:
        if bits & bit:
            value = value + bit - 2 * bit * lax.rem(lax.div(value, bit), 2)
        bit *= 2
    return value


def powers(axis):
    found, bit = [], 1
    while bit < lax.axis_size(axis):
        found.append(bit)
        bit *= 2
    return found


def slot_peer(r, count, exp_now, me):
    return {"exp": flip(exp_now, r // count), "ctx": flip(me, 2 * (r % count))}


def slot_swap(value, r, count):
    groups = lax.axis_size("exp")
    total = groups * lax.axis_size("ctx")
    apart = 2 * (r % count) * groups + r // count
    return lax.ppermute(value, ("ctx", "exp"), [(i, i ^ apart) for i in range(total)])


def remote(src, dst, sent, arrived, peer):
    return pltpu.make_async_remote_copy(
        src_ref=src, dst_ref=dst, send_sem=sent, recv_sem=arrived,
        device_id=peer, device_id_type=MESH,
    )


def greet(peers):
    barrier = pltpu.get_barrier_semaphore()
    for peer in peers:
        pl.semaphore_signal(barrier, inc=1, device_id=peer, device_id_type=MESH)
    return lambda: pl.semaphore_wait(barrier, len(peers))


anywhere = pl.BlockSpec(memory_space=pl.ANY)
scalars = pl.BlockSpec(memory_space=pltpu.SMEM)
vector = pl.BlockSpec(memory_space=pltpu.VMEM)
dma = pltpu.SemaphoreType.DMA


def add_low(*terms):
    total = terms[0].astype(f32)
    for term in terms[1:]:
        total = total + term.astype(f32)
    return total.astype(bf16)


def begin(x, grad, routes, gain, w_qkv, local):
    rows, width = x.shape
    members, groups = lax.axis_size("ctx"), lax.axis_size("exp")
    group_rows = rows * members
    heads = HEADS // members
    head_width = width // HEADS
    columns = heads * head_width
    places = groups * local
    odd = [r for r in range(places) if r % local]
    scale = head_width**-0.5
    tile = min(256, rows)
    per_member = rows // tile

    def body(*refs):
        x_hbm, dy_ref, route_ref, gain_ref, w_hbm = refs[:5]
        q_out, k_out, v_out, kt_out, vt_out, h_out, wt_out = refs[5:12]
        target_out, target_rows, chosen_out, near_out = refs[12:16]
        rest_out, refs = refs[16 : 16 + len(odd)], refs[:16] + refs[16 + len(odd) :]
        x_near, w_in, w_t, q_all, k_all, v_all, kt_all, vt_all, h_all, packed, near = refs[16:27]
        load_sem, x_s, x_r, r_s, r_r, out_sem, near_sem = refs[27:]
        me, exp_now = lax.axis_index("ctx"), lax.axis_index("exp")
        side = lax.div(me, 2)
        peers = [{"ctx": flip(me, 1)}, {"ctx": flip(me, 2)}]
        peers += [slot_peer(local * g, local, exp_now, me) for g in range(1, groups)]
        ready = greet(peers)
        own = pltpu.make_async_copy(x_hbm, x_near.at[0], load_sem.at[0])
        weights = pltpu.make_async_copy(w_hbm, w_in, load_sem.at[1])
        own.start()
        weights.start()

        def some(t):
            return pl.ds(pl.multiple_of(t * tile, tile), tile)

        def across(t):
            n = 2 + t
            return remote(
                x_hbm.at[some(t), :], x_near.at[2, some(t), :], x_s.at[n], x_r.at[n],
                {"ctx": flip(me, 2)},
            )

        def beside():
            return remote(x_hbm, x_near.at[1], x_s.at[1], x_r.at[1], {"ctx": flip(me, 1)})

        def passed(t):
            n = 2 + per_member + t
            return remote(
                x_near.at[2, some(t), :], x_near.at[3, some(t), :], x_s.at[n], x_r.at[n],
                {"ctx": flip(me, 1)},
            )

        def row_copy(g):
            return remote(
                packed.at[g], near.at[g], r_s.at[g], r_r.at[g],
                slot_peer(local * g, local, exp_now, me),
            )

        ready()
        for t in range(per_member):
            across(t).start()
        beside().start()

        lines = jnp.concatenate([route_ref[...].astype(f32), jnp.zeros((6, rows), f32)], axis=0)
        chosen = jnp.transpose(lines)[:, 0:2].astype(jnp.int32)
        chosen_out[...] = chosen
        expert_count = places
        lanes = lax.broadcasted_iota(jnp.int32, (rows, 128), 1)
        hits = [lanes == chosen[:, c : c + 1] for c in range(2)]
        hit = jnp.where((hits[0] | hits[1]) & (lanes < expert_count), 1.0, 0.0)
        later = lax.broadcasted_iota(jnp.int32, (rows, rows), 0)
        sooner = lax.broadcasted_iota(jnp.int32, (rows, rows), 1)
        ahead = mm(jnp.where(sooner < later, 1.0, 0.0).astype(bf16), hit.astype(bf16))
        spots = []
        for c in range(2):
            ids = chosen[:, c : c + 1]
            rank = jnp.sum(jnp.where(hits[c], ahead, 0.0), axis=1, keepdims=True).astype(jnp.int32)
            far_z = lax.div(ids, local)
            far_y = lax.rem(ids, local)
            z = jnp.zeros_like(ids)
            bit = 1
            while bit < groups:
                z = z + bit * jnp.where(
                    lax.rem(lax.div(far_z, bit), 2) == lax.rem(lax.div(exp_now, bit), 2), 0, 1
                )
                bit *= 2
            y = jnp.where(far_y == side, 0, 1)
            spots.append(jnp.where(ids < expert_count, (z * local + y) * CAP + rank, -1))
        target_out[...] = jnp.concatenate(spots, axis=1)
        wide = jnp.where(lanes == 0, spots[0], spots[1]).astype(f32)
        target_rows[...] = jnp.transpose(wide)[0:2, :].astype(jnp.int32)

        def pack(n, r):
            packed[n] = mm(slot_choice(r * CAP, CAP, target_rows), dy_ref[...]).astype(bf16)

        for g in range(groups - 1, -1, -1):
            pack(g, local * g)
            if g < groups - 1:
                row_copy(g + 1).start()
        for n, r in enumerate(odd):
            pack(groups + n, r)
        stores = [
            pltpu.make_async_copy(packed.at[0], near_out.at[0], near_sem.at[0]),
        ] + [
            pltpu.make_async_copy(packed.at[groups + n], rest_out[n], near_sem.at[groups + n])
            for n in range(len(odd))
        ]
        for copy in stores:
            copy.start()
        weights.wait()
        for w in range(3):
            w_t[w] = jnp.transpose(w_in[w])
        w_store = pltpu.make_async_copy(w_t, wt_out, load_sem.at[2])
        w_store.start()
        here = pl.ds(pl.multiple_of(me * columns, columns), columns)

        def chunk(j):
            def project(t, _):
                if j == 2:
                    across(t).wait()
                    passed(t).start()
                if j == 3:
                    passed(t).wait()
                at = pl.multiple_of(t * tile, tile)
                to = pl.ds(pl.multiple_of(j * rows + t * tile, tile), tile)
                value = x_near[j, pl.ds(at, tile), :].astype(f32)
                inverse = lax.rsqrt(jnp.mean(value * value, axis=1, keepdims=True) + norm_eps)
                low = (value * inverse * gain_ref[...]).astype(bf16)
                h_all[to, :] = low
                q = mm(low, w_t[0, here, :], NT).astype(bf16) * jnp.asarray(scale, bf16)
                k = mm(low, w_t[1, here, :], NT).astype(bf16)
                v = mm(low, w_t[2, here, :], NT).astype(bf16)
                for h in range(heads):
                    part = slice(h * head_width, (h + 1) * head_width)
                    q_all[h, to, :] = q[:, part]
                    k_all[h, to, :] = k[:, part]
                    v_all[h, to, :] = v[:, part]
                kt_all[:, to] = mm(w_t[1, here, :], low, NT).astype(bf16)
                vt_all[:, to] = mm(w_t[2, here, :], low, NT).astype(bf16)
                return 0

            lax.fori_loop(0, per_member, project, 0)
            for copy in chunk_stores(j):
                copy.start()

        def chunk_stores(j):
            to = pl.ds(j * rows, rows)
            pairs = [(q_all, q_out), (k_all, k_out), (v_all, v_out)]
            found = [(a.at[:, to, :], b.at[:, to, :]) for a, b in pairs]
            found += [(a.at[:, to], b.at[:, to]) for a, b in ((kt_all, kt_out), (vt_all, vt_out))]
            found += [(h_all.at[to, :], h_out.at[to, :])]
            return [
                pltpu.make_async_copy(a, b, out_sem.at[6 * j + n]) for n, (a, b) in enumerate(found)
            ]

        own.wait()
        chunk(0)
        beside().wait()
        chunk(1)
        chunk(2)
        chunk(3)
        for g in range(1, groups):
            row_copy(g).wait()
            pltpu.make_async_copy(near.at[g], near_out.at[g], near_sem.at[g]).start()
        for copy in stores:
            copy.wait()
        w_store.wait()
        for j in range(members):
            for copy in chunk_stores(j):
                copy.wait()
        for g in range(1, groups):
            pltpu.make_async_copy(near.at[g], near_out.at[g], near_sem.at[g]).wait()

    by_head = (heads, group_rows, head_width)
    by_column = (columns, group_rows)
    slots = (places, CAP, width)
    return run(
        body,
        (),
        [(x, anywhere), (grad, vector), (routes, vector), (gain, vector), (w_qkv, anywhere)],
        [(shape_of(by_head, bf16), anywhere)] * 3
        + [(shape_of(by_column, bf16), anywhere)] * 2
        + [(shape_of((group_rows, width), bf16), anywhere)]
        + [(shape_of((3, width, width), bf16), anywhere)]
        + [(shape_of((rows, 2), jnp.int32), vector), (shape_of((2, rows), jnp.int32), vector)]
        + [(shape_of((rows, 2), jnp.int32), vector)]
        + [(shape_of((groups, CAP, width), bf16), anywhere)]
        + [(shape_of((CAP, width), bf16), anywhere)] * len(odd),
        scratch=[
            pltpu.VMEM((members, rows, width), bf16),
            pltpu.VMEM((3, width, width), bf16),
            pltpu.VMEM((3, width, width), bf16),
            pltpu.VMEM(by_head, bf16), pltpu.VMEM(by_head, bf16), pltpu.VMEM(by_head, bf16),
            pltpu.VMEM(by_column, bf16), pltpu.VMEM(by_column, bf16),
            pltpu.VMEM((group_rows, width), bf16),
            pltpu.VMEM(slots, bf16), pltpu.VMEM(slots, bf16),
            dma((3,)), dma((2 + 2 * per_member,)), dma((2 + 2 * per_member,)),
            dma((places,)), dma((places,)), dma((6 * members,)), dma((places + 1,)),
        ],
        flops=2 * group_rows * width * columns * 5,
        moved=20 * 1024 * 1024,
        talks=4,
    )


def document_start(meta_ref, position, layout):
    start = jnp.zeros_like(position)
    end = jnp.int32(0)
    for s in range(layout["sequences"]):
        end = end + meta_ref[layout["lengths"] + s]
        start = jnp.where(position >= end, end, start)
    return start


def block_range(meta_ref, query_block, key_block, rows, layout):
    q_first = query_block * rows
    k_first = key_block * rows
    begin = document_start(meta_ref, q_first, layout)
    begin_last = document_start(meta_ref, q_first + rows - 1, layout)
    needed = (k_first <= q_first) & (k_first + rows - 1 >= begin)
    full = (k_first < q_first) & (k_first >= begin_last)
    return q_first, k_first, needed, full


def allowed_pairs(meta_ref, q_first, k_first, rows, layout):
    q_pos = q_first + lax.broadcasted_iota(jnp.int32, (1, rows), 1)
    k_pos = k_first + lax.broadcasted_iota(jnp.int32, (rows, 1), 0)
    return (k_pos <= q_pos) & (k_pos >= document_start(meta_ref, q_pos, layout))


def attend(meta, q, k, vt, rows, layout):
    heads, group_rows, head_width = q.shape
    blocks = group_rows // rows
    width = heads * head_width

    def body(meta_ref, q_ref, k_ref, vt_ref, o_ref, ot_ref, lse_ref, top_ref, m_ref, l_ref, a_ref, qt_ref):
        i = pl.program_id(0)
        m_ref[...] = jnp.full_like(m_ref, low_start)
        l_ref[...] = jnp.zeros_like(l_ref)
        a_ref[...] = jnp.zeros_like(a_ref)
        for h in range(heads):
            qt_ref[h] = jnp.transpose(q_ref[h])

        def one(j, _):
            q_first, k_first, needed, full = block_range(meta_ref, i, j, rows, layout)
            at = pl.multiple_of(meta_ref[layout["inverse"] + j] * rows, rows)

            def step(masked):
                if masked:
                    allowed = allowed_pairs(meta_ref, q_first, k_first, rows, layout)
                scores = [mm(k_ref[h, pl.ds(at, rows), :], qt_ref[h]) for h in range(heads)]
                if masked:
                    scores = [jnp.where(allowed, s, mask_fill) for s in scores]
                olds = [m_ref[h] for h in range(heads)]
                news = [
                    jnp.maximum(old, jnp.max(s, axis=0, keepdims=True))
                    for old, s in zip(olds, scores)
                ]
                chances = [jnp.exp(s - new) for s, new in zip(scores, news)]
                mixed = [
                    mm(
                        vt_ref[h * head_width : (h + 1) * head_width, pl.ds(at, rows)],
                        chances[h].astype(bf16),
                    )
                    for h in range(heads)
                ]
                for h in range(heads):
                    part = slice(h * head_width, (h + 1) * head_width)
                    shrink = jnp.exp(olds[h] - news[h])
                    m_ref[h] = news[h]
                    l_ref[h] = l_ref[h] * shrink + jnp.sum(chances[h], axis=0, keepdims=True)
                    a_ref[part, :] = a_ref[part, :] * shrink + mixed[h]

            @pl.when(full)
            def _():
                step(False)

            @pl.when(needed & jnp.logical_not(full))
            def _():
                step(True)

            return 0

        lax.fori_loop(0, i + 1, one, 0)
        for h in range(heads):
            part = slice(h * head_width, (h + 1) * head_width)
            ot_ref[part, :] = a_ref[part, :] / l_ref[h]
            lse_ref[pl.ds(h, 1), :] = m_ref[h] + jnp.log(l_ref[h])
            top = m_ref[h]

            @pl.when(i == 0)
            def _():
                top_ref[pl.ds(h, 1), :] = top

            @pl.when(i > 0)
            def _():
                top_ref[pl.ds(h, 1), :] = jnp.maximum(top_ref[pl.ds(h, 1), :], top)

        o_ref[...] = jnp.transpose(ot_ref[...]).astype(bf16)

    row = shape_of((heads, group_rows), f32)
    row_spec = pl.BlockSpec((heads, rows), lambda i, m: (0, i))
    return run(
        body,
        (blocks,),
        [
            (
                q,
                pl.BlockSpec(
                    (heads, rows, head_width), lambda i, m: (0, m[layout["inverse"] + i], 0)
                ),
            ),
            (k, whole(k)),
            (vt, whole(vt)),
        ],
        [
            (
                shape_of((group_rows, width), bf16),
                pl.BlockSpec((rows, width), lambda i, m: (m[layout["inverse"] + i], 0)),
            ),
            (shape_of((width, group_rows), f32), pl.BlockSpec((width, rows), lambda i, m: (0, i))),
            (row, row_spec),
            (shape_of((heads, rows), f32), pl.BlockSpec((heads, rows), lambda i, m: (0, 0))),
        ],
        scratch=[
            pltpu.VMEM((heads, 1, rows), f32),
            pltpu.VMEM((heads, 1, rows), f32),
            pltpu.VMEM((width, rows), f32),
            pltpu.VMEM((heads, head_width, rows), bf16),
        ],
        meta=meta,
        flops=2 * 2 * group_rows * group_rows * width,
        moved=group_rows * width * 14,
        exps=group_rows * group_rows * heads // 2,
    )


def attend_back(meta, q, k, v, kt, grad, w_out, ot, lse, rows, layout, shares):
    heads, group_rows, head_width = q.shape
    blocks = group_rows // rows
    width = heads * head_width
    scale = head_width**-0.5
    per = grad.shape[1] // rows

    _, half, lanes = shares[0].shape
    tall = 2 * half // blocks
    wide = lanes // blocks if lanes // blocks >= 128 else lanes
    last = lanes // wide

    def body(meta_ref, q_ref, k_ref, v_ref, kt_ref, grad_ref, w_ref, *refs):
        ot_ref, lse_ref = refs[:2]
        flat_refs, turned_refs = refs[2:6], refs[6:8]
        up_outs, down_out = refs[10:12], refs[12]
        refs = refs[:2] + refs[8:10] + refs[13:]
        ot_ref, lse_ref, out_ref, rows_ref, dk_ref, dv_ref, dq_ref, g_ref, delta_ref, sum_ref, qt_ref, gt_ref = refs
        i = pl.program_id(0)

        @pl.when(i == 0)
        def _():
            dk_ref[...] = jnp.zeros_like(dk_ref)
            dv_ref[...] = jnp.zeros_like(dv_ref)

        core = lax.div(i, blocks // 2)
        for n in range(2):

            @pl.when(core == (meta_ref[2] ^ n))
            def _():
                for g in range(2):
                    up_outs[g][0] = flat_refs[2 * n + g][0].astype(f32)

        @pl.when(i < last)
        def _():
            for n in range(2):
                to = pl.multiple_of((meta_ref[2] ^ n) * half, half)
                down_out[0, :, pl.ds(to, half)] = jnp.transpose(turned_refs[n][0].astype(f32))

        da = grad_ref[0]
        g = mm(da, w_ref[0], NT).astype(bf16)
        part_sum = mm(ot_ref[...].astype(bf16), da)

        @pl.when(i == 0)
        def _():
            sum_ref[...] = part_sum

        @pl.when(i > 0)
        def _():
            sum_ref[...] += part_sum

        for h in range(heads):
            g_ref[h] = g[:, h * head_width : (h + 1) * head_width]
        turned = jnp.transpose(g.astype(f32))
        gt_ref[...] = turned.astype(bf16)
        for h in range(heads):
            qt_ref[h] = jnp.transpose(q_ref[h])
        product = turned * ot_ref[...]
        for h in range(heads):
            part = slice(h * head_width, (h + 1) * head_width)
            delta_ref[h] = jnp.sum(product[part, :], axis=0, keepdims=True)

        dq_ref[...] = jnp.zeros_like(dq_ref)

        def one(j, _):
            q_first, k_first, needed, full = block_range(meta_ref, i, j, rows, layout)
            at = pl.multiple_of(meta_ref[layout["inverse"] + j] * rows, rows)
            to = pl.multiple_of(j * rows, rows)

            def step(masked):
                if masked:
                    allowed = allowed_pairs(meta_ref, q_first, k_first, rows, layout)
                parts = [slice(h * head_width, (h + 1) * head_width) for h in range(heads)]
                scores = [mm(k_ref[h, pl.ds(at, rows), :], qt_ref[h]) for h in range(heads)]
                downs = [
                    mm(v_ref[h, pl.ds(at, rows), :], gt_ref[parts[h], :]) for h in range(heads)
                ]
                if masked:
                    scores = [jnp.where(allowed, s, mask_fill) for s in scores]
                chances = [jnp.exp(scores[h] - lse_ref[pl.ds(h, 1), :]) for h in range(heads)]
                slopes = [
                    (chances[h] * (downs[h] - delta_ref[h])).astype(bf16) for h in range(heads)
                ]
                for h in range(heads):
                    dv_ref[h, pl.ds(to, rows), :] += mm(chances[h].astype(bf16), g_ref[h])
                    dk_ref[h, pl.ds(to, rows), :] += mm(slopes[h], q_ref[h])
                    dq_ref[parts[h], :] += mm(kt_ref[parts[h], pl.ds(at, rows)], slopes[h])

            @pl.when(full)
            def _():
                step(False)

            @pl.when(needed & jnp.logical_not(full))
            def _():
                step(True)

            return 0

        lax.fori_loop(0, i + 1, one, 0)
        here = pl.multiple_of(meta_ref[layout["inverse"] + i] * rows, rows)
        out_ref[pl.ds(here, rows), 0:width] = (jnp.transpose(dq_ref[...]) * scale).astype(bf16)

        @pl.when(i == blocks - 1)
        def _():
            rows_ref[...] = sum_ref[...].astype(bf16)

            def store(b, _):
                spot = pl.multiple_of(b * rows, rows)
                there = pl.multiple_of(meta_ref[layout["inverse"] + b] * rows, rows)
                out_ref[pl.ds(there, rows), width : 3 * width] = jnp.concatenate(
                    [dk_ref[h, pl.ds(spot, rows), :] for h in range(heads)]
                    + [dv_ref[h, pl.ds(spot, rows), :] for h in range(heads)],
                    axis=1,
                ).astype(bf16)
                return 0

            lax.fori_loop(0, blocks, store, 0)

    def flat_spec(g, n):
        def index(i, m):
            now = jnp.clip(i - (m[2] ^ n) * (blocks // 2), 0, blocks // 2 - 1)
            return (g, now, 0)

        return pl.BlockSpec((1, tall, lanes), index)

    def turned_place(i, m):
        return (2, 0, jnp.minimum(i, last - 1))

    local = layout["sides"]
    placed = [
        (
            shape_of((local, 2 * half, lanes), f32),
            pl.BlockSpec((1, tall, lanes), lambda i, m: (m[3], i, 0)),
        )
    ] * 2 + [
        (
            shape_of((local, lanes, 2 * half), f32),
            pl.BlockSpec(
                (1, wide, 2 * half), lambda i, m: (m[3], jnp.minimum(i, last - 1), 0)
            ),
        )
    ]
    out = shape_of((group_rows, 3 * width), bf16)
    out_rows = shape_of((width, grad.shape[2]), bf16)
    return run(
        body,
        (blocks,),
        [
            (
                q,
                pl.BlockSpec(
                    (heads, rows, head_width), lambda i, m: (0, m[layout["inverse"] + i], 0)
                ),
            ),
            (k, whole(k)),
            (v, whole(v)),
            (kt, whole(kt)),
        ]
        + [
            (
                grad,
                pl.BlockSpec(
                    (1, rows, grad.shape[2]),
                    lambda i, m: (
                        m[layout["inverse"] + i] // per, m[layout["inverse"] + i] % per, 0
                    ),
                ),
            ),
            (w_out, pl.BlockSpec((1, width, grad.shape[2]), lambda i, m: (m[0], 0, 0))),
            (ot, pl.BlockSpec((width, rows), lambda i, m: (0, i))),
            (lse, pl.BlockSpec((heads, rows), lambda i, m: (0, i))),
        ]
        + [(shares[n], flat_spec(g, n)) for n in range(2) for g in range(2)]
        + [(shares[n], pl.BlockSpec((1, half, wide), turned_place)) for n in range(2)],
        [(out, whole(out)), (out_rows, whole(out_rows))] + placed,
        scratch=[
            pltpu.VMEM((heads, group_rows, head_width), f32),
            pltpu.VMEM((heads, group_rows, head_width), f32),
            pltpu.VMEM((width, rows), f32),
            pltpu.VMEM((heads, rows, head_width), bf16),
            pltpu.VMEM((heads, 1, rows), f32),
            pltpu.VMEM((width, grad.shape[2]), f32),
            pltpu.VMEM((heads, head_width, rows), bf16),
            pltpu.VMEM((width, rows), bf16),
        ],
        meta=meta,
        flops=5 * 2 * group_rows * group_rows * width,
        moved=group_rows * width * 24,
        exps=group_rows * group_rows * heads // 2,
    )


def slot_choice(first, count, target_ref):
    rows = target_ref.shape[1]
    ids = first + lax.broadcasted_iota(jnp.int32, (count, rows), 0)
    match = (ids == target_ref[0:1, :]) | (ids == target_ref[1:2, :])
    return jnp.where(match, 1.0, 0.0).astype(bf16)


def token_front(
    x, o, w_out, gain, router_t, previous_t, w_carry, target_rows, grad, routes, logit_w, vectors, local
):
    rows, width = x.shape
    members, columns = w_out.shape[0], w_out.shape[1]
    expert_all = router_t.shape[0]
    groups = lax.axis_size("exp")
    places = groups * local
    expert_count = places
    kinds = vectors.shape[0]
    tile = 128

    def body(*refs):
        (x_ref, o_hbm, w_ref, gain_ref, router_ref, prev_ref, carry_ref, target_ref) = refs[:8]
        dy_ref, route_ref, lw_ref, vec_ref = refs[8:12]
        x1_ref, h2_ref, prob_ref, rows_out, gates_out, base_ref, dh_ref, dgate_ref, sums_ref = refs[12:21]
        o_near, low, split, packed, arrived, gate_mine, gate_near = refs[21:28]
        o_s, o_r, t_s, t_r, g_s, g_r, out_sem = refs[28:]
        me, exp_now = lax.axis_index("ctx"), lax.axis_index("exp")
        side = lax.div(me, 2)
        peers = [{"ctx": flip(me, j)} for j in range(1, members)]
        peers += [slot_peer(r, local, exp_now, me) for r in range(local, places)]
        ready = greet(peers)

        own_o = pltpu.make_async_copy(o_hbm.at[pl.ds(0, rows), :], o_near.at[0], o_r.at[0])

        def o_copy(j, t):
            src = o_hbm.at[pl.ds(pl.multiple_of(j * rows + t * tile, tile), tile), :]
            dst = o_near.at[j, pl.ds(pl.multiple_of(t * tile, tile), tile), :]
            n = j * (rows // tile) + t
            return remote(src, dst, o_s.at[n], o_r.at[n], {"ctx": flip(me, j)})

        def row_copy(r):
            return remote(
                packed.at[r], arrived.at[r], t_s.at[r], t_r.at[r], slot_peer(r, local, exp_now, me)
            )

        def gate_copy(r):
            return remote(
                gate_mine.at[r], gate_near.at[r], g_s.at[r], g_r.at[r],
                slot_peer(r, local, exp_now, me),
            )

        own_o.start()
        ready()
        for t in range(rows // tile):
            for j in range(members - 1, 0, -1):
                o_copy(j, t).start()
        own_o.wait()

        def front_rows(t, _):
            here = pl.ds(pl.multiple_of(t * tile, tile), tile)
            total = x_ref[here, :].astype(f32) + mm(o_near[0, here, :], w_ref[me])
            for j in range(1, members):
                o_copy(j, t).wait()
            for j in range(1, members):
                total = total + mm(o_near[j, here, :], w_ref[flip(me, j)])
            x1_ref[here, :] = total
            inverse = lax.rsqrt(jnp.mean(total * total, axis=1, keepdims=True) + norm_eps)
            h2 = total * inverse * gain_ref[...]
            h2_ref[here, :] = h2
            logits = mm_full(h2, router_ref[...], NT) + mm_full(
                prev_ref[:, here], carry_ref[...], TN
            )
            shifted = jnp.exp(logits - jnp.max(logits, axis=1, keepdims=True))
            prob = shifted / jnp.sum(shifted, axis=1, keepdims=True)
            prob_ref[here, :] = prob
            low[here, :] = h2.astype(bf16)
            top = prob.astype(bf16)
            rest = prob - top.astype(f32)
            middle = rest.astype(bf16)
            split[0, here, :] = top
            split[1, here, :] = middle
            split[2, here, :] = (rest - middle.astype(f32)).astype(bf16)
            return 0

        lax.fori_loop(0, rows // tile, front_rows, 0)
        diagonal = lax.broadcasted_iota(jnp.int32, (CAP, CAP), 0) == lax.broadcasted_iota(
            jnp.int32, (CAP, CAP), 1
        )
        lanes = lax.broadcasted_iota(jnp.int32, (CAP, expert_all), 1)
        for r in list(range(1, places)) + [0]:
            choice = slot_choice(r * CAP, CAP, target_ref)
            packed[r] = mm(choice, low[...]).astype(bf16)
            picked = mm(choice, split[0]) + mm(choice, split[1]) + mm(choice, split[2])
            expert = flip(exp_now, r // local) * local + flip(side, r % local)
            column = jnp.sum(jnp.where(lanes == expert, picked, 0.0), axis=1, keepdims=True)
            gate_mine[r] = jnp.sum(jnp.where(diagonal, column, 0.0), axis=0, keepdims=True)
            last = r - 1 if r else places - 1
            if last:
                row_copy(last).start()
                gate_copy(last).start()

        def own_copy(n):
            src, dst = (packed, rows_out) if n == 0 else (gate_mine, gates_out)
            return pltpu.make_async_copy(src.at[0], dst.at[0], out_sem.at[n])

        own_copy(0).start()
        own_copy(1).start()

        def zero_rows(t, _):
            here = pl.ds(pl.multiple_of(t * tile, tile), tile)
            h2 = h2_ref[here, :]
            dy = dy_ref[here, :].astype(f32)
            prob_now = prob_ref[here, :]
            classes = lax.broadcasted_iota(jnp.int32, (tile, expert_all), 1)
            chosen = route_ref[here, :]
            ids = [chosen[:, c : c + 1] for c in range(2)]
            gates = [
                jnp.sum(jnp.where(classes == r, prob_now, 0.0), axis=1, keepdims=True) for r in ids
            ]
            along = jnp.sum(dy * h2, axis=1, keepdims=True)
            copies = [(r == expert_count + 1).astype(f32) for r in ids]
            keep = copies[0] * gates[0] + copies[1] * gates[1]
            dgates = [copies[c] * along for c in range(2)]
            scores = [
                jnp.sum(h2 * lw_ref[n : n + 1, :], axis=1, keepdims=True) for n in range(2 * kinds)
            ]
            base = x1_ref[here, :]
            dh = jnp.zeros_like(h2)
            for j in range(kinds):
                top = jnp.maximum(scores[2 * j], scores[2 * j + 1])
                e0 = jnp.exp(scores[2 * j] - top)
                e1 = jnp.exp(scores[2 * j + 1] - top)
                a0 = e0 / (e0 + e1)
                a1 = e1 / (e0 + e1)
                vec = vec_ref[j : j + 1, :]
                along_vec = jnp.sum(dy * vec, axis=1, keepdims=True)
                these = [(r == expert_count + 2 + j).astype(f32) for r in ids]
                weight = these[0] * gates[0] + these[1] * gates[1]
                for c in range(2):
                    dgates[c] = dgates[c] + these[c] * (a0 * along + a1 * along_vec)
                keep = keep + weight * a0
                base = base + (weight * a1) * vec
                d0 = weight * along
                d1 = weight * along_vec
                mean = a0 * d0 + a1 * d1
                z0 = a0 * (d0 - mean)
                z1 = a1 * (d1 - mean)
                dh = dh + z0 * lw_ref[2 * j : 2 * j + 1, :] + z1 * lw_ref[2 * j + 1 : 2 * j + 2, :]
                sums_ref[j : j + 1, :] += jnp.sum((weight * a1) * dy, axis=0, keepdims=True)
                at = kinds + 2 * j
                sums_ref[at : at + 1, :] += jnp.sum(z0 * h2, axis=0, keepdims=True)
                sums_ref[at + 1 : at + 2, :] += jnp.sum(z1 * h2, axis=0, keepdims=True)
            base_ref[here, :] = base + keep * h2
            dh_ref[here, :] = dh + keep * dy
            dgate_ref[here, :] = jnp.concatenate(dgates, axis=1)
            return 0

        sums_ref[...] = jnp.zeros_like(sums_ref)
        lax.fori_loop(0, rows // tile, zero_rows, 0)

        def rows_store(r):
            return pltpu.make_async_copy(arrived.at[r], rows_out.at[r], out_sem.at[2 * r])

        def gates_store(r):
            return pltpu.make_async_copy(gate_near.at[r], gates_out.at[r], out_sem.at[2 * r + 1])

        for r in range(1, places):
            row_copy(r).wait()
            gate_copy(r).wait()
            rows_store(r).start()
            gates_store(r).start()
        own_copy(0).wait()
        own_copy(1).wait()
        for r in range(1, places):
            rows_store(r).wait()
            gates_store(r).wait()

    wide = shape_of((rows, width), f32)
    placed = shape_of((places, CAP, width), bf16)
    lines = shape_of((places, 1, CAP), f32)
    return run(
        body,
        (),
        [(x, vector), (o, anywhere), (w_out, vector), (gain, vector), (router_t, vector)]
        + [(previous_t, vector), (w_carry, vector), (target_rows, vector), (grad, vector)]
        + [(routes, vector), (logit_w, vector), (vectors, vector)],
        [(wide, vector), (wide, vector), (shape_of((rows, expert_all), f32), vector)]
        + [(placed, anywhere), (lines, anywhere), (wide, vector), (wide, vector)]
        + [(shape_of((rows, 2), f32), vector), (shape_of((3 * kinds, width), f32), vector)],
        scratch=[
            pltpu.VMEM((members, rows, columns), bf16),
            pltpu.VMEM((rows, width), bf16),
            pltpu.VMEM((3, rows, expert_all), bf16),
            pltpu.VMEM((places, CAP, width), bf16),
            pltpu.VMEM((places, CAP, width), bf16),
            pltpu.VMEM((places, 1, CAP), f32),
            pltpu.VMEM((places, 1, CAP), f32),
            dma((members * (rows // tile),)), dma((members * (rows // tile),)),
            dma((places,)), dma((places,)), dma((places,)), dma((places,)),
            dma((2 * places,)),
        ],
        flops=2 * rows * width * (width + places * CAP),
        moved=rows * width * 30,
        talks=1,
    )


def expert_layer(arrived, grads, late, gates, w_gate, w_up, w_down):
    places = arrived.shape[0]
    local = w_gate.shape[0]
    rows = places * CAP
    width, hidden = w_gate.shape[1], w_gate.shape[2]
    parts = lax.axis_size("dp")
    groups = places // local
    half = width // 2
    per_part = hidden // parts
    tile = min(256, per_part)
    steps = hidden // tile
    tiles = per_part // tile
    away = steps - tiles
    lead = (away + 2) // 4
    kept = steps - lead
    chunk = 256

    def body(*refs):
        x_ref, dy_ref, gates_ref, wg_hbm, wu_hbm, wd_hbm = refs[:6]
        dy_late, refs = refs[6 : 6 + len(late)], refs[:6] + refs[6 + len(late) :]
        dy_parts = [
            dy_late[r // local] if r % local else dy_ref.at[r // local] for r in range(places)
        ]
        y_out, refs = refs[6 : 6 + groups], refs[6 + groups :]
        it = iter(refs)

        def take(count):
            return [next(it) for _ in range(count)]

        dx_out, dots_out, sum_out, beside_out = take(4)
        x_all, xt_all, dy_all, dyt_all, gate_all, y_acc, dx_acc, dot_acc = take(8)
        wg_buf, wu_buf, wd_buf, wg_keep, wu_keep, wd_keep = take(6)
        hid_keep, dg_keep, du_keep, scaled_keep = take(4)
        send, total, taken, far, dx_low, dx_near, dots, dots_near = take(8)
        beside, y_odd, relay = take(3)
        in_sem, w_sem, keep_sem, c_s, c_r, f_s, f_r, b_s, b_r, d_s, d_r, out_sem = take(12)
        e_s, e_r, beside_sem, y_s, y_r, dx_sem = take(6)
        me, exp_now, dp_now = lax.axis_index("ctx"), lax.axis_index("exp"), lax.axis_index("dp")
        core, side = lax.rem(me, 2), lax.div(me, 2)
        sibling = {"ctx": flip(me, 1)}
        peers = [sibling] + [{"dp": flip(dp_now, d)} for d in range(1, parts)]
        peers += [slot_peer(r, local, exp_now, me) for r in range(1, places)]
        ready = greet(peers)
        diagonal = lax.broadcasted_iota(jnp.int32, (CAP, CAP), 0) == lax.broadcasted_iota(
            jnp.int32, (CAP, CAP), 1
        )

        def dp_of(f):
            distance = parts - 1 - lax.div(f, tiles)
            found, bit = dp_now, 1
            while bit < parts:
                on = lax.rem(lax.div(distance, bit), 2)
                now = lax.rem(lax.div(found, bit), 2)
                found = found + on * bit * (1 - 2 * now)
                bit *= 2
            return found

        def weights(f, slot):
            at = pl.multiple_of(dp_of(f) * per_part + lax.rem(f, tiles) * tile, tile)
            return [
                pltpu.make_async_copy(
                    wg_hbm.at[side, :, pl.ds(at, tile)], wg_buf.at[slot], w_sem.at[0, slot]
                ),
                pltpu.make_async_copy(
                    wu_hbm.at[side, :, pl.ds(at, tile)], wu_buf.at[slot], w_sem.at[1, slot]
                ),
                pltpu.make_async_copy(
                    wd_hbm.at[side, pl.ds(at, tile), :], wd_buf.at[slot], w_sem.at[2, slot]
                ),
            ]

        def core_copy(f, slot):
            return remote(send.at[slot], taken.at[f], c_s.at[slot], c_r.at[f], sibling)

        def far_copy(f):
            return remote(total.at[f], far.at[f], f_s.at[f], f_r.at[f], {"dp": dp_of(f)})

        def back_copy(r):
            return remote(
                dx_low.at[r], dx_near.at[r], b_s.at[r], b_r.at[r],
                slot_peer(r, local, exp_now, me),
            )

        def dots_copy(r):
            return remote(
                dots.at[r], dots_near.at[r], d_s.at[r], d_r.at[r],
                slot_peer(r, local, exp_now, me),
            )

        def keep_weights(k):
            f = lead + k
            at = pl.multiple_of(dp_of(f) * per_part + (f % tiles) * tile, tile)
            return [
                pltpu.make_async_copy(
                    wg_hbm.at[side, :, pl.ds(at, tile)], wg_keep.at[k], keep_sem.at[0, k]
                ),
                pltpu.make_async_copy(
                    wu_hbm.at[side, :, pl.ds(at, tile)], wu_keep.at[k], keep_sem.at[1, k]
                ),
                pltpu.make_async_copy(
                    wd_hbm.at[side, pl.ds(at, tile), :], wd_keep.at[k], keep_sem.at[2, k]
                ),
            ]

        def rows_in(r):
            here = pl.ds(r * CAP, CAP)
            return [
                pltpu.make_async_copy(x_ref.at[r], x_all.at[here, :], in_sem.at[r]),
                pltpu.make_async_copy(dy_parts[r], dy_all.at[here, :], in_sem.at[places + r]),
            ]

        for r in range(places):
            for copy in rows_in(r):
                copy.start()
        if lead:
            for copy in weights(0, 0):
                copy.start()
        for k in range(kept):
            for copy in keep_weights(k):
                copy.start()
        first_half = pl.ds(pl.multiple_of((1 - core) * half, half), half)
        second_half = pl.ds(pl.multiple_of(core * half, half), half)
        for r in range(places):
            here = slice(r * CAP, (r + 1) * CAP)
            for copy in rows_in(r):
                copy.wait()
            turned = jnp.transpose(x_all[here, :])
            xt_all[first_half, here] = turned[:half, :]
            xt_all[second_half, here] = turned[half:, :]
            turned = jnp.transpose(dy_all[here, :])
            dyt_all[first_half, here] = turned[:half, :]
            dyt_all[second_half, here] = turned[half:, :]
            gate_all[here, :] = jnp.sum(
                jnp.where(diagonal, gates_ref[r], 0.0), axis=1, keepdims=True
            )
        y_acc[...] = jnp.zeros_like(y_acc)
        dx_acc[...] = jnp.zeros_like(dx_acc)
        dot_acc[...] = jnp.zeros_like(dot_acc)
        ready()

        def core_sum(f):
            core_copy(f, lax.rem(f, 2)).wait_recv()
            for n in range(3):
                total[f, n] = (total[f, n].astype(f32) + taken[f, n].astype(f32)).astype(bf16)

        def forward_back(here, wg, wu, wd, hid_ref, dg_ref, du_ref, scaled_ref):
            g_pre = mm(x_all[here, :], wg)
            u_pre = mm(x_all[here, :], wu)
            back = mm(dy_all[here, :], wd, NT)
            gate = gate_all[here, :]
            sig = 1.0 / (1.0 + jnp.exp(-g_pre))
            act = g_pre * sig
            hid = act * u_pre
            hid_ref[here, :] = hid.astype(bf16)
            scaled_ref[here, :] = (gate * hid).astype(bf16)
            along = hid * back
            lines = along[:, 0:128]
            for n in range(1, tile // 128):
                lines = lines + along[:, n * 128 : (n + 1) * 128]
            dot_acc[here, :] += lines
            dhid = gate * back
            dg = (dhid * u_pre * sig * (1.0 + g_pre * (1.0 - sig))).astype(bf16)
            du = (dhid * act).astype(bf16)
            dg_ref[here, :] = dg
            du_ref[here, :] = du

        def rows_back(here, wg, wu, dg_ref, du_ref):
            dx_acc[here, :] += mm(dg_ref[here, :], wg, NT) + mm(du_ref[here, :], wu, NT)

        def weight_sums(f, slot, dg_ref, du_ref, scaled_ref, first):
            @pl.when(f > first)
            def _():
                core_sum(f - 1)

            @pl.when(f >= 2)
            def _():
                core_copy(f - 2, slot).wait_send()

            for n, (left, right) in enumerate(
                ((xt_all, dg_ref), (xt_all, du_ref), (dyt_all, scaled_ref))
            ):
                found = mm(left[...], right[...]).astype(bf16)
                send[slot, n] = found[:half, :]
                total[f, n] = found[half:, :]
            core_copy(f, slot).start()

            @pl.when((f > first) & (f - 1 < away))
            def _():
                far_copy(f - 1).start()

        def lead_step(f, _):
            slot = lax.rem(f, 2)
            for copy in weights(f, slot):
                copy.wait()

            @pl.when(f + 1 < lead)
            def _():
                for copy in weights(f + 1, 1 - slot):
                    copy.start()

            hid, dg, du, scaled = (a.at[0] for a in (hid_keep, dg_keep, du_keep, scaled_keep))

            def row_chunk(c, _):
                here = pl.ds(pl.multiple_of(c * chunk, chunk), chunk)
                forward_back(here, wg_buf[slot], wu_buf[slot], wd_buf[slot], hid, dg, du, scaled)
                return 0

            lax.fori_loop(0, rows // chunk, row_chunk, 0)
            weight_sums(f, slot, dg, du, scaled, 0)
            y_acc[...] += mm(hid[...], wd_buf[slot])
            rows_back(slice(0, rows), wg_buf[slot], wu_buf[slot], dg, du)
            return 0

        lax.fori_loop(0, lead, lead_step, 0)
        if lead:
            core_sum(lead - 1)
            far_copy(lead - 1).start()
        for k in range(kept):
            for copy in keep_weights(k):
                copy.wait()

        def keep_rows(k, first, count):
            size = min(chunk, count)
            for c in range(count // size):
                forward_back(
                    slice(first + c * size, first + (c + 1) * size),
                    wg_keep[k], wu_keep[k], wd_keep[k],
                    hid_keep.at[k], dg_keep.at[k], du_keep.at[k], scaled_keep.at[k],
                )
            rows_back(
                slice(first, first + count), wg_keep[k], wu_keep[k], dg_keep.at[k], du_keep.at[k]
            )

        def send_back(first, last):
            for r in range(first, last):
                here = slice(r * CAP, (r + 1) * CAP)
                dx_low[r] = dx_acc[here, :].astype(bf16)
                column = jnp.sum(dot_acc[here, :], axis=1, keepdims=True)
                dots[r] = jnp.sum(jnp.where(diagonal, column, 0.0), axis=0, keepdims=True)
                if r - 1 >= max(1, first):
                    back_copy(r - 1).start()
                    dots_copy(r - 1).start()

        def send_last(r):
            back_copy(r).start()
            dots_copy(r).start()

        middle = places // 2
        near_rows = middle * CAP

        def far_step(k, _):
            keep_rows(k, near_rows, rows - near_rows)
            return 0

        lax.fori_loop(0, kept, far_step, 0)
        send_back(middle, places)

        def away_step(f, _):
            k = f - lead

            keep_rows(k, 0, near_rows)

            @pl.when(k == 0)
            def _():
                send_last(places - 1)

            weight_sums(
                f, lax.rem(f, 2), dg_keep.at[k], du_keep.at[k], scaled_keep.at[k], lead
            )
            return 0

        lax.fori_loop(lead, away, away_step, 0)
        if away == lead:
            send_last(places - 1)
        else:
            core_sum(away - 1)
            far_copy(away - 1).start()

        def near_step(k, _):
            keep_rows(k, 0, near_rows)
            return 0

        lax.fori_loop(away - lead, kept, near_step, 0)
        send_back(0, middle)

        def own_result(k, _):
            y_acc[...] += mm(hid_keep[k], wd_keep[k])
            return 0

        lax.fori_loop(0, kept, own_result, 0)
        send_last(middle - 1)

        def relay_copy(g):
            return remote(y_odd.at[g], relay.at[g], y_s.at[g], y_r.at[g], {"ctx": flip(me, 2)})

        def result(r):
            here = slice(r * CAP, (r + 1) * CAP)
            return (gate_all[here, :] * y_acc[here, :]).astype(bf16)

        for g in range(groups):
            y_odd[g] = result(local * g + 1)
            if g:
                relay_copy(g - 1).start()
        for g in range(groups):
            y_out[g][0] = result(local * g)
        relay_copy(groups - 1).start()

        def own_step(f, _):
            k = f - lead
            weight_sums(
                f, lax.rem(f, 2), dg_keep.at[k], du_keep.at[k], scaled_keep.at[k], away
            )
            return 0

        lax.fori_loop(away, steps, own_step, 0)
        core_sum(steps - 1)

        def beside_copy(i):
            return remote(total.at[away + i], beside.at[i], e_s.at[i], e_r.at[i], sibling)

        def beside_store(i):
            return pltpu.make_async_copy(
                beside.at[i], beside_out.at[:, :, pl.ds(i * tile, tile)], beside_sem.at[i]
            )

        def sum_store(i):
            return pltpu.make_async_copy(
                total.at[away + i], sum_out.at[:, :, pl.ds(i * tile, tile)], out_sem.at[i]
            )

        for i in range(tiles):
            for d in range(1, parts):
                far_copy((parts - 1 - d) * tiles + i).wait_recv()
            for n in range(3):
                value = total[away + i, n].astype(f32)
                for d in range(1, parts):
                    value = value + far[(parts - 1 - d) * tiles + i, n].astype(f32)
                total[away + i, n] = value.astype(bf16)
            if i:
                beside_copy(i - 1).start()
            sum_store(i).start()
        beside_copy(tiles - 1).start()
        for f in range(away):
            far_copy(f).wait_send()
        for f in range(max(0, steps - 2), steps):
            core_copy(f, f % 2).wait_send()

        def dx_store(r):
            src = dx_near.at[r] if r else dx_low.at[0]
            return pltpu.make_async_copy(src, dx_out.at[r], dx_sem.at[r])

        dots_out[0] = dots[0]
        dx_store(0).start()
        for r in range(1, places):
            back_copy(r).wait()
            dots_copy(r).wait()
            dx_store(r).start()
            dots_out[r] = dots_near[r]
        for g in range(groups):
            relay_copy(g).wait()
            y_out[g][1] = relay[g]
        for i in range(tiles):
            beside_copy(i).wait()
            beside_store(i).start()
        for i in range(tiles):
            sum_store(i).wait()
            beside_store(i).wait()
        for r in range(places):
            dx_store(r).wait()

    placed = shape_of((places, CAP, width), bf16)
    pair = shape_of((local, CAP, width), bf16)
    lines = shape_of((places, 1, CAP), f32)
    return run(
        body,
        (),
        [(arrived, anywhere), (grads, anywhere), (gates, vector)]
        + [(w, anywhere) for w in (w_gate, w_up, w_down)]
        + [(g, anywhere) for g in late],
        [(pair, vector)] * groups
        + [(placed, anywhere), (lines, vector)]
        + [(shape_of((3, half, per_part), bf16), anywhere)] * 2,
        scratch=[
            pltpu.VMEM((rows, width), bf16),
            pltpu.VMEM((width, rows), bf16),
            pltpu.VMEM((rows, width), bf16),
            pltpu.VMEM((width, rows), bf16),
            pltpu.VMEM((rows, 1), f32),
            pltpu.VMEM((rows, width), f32),
            pltpu.VMEM((rows, width), f32),
            pltpu.VMEM((rows, 128), f32),
            pltpu.VMEM((2, width, tile), bf16),
            pltpu.VMEM((2, width, tile), bf16),
            pltpu.VMEM((2, tile, width), bf16),
            pltpu.VMEM((kept, width, tile), bf16),
            pltpu.VMEM((kept, width, tile), bf16),
            pltpu.VMEM((kept, tile, width), bf16),
            pltpu.VMEM((kept, rows, tile), bf16),
            pltpu.VMEM((kept, rows, tile), bf16),
            pltpu.VMEM((kept, rows, tile), bf16),
            pltpu.VMEM((kept, rows, tile), bf16),
            pltpu.VMEM((2, 3, half, tile), bf16),
            pltpu.VMEM((steps, 3, half, tile), bf16),
            pltpu.VMEM((steps, 3, half, tile), bf16),
            pltpu.VMEM((max(1, away), 3, half, tile), bf16),
            pltpu.VMEM((places, CAP, width), bf16),
            pltpu.VMEM((places, CAP, width), bf16),
            pltpu.VMEM((places, 1, CAP), f32),
            pltpu.VMEM((places, 1, CAP), f32),
            pltpu.VMEM((tiles, 3, half, tile), bf16),
            pltpu.VMEM((groups, CAP, width), bf16),
            pltpu.VMEM((groups, CAP, width), bf16),
            dma((2 * places,)), dma((3, 2)), dma((3, kept)), dma((2,)), dma((steps,)),
            dma((max(1, away),)), dma((max(1, away),)),
            dma((places,)), dma((places,)), dma((places,)), dma((places,)),
            dma((tiles,)), dma((tiles,)), dma((tiles,)), dma((tiles,)),
            dma((groups,)), dma((groups,)), dma((places,)),
        ],
        flops=9 * 2 * rows * width * hidden,
        moved=12 * width * hidden + rows * width * 8,
        exps=rows * hidden,
        talks=2,
    )


def slot_sum(targets, source_ref):
    tile = targets.shape[0]
    total = None
    for r in range(source_ref.shape[0]):
        ids = r * CAP + lax.broadcasted_iota(jnp.int32, (tile, CAP), 1)
        choice = jnp.where((ids == targets[:, 0:1]) | (ids == targets[:, 1:2]), 1.0, 0.0)
        part = mm(choice.astype(bf16), source_ref[r])
        total = part if total is None else total + part
    return total


def token_back(
    x1, h2, grad, prob, previous_t, routes, targets, back, dots, dgate_zero, dh_zero, gain, router_t,
    zero_sums,
):
    rows, width = x1.shape
    tile = 128
    tiles = rows // tile
    places = back.shape[0]
    expert_all = prob.shape[1]
    members = lax.axis_size("ctx")
    last = expert_all + 1 + zero_sums.shape[0]

    def body(*refs):
        (x1_ref, h2_ref, dy_ref, prob_ref, prev_ref, route_ref, target_ref) = refs[:7]
        back_ref, dots_ref, dz_ref, dh_ref, gain_ref, router_ref, zero_ref = refs[7:14]
        dx1_ref, sums_ref, da_out, da_near, a_s, a_r, out_sem = refs[14:]
        me = lax.axis_index("ctx")
        peers = [{"ctx": flip(me, 1)}, {"ctx": flip(me, 2)}]
        ready = greet(peers)

        def da_copy(kind, t):
            here = pl.ds(pl.multiple_of(t * tile, tile), tile)
            n = kind * tiles + t
            src, dst = ((0, 1), (0, 2), (2, 3))[kind]
            return remote(
                da_near.at[src, here, :], da_near.at[dst, here, :], a_s.at[n], a_r.at[n],
                {"ctx": flip(me, 2 if kind == 1 else 1)},
            )

        sums_ref[...] = jnp.zeros_like(sums_ref)
        sums_ref[expert_all + 1 : last, :] = zero_ref[...]
        ready()

        def token_rows(t, _):
            here = pl.ds(pl.multiple_of(t * tile, tile), tile)
            prob_now = prob_ref[here, :]
            chosen, target, zero = route_ref[here, :], target_ref[here, :], dz_ref[here, :]
            lanes = lax.broadcasted_iota(jnp.int32, (tile, expert_all), 1)
            dprob = jnp.zeros_like(prob_now)
            for c in range(2):
                dgate = zero[:, c : c + 1]
                for n in range(places):
                    ids = n * CAP + lax.broadcasted_iota(jnp.int32, (tile, CAP), 1)
                    dgate = dgate + jnp.sum(
                        jnp.where(ids == target[:, c : c + 1], dots_ref[n], 0.0),
                        axis=1,
                        keepdims=True,
                    )
                dprob = dprob + jnp.where(lanes == chosen[:, c : c + 1], dgate, 0.0)
            dlogit = prob_now * (dprob - jnp.sum(prob_now * dprob, axis=1, keepdims=True))
            h2 = h2_ref[here, :]
            dh2 = slot_sum(target, back_ref) + dh_ref[here, :] + mm_full(dlogit, router_ref[...])
            x1 = x1_ref[here, :]
            inverse = lax.rsqrt(jnp.mean(x1 * x1, axis=1, keepdims=True) + norm_eps)
            normed = x1 * inverse
            dn = dh2 * gain_ref[...]
            dx1 = dy_ref[here, :].astype(f32) + inverse * (
                dn - normed * jnp.mean(dn * normed, axis=1, keepdims=True)
            )
            dx1_ref[here, :] = dx1
            da_near[0, here, :] = dx1.astype(bf16)
            sums_ref[0:expert_all, :] += mm_full(dlogit, h2, TN)
            sums_ref[expert_all : expert_all + 1, :] += jnp.sum(dh2 * normed, axis=0, keepdims=True)
            sums_ref[last:, 0:expert_all] += mm_full(prev_ref[:, here], dlogit)
            da_copy(1, t).start()
            da_copy(0, t).start()

            @pl.when(t >= 2)
            def _():
                da_copy(1, t - 2).wait_recv()
                da_copy(2, t - 2).start()

            return 0

        lax.fori_loop(0, tiles, token_rows, 0)
        for t in range(max(0, tiles - 2), tiles):
            da_copy(1, t).wait_recv()
            da_copy(2, t).start()
        mine = pltpu.make_async_copy(da_near.at[0], da_out.at[0], out_sem.at[0])
        mine.start()
        for t in range(tiles):
            da_copy(0, t).wait()
            da_copy(1, t).wait_send()
            da_copy(2, t).wait()
        rest = pltpu.make_async_copy(
            da_near.at[pl.ds(1, members - 1)], da_out.at[pl.ds(1, members - 1)], out_sem.at[1]
        )
        rest.start()
        mine.wait()
        rest.wait()

    return run(
        body,
        (),
        [(a, vector) for a in (x1, h2, grad, prob, previous_t, routes, targets, back, dots)]
        + [(a, vector) for a in (dgate_zero, dh_zero, gain, router_t, zero_sums)],
        [(shape_of((rows, width), f32), vector)]
        + [(shape_of((last + expert_all, width), f32), vector)]
        + [(shape_of((members, rows, width), bf16), anywhere)],
        scratch=[
            pltpu.VMEM((members, rows, width), bf16),
            dma((3 * tiles,)), dma((3 * tiles,)), dma((2,)),
        ],
        flops=2 * rows * width * (places * CAP + width),
        moved=rows * width * 24,
        talks=5,
    )


def finish(dqkv_all, h1, x, gain, dx1, weights_t, out_sum, small, tops, produced, base, targets):
    members, per_group = weights_t.shape[1], weights_t.shape[2]
    rows, width = x.shape
    group_rows = dqkv_all.shape[0]
    parts, groups = lax.axis_size("dp"), lax.axis_size("exp")
    team = parts * groups
    local = produced[0].shape[0]
    places = groups * local
    wide_share, out_share = width // (2 * team), per_group // team
    small_rows = small.shape[0]
    small_steps = [(axis, bit) for axis in ("ctx", "dp", "exp") for bit in powers(axis)]
    hops = len(small_steps)
    row_tile = min(256, rows)

    def body(*refs):
        it = iter(refs)

        def take(count=None):
            return next(it) if count is None else [next(it) for _ in range(count)]

        dqkv_hbm, h1_hbm, x_hbm, gain_ref, dx1_hbm, w_hbm, out_ref = take(7)
        small_ref, tops_ref, base_hbm, target_ref = take(4)
        produced_hbm = take(groups)
        input_out, wide_out, flat_out, small_out, gain_out, tops_out, result_out = take(7)
        dqkv, product, h1_all, x_all, dx1_all, w_all, base_all, y_near = take(8)
        part_send, part_core, part_y, y_got, part_own = take(5)
        wide_mine, wide_far_x, wide_far_z, wide_all = take(4)
        flat_mine, flat_far_x, flat_far_z, flat_all = take(4)
        small_acc, small_far, gain_acc, gain_far, tops_acc, tops_far = take(6)
        load_sem, near_s, near_r = take(3)
        wide_sems, flat_sems = [take(12), take(12)], take(12)
        hop_s, hop_r, gain_s, gain_r, top_s, top_r = take(6)

        me = lax.axis_index("ctx")
        dp_now, exp_now = lax.axis_index("dp"), lax.axis_index("exp")
        seat = dp_now * groups + exp_now

        def near_peer(j):
            return {"ctx": flip(me, j)}

        def team_peer(r):
            return {"dp": flip(dp_now, r // groups), "exp": flip(exp_now, r % groups)}

        peers = [near_peer(j) for j in range(1, members)]
        peers += [team_peer(r) for r in range(1, team)]
        ready = greet(peers)

        loads = [
            (dqkv_hbm, dqkv), (h1_hbm, h1_all), (x_hbm, x_all), (dx1_hbm, dx1_all),
            (w_hbm.at[:, me], w_all), (base_hbm, base_all),
        ]
        loads += [
            (produced_hbm[g], y_near.at[pl.ds(g * local, local)]) for g in range(groups)
        ]

        def load(n):
            return pltpu.make_async_copy(loads[n][0], loads[n][1], load_sem.at[n])

        class Dense:
            def __init__(self, mine, far_x, far_z, all_buf, sems):
                self.mine, self.far_x, self.far_z, self.all = mine, far_x, far_z, all_buf
                self.sems = sems

            def own_block(self, d=0):
                return pl.ds(flip(dp_now, d) * groups, groups)

            def x_copy(self, d):
                return remote(
                    self.mine.at[self.own_block(d)], self.far_x.at[d - 1], self.sems[0].at[d],
                    self.sems[1].at[d], {"dp": flip(dp_now, d)},
                )

            def z_copy(self, g):
                return remote(
                    self.mine.at[dp_now * groups + flip(exp_now, g)], self.far_z.at[g - 1],
                    self.sems[2].at[g], self.sems[3].at[g], {"exp": flip(exp_now, g)},
                )

            def gz_copy(self, g, theirs=False):
                spot = self.all.at[0, dp_now * groups + flip(exp_now, g) if theirs else seat]
                return remote(
                    spot, spot, self.sems[4].at[g], self.sems[5].at[g], {"exp": flip(exp_now, g)}
                )

            def gx_copy(self, d, theirs=False):
                spot = self.all.at[0, self.own_block(d if theirs else 0)]
                return remote(
                    spot, spot, self.sems[6].at[d], self.sems[7].at[d], {"dp": flip(dp_now, d)}
                )

            def y_copy(self, d):
                return remote(
                    self.all.at[0, self.own_block(d)], self.all.at[2, self.own_block(d)],
                    self.sems[8].at[d], self.sems[9].at[d], near_peer(2),
                )

            def core_copy(self, n):
                return remote(
                    self.all.at[2 * n], self.all.at[2 * n + 1], self.sems[10].at[n],
                    self.sems[11].at[n], near_peer(1),
                )

            def start(self):
                for d in range(1, parts):
                    self.x_copy(d).start()

            def to_z(self):
                for d in range(1, parts):
                    self.x_copy(d).wait()
                for g in list(range(1, groups)) + [0]:
                    c = dp_now * groups + flip(exp_now, g)
                    value = self.mine[c].astype(f32)
                    for d in range(1, parts):
                        value = value + self.far_x[d - 1, flip(exp_now, g)].astype(f32)
                    self.mine[c] = value.astype(bf16)
                for g in range(1, groups):
                    self.z_copy(g).start()

            def to_gather(self):
                for g in range(1, groups):
                    self.z_copy(g).wait()
                value = self.mine[seat].astype(f32)
                for g in range(1, groups):
                    value = value + self.far_z[g - 1].astype(f32)
                self.all[0, seat] = value.astype(bf16)

            def gather(self):
                for g in range(1, groups):
                    self.gz_copy(g).start()

            def to_x(self):
                for g in range(1, groups):
                    self.gz_copy(g).wait_send()
                    self.gz_copy(g, True).wait_recv()
                for d in range(1, parts):
                    self.gx_copy(d).start()
                self.y_copy(0).start()

            def to_y(self):
                for d in range(1, parts):
                    self.gx_copy(d).wait_send()
                    self.gx_copy(d, True).wait_recv()
                    self.y_copy(d).start()
                self.core_copy(0).start()

            def to_core(self):
                for d in range(parts):
                    self.y_copy(d).wait()
                self.core_copy(1).start()

            def done(self):
                for n in range(2):
                    self.core_copy(n).wait()

        wides = [
            Dense(wide_mine.at[n], wide_far_x.at[n], wide_far_z.at[n], wide_all.at[n], wide_sems[n])
            for n in range(2)
        ]
        flat = Dense(flat_mine, flat_far_x, flat_far_z, flat_all, flat_sems)

        def hop_peer(n):
            axis, bit = small_steps[n]
            return {axis: flip(lax.axis_index(axis), bit)}

        def small_copy(n):
            return remote(small_acc.at[n], small_far.at[n], hop_s.at[n], hop_r.at[n], hop_peer(n))

        def tops_copy(n):
            return remote(tops_acc.at[n], tops_far.at[n], top_s.at[n], top_r.at[n], hop_peer(n))

        def gain_pack(j, theirs=False):
            spot = gain_acc.at[flip(me, j) if theirs else me]
            return remote(spot, spot, gain_s.at[j], gain_r.at[j], near_peer(j))

        def gain_team(r, theirs=False):
            spot = gain_far.at[flip(seat, r) if theirs else seat]
            n = members + r
            return remote(spot, spot, gain_s.at[n], gain_r.at[n], team_peer(r))

        def small_start(n):
            small_copy(n).start()
            tops_copy(n).start()

        def small_sum(n):
            small_copy(n).wait()
            tops_copy(n).wait()
            small_acc[n + 1] = small_acc[n] + small_far[n]
            tops_acc[n + 1] = jnp.maximum(tops_acc[n], tops_far[n])

        small_hops = list(range(hops))

        def small_next():
            if small_hops:
                n = small_hops.pop(0)
                small_sum(n)
                if n + 1 < hops:
                    small_start(n + 1)

        row_tiles = rows // row_tile

        def tile_rows(t, first=0):
            return pl.ds(first + t * row_tile, row_tile)

        def core_part(j, t):
            n = j // 2
            return remote(
                part_send.at[n, tile_rows(t), :], part_core.at[n, tile_rows(t), :],
                near_s.at[n * row_tiles + t], near_r.at[n * row_tiles + t], near_peer(1),
            )

        def y_part(t):
            n = 2 * row_tiles + t
            return remote(
                part_y.at[tile_rows(t), :], y_got.at[tile_rows(t), :], near_s.at[n], near_r.at[n],
                near_peer(2),
            )

        def part(j, t):
            here = pl.ds(j * rows + t * row_tile, row_tile)
            found = None
            for w in range(3):
                add = mm(dqkv[here, w * per_group : (w + 1) * per_group], w_all[w])
                found = add if found is None else found + add
            return found

        for n in range(len(loads)):
            load(n).start()
        small_acc[0] = small_ref[...]
        lanes = lax.broadcasted_iota(jnp.int32, tops_acc.shape[1:], 1)
        tops_acc[0] = jnp.where(
            lanes == me, jnp.max(tops_ref[...], axis=1, keepdims=True), low_start
        )
        flat_rows = out_ref[...].astype(f32)
        for c in range(team):
            flat_mine[c] = flat_rows[c * out_share : (c + 1) * out_share, :].astype(bf16)
        ready()
        flat.start()
        small_start(0)
        load(0).wait()
        load(1).wait()

        def weigh(n, _):
            here = pl.ds(pl.multiple_of(n * rows, rows), rows)
            product[...] += mm(h1_all[here, :], dqkv[here, :], TN)
            return 0

        product[...] = mm(h1_all[0:rows, :], dqkv[0:rows, :], TN)
        lax.fori_loop(1, group_rows // rows, weigh, 0)
        for n in range(2):
            for c in range(team):
                at = (n * team + c) * wide_share
                wide_mine[n, c] = product[at : at + wide_share, :].astype(bf16)
            if n:
                wides[0].start()
        flat.to_z()
        wides[1].start()
        for n in range(2, len(loads)):
            load(n).wait()
        queue = [(j, t) for j in (3, 1) for t in range(row_tiles)]
        for n, (j, t) in enumerate(queue):
            part_send[j // 2, tile_rows(t), :] = part(j, t).astype(bf16)
            if n:
                core_part(*queue[n - 1]).start()
        own_part = [part(2, t) for t in range(1)]
        core_part(*queue[-1]).start()
        for t in range(row_tiles):
            value = own_part[0] if t == 0 else part(2, t)
            core_part(3, t).wait_recv()
            part_y[tile_rows(t), :] = (
                value + part_core[1, tile_rows(t), :].astype(f32)
            ).astype(bf16)
            if t:
                y_part(t - 1).start()
        part_own[tile_rows(0), :] = part(0, 0)
        y_part(row_tiles - 1).start()
        for t in range(1, row_tiles):
            part_own[tile_rows(t), :] = part(0, t)
        wides[0].to_z()
        flat.to_gather()
        small_next()
        wides[1].to_z()
        flat.gather()
        wides[0].to_gather()

        def token_rows(t, _):
            here = pl.ds(pl.multiple_of(t * 128, 128), 128)
            result_out[here, :] = (
                base_all[here, :] + slot_sum(target_ref[here, :], y_near)
            ).astype(bf16)
            return 0

        lax.fori_loop(0, rows // 256, token_rows, 0)
        wides[0].gather()
        small_next()
        flat.to_x()
        wides[1].to_gather()
        lax.fori_loop(rows // 256, rows // 128, token_rows, 0)
        wides[1].gather()
        wides[0].to_x()
        small_next()
        for t in range(row_tiles):
            core_part(1, t).wait()
            core_part(3, t).wait_send()
            y_part(t).wait()

        def input_rows(t, gain_part):
            here = pl.ds(pl.multiple_of(t * row_tile, row_tile), row_tile)
            dh = (
                part_own[here, :] + part_core[0, here, :].astype(f32) + y_got[here, :].astype(f32)
            )
            x_now = x_all[here, :].astype(f32)
            inv = lax.rsqrt(jnp.mean(x_now * x_now, axis=1, keepdims=True) + norm_eps)
            normed = x_now * inv
            dn = dh * gain_ref[...]
            dx1_all[here, :] = dx1_all[here, :] + inv * (
                dn - normed * jnp.mean(dn * normed, axis=1, keepdims=True)
            )
            return gain_part + jnp.sum(dh * normed, axis=0, keepdims=True)

        gain_acc[me] = lax.fori_loop(
            0, rows // row_tile, input_rows, jnp.zeros((1, width), f32)
        )
        store = pltpu.make_async_copy(dx1_all, input_out, load_sem.at[len(loads)])
        store.start()
        flat.to_y()
        for j in range(1, members):
            gain_pack(j).start()
        wides[1].to_x()
        wides[0].to_y()
        for j in range(1, members):
            gain_pack(j).wait_send()
            gain_pack(j, True).wait_recv()
        value = gain_acc[0]
        for n in range(1, members):
            value = value + gain_acc[n]
        gain_far[seat] = value
        small_next()
        flat.to_core()
        for r in range(1, team):
            gain_team(r).start()
        wides[1].to_y()
        wides[0].to_core()
        while small_hops:
            small_next()
        flat.done()
        wides[1].to_core()
        for r in range(1, team):
            gain_team(r).wait_send()
            gain_team(r, True).wait_recv()
        value = gain_far[0]
        for n in range(1, team):
            value = value + gain_far[n]
        gain_out[...] = value[0]
        final = [pltpu.make_async_copy(flat_all, flat_out, load_sem.at[len(loads) + 1])]
        for n in range(2):
            wides[n].done()
            final.append(
                pltpu.make_async_copy(
                    wide_all.at[n], wide_out.at[n], load_sem.at[len(loads) + 2 + n]
                )
            )
        for copy in final:
            copy.start()
        small_out[...] = small_acc[hops]
        tops_out[...] = tops_acc[hops]
        store.wait()
        for copy in final:
            copy.wait()

    def dense_scratch(share, across, lead=()):
        return [
            pltpu.VMEM(lead + (team, share, across), bf16),
            pltpu.VMEM(lead + (max(1, parts - 1), groups, share, across), bf16),
            pltpu.VMEM(lead + (max(1, groups - 1), share, across), bf16),
            pltpu.VMEM(lead + (members, team, share, across), bf16),
        ]

    dense_sem = (
        [dma((parts,))] * 2 + [dma((groups,))] * 4 + [dma((parts,))] * 4 + [dma((2,))] * 2
    )
    wide_rows = shape_of((rows, width), f32)
    return run(
        body,
        (),
        [(dqkv_all, anywhere), (h1, anywhere), (x, anywhere), (gain, vector), (dx1, anywhere)]
        + [(weights_t, anywhere), (out_sum, vector), (small, vector), (tops, vector)]
        + [(base, anywhere), (targets, vector)]
        + [(a, anywhere) for a in produced],
        [
            (wide_rows, anywhere),
            (shape_of((2, members, team, wide_share, 3 * per_group), bf16), anywhere),
            (shape_of((members, team, out_share, width), bf16), anywhere),
            (shape_of((small_rows, width), f32), vector),
            (shape_of((width,), f32), vector),
            (shape_of((tops.shape[0], 128), f32), vector),
            (shape_of((rows, width), bf16), vector),
        ],
        scratch=[
            pltpu.VMEM((group_rows, 3 * per_group), bf16),
            pltpu.VMEM((width, 3 * per_group), f32),
            pltpu.VMEM((group_rows, width), bf16),
            pltpu.VMEM((rows, width), bf16),
            pltpu.VMEM((rows, width), f32),
            pltpu.VMEM((3, per_group, width), bf16),
            pltpu.VMEM((rows, width), f32),
            pltpu.VMEM((places, CAP, width), bf16),
            pltpu.VMEM((2, rows, width), bf16),
            pltpu.VMEM((2, rows, width), bf16),
            pltpu.VMEM((rows, width), bf16),
            pltpu.VMEM((rows, width), bf16),
            pltpu.VMEM((rows, width), f32),
        ]
        + dense_scratch(wide_share, 3 * per_group, (2,))
        + dense_scratch(out_share, width)
        + [pltpu.VMEM((hops + 1, small_rows, width), f32), pltpu.VMEM((hops, small_rows, width), f32)]
        + [pltpu.VMEM((members, 1, width), f32), pltpu.VMEM((team, 1, width), f32)]
        + [pltpu.VMEM((hops + 1, tops.shape[0], 128), f32), pltpu.VMEM((hops, tops.shape[0], 128), f32)]
        + [dma((12 + places,))] + [dma((3 * (rows // row_tile),))] * 2
        + dense_sem * 3
        + [dma((hops,))] * 2
        + [dma((members + team,))] * 2
        + [dma((hops,))] * 2,
        flops=4 * 2 * rows * width * width * 3,
        moved=20 * 1024 * 1024,
        talks=3,
    )


def place_experts(meta, near, begun):
    _, half, columns = near[0].shape
    tile = 128
    tiles = half // tile
    count = 3

    def body(meta_ref, *refs):
        outs = refs[2 * count + count :]
        for j in range(2):

            @pl.when(pl.program_id(0) == j)
            def _():
                for n in range(count):
                    piece = refs[n * 2 + j][0].astype(f32)
                    outs[n][0] = jnp.transpose(piece) if n == 2 else piece

    def in_spec(which, j):
        def index(c, t, m):
            return (which, jnp.where(c == j, t, jnp.where(c < j, 0, tiles - 1)), 0)

        return pl.BlockSpec((1, tile, columns), index)

    flat = pl.BlockSpec((1, tile, columns), lambda c, t, m: (m[3] ^ 1, (m[2] ^ c) * tiles + t, 0))
    turned = pl.BlockSpec((1, columns, tile), lambda c, t, m: (m[3] ^ 1, 0, (m[2] ^ c) * tiles + t))
    return run(
        body,
        (2, tiles),
        [(near[j], in_spec(n, j)) for n in range(count) for j in range(2)]
        + [(a, anywhere) for a in begun],
        [
            (shape_of(a.shape, f32), turned if n == 2 else flat)
            for n, a in enumerate(begun)
        ],
        meta=meta,
        moved=count * 2 * half * columns * 6,
        aliases={1 + 2 * count + n: n for n in range(count)},
    )


def place_dense(meta, near, flat, tops, small, w_qkv, kinds):
    _, members, team, share, lanes = near.shape
    per_group = lanes // 3
    half = team * share
    width = 2 * half
    rows_all = flat.shape[1] * flat.shape[2]
    step = 8 // math.gcd(share, 8)
    while team // step > 4:
        step *= 2
    per_half = team // step
    tall = step * share

    heads = HEADS // members
    head_width = width // HEADS
    expert_all = (small.shape[0] - 1 - 3 * kinds) // 2
    at_vec = expert_all + 1
    at_logit = at_vec + kinds
    at_carry = at_logit + 2 * kinds

    def body(meta_ref, near_ref, flat_ref, tops_ref, small_ref, w_ref, *outs):
        out_ref, flat_out, clip_ref, router_out, norm_out, vec_out, logit_out, carry_out = outs[:8]
        scale_ref = outs[8]

        @pl.when((pl.program_id(0) == 0) & (pl.program_id(1) == 0))
        def _():
            lanes = lax.broadcasted_iota(jnp.int32, (1, width), 1)
            scale = jnp.zeros((1, width), f32)
            for n in range(HEADS):
                top = tops_ref[n % heads : n % heads + 1, n // heads : n // heads + 1]
                ratio = jnp.sqrt(jnp.minimum(1.0, clip_limit / top))
                inside = (lanes >= n * head_width) & (lanes < (n + 1) * head_width)
                scale = jnp.where(inside, ratio, scale)
            scale_ref[...] = scale
            router_out[...] = small_ref[0:expert_all, :]
            norm_out[...] = small_ref[expert_all, :]
            vec_out[...] = small_ref[at_vec : at_vec + kinds, :]
            for n in range(kinds):
                logit_out[n] = small_ref[at_logit + 2 * n : at_logit + 2 * n + 2, :]
            carry_out[...] = small_ref[at_carry:, 0:expert_all]

        for c in range(step):
            pieces = [near_ref[0, meta_ref[0] ^ g, c] for g in range(members)]
            for w in range(3):
                at = slice(w * per_group, (w + 1) * per_group)
                out_ref[w, c * share : (c + 1) * share, :] = jnp.concatenate(
                    [piece[:, at] for piece in pieces], axis=1
                ).astype(f32)
        clip_ref[...] = w_ref[...].astype(f32) * scale_ref[...]

        @pl.when(pl.program_id(1) == 0)
        def _():
            for c in range(team):
                at = slice(c * flat.shape[2], (c + 1) * flat.shape[2])
                for j in range(2):
                    member = pl.program_id(0) * 2 + j
                    flat_out[j, at, :] = flat_ref[meta_ref[0] ^ member, c].astype(f32)

    square = shape_of((3, width, width), f32)
    return run(
        body,
        (2, per_half),
        [
            (
                near,
                pl.BlockSpec((1, members, step, share, lanes), lambda n, c, m: (n, 0, c, 0, 0)),
            ),
            (flat, whole(flat)),
            (tops, whole(tops)),
            (small, whole(small)),
            (w_qkv, pl.BlockSpec((2, tall, width), lambda n, c, m: (0, n * per_half + c, 0))),
        ],
        [
            (square, pl.BlockSpec((3, tall, width), lambda n, c, m: (0, n * per_half + c, 0))),
            (
                shape_of((members, rows_all, width), f32),
                pl.BlockSpec((2, rows_all, width), lambda n, c, m: (n, 0, 0)),
            ),
            (
                shape_of((2, width, width), f32),
                pl.BlockSpec((2, tall, width), lambda n, c, m: (0, n * per_half + c, 0)),
            ),
        ]
        + [
            (o, whole(o))
            for o in (
                shape_of((expert_all, width), f32),
                shape_of((width,), f32),
                shape_of((kinds, width), f32),
                shape_of((kinds, 2, width), f32),
                shape_of((expert_all, expert_all), f32),
            )
        ],
        scratch=[pltpu.VMEM((1, width), f32)],
        meta=meta,
        moved=square.size * 12,
    )


def shards(
    inputs,
    lengths,
    block_order,
    routes,
    prev_logits,
    norm1_gain,
    norm2_gain,
    w_qkv,
    w_out,
    w_router,
    w_carry,
    const_logit_w,
    const_vec,
    w_gate,
    w_up,
    w_down,
    cotangent,
):
    members = lax.axis_size("ctx")
    groups = lax.axis_size("exp")
    parts = lax.axis_size("dp")
    me = lax.axis_index("ctx")
    mine = lax.axis_index("exp")
    x, grad = inputs[0], cotangent[0]
    rows, width = x.shape
    group_rows = rows * members
    deal_block = group_rows // block_order.shape[1]
    per_member = rows // deal_block
    local = w_gate.shape[0]
    expert_count = local * groups
    head_width = width // HEADS
    heads = HEADS // members
    per_group = heads * head_width
    blocks = block_order.shape[1]
    layout = {
        "order": 4, "lengths": 4 + blocks, "sequences": lengths.shape[1],
        "inverse": 4 + blocks + lengths.shape[1], "sides": local,
    }
    numbers = jnp.arange(blocks, dtype=jnp.int32)
    given = jnp.sum(jnp.where(block_order[0][None, :] == numbers[:, None], numbers[None, :], 0), axis=1)
    inverse = (((given // per_member) ^ me) * per_member + given % per_member).astype(jnp.int32)
    meta = jnp.concatenate(
        [
            jnp.stack([me, mine, me % 2, me // 2]).astype(jnp.int32),
            block_order[0],
            lengths[0],
            inverse,
        ]
    )
    gain1, gain2 = norm1_gain, norm2_gain
    w_out_parts = w_out.reshape(members, per_group, width)
    previous_t = jnp.transpose(prev_logits[0])
    router_t = jnp.transpose(w_router)
    odd = [r for r in range(groups * local) if r % local]

    begun = begin(x, grad, jnp.transpose(routes[0]), gain1, w_qkv, local)
    q, k, v, kt, vt, h1, weights_t, targets, target_rows, route_ids, grad_near = begun[:11]
    grad_rest = begun[11:]
    weights_t = weights_t.reshape(3, members, per_group, width)
    grad_late = [slot_swap(grad_rest[n], r, local) for n, r in enumerate(odd)]
    o, ot, lse, tops = attend(meta, q, k, vt, deal_block, layout)
    logit_rows = jnp.swapaxes(const_logit_w, 1, 2).reshape(-1, width)
    x1, h2, prob, token_near, gate_near, base, dh_zero, dgate_zero, zero_sums = token_front(
        x, o, w_out_parts, gain2, router_t, previous_t, w_carry, target_rows, grad, route_ids,
        logit_rows, const_vec, local,
    )
    worked = expert_layer(token_near, grad_near, grad_late, gate_near, w_gate, w_up, w_down)
    produced = worked[:groups]
    token_back_rows, dots, expert_sum, beside = worked[groups:]
    dx1, small, da_near = token_back(
        x1, h2, grad, prob, previous_t, route_ids, targets, token_back_rows, dots, dgate_zero,
        dh_zero, gain2, router_t, zero_sums,
    )
    expert_now, da_near = lax.optimization_barrier((expert_sum, da_near))
    over = swap(expert_now, "ctx", 2)
    y_near = [swap(produced[g], "exp", g) if g else produced[0] for g in range(groups)]
    dqkv, out_sum, *begun_grads = attend_back(
        meta, q, k, v, kt, da_near, w_out_parts, ot, lse, deal_block, layout, (expert_sum, beside)
    )

    input_grad, qkv_near, out_near, small, norm1_grad, top_all, result = finish(
        dqkv, h1, x, gain1, dx1, weights_t, out_sum, small, tops, y_near, base, targets
    )
    over, qkv_near = lax.optimization_barrier((over, qkv_near))
    corner = swap(over, "ctx", 1)
    dense = place_dense(meta, qkv_near, out_near, top_all, small, w_qkv, const_vec.shape[0])
    qkv_grad, out_grad, clipped, router_grad, norm2_grad, vec_grad, logit_grad, carry_grad = dense
    router_grad, logit_grad = jnp.transpose(router_grad), jnp.swapaxes(logit_grad, 1, 2)
    out_grad = out_grad.reshape(width, width)
    gate_grad, up_grad, down_grad = place_experts(meta, (over, corner), begun_grads)
    return (
        result[None],
        input_grad[None],
        norm1_grad,
        norm2_grad,
        qkv_grad,
        out_grad,
        router_grad,
        carry_grad,
        logit_grad,
        vec_grad,
        gate_grad,
        up_grad,
        down_grad,
        clipped,
    )


def solution(mesh):
    tokens = P(("dp", "exp"), "ctx", None)
    packs = P(("dp", "exp"), None)
    experts = P("exp", None, None)
    in_specs = (
        tokens, packs, packs, tokens, tokens, P(), P(), P(), P(), P(), P(), P(), P(),
        experts, experts, experts, tokens,
    )
    out_specs = (
        tokens, tokens, P(), P(), P(), P(), P(), P(), P(), P(),
        P("exp", None, "dp"), P("exp", None, "dp"), P("exp", "dp", None), P(),
    )
    return jax.shard_map(shards, mesh=mesh, in_specs=in_specs, out_specs=out_specs, check_vma=False)
```

```python
import math

import jax
import jax.numpy as jnp
from jax import lax
from jax.experimental import pallas as pl
from jax.experimental.pallas import tpu as pltpu
from jax.sharding import PartitionSpec as P

HEADS = 12
CAP = 128

norm_eps = 1e-05
clip_limit = 3.0
low_start = -1e30
mask_fill = -3e38
highest = lax.Precision.HIGHEST
NN = (((1,), (0,)), ((), ()))
NT = (((1,), (1,)), ((), ()))
TN = (((0,), (0,)), ((), ()))
f32 = jnp.float32
bf16 = jnp.bfloat16
MESH = pl.DeviceIdType.MESH


def mm(left, right, dims=NN):
    return lax.dot_general(left, right, dims, preferred_element_type=f32)


def mm_full(left, right, dims=NN):
    return lax.dot_general(left, right, dims, precision=highest, preferred_element_type=f32)


def shape_of(shape, dtype):
    return jax.ShapeDtypeStruct(shape, dtype)


def whole(array):
    rank = len(array.shape)
    return pl.BlockSpec(array.shape, lambda *_: (0,) * rank)


def cost(flops, moved, exps=0):
    return pl.CostEstimate(flops=int(flops), bytes_accessed=int(moved), transcendentals=int(exps))


def run(body, grid, inputs, outputs, scratch=(), meta=None, flops=0, moved=0, exps=0, aliases=None, talks=None):
    prefetch = 0 if meta is None else 1
    args = ([] if meta is None else [meta]) + [a for a, _ in inputs]
    return pl.pallas_call(
        body,
        out_shape=[o for o, _ in outputs],
        grid_spec=pltpu.PrefetchScalarGridSpec(
            num_scalar_prefetch=prefetch,
            grid=grid,
            in_specs=[s for _, s in inputs],
            out_specs=[s for _, s in outputs],
            scratch_shapes=list(scratch),
        ),
        compiler_params=pltpu.CompilerParams(
            dimension_semantics=("arbitrary",) * len(grid),
            vmem_limit_bytes=63 * 1024 * 1024,
            collective_id=talks,
            has_side_effects=talks is not None,
        ),
        cost_estimate=cost(flops, moved, exps),
        input_output_aliases={} if aliases is None else aliases,
    )(*args)


def swap(value, axis, distance):
    count = lax.axis_size(axis)
    return lax.ppermute(value, axis, [(i, i ^ distance) for i in range(count)])


def flip(value, bits):
    bit = 1
    while bit <= bits:
        if bits & bit:
            value = value + bit - 2 * bit * lax.rem(lax.div(value, bit), 2)
        bit *= 2
    return value


def powers(axis):
    found, bit = [], 1
    while bit < lax.axis_size(axis):
        found.append(bit)
        bit *= 2
    return found


def slot_peer(r, count, exp_now, me):
    return {"exp": flip(exp_now, r // count), "ctx": flip(me, 2 * (r % count))}


def slot_swap(value, r, count):
    groups = lax.axis_size("exp")
    total = groups * lax.axis_size("ctx")
    apart = 2 * (r % count) * groups + r // count
    return lax.ppermute(value, ("ctx", "exp"), [(i, i ^ apart) for i in range(total)])


def remote(src, dst, sent, arrived, peer):
    return pltpu.make_async_remote_copy(
        src_ref=src, dst_ref=dst, send_sem=sent, recv_sem=arrived,
        device_id=peer, device_id_type=MESH,
    )


def greet(peers):
    barrier = pltpu.get_barrier_semaphore()
    for peer in peers:
        pl.semaphore_signal(barrier, inc=1, device_id=peer, device_id_type=MESH)
    return lambda: pl.semaphore_wait(barrier, len(peers))


anywhere = pl.BlockSpec(memory_space=pl.ANY)
scalars = pl.BlockSpec(memory_space=pltpu.SMEM)
vector = pl.BlockSpec(memory_space=pltpu.VMEM)
dma = pltpu.SemaphoreType.DMA


def add_low(*terms):
    total = terms[0].astype(f32)
    for term in terms[1:]:
        total = total + term.astype(f32)
    return total.astype(bf16)


def begin(x, grad, routes, gain, w_qkv, local):
    rows, width = x.shape
    members, groups = lax.axis_size("ctx"), lax.axis_size("exp")
    group_rows = rows * members
    heads = HEADS // members
    head_width = width // HEADS
    columns = heads * head_width
    places = groups * local
    odd = [r for r in range(places) if r % local]
    scale = head_width**-0.5
    tile = min(256, rows)
    per_member = rows // tile

    def body(*refs):
        x_hbm, dy_ref, route_ref, gain_ref, w_hbm = refs[:5]
        q_out, k_out, v_out, kt_out, vt_out, h_out, wt_out = refs[5:12]
        target_out, target_rows, chosen_out, near_out = refs[12:16]
        rest_out, refs = refs[16 : 16 + len(odd)], refs[:16] + refs[16 + len(odd) :]
        x_near, w_in, w_t, q_all, k_all, v_all, kt_all, vt_all, h_all, packed, near = refs[16:27]
        load_sem, x_s, x_r, r_s, r_r, out_sem, near_sem = refs[27:]
        me, exp_now = lax.axis_index("ctx"), lax.axis_index("exp")
        side = lax.div(me, 2)
        peers = [{"ctx": flip(me, 1)}, {"ctx": flip(me, 2)}]
        peers += [slot_peer(local * g, local, exp_now, me) for g in range(1, groups)]
        ready = greet(peers)
        own = pltpu.make_async_copy(x_hbm, x_near.at[0], load_sem.at[0])
        weights = pltpu.make_async_copy(w_hbm, w_in, load_sem.at[1])
        own.start()
        weights.start()

        def some(t):
            return pl.ds(pl.multiple_of(t * tile, tile), tile)

        def across(t):
            n = 2 + t
            return remote(
                x_hbm.at[some(t), :], x_near.at[2, some(t), :], x_s.at[n], x_r.at[n],
                {"ctx": flip(me, 2)},
            )

        def beside():
            return remote(x_hbm, x_near.at[1], x_s.at[1], x_r.at[1], {"ctx": flip(me, 1)})

        def passed(t):
            n = 2 + per_member + t
            return remote(
                x_near.at[2, some(t), :], x_near.at[3, some(t), :], x_s.at[n], x_r.at[n],
                {"ctx": flip(me, 1)},
            )

        def row_copy(g):
            return remote(
                packed.at[g], near.at[g], r_s.at[g], r_r.at[g],
                slot_peer(local * g, local, exp_now, me),
            )

        ready()
        for t in range(per_member):
            across(t).start()
        beside().start()

        lines = jnp.concatenate([route_ref[...].astype(f32), jnp.zeros((6, rows), f32)], axis=0)
        chosen = jnp.transpose(lines)[:, 0:2].astype(jnp.int32)
        chosen_out[...] = chosen
        expert_count = places
        lanes = lax.broadcasted_iota(jnp.int32, (rows, 128), 1)
        hits = [lanes == chosen[:, c : c + 1] for c in range(2)]
        hit = jnp.where((hits[0] | hits[1]) & (lanes < expert_count), 1.0, 0.0)
        later = lax.broadcasted_iota(jnp.int32, (rows, rows), 0)
        sooner = lax.broadcasted_iota(jnp.int32, (rows, rows), 1)
        ahead = mm(jnp.where(sooner < later, 1.0, 0.0).astype(bf16), hit.astype(bf16))
        spots = []
        for c in range(2):
            ids = chosen[:, c : c + 1]
            rank = jnp.sum(jnp.where(hits[c], ahead, 0.0), axis=1, keepdims=True).astype(jnp.int32)
            far_z = lax.div(ids, local)
            far_y = lax.rem(ids, local)
            z = jnp.zeros_like(ids)
            bit = 1
            while bit < groups:
                z = z + bit * jnp.where(
                    lax.rem(lax.div(far_z, bit), 2) == lax.rem(lax.div(exp_now, bit), 2), 0, 1
                )
                bit *= 2
            y = jnp.where(far_y == side, 0, 1)
            spots.append(jnp.where(ids < expert_count, (z * local + y) * CAP + rank, -1))
        target_out[...] = jnp.concatenate(spots, axis=1)
        wide = jnp.where(lanes == 0, spots[0], spots[1]).astype(f32)
        target_rows[...] = jnp.transpose(wide)[0:2, :].astype(jnp.int32)

        def pack(n, r):
            packed[n] = mm(slot_choice(r * CAP, CAP, target_rows), dy_ref[...]).astype(bf16)

        for g in range(groups - 1, -1, -1):
            pack(g, local * g)
            if g < groups - 1:
                row_copy(g + 1).start()
        for n, r in enumerate(odd):
            pack(groups + n, r)
        stores = [
            pltpu.make_async_copy(packed.at[0], near_out.at[0], near_sem.at[0]),
        ] + [
            pltpu.make_async_copy(packed.at[groups + n], rest_out[n], near_sem.at[groups + n])
            for n in range(len(odd))
        ]
        for copy in stores:
            copy.start()
        weights.wait()
        for w in range(3):
            w_t[w] = jnp.transpose(w_in[w])
        w_store = pltpu.make_async_copy(w_t, wt_out, load_sem.at[2])
        w_store.start()
        here = pl.ds(pl.multiple_of(me * columns, columns), columns)

        def chunk(j):
            def project(t, _):
                if j == 2:
                    across(t).wait()
                    passed(t).start()
                if j == 3:
                    passed(t).wait()
                at = pl.multiple_of(t * tile, tile)
                to = pl.ds(pl.multiple_of(j * rows + t * tile, tile), tile)
                value = x_near[j, pl.ds(at, tile), :].astype(f32)
                inverse = lax.rsqrt(jnp.mean(value * value, axis=1, keepdims=True) + norm_eps)
                low = (value * inverse * gain_ref[...]).astype(bf16)
                h_all[to, :] = low
                q = mm(low, w_t[0, here, :], NT).astype(bf16) * jnp.asarray(scale, bf16)
                k = mm(low, w_t[1, here, :], NT).astype(bf16)
                v = mm(low, w_t[2, here, :], NT).astype(bf16)
                for h in range(heads):
                    part = slice(h * head_width, (h + 1) * head_width)
                    q_all[h, to, :] = q[:, part]
                    k_all[h, to, :] = k[:, part]
                    v_all[h, to, :] = v[:, part]
                kt_all[:, to] = mm(w_t[1, here, :], low, NT).astype(bf16)
                vt_all[:, to] = mm(w_t[2, here, :], low, NT).astype(bf16)
                return 0

            lax.fori_loop(0, per_member, project, 0)
            for copy in chunk_stores(j):
                copy.start()

        def chunk_stores(j):
            to = pl.ds(j * rows, rows)
            pairs = [(q_all, q_out), (k_all, k_out), (v_all, v_out)]
            found = [(a.at[:, to, :], b.at[:, to, :]) for a, b in pairs]
            found += [(a.at[:, to], b.at[:, to]) for a, b in ((kt_all, kt_out), (vt_all, vt_out))]
            found += [(h_all.at[to, :], h_out.at[to, :])]
            return [
                pltpu.make_async_copy(a, b, out_sem.at[6 * j + n]) for n, (a, b) in enumerate(found)
            ]

        own.wait()
        chunk(0)
        beside().wait()
        chunk(1)
        chunk(2)
        chunk(3)
        for g in range(1, groups):
            row_copy(g).wait()
            pltpu.make_async_copy(near.at[g], near_out.at[g], near_sem.at[g]).start()
        for copy in stores:
            copy.wait()
        w_store.wait()
        for j in range(members):
            for copy in chunk_stores(j):
                copy.wait()
        for g in range(1, groups):
            pltpu.make_async_copy(near.at[g], near_out.at[g], near_sem.at[g]).wait()

    by_head = (heads, group_rows, head_width)
    by_column = (columns, group_rows)
    slots = (places, CAP, width)
    return run(
        body,
        (),
        [(x, anywhere), (grad, vector), (routes, vector), (gain, vector), (w_qkv, anywhere)],
        [(shape_of(by_head, bf16), anywhere)] * 3
        + [(shape_of(by_column, bf16), anywhere)] * 2
        + [(shape_of((group_rows, width), bf16), anywhere)]
        + [(shape_of((3, width, width), bf16), anywhere)]
        + [(shape_of((rows, 2), jnp.int32), vector), (shape_of((2, rows), jnp.int32), vector)]
        + [(shape_of((rows, 2), jnp.int32), vector)]
        + [(shape_of((groups, CAP, width), bf16), anywhere)]
        + [(shape_of((CAP, width), bf16), anywhere)] * len(odd),
        scratch=[
            pltpu.VMEM((members, rows, width), bf16),
            pltpu.VMEM((3, width, width), bf16),
            pltpu.VMEM((3, width, width), bf16),
            pltpu.VMEM(by_head, bf16), pltpu.VMEM(by_head, bf16), pltpu.VMEM(by_head, bf16),
            pltpu.VMEM(by_column, bf16), pltpu.VMEM(by_column, bf16),
            pltpu.VMEM((group_rows, width), bf16),
            pltpu.VMEM(slots, bf16), pltpu.VMEM(slots, bf16),
            dma((3,)), dma((2 + 2 * per_member,)), dma((2 + 2 * per_member,)),
            dma((places,)), dma((places,)), dma((6 * members,)), dma((places + 1,)),
        ],
        flops=2 * group_rows * width * columns * 5,
        moved=20 * 1024 * 1024,
        talks=4,
    )


def document_start(meta_ref, position, layout):
    start = jnp.zeros_like(position)
    end = jnp.int32(0)
    for s in range(layout["sequences"]):
        end = end + meta_ref[layout["lengths"] + s]
        start = jnp.where(position >= end, end, start)
    return start


def block_range(meta_ref, query_block, key_block, rows, layout):
    q_first = query_block * rows
    k_first = key_block * rows
    begin = document_start(meta_ref, q_first, layout)
    begin_last = document_start(meta_ref, q_first + rows - 1, layout)
    needed = (k_first <= q_first) & (k_first + rows - 1 >= begin)
    full = (k_first < q_first) & (k_first >= begin_last)
    return q_first, k_first, needed, full


def allowed_pairs(meta_ref, q_first, k_first, rows, layout):
    q_pos = q_first + lax.broadcasted_iota(jnp.int32, (1, rows), 1)
    k_pos = k_first + lax.broadcasted_iota(jnp.int32, (rows, 1), 0)
    return (k_pos <= q_pos) & (k_pos >= document_start(meta_ref, q_pos, layout))


def attend(meta, q, k, vt, rows, layout):
    heads, group_rows, head_width = q.shape
    blocks = group_rows // rows
    width = heads * head_width

    def body(meta_ref, q_ref, k_ref, vt_ref, o_ref, ot_ref, lse_ref, top_ref, m_ref, l_ref, a_ref, qt_ref):
        i = pl.program_id(0)
        m_ref[...] = jnp.full_like(m_ref, low_start)
        l_ref[...] = jnp.zeros_like(l_ref)
        a_ref[...] = jnp.zeros_like(a_ref)
        for h in range(heads):
            qt_ref[h] = jnp.transpose(q_ref[h])

        def one(j, _):
            q_first, k_first, needed, full = block_range(meta_ref, i, j, rows, layout)
            at = pl.multiple_of(meta_ref[layout["inverse"] + j] * rows, rows)

            def step(masked):
                if masked:
                    allowed = allowed_pairs(meta_ref, q_first, k_first, rows, layout)
                scores = [mm(k_ref[h, pl.ds(at, rows), :], qt_ref[h]) for h in range(heads)]
                if masked:
                    scores = [jnp.where(allowed, s, mask_fill) for s in scores]
                olds = [m_ref[h] for h in range(heads)]
                news = [
                    jnp.maximum(old, jnp.max(s, axis=0, keepdims=True))
                    for old, s in zip(olds, scores)
                ]
                chances = [jnp.exp(s - new) for s, new in zip(scores, news)]
                mixed = [
                    mm(
                        vt_ref[h * head_width : (h + 1) * head_width, pl.ds(at, rows)],
                        chances[h].astype(bf16),
                    )
                    for h in range(heads)
                ]
                for h in range(heads):
                    part = slice(h * head_width, (h + 1) * head_width)
                    shrink = jnp.exp(olds[h] - news[h])
                    m_ref[h] = news[h]
                    l_ref[h] = l_ref[h] * shrink + jnp.sum(chances[h], axis=0, keepdims=True)
                    a_ref[part, :] = a_ref[part, :] * shrink + mixed[h]

            @pl.when(full)
            def _():
                step(False)

            @pl.when(needed & jnp.logical_not(full))
            def _():
                step(True)

            return 0

        lax.fori_loop(0, i + 1, one, 0)
        for h in range(heads):
            part = slice(h * head_width, (h + 1) * head_width)
            ot_ref[part, :] = a_ref[part, :] / l_ref[h]
            lse_ref[pl.ds(h, 1), :] = m_ref[h] + jnp.log(l_ref[h])
            top = m_ref[h]

            @pl.when(i == 0)
            def _():
                top_ref[pl.ds(h, 1), :] = top

            @pl.when(i > 0)
            def _():
                top_ref[pl.ds(h, 1), :] = jnp.maximum(top_ref[pl.ds(h, 1), :], top)

        o_ref[...] = jnp.transpose(ot_ref[...]).astype(bf16)

    row = shape_of((heads, group_rows), f32)
    row_spec = pl.BlockSpec((heads, rows), lambda i, m: (0, i))
    return run(
        body,
        (blocks,),
        [
            (
                q,
                pl.BlockSpec(
                    (heads, rows, head_width), lambda i, m: (0, m[layout["inverse"] + i], 0)
                ),
            ),
            (k, whole(k)),
            (vt, whole(vt)),
        ],
        [
            (
                shape_of((group_rows, width), bf16),
                pl.BlockSpec((rows, width), lambda i, m: (m[layout["inverse"] + i], 0)),
            ),
            (shape_of((width, group_rows), f32), pl.BlockSpec((width, rows), lambda i, m: (0, i))),
            (row, row_spec),
            (shape_of((heads, rows), f32), pl.BlockSpec((heads, rows), lambda i, m: (0, 0))),
        ],
        scratch=[
            pltpu.VMEM((heads, 1, rows), f32),
            pltpu.VMEM((heads, 1, rows), f32),
            pltpu.VMEM((width, rows), f32),
            pltpu.VMEM((heads, head_width, rows), bf16),
        ],
        meta=meta,
        flops=2 * 2 * group_rows * group_rows * width,
        moved=group_rows * width * 14,
        exps=group_rows * group_rows * heads // 2,
    )


def attend_back(meta, q, k, v, kt, grad, w_out, ot, lse, rows, layout, shares):
    heads, group_rows, head_width = q.shape
    blocks = group_rows // rows
    width = heads * head_width
    scale = head_width**-0.5
    per = grad.shape[1] // rows

    _, half, lanes = shares[0].shape
    tall = 2 * half // blocks
    wide = lanes // blocks if lanes // blocks >= 128 else lanes
    last = lanes // wide

    def body(meta_ref, q_ref, k_ref, v_ref, kt_ref, grad_ref, w_ref, *refs):
        ot_ref, lse_ref = refs[:2]
        flat_refs, turned_refs = refs[2:6], refs[6:8]
        up_outs, down_out = refs[10:12], refs[12]
        refs = refs[:2] + refs[8:10] + refs[13:]
        ot_ref, lse_ref, out_ref, rows_ref, dk_ref, dv_ref, dq_ref, g_ref, delta_ref, sum_ref, qt_ref, gt_ref = refs
        i = pl.program_id(0)

        @pl.when(i == 0)
        def _():
            dk_ref[...] = jnp.zeros_like(dk_ref)
            dv_ref[...] = jnp.zeros_like(dv_ref)

        core = lax.div(i, blocks // 2)
        for n in range(2):

            @pl.when(core == (meta_ref[2] ^ n))
            def _():
                for g in range(2):
                    up_outs[g][0] = flat_refs[2 * n + g][0].astype(f32)

        @pl.when(i < last)
        def _():
            for n in range(2):
                to = pl.multiple_of((meta_ref[2] ^ n) * half, half)
                down_out[0, :, pl.ds(to, half)] = jnp.transpose(turned_refs[n][0].astype(f32))

        da = grad_ref[0]
        g = mm(da, w_ref[0], NT).astype(bf16)
        part_sum = mm(ot_ref[...].astype(bf16), da)

        @pl.when(i == 0)
        def _():
            sum_ref[...] = part_sum

        @pl.when(i > 0)
        def _():
            sum_ref[...] += part_sum

        for h in range(heads):
            g_ref[h] = g[:, h * head_width : (h + 1) * head_width]
        turned = jnp.transpose(g.astype(f32))
        gt_ref[...] = turned.astype(bf16)
        for h in range(heads):
            qt_ref[h] = jnp.transpose(q_ref[h])
        product = turned * ot_ref[...]
        for h in range(heads):
            part = slice(h * head_width, (h + 1) * head_width)
            delta_ref[h] = jnp.sum(product[part, :], axis=0, keepdims=True)

        dq_ref[...] = jnp.zeros_like(dq_ref)

        def one(j, _):
            q_first, k_first, needed, full = block_range(meta_ref, i, j, rows, layout)
            at = pl.multiple_of(meta_ref[layout["inverse"] + j] * rows, rows)
            to = pl.multiple_of(j * rows, rows)

            def step(masked):
                if masked:
                    allowed = allowed_pairs(meta_ref, q_first, k_first, rows, layout)
                parts = [slice(h * head_width, (h + 1) * head_width) for h in range(heads)]
                scores = [mm(k_ref[h, pl.ds(at, rows), :], qt_ref[h]) for h in range(heads)]
                downs = [
                    mm(v_ref[h, pl.ds(at, rows), :], gt_ref[parts[h], :]) for h in range(heads)
                ]
                if masked:
                    scores = [jnp.where(allowed, s, mask_fill) for s in scores]
                chances = [jnp.exp(scores[h] - lse_ref[pl.ds(h, 1), :]) for h in range(heads)]
                slopes = [
                    (chances[h] * (downs[h] - delta_ref[h])).astype(bf16) for h in range(heads)
                ]
                for h in range(heads):
                    dv_ref[h, pl.ds(to, rows), :] += mm(chances[h].astype(bf16), g_ref[h])
                    dk_ref[h, pl.ds(to, rows), :] += mm(slopes[h], q_ref[h])
                    dq_ref[parts[h], :] += mm(kt_ref[parts[h], pl.ds(at, rows)], slopes[h])

            @pl.when(full)
            def _():
                step(False)

            @pl.when(needed & jnp.logical_not(full))
            def _():
                step(True)

            return 0

        lax.fori_loop(0, i + 1, one, 0)
        here = pl.multiple_of(meta_ref[layout["inverse"] + i] * rows, rows)
        out_ref[pl.ds(here, rows), 0:width] = (jnp.transpose(dq_ref[...]) * scale).astype(bf16)

        @pl.when(i == blocks - 1)
        def _():
            rows_ref[...] = sum_ref[...].astype(bf16)

            def store(b, _):
                spot = pl.multiple_of(b * rows, rows)
                there = pl.multiple_of(meta_ref[layout["inverse"] + b] * rows, rows)
                out_ref[pl.ds(there, rows), width : 3 * width] = jnp.concatenate(
                    [dk_ref[h, pl.ds(spot, rows), :] for h in range(heads)]
                    + [dv_ref[h, pl.ds(spot, rows), :] for h in range(heads)],
                    axis=1,
                ).astype(bf16)
                return 0

            lax.fori_loop(0, blocks, store, 0)

    def flat_spec(g, n):
        def index(i, m):
            now = jnp.clip(i - (m[2] ^ n) * (blocks // 2), 0, blocks // 2 - 1)
            return (g, now, 0)

        return pl.BlockSpec((1, tall, lanes), index)

    def turned_place(i, m):
        return (2, 0, jnp.minimum(i, last - 1))

    local = layout["sides"]
    placed = [
        (
            shape_of((local, 2 * half, lanes), f32),
            pl.BlockSpec((1, tall, lanes), lambda i, m: (m[3], i, 0)),
        )
    ] * 2 + [
        (
            shape_of((local, lanes, 2 * half), f32),
            pl.BlockSpec(
                (1, wide, 2 * half), lambda i, m: (m[3], jnp.minimum(i, last - 1), 0)
            ),
        )
    ]
    out = shape_of((group_rows, 3 * width), bf16)
    out_rows = shape_of((width, grad.shape[2]), bf16)
    return run(
        body,
        (blocks,),
        [
            (
                q,
                pl.BlockSpec(
                    (heads, rows, head_width), lambda i, m: (0, m[layout["inverse"] + i], 0)
                ),
            ),
            (k, whole(k)),
            (v, whole(v)),
            (kt, whole(kt)),
        ]
        + [
            (
                grad,
                pl.BlockSpec(
                    (1, rows, grad.shape[2]),
                    lambda i, m: (
                        m[layout["inverse"] + i] // per, m[layout["inverse"] + i] % per, 0
                    ),
                ),
            ),
            (w_out, pl.BlockSpec((1, width, grad.shape[2]), lambda i, m: (m[0], 0, 0))),
            (ot, pl.BlockSpec((width, rows), lambda i, m: (0, i))),
            (lse, pl.BlockSpec((heads, rows), lambda i, m: (0, i))),
        ]
        + [(shares[n], flat_spec(g, n)) for n in range(2) for g in range(2)]
        + [(shares[n], pl.BlockSpec((1, half, wide), turned_place)) for n in range(2)],
        [(out, whole(out)), (out_rows, whole(out_rows))] + placed,
        scratch=[
            pltpu.VMEM((heads, group_rows, head_width), f32),
            pltpu.VMEM((heads, group_rows, head_width), f32),
            pltpu.VMEM((width, rows), f32),
            pltpu.VMEM((heads, rows, head_width), bf16),
            pltpu.VMEM((heads, 1, rows), f32),
            pltpu.VMEM((width, grad.shape[2]), f32),
            pltpu.VMEM((heads, head_width, rows), bf16),
            pltpu.VMEM((width, rows), bf16),
        ],
        meta=meta,
        flops=5 * 2 * group_rows * group_rows * width,
        moved=group_rows * width * 24,
        exps=group_rows * group_rows * heads // 2,
    )


def slot_choice(first, count, target_ref):
    rows = target_ref.shape[1]
    ids = first + lax.broadcasted_iota(jnp.int32, (count, rows), 0)
    match = (ids == target_ref[0:1, :]) | (ids == target_ref[1:2, :])
    return jnp.where(match, 1.0, 0.0).astype(bf16)


def token_front(
    x, o, w_out, gain, router_t, previous_t, w_carry, target_rows, grad, routes, logit_w, vectors, local
):
    rows, width = x.shape
    members, columns = w_out.shape[0], w_out.shape[1]
    expert_all = router_t.shape[0]
    groups = lax.axis_size("exp")
    places = groups * local
    expert_count = places
    kinds = vectors.shape[0]
    tile = 128

    def body(*refs):
        (x_ref, o_hbm, w_ref, gain_ref, router_ref, prev_ref, carry_ref, target_ref) = refs[:8]
        dy_ref, route_ref, lw_ref, vec_ref = refs[8:12]
        x1_ref, h2_ref, prob_ref, rows_out, gates_out, base_ref, dh_ref, dgate_ref, sums_ref = refs[12:21]
        o_near, low, split, packed, arrived, gate_mine, gate_near = refs[21:28]
        o_s, o_r, t_s, t_r, g_s, g_r, out_sem = refs[28:]
        me, exp_now = lax.axis_index("ctx"), lax.axis_index("exp")
        side = lax.div(me, 2)
        peers = [{"ctx": flip(me, j)} for j in range(1, members)]
        peers += [slot_peer(r, local, exp_now, me) for r in range(local, places)]
        ready = greet(peers)

        own_o = pltpu.make_async_copy(o_hbm.at[pl.ds(0, rows), :], o_near.at[0], o_r.at[0])

        def o_copy(j, t):
            src = o_hbm.at[pl.ds(pl.multiple_of(j * rows + t * tile, tile), tile), :]
            dst = o_near.at[j, pl.ds(pl.multiple_of(t * tile, tile), tile), :]
            n = j * (rows // tile) + t
            return remote(src, dst, o_s.at[n], o_r.at[n], {"ctx": flip(me, j)})

        def row_copy(r):
            return remote(
                packed.at[r], arrived.at[r], t_s.at[r], t_r.at[r], slot_peer(r, local, exp_now, me)
            )

        def gate_copy(r):
            return remote(
                gate_mine.at[r], gate_near.at[r], g_s.at[r], g_r.at[r],
                slot_peer(r, local, exp_now, me),
            )

        own_o.start()
        ready()
        for t in range(rows // tile):
            for j in range(members - 1, 0, -1):
                o_copy(j, t).start()
        own_o.wait()

        def front_rows(t, _):
            here = pl.ds(pl.multiple_of(t * tile, tile), tile)
            total = x_ref[here, :].astype(f32) + mm(o_near[0, here, :], w_ref[me])
            for j in range(1, members):
                o_copy(j, t).wait()
            for j in range(1, members):
                total = total + mm(o_near[j, here, :], w_ref[flip(me, j)])
            x1_ref[here, :] = total
            inverse = lax.rsqrt(jnp.mean(total * total, axis=1, keepdims=True) + norm_eps)
            h2 = total * inverse * gain_ref[...]
            h2_ref[here, :] = h2
            logits = mm_full(h2, router_ref[...], NT) + mm_full(
                prev_ref[:, here], carry_ref[...], TN
            )
            shifted = jnp.exp(logits - jnp.max(logits, axis=1, keepdims=True))
            prob = shifted / jnp.sum(shifted, axis=1, keepdims=True)
            prob_ref[here, :] = prob
            low[here, :] = h2.astype(bf16)
            top = prob.astype(bf16)
            rest = prob - top.astype(f32)
            middle = rest.astype(bf16)
            split[0, here, :] = top
            split[1, here, :] = middle
            split[2, here, :] = (rest - middle.astype(f32)).astype(bf16)
            return 0

        lax.fori_loop(0, rows // tile, front_rows, 0)
        diagonal = lax.broadcasted_iota(jnp.int32, (CAP, CAP), 0) == lax.broadcasted_iota(
            jnp.int32, (CAP, CAP), 1
        )
        lanes = lax.broadcasted_iota(jnp.int32, (CAP, expert_all), 1)
        for r in list(range(1, places)) + [0]:
            choice = slot_choice(r * CAP, CAP, target_ref)
            packed[r] = mm(choice, low[...]).astype(bf16)
            picked = mm(choice, split[0]) + mm(choice, split[1]) + mm(choice, split[2])
            expert = flip(exp_now, r // local) * local + flip(side, r % local)
            column = jnp.sum(jnp.where(lanes == expert, picked, 0.0), axis=1, keepdims=True)
            gate_mine[r] = jnp.sum(jnp.where(diagonal, column, 0.0), axis=0, keepdims=True)
            last = r - 1 if r else places - 1
            if last:
                row_copy(last).start()
                gate_copy(last).start()

        def own_copy(n):
            src, dst = (packed, rows_out) if n == 0 else (gate_mine, gates_out)
            return pltpu.make_async_copy(src.at[0], dst.at[0], out_sem.at[n])

        own_copy(0).start()
        own_copy(1).start()

        def zero_rows(t, _):
            here = pl.ds(pl.multiple_of(t * tile, tile), tile)
            h2 = h2_ref[here, :]
            dy = dy_ref[here, :].astype(f32)
            prob_now = prob_ref[here, :]
            classes = lax.broadcasted_iota(jnp.int32, (tile, expert_all), 1)
            chosen = route_ref[here, :]
            ids = [chosen[:, c : c + 1] for c in range(2)]
            gates = [
                jnp.sum(jnp.where(classes == r, prob_now, 0.0), axis=1, keepdims=True) for r in ids
            ]
            along = jnp.sum(dy * h2, axis=1, keepdims=True)
            copies = [(r == expert_count + 1).astype(f32) for r in ids]
            keep = copies[0] * gates[0] + copies[1] * gates[1]
            dgates = [copies[c] * along for c in range(2)]
            scores = [
                jnp.sum(h2 * lw_ref[n : n + 1, :], axis=1, keepdims=True) for n in range(2 * kinds)
            ]
            base = x1_ref[here, :]
            dh = jnp.zeros_like(h2)
            for j in range(kinds):
                top = jnp.maximum(scores[2 * j], scores[2 * j + 1])
                e0 = jnp.exp(scores[2 * j] - top)
                e1 = jnp.exp(scores[2 * j + 1] - top)
                a0 = e0 / (e0 + e1)
                a1 = e1 / (e0 + e1)
                vec = vec_ref[j : j + 1, :]
                along_vec = jnp.sum(dy * vec, axis=1, keepdims=True)
                these = [(r == expert_count + 2 + j).astype(f32) for r in ids]
                weight = these[0] * gates[0] + these[1] * gates[1]
                for c in range(2):
                    dgates[c] = dgates[c] + these[c] * (a0 * along + a1 * along_vec)
                keep = keep + weight * a0
                base = base + (weight * a1) * vec
                d0 = weight * along
                d1 = weight * along_vec
                mean = a0 * d0 + a1 * d1
                z0 = a0 * (d0 - mean)
                z1 = a1 * (d1 - mean)
                dh = dh + z0 * lw_ref[2 * j : 2 * j + 1, :] + z1 * lw_ref[2 * j + 1 : 2 * j + 2, :]
                sums_ref[j : j + 1, :] += jnp.sum((weight * a1) * dy, axis=0, keepdims=True)
                at = kinds + 2 * j
                sums_ref[at : at + 1, :] += jnp.sum(z0 * h2, axis=0, keepdims=True)
                sums_ref[at + 1 : at + 2, :] += jnp.sum(z1 * h2, axis=0, keepdims=True)
            base_ref[here, :] = base + keep * h2
            dh_ref[here, :] = dh + keep * dy
            dgate_ref[here, :] = jnp.concatenate(dgates, axis=1)
            return 0

        sums_ref[...] = jnp.zeros_like(sums_ref)
        lax.fori_loop(0, rows // tile, zero_rows, 0)

        def rows_store(r):
            return pltpu.make_async_copy(arrived.at[r], rows_out.at[r], out_sem.at[2 * r])

        def gates_store(r):
            return pltpu.make_async_copy(gate_near.at[r], gates_out.at[r], out_sem.at[2 * r + 1])

        for r in range(1, places):
            row_copy(r).wait()
            gate_copy(r).wait()
            rows_store(r).start()
            gates_store(r).start()
        own_copy(0).wait()
        own_copy(1).wait()
        for r in range(1, places):
            rows_store(r).wait()
            gates_store(r).wait()

    wide = shape_of((rows, width), f32)
    placed = shape_of((places, CAP, width), bf16)
    lines = shape_of((places, 1, CAP), f32)
    return run(
        body,
        (),
        [(x, vector), (o, anywhere), (w_out, vector), (gain, vector), (router_t, vector)]
        + [(previous_t, vector), (w_carry, vector), (target_rows, vector), (grad, vector)]
        + [(routes, vector), (logit_w, vector), (vectors, vector)],
        [(wide, vector), (wide, vector), (shape_of((rows, expert_all), f32), vector)]
        + [(placed, anywhere), (lines, anywhere), (wide, vector), (wide, vector)]
        + [(shape_of((rows, 2), f32), vector), (shape_of((3 * kinds, width), f32), vector)],
        scratch=[
            pltpu.VMEM((members, rows, columns), bf16),
            pltpu.VMEM((rows, width), bf16),
            pltpu.VMEM((3, rows, expert_all), bf16),
            pltpu.VMEM((places, CAP, width), bf16),
            pltpu.VMEM((places, CAP, width), bf16),
            pltpu.VMEM((places, 1, CAP), f32),
            pltpu.VMEM((places, 1, CAP), f32),
            dma((members * (rows // tile),)), dma((members * (rows // tile),)),
            dma((places,)), dma((places,)), dma((places,)), dma((places,)),
            dma((2 * places,)),
        ],
        flops=2 * rows * width * (width + places * CAP),
        moved=rows * width * 30,
        talks=1,
    )


def expert_layer(arrived, grads, late, gates, w_gate, w_up, w_down):
    places = arrived.shape[0]
    local = w_gate.shape[0]
    rows = places * CAP
    width, hidden = w_gate.shape[1], w_gate.shape[2]
    parts = lax.axis_size("dp")
    groups = places // local
    half = width // 2
    per_part = hidden // parts
    tile = min(256, per_part)
    steps = hidden // tile
    tiles = per_part // tile
    away = steps - tiles
    lead = (away + 2) // 4
    kept = steps - lead
    chunk = 256

    def body(*refs):
        x_ref, dy_ref, gates_ref, wg_hbm, wu_hbm, wd_hbm = refs[:6]
        dy_late, refs = refs[6 : 6 + len(late)], refs[:6] + refs[6 + len(late) :]
        dy_parts = [
            dy_late[r // local] if r % local else dy_ref.at[r // local] for r in range(places)
        ]
        y_out, refs = refs[6 : 6 + groups], refs[6 + groups :]
        it = iter(refs)

        def take(count):
            return [next(it) for _ in range(count)]

        dx_out, dots_out, sum_out, beside_out = take(4)
        x_all, xt_all, dy_all, dyt_all, gate_all, y_acc, dx_acc, dot_acc = take(8)
        wg_buf, wu_buf, wd_buf, wg_keep, wu_keep, wd_keep = take(6)
        hid_keep, dg_keep, du_keep, scaled_keep = take(4)
        send, total, taken, far, dx_low, dx_near, dots, dots_near = take(8)
        beside, y_odd, relay = take(3)
        in_sem, w_sem, keep_sem, c_s, c_r, f_s, f_r, b_s, b_r, d_s, d_r, out_sem = take(12)
        e_s, e_r, beside_sem, y_s, y_r, dx_sem = take(6)
        me, exp_now, dp_now = lax.axis_index("ctx"), lax.axis_index("exp"), lax.axis_index("dp")
        core, side = lax.rem(me, 2), lax.div(me, 2)
        sibling = {"ctx": flip(me, 1)}
        peers = [sibling] + [{"dp": flip(dp_now, d)} for d in range(1, parts)]
        peers += [slot_peer(r, local, exp_now, me) for r in range(1, places)]
        ready = greet(peers)
        diagonal = lax.broadcasted_iota(jnp.int32, (CAP, CAP), 0) == lax.broadcasted_iota(
            jnp.int32, (CAP, CAP), 1
        )

        def dp_of(f):
            distance = parts - 1 - lax.div(f, tiles)
            found, bit = dp_now, 1
            while bit < parts:
                on = lax.rem(lax.div(distance, bit), 2)
                now = lax.rem(lax.div(found, bit), 2)
                found = found + on * bit * (1 - 2 * now)
                bit *= 2
            return found

        def weights(f, slot):
            at = pl.multiple_of(dp_of(f) * per_part + lax.rem(f, tiles) * tile, tile)
            return [
                pltpu.make_async_copy(
                    wg_hbm.at[side, :, pl.ds(at, tile)], wg_buf.at[slot], w_sem.at[0, slot]
                ),
                pltpu.make_async_copy(
                    wu_hbm.at[side, :, pl.ds(at, tile)], wu_buf.at[slot], w_sem.at[1, slot]
                ),
                pltpu.make_async_copy(
                    wd_hbm.at[side, pl.ds(at, tile), :], wd_buf.at[slot], w_sem.at[2, slot]
                ),
            ]

        def core_copy(f, slot):
            return remote(send.at[slot], taken.at[f], c_s.at[slot], c_r.at[f], sibling)

        def far_copy(f):
            return remote(total.at[f], far.at[f], f_s.at[f], f_r.at[f], {"dp": dp_of(f)})

        def back_copy(r):
            return remote(
                dx_low.at[r], dx_near.at[r], b_s.at[r], b_r.at[r],
                slot_peer(r, local, exp_now, me),
            )

        def dots_copy(r):
            return remote(
                dots.at[r], dots_near.at[r], d_s.at[r], d_r.at[r],
                slot_peer(r, local, exp_now, me),
            )

        def keep_weights(k):
            f = lead + k
            at = pl.multiple_of(dp_of(f) * per_part + (f % tiles) * tile, tile)
            return [
                pltpu.make_async_copy(
                    wg_hbm.at[side, :, pl.ds(at, tile)], wg_keep.at[k], keep_sem.at[0, k]
                ),
                pltpu.make_async_copy(
                    wu_hbm.at[side, :, pl.ds(at, tile)], wu_keep.at[k], keep_sem.at[1, k]
                ),
                pltpu.make_async_copy(
                    wd_hbm.at[side, pl.ds(at, tile), :], wd_keep.at[k], keep_sem.at[2, k]
                ),
            ]

        def rows_in(r):
            here = pl.ds(r * CAP, CAP)
            return [
                pltpu.make_async_copy(x_ref.at[r], x_all.at[here, :], in_sem.at[r]),
                pltpu.make_async_copy(dy_parts[r], dy_all.at[here, :], in_sem.at[places + r]),
            ]

        for r in range(places):
            for copy in rows_in(r):
                copy.start()
        if lead:
            for copy in weights(0, 0):
                copy.start()
        for k in range(kept):
            for copy in keep_weights(k):
                copy.start()
        first_half = pl.ds(pl.multiple_of((1 - core) * half, half), half)
        second_half = pl.ds(pl.multiple_of(core * half, half), half)
        for r in range(places):
            here = slice(r * CAP, (r + 1) * CAP)
            for copy in rows_in(r):
                copy.wait()
            turned = jnp.transpose(x_all[here, :])
            xt_all[first_half, here] = turned[:half, :]
            xt_all[second_half, here] = turned[half:, :]
            turned = jnp.transpose(dy_all[here, :])
            dyt_all[first_half, here] = turned[:half, :]
            dyt_all[second_half, here] = turned[half:, :]
            gate_all[here, :] = jnp.sum(
                jnp.where(diagonal, gates_ref[r], 0.0), axis=1, keepdims=True
            )
        y_acc[...] = jnp.zeros_like(y_acc)
        dx_acc[...] = jnp.zeros_like(dx_acc)
        dot_acc[...] = jnp.zeros_like(dot_acc)
        ready()

        def core_sum(f):
            core_copy(f, lax.rem(f, 2)).wait_recv()
            for n in range(3):
                total[f, n] = (total[f, n].astype(f32) + taken[f, n].astype(f32)).astype(bf16)

        def forward_back(here, wg, wu, wd, hid_ref, dg_ref, du_ref, scaled_ref):
            g_pre = mm(x_all[here, :], wg)
            u_pre = mm(x_all[here, :], wu)
            back = mm(dy_all[here, :], wd, NT)
            gate = gate_all[here, :]
            sig = 1.0 / (1.0 + jnp.exp(-g_pre))
            act = g_pre * sig
            hid = act * u_pre
            hid_ref[here, :] = hid.astype(bf16)
            scaled_ref[here, :] = (gate * hid).astype(bf16)
            along = hid * back
            lines = along[:, 0:128]
            for n in range(1, tile // 128):
                lines = lines + along[:, n * 128 : (n + 1) * 128]
            dot_acc[here, :] += lines
            dhid = gate * back
            dg = (dhid * u_pre * sig * (1.0 + g_pre * (1.0 - sig))).astype(bf16)
            du = (dhid * act).astype(bf16)
            dg_ref[here, :] = dg
            du_ref[here, :] = du

        def rows_back(here, wg, wu, dg_ref, du_ref):
            dx_acc[here, :] += mm(dg_ref[here, :], wg, NT) + mm(du_ref[here, :], wu, NT)

        def weight_sums(f, slot, dg_ref, du_ref, scaled_ref, first):
            @pl.when(f > first)
            def _():
                core_sum(f - 1)

            @pl.when(f >= 2)
            def _():
                core_copy(f - 2, slot).wait_send()

            for n, (left, right) in enumerate(
                ((xt_all, dg_ref), (xt_all, du_ref), (dyt_all, scaled_ref))
            ):
                found = mm(left[...], right[...]).astype(bf16)
                send[slot, n] = found[:half, :]
                total[f, n] = found[half:, :]
            core_copy(f, slot).start()

            @pl.when((f > first) & (f - 1 < away))
            def _():
                far_copy(f - 1).start()

        def lead_step(f, _):
            slot = lax.rem(f, 2)
            for copy in weights(f, slot):
                copy.wait()

            @pl.when(f + 1 < lead)
            def _():
                for copy in weights(f + 1, 1 - slot):
                    copy.start()

            hid, dg, du, scaled = (a.at[0] for a in (hid_keep, dg_keep, du_keep, scaled_keep))

            def row_chunk(c, _):
                here = pl.ds(pl.multiple_of(c * chunk, chunk), chunk)
                forward_back(here, wg_buf[slot], wu_buf[slot], wd_buf[slot], hid, dg, du, scaled)
                return 0

            lax.fori_loop(0, rows // chunk, row_chunk, 0)
            weight_sums(f, slot, dg, du, scaled, 0)
            y_acc[...] += mm(hid[...], wd_buf[slot])
            rows_back(slice(0, rows), wg_buf[slot], wu_buf[slot], dg, du)
            return 0

        lax.fori_loop(0, lead, lead_step, 0)
        if lead:
            core_sum(lead - 1)
            far_copy(lead - 1).start()
        for k in range(kept):
            for copy in keep_weights(k):
                copy.wait()

        def keep_rows(k, first, count):
            size = min(chunk, count)
            for c in range(count // size):
                forward_back(
                    slice(first + c * size, first + (c + 1) * size),
                    wg_keep[k], wu_keep[k], wd_keep[k],
                    hid_keep.at[k], dg_keep.at[k], du_keep.at[k], scaled_keep.at[k],
                )
            rows_back(
                slice(first, first + count), wg_keep[k], wu_keep[k], dg_keep.at[k], du_keep.at[k]
            )

        def send_back(first, last):
            for r in range(first, last):
                here = slice(r * CAP, (r + 1) * CAP)
                dx_low[r] = dx_acc[here, :].astype(bf16)
                column = jnp.sum(dot_acc[here, :], axis=1, keepdims=True)
                dots[r] = jnp.sum(jnp.where(diagonal, column, 0.0), axis=0, keepdims=True)
                if r - 1 >= max(1, first):
                    back_copy(r - 1).start()
                    dots_copy(r - 1).start()

        def send_last(r):
            back_copy(r).start()
            dots_copy(r).start()

        middle = places // 2
        near_rows = middle * CAP

        def far_step(k, _):
            keep_rows(k, near_rows, rows - near_rows)
            return 0

        lax.fori_loop(0, kept, far_step, 0)
        send_back(middle, places)

        def away_step(f, _):
            k = f - lead

            keep_rows(k, 0, near_rows)

            @pl.when(k == 0)
            def _():
                send_last(places - 1)

            weight_sums(
                f, lax.rem(f, 2), dg_keep.at[k], du_keep.at[k], scaled_keep.at[k], lead
            )
            return 0

        lax.fori_loop(lead, away, away_step, 0)
        if away == lead:
            send_last(places - 1)
        else:
            core_sum(away - 1)
            far_copy(away - 1).start()

        def near_step(k, _):
            keep_rows(k, 0, near_rows)
            return 0

        lax.fori_loop(away - lead, kept, near_step, 0)
        send_back(0, middle)

        def own_result(k, _):
            y_acc[...] += mm(hid_keep[k], wd_keep[k])
            return 0

        lax.fori_loop(0, kept, own_result, 0)
        send_last(middle - 1)

        def relay_copy(g):
            return remote(y_odd.at[g], relay.at[g], y_s.at[g], y_r.at[g], {"ctx": flip(me, 2)})

        def result(r):
            here = slice(r * CAP, (r + 1) * CAP)
            return (gate_all[here, :] * y_acc[here, :]).astype(bf16)

        for g in range(groups):
            y_odd[g] = result(local * g + 1)
            if g:
                relay_copy(g - 1).start()
        for g in range(groups):
            y_out[g][0] = result(local * g)
        relay_copy(groups - 1).start()

        def own_step(f, _):
            k = f - lead
            weight_sums(
                f, lax.rem(f, 2), dg_keep.at[k], du_keep.at[k], scaled_keep.at[k], away
            )
            return 0

        lax.fori_loop(away, steps, own_step, 0)
        core_sum(steps - 1)

        def beside_copy(i):
            return remote(total.at[away + i], beside.at[i], e_s.at[i], e_r.at[i], sibling)

        def beside_store(i):
            return pltpu.make_async_copy(
                beside.at[i], beside_out.at[:, :, pl.ds(i * tile, tile)], beside_sem.at[i]
            )

        def sum_store(i):
            return pltpu.make_async_copy(
                total.at[away + i], sum_out.at[:, :, pl.ds(i * tile, tile)], out_sem.at[i]
            )

        for i in range(tiles):
            for d in range(1, parts):
                far_copy((parts - 1 - d) * tiles + i).wait_recv()
            for n in range(3):
                value = total[away + i, n].astype(f32)
                for d in range(1, parts):
                    value = value + far[(parts - 1 - d) * tiles + i, n].astype(f32)
                total[away + i, n] = value.astype(bf16)
            if i:
                beside_copy(i - 1).start()
            sum_store(i).start()
        beside_copy(tiles - 1).start()
        for f in range(away):
            far_copy(f).wait_send()
        for f in range(max(0, steps - 2), steps):
            core_copy(f, f % 2).wait_send()

        def dx_store(r):
            src = dx_near.at[r] if r else dx_low.at[0]
            return pltpu.make_async_copy(src, dx_out.at[r], dx_sem.at[r])

        dots_out[0] = dots[0]
        dx_store(0).start()
        for r in range(1, places):
            back_copy(r).wait()
            dots_copy(r).wait()
            dx_store(r).start()
            dots_out[r] = dots_near[r]
        for g in range(groups):
            relay_copy(g).wait()
            y_out[g][1] = relay[g]
        for i in range(tiles):
            beside_copy(i).wait()
            beside_store(i).start()
        for i in range(tiles):
            sum_store(i).wait()
            beside_store(i).wait()
        for r in range(places):
            dx_store(r).wait()

    placed = shape_of((places, CAP, width), bf16)
    pair = shape_of((local, CAP, width), bf16)
    lines = shape_of((places, 1, CAP), f32)
    return run(
        body,
        (),
        [(arrived, anywhere), (grads, anywhere), (gates, vector)]
        + [(w, anywhere) for w in (w_gate, w_up, w_down)]
        + [(g, anywhere) for g in late],
        [(pair, vector)] * groups
        + [(placed, anywhere), (lines, vector)]
        + [(shape_of((3, half, per_part), bf16), anywhere)] * 2,
        scratch=[
            pltpu.VMEM((rows, width), bf16),
            pltpu.VMEM((width, rows), bf16),
            pltpu.VMEM((rows, width), bf16),
            pltpu.VMEM((width, rows), bf16),
            pltpu.VMEM((rows, 1), f32),
            pltpu.VMEM((rows, width), f32),
            pltpu.VMEM((rows, width), f32),
            pltpu.VMEM((rows, 128), f32),
            pltpu.VMEM((2, width, tile), bf16),
            pltpu.VMEM((2, width, tile), bf16),
            pltpu.VMEM((2, tile, width), bf16),
            pltpu.VMEM((kept, width, tile), bf16),
            pltpu.VMEM((kept, width, tile), bf16),
            pltpu.VMEM((kept, tile, width), bf16),
            pltpu.VMEM((kept, rows, tile), bf16),
            pltpu.VMEM((kept, rows, tile), bf16),
            pltpu.VMEM((kept, rows, tile), bf16),
            pltpu.VMEM((kept, rows, tile), bf16),
            pltpu.VMEM((2, 3, half, tile), bf16),
            pltpu.VMEM((steps, 3, half, tile), bf16),
            pltpu.VMEM((steps, 3, half, tile), bf16),
            pltpu.VMEM((max(1, away), 3, half, tile), bf16),
            pltpu.VMEM((places, CAP, width), bf16),
            pltpu.VMEM((places, CAP, width), bf16),
            pltpu.VMEM((places, 1, CAP), f32),
            pltpu.VMEM((places, 1, CAP), f32),
            pltpu.VMEM((tiles, 3, half, tile), bf16),
            pltpu.VMEM((groups, CAP, width), bf16),
            pltpu.VMEM((groups, CAP, width), bf16),
            dma((2 * places,)), dma((3, 2)), dma((3, kept)), dma((2,)), dma((steps,)),
            dma((max(1, away),)), dma((max(1, away),)),
            dma((places,)), dma((places,)), dma((places,)), dma((places,)),
            dma((tiles,)), dma((tiles,)), dma((tiles,)), dma((tiles,)),
            dma((groups,)), dma((groups,)), dma((places,)),
        ],
        flops=9 * 2 * rows * width * hidden,
        moved=12 * width * hidden + rows * width * 8,
        exps=rows * hidden,
        talks=2,
    )


def slot_sum(targets, source_ref):
    tile = targets.shape[0]
    total = None
    for r in range(source_ref.shape[0]):
        ids = r * CAP + lax.broadcasted_iota(jnp.int32, (tile, CAP), 1)
        choice = jnp.where((ids == targets[:, 0:1]) | (ids == targets[:, 1:2]), 1.0, 0.0)
        part = mm(choice.astype(bf16), source_ref[r])
        total = part if total is None else total + part
    return total


def token_back(
    x1, h2, grad, prob, previous_t, routes, targets, back, dots, dgate_zero, dh_zero, gain, router_t,
    zero_sums,
):
    rows, width = x1.shape
    tile = 128
    tiles = rows // tile
    places = back.shape[0]
    expert_all = prob.shape[1]
    members = lax.axis_size("ctx")
    last = expert_all + 1 + zero_sums.shape[0]

    def body(*refs):
        (x1_ref, h2_ref, dy_ref, prob_ref, prev_ref, route_ref, target_ref) = refs[:7]
        back_ref, dots_ref, dz_ref, dh_ref, gain_ref, router_ref, zero_ref = refs[7:14]
        dx1_ref, sums_ref, da_out, da_near, a_s, a_r, out_sem = refs[14:]
        me = lax.axis_index("ctx")
        peers = [{"ctx": flip(me, 1)}, {"ctx": flip(me, 2)}]
        ready = greet(peers)

        def da_copy(kind, t):
            here = pl.ds(pl.multiple_of(t * tile, tile), tile)
            n = kind * tiles + t
            src, dst = ((0, 1), (0, 2), (2, 3))[kind]
            return remote(
                da_near.at[src, here, :], da_near.at[dst, here, :], a_s.at[n], a_r.at[n],
                {"ctx": flip(me, 2 if kind == 1 else 1)},
            )

        sums_ref[...] = jnp.zeros_like(sums_ref)
        sums_ref[expert_all + 1 : last, :] = zero_ref[...]
        ready()

        def token_rows(t, _):
            here = pl.ds(pl.multiple_of(t * tile, tile), tile)
            prob_now = prob_ref[here, :]
            chosen, target, zero = route_ref[here, :], target_ref[here, :], dz_ref[here, :]
            lanes = lax.broadcasted_iota(jnp.int32, (tile, expert_all), 1)
            dprob = jnp.zeros_like(prob_now)
            for c in range(2):
                dgate = zero[:, c : c + 1]
                for n in range(places):
                    ids = n * CAP + lax.broadcasted_iota(jnp.int32, (tile, CAP), 1)
                    dgate = dgate + jnp.sum(
                        jnp.where(ids == target[:, c : c + 1], dots_ref[n], 0.0),
                        axis=1,
                        keepdims=True,
                    )
                dprob = dprob + jnp.where(lanes == chosen[:, c : c + 1], dgate, 0.0)
            dlogit = prob_now * (dprob - jnp.sum(prob_now * dprob, axis=1, keepdims=True))
            h2 = h2_ref[here, :]
            dh2 = slot_sum(target, back_ref) + dh_ref[here, :] + mm_full(dlogit, router_ref[...])
            x1 = x1_ref[here, :]
            inverse = lax.rsqrt(jnp.mean(x1 * x1, axis=1, keepdims=True) + norm_eps)
            normed = x1 * inverse
            dn = dh2 * gain_ref[...]
            dx1 = dy_ref[here, :].astype(f32) + inverse * (
                dn - normed * jnp.mean(dn * normed, axis=1, keepdims=True)
            )
            dx1_ref[here, :] = dx1
            da_near[0, here, :] = dx1.astype(bf16)
            sums_ref[0:expert_all, :] += mm_full(dlogit, h2, TN)
            sums_ref[expert_all : expert_all + 1, :] += jnp.sum(dh2 * normed, axis=0, keepdims=True)
            sums_ref[last:, 0:expert_all] += mm_full(prev_ref[:, here], dlogit)
            da_copy(1, t).start()
            da_copy(0, t).start()

            @pl.when(t >= 2)
            def _():
                da_copy(1, t - 2).wait_recv()
                da_copy(2, t - 2).start()

            return 0

        lax.fori_loop(0, tiles, token_rows, 0)
        for t in range(max(0, tiles - 2), tiles):
            da_copy(1, t).wait_recv()
            da_copy(2, t).start()
        def da_store(n):
            return pltpu.make_async_copy(da_near.at[n], da_out.at[n], out_sem.at[n])

        da_store(0).start()
        da_store(2).start()
        for t in range(tiles):
            da_copy(0, t).wait()
        da_store(1).start()
        for t in range(tiles):
            da_copy(1, t).wait_send()
            da_copy(2, t).wait()
        da_store(3).start()
        for n in range(members):
            da_store(n).wait()

    return run(
        body,
        (),
        [(a, vector) for a in (x1, h2, grad, prob, previous_t, routes, targets, back, dots)]
        + [(a, vector) for a in (dgate_zero, dh_zero, gain, router_t, zero_sums)],
        [(shape_of((rows, width), f32), vector)]
        + [(shape_of((last + expert_all, width), f32), vector)]
        + [(shape_of((members, rows, width), bf16), anywhere)],
        scratch=[
            pltpu.VMEM((members, rows, width), bf16),
            dma((3 * tiles,)), dma((3 * tiles,)), dma((members,)),
        ],
        flops=2 * rows * width * (places * CAP + width),
        moved=rows * width * 24,
        talks=5,
    )


def finish(dqkv_all, h1, x, gain, dx1, weights_t, out_sum, small, tops, produced, base, targets):
    members, per_group = weights_t.shape[1], weights_t.shape[2]
    rows, width = x.shape
    group_rows = dqkv_all.shape[0]
    parts, groups = lax.axis_size("dp"), lax.axis_size("exp")
    team = parts * groups
    local = produced[0].shape[0]
    places = groups * local
    wide_share, out_share = width // (2 * team), per_group // team
    small_rows = small.shape[0]
    small_steps = [(axis, bit) for axis in ("ctx", "dp", "exp") for bit in powers(axis)]
    hops = len(small_steps)
    row_tile = min(256, rows)

    def body(*refs):
        it = iter(refs)

        def take(count=None):
            return next(it) if count is None else [next(it) for _ in range(count)]

        dqkv_hbm, h1_hbm, x_hbm, gain_ref, dx1_hbm, w_hbm, out_ref = take(7)
        small_ref, tops_ref, base_hbm, target_ref = take(4)
        produced_hbm = take(groups)
        input_out, wide_out, flat_out, small_out, gain_out, tops_out, result_out = take(7)
        dqkv, product, h1_all, x_all, dx1_all, w_all, base_all, y_near = take(8)
        part_send, part_core, part_y, y_got, part_own = take(5)
        wide_mine, wide_far_x, wide_far_z, wide_all = take(4)
        flat_mine, flat_far_x, flat_far_z, flat_all = take(4)
        small_acc, small_far, gain_acc, gain_far, tops_acc, tops_far = take(6)
        load_sem, near_s, near_r = take(3)
        wide_sems, flat_sems = [take(12), take(12)], take(12)
        hop_s, hop_r, gain_s, gain_r, top_s, top_r = take(6)

        me = lax.axis_index("ctx")
        dp_now, exp_now = lax.axis_index("dp"), lax.axis_index("exp")
        seat = dp_now * groups + exp_now

        def near_peer(j):
            return {"ctx": flip(me, j)}

        def team_peer(r):
            return {"dp": flip(dp_now, r // groups), "exp": flip(exp_now, r % groups)}

        peers = [near_peer(j) for j in range(1, members)]
        peers += [team_peer(r) for r in range(1, team)]
        ready = greet(peers)

        loads = [
            (dqkv_hbm, dqkv), (h1_hbm, h1_all), (x_hbm, x_all), (dx1_hbm, dx1_all),
            (w_hbm.at[:, me], w_all), (base_hbm, base_all),
        ]
        loads += [
            (produced_hbm[g], y_near.at[pl.ds(g * local, local)]) for g in range(groups)
        ]

        def load(n):
            return pltpu.make_async_copy(loads[n][0], loads[n][1], load_sem.at[n])

        class Dense:
            def __init__(self, mine, far_x, far_z, all_buf, sems):
                self.mine, self.far_x, self.far_z, self.all = mine, far_x, far_z, all_buf
                self.sems = sems

            def own_block(self, d=0):
                return pl.ds(flip(dp_now, d) * groups, groups)

            def x_copy(self, d):
                return remote(
                    self.mine.at[self.own_block(d)], self.far_x.at[d - 1], self.sems[0].at[d],
                    self.sems[1].at[d], {"dp": flip(dp_now, d)},
                )

            def z_copy(self, g):
                return remote(
                    self.mine.at[dp_now * groups + flip(exp_now, g)], self.far_z.at[g - 1],
                    self.sems[2].at[g], self.sems[3].at[g], {"exp": flip(exp_now, g)},
                )

            def gz_copy(self, g, theirs=False):
                spot = self.all.at[0, dp_now * groups + flip(exp_now, g) if theirs else seat]
                return remote(
                    spot, spot, self.sems[4].at[g], self.sems[5].at[g], {"exp": flip(exp_now, g)}
                )

            def gx_copy(self, d, theirs=False):
                spot = self.all.at[0, self.own_block(d if theirs else 0)]
                return remote(
                    spot, spot, self.sems[6].at[d], self.sems[7].at[d], {"dp": flip(dp_now, d)}
                )

            def y_copy(self, d):
                return remote(
                    self.all.at[0, self.own_block(d)], self.all.at[2, self.own_block(d)],
                    self.sems[8].at[d], self.sems[9].at[d], near_peer(2),
                )

            def core_copy(self, n):
                return remote(
                    self.all.at[2 * n], self.all.at[2 * n + 1], self.sems[10].at[n],
                    self.sems[11].at[n], near_peer(1),
                )

            def start(self):
                for d in range(1, parts):
                    self.x_copy(d).start()

            def to_z(self):
                for d in range(1, parts):
                    self.x_copy(d).wait()
                for g in list(range(1, groups)) + [0]:
                    c = dp_now * groups + flip(exp_now, g)
                    value = self.mine[c].astype(f32)
                    for d in range(1, parts):
                        value = value + self.far_x[d - 1, flip(exp_now, g)].astype(f32)
                    self.mine[c] = value.astype(bf16)
                for g in range(1, groups):
                    self.z_copy(g).start()

            def to_gather(self):
                for g in range(1, groups):
                    self.z_copy(g).wait()
                value = self.mine[seat].astype(f32)
                for g in range(1, groups):
                    value = value + self.far_z[g - 1].astype(f32)
                self.all[0, seat] = value.astype(bf16)

            def gather(self):
                for g in range(1, groups):
                    self.gz_copy(g).start()

            def to_x(self):
                for g in range(1, groups):
                    self.gz_copy(g).wait_send()
                    self.gz_copy(g, True).wait_recv()
                for d in range(1, parts):
                    self.gx_copy(d).start()
                self.y_copy(0).start()

            def to_y(self):
                for d in range(1, parts):
                    self.gx_copy(d).wait_send()
                    self.gx_copy(d, True).wait_recv()
                    self.y_copy(d).start()
                self.core_copy(0).start()

            def to_core(self):
                for d in range(parts):
                    self.y_copy(d).wait()
                self.core_copy(1).start()

            def done(self):
                for n in range(2):
                    self.core_copy(n).wait()

        wides = [
            Dense(wide_mine.at[n], wide_far_x.at[n], wide_far_z.at[n], wide_all.at[n], wide_sems[n])
            for n in range(2)
        ]
        flat = Dense(flat_mine, flat_far_x, flat_far_z, flat_all, flat_sems)

        def hop_peer(n):
            axis, bit = small_steps[n]
            return {axis: flip(lax.axis_index(axis), bit)}

        def small_copy(n):
            return remote(small_acc.at[n], small_far.at[n], hop_s.at[n], hop_r.at[n], hop_peer(n))

        def tops_copy(n):
            return remote(tops_acc.at[n], tops_far.at[n], top_s.at[n], top_r.at[n], hop_peer(n))

        def gain_pack(j, theirs=False):
            spot = gain_acc.at[flip(me, j) if theirs else me]
            return remote(spot, spot, gain_s.at[j], gain_r.at[j], near_peer(j))

        def gain_team(r, theirs=False):
            spot = gain_far.at[flip(seat, r) if theirs else seat]
            n = members + r
            return remote(spot, spot, gain_s.at[n], gain_r.at[n], team_peer(r))

        def small_start(n):
            small_copy(n).start()
            tops_copy(n).start()

        def small_sum(n):
            small_copy(n).wait()
            tops_copy(n).wait()
            small_acc[n + 1] = small_acc[n] + small_far[n]
            tops_acc[n + 1] = jnp.maximum(tops_acc[n], tops_far[n])

        small_hops = list(range(hops))

        def small_next():
            if small_hops:
                n = small_hops.pop(0)
                small_sum(n)
                if n + 1 < hops:
                    small_start(n + 1)

        row_tiles = rows // row_tile

        def tile_rows(t, first=0):
            return pl.ds(first + t * row_tile, row_tile)

        def core_part(j, t):
            n = j // 2
            return remote(
                part_send.at[n, tile_rows(t), :], part_core.at[n, tile_rows(t), :],
                near_s.at[n * row_tiles + t], near_r.at[n * row_tiles + t], near_peer(1),
            )

        def y_part(t):
            n = 2 * row_tiles + t
            return remote(
                part_y.at[tile_rows(t), :], y_got.at[tile_rows(t), :], near_s.at[n], near_r.at[n],
                near_peer(2),
            )

        def part(j, t):
            here = pl.ds(j * rows + t * row_tile, row_tile)
            found = None
            for w in range(3):
                add = mm(dqkv[here, w * per_group : (w + 1) * per_group], w_all[w])
                found = add if found is None else found + add
            return found

        for n in range(len(loads)):
            load(n).start()
        small_acc[0] = small_ref[...]
        lanes = lax.broadcasted_iota(jnp.int32, tops_acc.shape[1:], 1)
        tops_acc[0] = jnp.where(
            lanes == me, jnp.max(tops_ref[...], axis=1, keepdims=True), low_start
        )
        flat_rows = out_ref[...].astype(f32)
        for c in range(team):
            flat_mine[c] = flat_rows[c * out_share : (c + 1) * out_share, :].astype(bf16)
        ready()
        flat.start()
        small_start(0)
        load(0).wait()
        load(1).wait()

        def weigh(n, _):
            here = pl.ds(pl.multiple_of(n * rows, rows), rows)
            product[...] += mm(h1_all[here, :], dqkv[here, :], TN)
            return 0

        product[...] = mm(h1_all[0:rows, :], dqkv[0:rows, :], TN)
        lax.fori_loop(1, group_rows // rows, weigh, 0)
        for n in range(2):
            for c in range(team):
                at = (n * team + c) * wide_share
                wide_mine[n, c] = product[at : at + wide_share, :].astype(bf16)
            if n:
                wides[0].start()
        flat.to_z()
        wides[1].start()
        for n in range(2, len(loads)):
            load(n).wait()
        queue = [(j, t) for j in (3, 1) for t in range(row_tiles)]
        for n, (j, t) in enumerate(queue):
            part_send[j // 2, tile_rows(t), :] = part(j, t).astype(bf16)
            if n:
                core_part(*queue[n - 1]).start()
        own_part = [part(2, t) for t in range(1)]
        core_part(*queue[-1]).start()
        for t in range(row_tiles):
            value = own_part[0] if t == 0 else part(2, t)
            core_part(3, t).wait_recv()
            part_y[tile_rows(t), :] = (
                value + part_core[1, tile_rows(t), :].astype(f32)
            ).astype(bf16)
            if t:
                y_part(t - 1).start()
        part_own[tile_rows(0), :] = part(0, 0)
        y_part(row_tiles - 1).start()
        for t in range(1, row_tiles):
            part_own[tile_rows(t), :] = part(0, t)
        wides[0].to_z()
        flat.to_gather()
        small_next()
        wides[1].to_z()
        flat.gather()
        wides[0].to_gather()

        def token_rows(t, _):
            here = pl.ds(pl.multiple_of(t * 128, 128), 128)
            result_out[here, :] = (
                base_all[here, :] + slot_sum(target_ref[here, :], y_near)
            ).astype(bf16)
            return 0

        lax.fori_loop(0, rows // 256, token_rows, 0)
        wides[0].gather()
        small_next()
        flat.to_x()
        wides[1].to_gather()
        lax.fori_loop(rows // 256, rows // 128, token_rows, 0)
        wides[1].gather()
        wides[0].to_x()
        small_next()
        for t in range(row_tiles):
            core_part(1, t).wait()
            core_part(3, t).wait_send()
            y_part(t).wait()

        def input_rows(t, gain_part):
            here = pl.ds(pl.multiple_of(t * row_tile, row_tile), row_tile)
            dh = (
                part_own[here, :] + part_core[0, here, :].astype(f32) + y_got[here, :].astype(f32)
            )
            x_now = x_all[here, :].astype(f32)
            inv = lax.rsqrt(jnp.mean(x_now * x_now, axis=1, keepdims=True) + norm_eps)
            normed = x_now * inv
            dn = dh * gain_ref[...]
            dx1_all[here, :] = dx1_all[here, :] + inv * (
                dn - normed * jnp.mean(dn * normed, axis=1, keepdims=True)
            )
            return gain_part + jnp.sum(dh * normed, axis=0, keepdims=True)

        gain_acc[me] = lax.fori_loop(
            0, rows // row_tile, input_rows, jnp.zeros((1, width), f32)
        )
        store = pltpu.make_async_copy(dx1_all, input_out, load_sem.at[len(loads)])
        store.start()
        flat.to_y()
        for j in range(1, members):
            gain_pack(j).start()
        wides[1].to_x()
        wides[0].to_y()
        for j in range(1, members):
            gain_pack(j).wait_send()
            gain_pack(j, True).wait_recv()
        value = gain_acc[0]
        for n in range(1, members):
            value = value + gain_acc[n]
        gain_far[seat] = value
        small_next()
        flat.to_core()
        for r in range(1, team):
            gain_team(r).start()
        wides[1].to_y()
        wides[0].to_core()
        while small_hops:
            small_next()
        flat.done()
        wides[1].to_core()
        for r in range(1, team):
            gain_team(r).wait_send()
            gain_team(r, True).wait_recv()
        value = gain_far[0]
        for n in range(1, team):
            value = value + gain_far[n]
        gain_out[...] = value[0]
        final = [pltpu.make_async_copy(flat_all, flat_out, load_sem.at[len(loads) + 1])]
        for n in range(2):
            wides[n].done()
            final.append(
                pltpu.make_async_copy(
                    wide_all.at[n], wide_out.at[n], load_sem.at[len(loads) + 2 + n]
                )
            )
        for copy in final:
            copy.start()
        small_out[...] = small_acc[hops]
        tops_out[...] = tops_acc[hops]
        store.wait()
        for copy in final:
            copy.wait()

    def dense_scratch(share, across, lead=()):
        return [
            pltpu.VMEM(lead + (team, share, across), bf16),
            pltpu.VMEM(lead + (max(1, parts - 1), groups, share, across), bf16),
            pltpu.VMEM(lead + (max(1, groups - 1), share, across), bf16),
            pltpu.VMEM(lead + (members, team, share, across), bf16),
        ]

    dense_sem = (
        [dma((parts,))] * 2 + [dma((groups,))] * 4 + [dma((parts,))] * 4 + [dma((2,))] * 2
    )
    wide_rows = shape_of((rows, width), f32)
    return run(
        body,
        (),
        [(dqkv_all, anywhere), (h1, anywhere), (x, anywhere), (gain, vector), (dx1, anywhere)]
        + [(weights_t, anywhere), (out_sum, vector), (small, vector), (tops, vector)]
        + [(base, anywhere), (targets, vector)]
        + [(a, anywhere) for a in produced],
        [
            (wide_rows, anywhere),
            (shape_of((2, members, team, wide_share, 3 * per_group), bf16), anywhere),
            (shape_of((members, team, out_share, width), bf16), anywhere),
            (shape_of((small_rows, width), f32), vector),
            (shape_of((width,), f32), vector),
            (shape_of((tops.shape[0], 128), f32), vector),
            (shape_of((rows, width), bf16), vector),
        ],
        scratch=[
            pltpu.VMEM((group_rows, 3 * per_group), bf16),
            pltpu.VMEM((width, 3 * per_group), f32),
            pltpu.VMEM((group_rows, width), bf16),
            pltpu.VMEM((rows, width), bf16),
            pltpu.VMEM((rows, width), f32),
            pltpu.VMEM((3, per_group, width), bf16),
            pltpu.VMEM((rows, width), f32),
            pltpu.VMEM((places, CAP, width), bf16),
            pltpu.VMEM((2, rows, width), bf16),
            pltpu.VMEM((2, rows, width), bf16),
            pltpu.VMEM((rows, width), bf16),
            pltpu.VMEM((rows, width), bf16),
            pltpu.VMEM((rows, width), f32),
        ]
        + dense_scratch(wide_share, 3 * per_group, (2,))
        + dense_scratch(out_share, width)
        + [pltpu.VMEM((hops + 1, small_rows, width), f32), pltpu.VMEM((hops, small_rows, width), f32)]
        + [pltpu.VMEM((members, 1, width), f32), pltpu.VMEM((team, 1, width), f32)]
        + [pltpu.VMEM((hops + 1, tops.shape[0], 128), f32), pltpu.VMEM((hops, tops.shape[0], 128), f32)]
        + [dma((12 + places,))] + [dma((3 * (rows // row_tile),))] * 2
        + dense_sem * 3
        + [dma((hops,))] * 2
        + [dma((members + team,))] * 2
        + [dma((hops,))] * 2,
        flops=4 * 2 * rows * width * width * 3,
        moved=20 * 1024 * 1024,
        talks=3,
    )


def place_experts(meta, near, begun):
    _, half, columns = near[0].shape
    tile = 128
    tiles = half // tile
    count = 3

    def body(meta_ref, *refs):
        outs = refs[2 * count + count :]
        for j in range(2):

            @pl.when(pl.program_id(0) == j)
            def _():
                for n in range(count):
                    piece = refs[n * 2 + j][0].astype(f32)
                    outs[n][0] = jnp.transpose(piece) if n == 2 else piece

    def in_spec(which, j):
        def index(c, t, m):
            return (which, jnp.where(c == j, t, jnp.where(c < j, 0, tiles - 1)), 0)

        return pl.BlockSpec((1, tile, columns), index)

    flat = pl.BlockSpec((1, tile, columns), lambda c, t, m: (m[3] ^ 1, (m[2] ^ c) * tiles + t, 0))
    turned = pl.BlockSpec((1, columns, tile), lambda c, t, m: (m[3] ^ 1, 0, (m[2] ^ c) * tiles + t))
    return run(
        body,
        (2, tiles),
        [(near[j], in_spec(n, j)) for n in range(count) for j in range(2)]
        + [(a, anywhere) for a in begun],
        [
            (shape_of(a.shape, f32), turned if n == 2 else flat)
            for n, a in enumerate(begun)
        ],
        meta=meta,
        moved=count * 2 * half * columns * 6,
        aliases={1 + 2 * count + n: n for n in range(count)},
    )


def place_dense(meta, near, flat, tops, small, w_qkv, kinds):
    _, members, team, share, lanes = near.shape
    per_group = lanes // 3
    half = team * share
    width = 2 * half
    rows_all = flat.shape[1] * flat.shape[2]
    step = 8 // math.gcd(share, 8)
    while team // step > 4:
        step *= 2
    per_half = team // step
    tall = step * share

    heads = HEADS // members
    head_width = width // HEADS
    expert_all = (small.shape[0] - 1 - 3 * kinds) // 2
    at_vec = expert_all + 1
    at_logit = at_vec + kinds
    at_carry = at_logit + 2 * kinds

    def body(meta_ref, near_ref, flat_ref, tops_ref, small_ref, w_ref, *outs):
        out_ref, flat_out, clip_ref, router_out, norm_out, vec_out, logit_out, carry_out = outs[:8]
        scale_ref = outs[8]

        @pl.when((pl.program_id(0) == 0) & (pl.program_id(1) == 0))
        def _():
            lanes = lax.broadcasted_iota(jnp.int32, (1, width), 1)
            scale = jnp.zeros((1, width), f32)
            for n in range(HEADS):
                top = tops_ref[n % heads : n % heads + 1, n // heads : n // heads + 1]
                ratio = jnp.sqrt(jnp.minimum(1.0, clip_limit / top))
                inside = (lanes >= n * head_width) & (lanes < (n + 1) * head_width)
                scale = jnp.where(inside, ratio, scale)
            scale_ref[...] = scale
            router_out[...] = small_ref[0:expert_all, :]
            norm_out[...] = small_ref[expert_all, :]
            vec_out[...] = small_ref[at_vec : at_vec + kinds, :]
            for n in range(kinds):
                logit_out[n] = small_ref[at_logit + 2 * n : at_logit + 2 * n + 2, :]
            carry_out[...] = small_ref[at_carry:, 0:expert_all]

        for c in range(step):
            pieces = [near_ref[0, meta_ref[0] ^ g, c] for g in range(members)]
            for w in range(3):
                at = slice(w * per_group, (w + 1) * per_group)
                out_ref[w, c * share : (c + 1) * share, :] = jnp.concatenate(
                    [piece[:, at] for piece in pieces], axis=1
                ).astype(f32)
        clip_ref[...] = w_ref[...].astype(f32) * scale_ref[...]

        @pl.when(pl.program_id(1) == 0)
        def _():
            for c in range(team):
                at = slice(c * flat.shape[2], (c + 1) * flat.shape[2])
                for j in range(2):
                    member = pl.program_id(0) * 2 + j
                    flat_out[j, at, :] = flat_ref[meta_ref[0] ^ member, c].astype(f32)

    square = shape_of((3, width, width), f32)
    return run(
        body,
        (2, per_half),
        [
            (
                near,
                pl.BlockSpec((1, members, step, share, lanes), lambda n, c, m: (n, 0, c, 0, 0)),
            ),
            (flat, whole(flat)),
            (tops, whole(tops)),
            (small, whole(small)),
            (w_qkv, pl.BlockSpec((2, tall, width), lambda n, c, m: (0, n * per_half + c, 0))),
        ],
        [
            (square, pl.BlockSpec((3, tall, width), lambda n, c, m: (0, n * per_half + c, 0))),
            (
                shape_of((members, rows_all, width), f32),
                pl.BlockSpec((2, rows_all, width), lambda n, c, m: (n, 0, 0)),
            ),
            (
                shape_of((2, width, width), f32),
                pl.BlockSpec((2, tall, width), lambda n, c, m: (0, n * per_half + c, 0)),
            ),
        ]
        + [
            (o, whole(o))
            for o in (
                shape_of((expert_all, width), f32),
                shape_of((width,), f32),
                shape_of((kinds, width), f32),
                shape_of((kinds, 2, width), f32),
                shape_of((expert_all, expert_all), f32),
            )
        ],
        scratch=[pltpu.VMEM((1, width), f32)],
        meta=meta,
        moved=square.size * 12,
    )


def shards(
    inputs,
    lengths,
    block_order,
    routes,
    prev_logits,
    norm1_gain,
    norm2_gain,
    w_qkv,
    w_out,
    w_router,
    w_carry,
    const_logit_w,
    const_vec,
    w_gate,
    w_up,
    w_down,
    cotangent,
):
    members = lax.axis_size("ctx")
    groups = lax.axis_size("exp")
    parts = lax.axis_size("dp")
    me = lax.axis_index("ctx")
    mine = lax.axis_index("exp")
    x, grad = inputs[0], cotangent[0]
    rows, width = x.shape
    group_rows = rows * members
    deal_block = group_rows // block_order.shape[1]
    per_member = rows // deal_block
    local = w_gate.shape[0]
    expert_count = local * groups
    head_width = width // HEADS
    heads = HEADS // members
    per_group = heads * head_width
    blocks = block_order.shape[1]
    layout = {
        "order": 4, "lengths": 4 + blocks, "sequences": lengths.shape[1],
        "inverse": 4 + blocks + lengths.shape[1], "sides": local,
    }
    numbers = jnp.arange(blocks, dtype=jnp.int32)
    given = jnp.sum(jnp.where(block_order[0][None, :] == numbers[:, None], numbers[None, :], 0), axis=1)
    inverse = (((given // per_member) ^ me) * per_member + given % per_member).astype(jnp.int32)
    meta = jnp.concatenate(
        [
            jnp.stack([me, mine, me % 2, me // 2]).astype(jnp.int32),
            block_order[0],
            lengths[0],
            inverse,
        ]
    )
    gain1, gain2 = norm1_gain, norm2_gain
    w_out_parts = w_out.reshape(members, per_group, width)
    previous_t = jnp.transpose(prev_logits[0])
    router_t = jnp.transpose(w_router)
    odd = [r for r in range(groups * local) if r % local]

    begun = begin(x, grad, jnp.transpose(routes[0]), gain1, w_qkv, local)
    q, k, v, kt, vt, h1, weights_t, targets, target_rows, route_ids, grad_near = begun[:11]
    grad_rest = begun[11:]
    weights_t = weights_t.reshape(3, members, per_group, width)
    grad_late = [slot_swap(grad_rest[n], r, local) for n, r in enumerate(odd)]
    o, ot, lse, tops = attend(meta, q, k, vt, deal_block, layout)
    logit_rows = jnp.swapaxes(const_logit_w, 1, 2).reshape(-1, width)
    x1, h2, prob, token_near, gate_near, base, dh_zero, dgate_zero, zero_sums = token_front(
        x, o, w_out_parts, gain2, router_t, previous_t, w_carry, target_rows, grad, route_ids,
        logit_rows, const_vec, local,
    )
    worked = expert_layer(token_near, grad_near, grad_late, gate_near, w_gate, w_up, w_down)
    produced = worked[:groups]
    token_back_rows, dots, expert_sum, beside = worked[groups:]
    dx1, small, da_near = token_back(
        x1, h2, grad, prob, previous_t, route_ids, targets, token_back_rows, dots, dgate_zero,
        dh_zero, gain2, router_t, zero_sums,
    )
    expert_now, da_near = lax.optimization_barrier((expert_sum, da_near))
    over = swap(expert_now, "ctx", 2)
    y_near = [swap(produced[g], "exp", g) if g else produced[0] for g in range(groups)]
    dqkv, out_sum, *begun_grads = attend_back(
        meta, q, k, v, kt, da_near, w_out_parts, ot, lse, deal_block, layout, (expert_sum, beside)
    )

    input_grad, qkv_near, out_near, small, norm1_grad, top_all, result = finish(
        dqkv, h1, x, gain1, dx1, weights_t, out_sum, small, tops, y_near, base, targets
    )
    over, qkv_near = lax.optimization_barrier((over, qkv_near))
    corner = swap(over, "ctx", 1)
    dense = place_dense(meta, qkv_near, out_near, top_all, small, w_qkv, const_vec.shape[0])
    qkv_grad, out_grad, clipped, router_grad, norm2_grad, vec_grad, logit_grad, carry_grad = dense
    router_grad, logit_grad = jnp.transpose(router_grad), jnp.swapaxes(logit_grad, 1, 2)
    out_grad = out_grad.reshape(width, width)
    gate_grad, up_grad, down_grad = place_experts(meta, (over, corner), begun_grads)
    return (
        result[None],
        input_grad[None],
        norm1_grad,
        norm2_grad,
        qkv_grad,
        out_grad,
        router_grad,
        carry_grad,
        logit_grad,
        vec_grad,
        gate_grad,
        up_grad,
        down_grad,
        clipped,
    )


def solution(mesh):
    tokens = P(("dp", "exp"), "ctx", None)
    packs = P(("dp", "exp"), None)
    experts = P("exp", None, None)
    in_specs = (
        tokens, packs, packs, tokens, tokens, P(), P(), P(), P(), P(), P(), P(), P(),
        experts, experts, experts, tokens,
    )
    out_specs = (
        tokens, tokens, P(), P(), P(), P(), P(), P(), P(), P(),
        P("exp", None, "dp"), P("exp", None, "dp"), P("exp", "dp", None), P(),
    )
    return jax.shard_map(shards, mesh=mesh, in_specs=in_specs, out_specs=out_specs, check_vma=False)
```
